32 devices in a mesh: dp: 8 (over z, x), patch: 4 (over y, core).
Axes of the slice: x: 2, y: 2, z: 4, core: 2. Of those that a mesh axis runs over, the one named last changes fastest.
Arguments:
- text_in: bfloat16 [2, 16384, 768], P(None, ('dp', 'patch')), may hold values from -6 to 6
- image_grid: bfloat16 [2, 128, 144, 1024], P(None, 'dp', 'patch'), may hold values from -6 to 6
- image_cls: bfloat16 [2, 128, 1024], P(None, ('dp', 'patch')), may hold values from -6 to 6
- text_lengths: int32 [2, 128], P(None, ('dp', 'patch')), may hold values from 8 to 128, as said below
- phrase_counts: int32 [2, 128], P(None, ('dp', 'patch')), may hold values from 0 to 6, as said below
- phrase_boxes: int32 [2, 128, 6, 144], P(None, ('dp', 'patch')), may hold values from 0 to 1, as said below
- cotangent: bfloat16 [2, 16384, 768], P(None, ('dp', 'patch')), may hold values from -6 to 6
- self_qkv: bfloat16 [768, 2304], P('dp', 'patch'), may hold values from -0.21875 to 0.21875
- self_out: bfloat16 [768, 768], P('dp', 'patch'), may hold values from -1.75 to 1.75
- cross_q: bfloat16 [768, 768], P('dp', 'patch'), may hold values from -0.21875 to 0.21875
- cross_kv: bfloat16 [1024, 1536], P('dp', 'patch'), may hold values from -0.1875 to 0.1875
- cross_out: bfloat16 [768, 768], P('dp', 'patch'), may hold values from -0.875 to 0.875
- ffn_in: bfloat16 [768, 3072], P('dp', 'patch'), may hold values from -0.21875 to 0.21875
- ffn_out: bfloat16 [3072, 768], P('dp', 'patch'), may hold values from -0.109375 to 0.109375
- vectors: bfloat16 [13, 768], P(None, 'dp'), as said below
- ffn_bias_in: bfloat16 [3072], P('dp'), may hold values from -3 to 3
Outputs:
- layer_out: float32 [2, 16384, 768], P(None, ('dp', 'patch'))
- text_grad: float32 [2, 16384, 768], P(None, ('dp', 'patch'))
- grid_grad: float32 [2, 128, 144, 1024], P(None, 'dp', 'patch')
- cls_grad: float32 [2, 128, 1024], P(None, ('dp', 'patch'))
- self_qkv_grad: float32 [768, 2304], P('dp', 'patch')
- self_out_grad: float32 [768, 768], P('dp', 'patch')
- cross_q_grad: float32 [768, 768], P('dp', 'patch')
- cross_kv_grad: float32 [1024, 1536], P('dp', 'patch')
- cross_out_grad: float32 [768, 768], P('dp', 'patch')
- ffn_in_grad: float32 [768, 3072], P('dp', 'patch')
- ffn_out_grad: float32 [3072, 768], P('dp', 'patch')
- vectors_grad: float32 [13, 768], P(None, 'dp')
- ffn_bias_in_grad: float32 [3072], P('dp')
The draws below stay inside these ranges and needn't reach their ends.
Inputs may be any that keep to these rules, and one draw needn't show every extreme that they name: `text_lengths`: the first item of every micro-batch has 128 positions. `phrase_counts`: the second item of every micro-batch has 6 phrases. `phrase_boxes`: cells are row-major over a 12 by 12 grid; each phrase's box is a rectangle of one or more whole cells. `vectors`: rows 3, 8 and 11 are gains near one; the other rows are biases.
All inputs are finite; a program needn't handle non-finite values.
Results may differ from the reference program's by a relative error of at most 0.02.
Values may be sent and summed in bfloat16 or wider, within the bound.
No kernel may reach another device: no remote copies, remote signals or barrier semaphores. Data moves between devices by JAX's collectives and lax.ppermute only.
A program may use at most 256 MiB of HBM per device.

```python
import jax
import jax.numpy as jnp
from jax import lax

D = 768
HEADS = 12
HEAD = 64
FF = 3072
VIS = 1024
GRID_SIDE = 12
GRID = 144
LEN = 128
PHRASES = 6
MICRO = 2
ITEMS = 128
TOKENS = 16384


def draw_text_lengths(key, part):
    raw_draw = jax.random.randint(key, (MICRO, ITEMS), 0, LEN - 7)
    lengths = 8 + raw_draw * raw_draw // (LEN - 8)
    return lengths.at[:, 0].set(LEN).astype(jnp.int32)


def draw_phrase_counts(key, part):
    raw_draw = jax.random.randint(key, (MICRO, ITEMS), 0, PHRASES + 1)
    counts = raw_draw * raw_draw // PHRASES
    return counts.at[:, 1].set(PHRASES).astype(jnp.int32)


def draw_phrase_boxes(key, part):
    subkeys = jax.random.split(key, 4)
    box_shape = (MICRO, ITEMS, PHRASES)
    col_start = jax.random.randint(subkeys[0], box_shape, 0, GRID_SIDE)
    row_start = jax.random.randint(subkeys[1], box_shape, 0, GRID_SIDE)
    col_span = 1 + jax.random.randint(subkeys[2], box_shape, 0, (GRID_SIDE + 1) // 2)
    row_span = 1 + jax.random.randint(subkeys[3], box_shape, 0, (GRID_SIDE + 1) // 2)
    cell_ids = jnp.arange(GRID, dtype=jnp.int32)
    col_of = cell_ids % GRID_SIDE
    row_of = cell_ids // GRID_SIDE
    inside = (col_of >= col_start[..., None]) & (col_of < col_start[..., None] + col_span[..., None])
    inside = inside & (row_of >= row_start[..., None]) & (row_of < row_start[..., None] + row_span[..., None])
    return inside.astype(jnp.int32)


def draw_vectors(key, part):
    base_draw = jax.random.normal(key, (13, D), jnp.float32)
    row_ids = jnp.arange(13)[:, None]
    is_gain = (row_ids == 3) | (row_ids == 8) | (row_ids == 11)
    return jnp.where(is_gain, 1.0 + 0.15 * base_draw, 0.3 * base_draw).astype(jnp.bfloat16)


def block_scale(own_key, dims, cuts, smallest, largest):
    loudness, own = 1.0, jax.random.fold_in(own_key, 6)
    for axis_at, blocks in cuts:
        draws = jnp.exp(jax.random.uniform(jax.random.fold_in(own, axis_at), (blocks,), jnp.float32, smallest / len(cuts), largest / len(cuts)))
        loudness = loudness * jnp.repeat(draws, dims[axis_at] // blocks).reshape([-1 if axis == axis_at else 1 for axis in range(len(dims))])
    return loudness


def normal_values(key, extent, deviation, bound, shards=(), held_as=jnp.bfloat16):
    factor_of = block_scale(key, extent, shards, -0.22, 0.18) if shards else 1.0
    entries = jax.random.normal(key, extent, jnp.float32) * deviation * factor_of
    return jnp.minimum(jnp.maximum(entries, -bound), bound).astype(held_as)


def setup_inputs(seed: int = 0) -> dict:
    splits = jax.random.split(jax.random.key(seed), 17)
    return {
        "text_in": normal_values(splits[0], (MICRO, TOKENS, D), 1.0, 6.0, ((1, 32),)),
        "image_grid": normal_values(splits[1], (MICRO, ITEMS, GRID, VIS), 1.0, 6.0, ((1, 8), (2, 4))),
        "image_cls": normal_values(splits[2], (MICRO, ITEMS, VIS), 1.0, 6.0, ((1, 32),)),
        "text_lengths": draw_text_lengths(jax.random.fold_in(splits[16], 71), 0),
        "phrase_counts": draw_phrase_counts(jax.random.fold_in(splits[16], 71), 0),
        "phrase_boxes": draw_phrase_boxes(jax.random.fold_in(splits[16], 71), 0),
        "cotangent": normal_values(splits[6], (MICRO, TOKENS, D), 1.0, 6.0, ((1, 32),)),
        "self_qkv": normal_values(splits[7], (D, 3 * D), D ** -0.5, 0.21875, ((0, 8), (1, 4))),
        "self_out": normal_values(splits[8], (D, D), (D // 64) ** -0.5, 1.75, ((0, 8), (1, 4))),
        "cross_q": normal_values(splits[9], (D, D), D ** -0.5, 0.21875, ((0, 8), (1, 4))),
        "cross_kv": normal_values(splits[10], (VIS, 2 * D), VIS ** -0.5, 0.1875, ((0, 8), (1, 4))),
        "cross_out": normal_values(splits[11], (D, D), (D // 16) ** -0.5, 0.875, ((0, 8), (1, 4))),
        "ffn_in": normal_values(splits[12], (D, FF), D ** -0.5, 0.21875, ((0, 8), (1, 4))),
        "ffn_out": normal_values(splits[13], (FF, D), FF ** -0.5, 0.109375, ((0, 8), (1, 4))),
        "vectors": draw_vectors(jax.random.fold_in(splits[16], 71), 0),
        "ffn_bias_in": normal_values(splits[15], (FF,), 0.5, 3.0, ((0, 8),)),
    }


HIGH = lax.Precision.HIGHEST
EPS = 1e-06
NEG = -1e+30

@jax.custom_vjp
def low(v):
    return lax.optimization_barrier(v.astype(jnp.bfloat16)).astype(jnp.float32)

@jax.custom_vjp
def low_back(v):
    return v

def low_keep(v):
    return (low(v), None)

def low_pass(kept, grad):
    return (grad,)

def back_keep(v):
    return (v, None)

def back_low(kept, grad):
    return (low(grad),)
low.defvjp(low_keep, low_pass)
low_back.defvjp(back_keep, back_low)

def layer_norm(total_in, gain_row, shift_row):
    center = total_in - lax.optimization_barrier(jnp.mean(total_in, -1, keepdims=True))
    spread = lax.rsqrt(lax.optimization_barrier(jnp.mean(center * center, -1, keepdims=True)) + EPS)
    return center * spread * gain_row + shift_row

def self_allowed(lengths, length_max):
    positions = jnp.arange(length_max, dtype=jnp.int32)
    key_ok = positions[None, :] < lengths[:, None]
    return jnp.broadcast_to(key_ok[:, None, :], (lengths.shape[0], length_max, length_max))

def cross_allowed(lengths, counts, boxes, length_max):
    positions = jnp.arange(length_max, dtype=jnp.int32)[None, :]
    uses_box = (counts[:, None] > 0) & (positions < lengths[:, None])
    phrase_of = jnp.where(uses_box, positions * counts[:, None] // lengths[:, None], 0)
    phrase_ids = jnp.arange(boxes.shape[1], dtype=jnp.int32)
    chosen = phrase_of[:, :, None] == phrase_ids[None, None, :]
    in_box = jnp.any(chosen[:, :, :, None] & (boxes[:, None] > 0), axis=2)
    grid_ok = jnp.where(uses_box[:, :, None], in_box, True)
    cls_column = jnp.ones(grid_ok.shape[:2] + (1,), dtype=jnp.bool_)
    return jnp.concatenate([cls_column, grid_ok], -1)

def attend(queries, key_in, values, allowed):
    scores = jnp.einsum('iqhd,ikhd->ihqk', queries, key_in, precision=HIGH) * HEAD ** (-0.5)
    scores = low_back(scores)
    scores = jnp.where(allowed[:, None], scores, NEG)
    top_score = lax.optimization_barrier(jnp.max(scores, -1, keepdims=True))
    exponent = jnp.exp(scores - top_score)
    soft_probs = exponent / lax.optimization_barrier(jnp.sum(exponent, -1, keepdims=True))
    probs_low = low(soft_probs)
    return jnp.einsum('ihqk,ikhd->iqhd', probs_low, values, precision=HIGH)

def item_block(weights, text_block, grid_block, cls_block, lengths, counts, boxes):
    w_qkv, w_out, w_cq, w_ckv, w_cout, w_fin, w_fout, vec_rows, bias_in = weights
    item_count = text_block.shape[0]
    seq_len = text_block.shape[1]
    zero_row = jnp.zeros((D,), jnp.float32)
    qkv_full = jnp.einsum('ild,de->ile', text_block, w_qkv, precision=HIGH) + jnp.concatenate([vec_rows[0], zero_row, vec_rows[1]])
    qkv_low = low(low_back(qkv_full)).reshape(item_count, seq_len, 3, HEADS, HEAD)
    self_res = attend(qkv_low[:, :, 0], qkv_low[:, :, 1], qkv_low[:, :, 2], self_allowed(lengths, seq_len))
    attn_low = low(low_back(self_res.reshape(item_count, seq_len, D)))
    branch_one = low_back(jnp.einsum('ild,de->ile', attn_low, w_out, precision=HIGH) + vec_rows[2])
    hidden_one = layer_norm(text_block + branch_one, vec_rows[3], vec_rows[4])
    cross_query = low(low_back(jnp.einsum('ild,de->ile', low(hidden_one), w_cq, precision=HIGH) + vec_rows[5]))
    cross_query = cross_query.reshape(item_count, seq_len, HEADS, HEAD)
    patches = jnp.concatenate([cls_block[:, None], grid_block], 1)
    patch_count = patches.shape[1]
    patch_kv = jnp.einsum('ipv,ve->ipe', patches, w_ckv, precision=HIGH) + jnp.concatenate([zero_row, vec_rows[6]])
    patch_kv = low(low_back(patch_kv))
    cross_key = patch_kv[:, :, :D].reshape(item_count, patch_count, HEADS, HEAD)
    cross_value = patch_kv[:, :, D:].reshape(item_count, patch_count, HEADS, HEAD)
    cross_res = attend(cross_query, cross_key, cross_value, cross_allowed(lengths, counts, boxes, seq_len))
    cross_low = low(low_back(cross_res.reshape(item_count, seq_len, D)))
    branch_two = low_back(jnp.einsum('ild,de->ile', cross_low, w_cout, precision=HIGH) + vec_rows[7])
    hidden_two = layer_norm(hidden_one + branch_two, vec_rows[8], vec_rows[9])
    pre_act = low_back(jnp.einsum('ild,df->ilf', low(hidden_two), w_fin, precision=HIGH) + bias_in)
    act_low = low(jax.nn.gelu(pre_act, approximate=False))
    branch_three = low_back(jnp.einsum('ilf,fd->ild', act_low, w_fout, precision=HIGH) + vec_rows[10])
    return layer_norm(hidden_two + branch_three, vec_rows[11], vec_rows[12])

def reference(text_in, image_grid, image_cls, text_lengths, phrase_counts, phrase_boxes, cotangent, self_qkv, self_out, cross_q, cross_kv, cross_out, ffn_in, ffn_out, vectors, ffn_bias_in):
    params = (self_qkv.astype(jnp.float32), self_out.astype(jnp.float32), cross_q.astype(jnp.float32), cross_kv.astype(jnp.float32), cross_out.astype(jnp.float32), ffn_in.astype(jnp.float32), ffn_out.astype(jnp.float32), vectors.astype(jnp.float32), ffn_bias_in.astype(jnp.float32))
    block_items = 32
    block_count = ITEMS // block_items
    out_list = []
    text_list = []
    grid_list = []
    cls_list = []
    summed = None
    for micro_index in range(MICRO):
        lengths = text_lengths[micro_index].reshape(block_count, block_items)
        counts = phrase_counts[micro_index].reshape(block_count, block_items)
        boxes = phrase_boxes[micro_index].reshape(block_count, block_items, PHRASES, GRID)

        def forward(weights, text_all, grid_all, cls_all):

            def one_block(pieces):
                return item_block(weights, pieces[0], pieces[1], pieces[2], pieces[3], pieces[4], pieces[5])
            blocks = (text_all.reshape(block_count, block_items, LEN, D), grid_all.reshape(block_count, block_items, GRID, VIS), cls_all.reshape(block_count, block_items, VIS), lengths, counts, boxes)
            return lax.map(jax.checkpoint(one_block), blocks).reshape(ITEMS * LEN, D)
        text_all = text_in[micro_index].astype(jnp.float32)
        grid_all = image_grid[micro_index].astype(jnp.float32)
        cls_all = image_cls[micro_index].astype(jnp.float32)
        layer_out, pull_back = jax.vjp(forward, params, text_all, grid_all, cls_all)
        weight_grads, text_grad, grid_grad, cls_grad = pull_back(cotangent[micro_index].astype(jnp.float32))
        out_list.append(layer_out)
        text_list.append(text_grad)
        grid_list.append(grid_grad)
        cls_list.append(cls_grad)
        summed = weight_grads if summed is None else jax.tree.map(jnp.add, summed, weight_grads)
    return (jnp.stack(out_list), jnp.stack(text_list), jnp.stack(grid_list), jnp.stack(cls_list), summed[0], summed[1], summed[2], summed[3], summed[4], summed[5], summed[6], summed[7], summed[8])
```

```python
import functools

import jax
import jax.numpy as jnp
from jax import lax
from jax.experimental import pallas as pl
from jax.experimental.pallas import tpu as pltpu
from jax.sharding import PartitionSpec as P

HEAD = 64
EPS = 1e-06
NEG = -1e30
BF16 = jnp.bfloat16
F32 = jnp.float32
AXES = ("dp", "patch")
VMEM_SPEC = pl.BlockSpec(memory_space=pltpu.VMEM)
SMEM_SPEC = pl.BlockSpec(memory_space=pltpu.SMEM)
PARAMS = pltpu.CompilerParams(vmem_limit_bytes=62 * 2**20)

QKV, OUT, CQ, CKV, COUT, FIN, FOUT = range(7)
GROUPS = ((QKV, OUT), (CQ, CKV, COUT), (FIN,), (FOUT,))


class Plan:
    def __init__(self, dp, patch, shards):
        self.dp, self.patch = dp, patch
        self.zs = dp // 2
        self.devices = dp * patch
        self.chunk = shards[OUT][1] * 2
        self.half = [s[0] // 2 for s in shards]
        self.cols = [s[1] for s in shards]
        self.chunks = [s[1] * 2 // self.chunk for s in shards]
        self.full = [(s[0] * dp, s[1] * patch) for s in shards]
        self.rows = [sum(self.half[w] * self.chunks[w] for w in g) for g in GROUPS]
        self.fast = (
            dp % 2 == 0
            and patch == 4
            and all(h % 16 == 0 for h in self.half)
            and all(s[1] * 2 % self.chunk == 0 for s in shards)
            and self.chunk % 128 == 0
        )

    def flip(self, pick):
        return [(i, i ^ pick(i)) for i in range(self.devices)]

    def core(self):
        return self.flip(lambda i: 1)

    def first(self):
        return self.flip(lambda i: 4 if i % 2 == 0 else 2)

    def second(self):
        return self.flip(lambda i: 2 if i % 2 == 0 else 4)

    def z_up(self, k):
        return [(i, (i + 8 * k) % self.devices) for i in range(self.devices)]


def send(value, perm):
    return lax.ppermute(value, AXES, perm)


def coords():
    dp, patch = lax.axis_index("dp"), lax.axis_index("patch")
    return jnp.stack([dp // 2, dp % 2, patch // 2, patch % 2]).astype(jnp.int32)


def piece_rows(group, plan):
    at, found = 0, []
    for w in group:
        for j in range(plan.chunks[w]):
            found.append((w, j, at))
            at += plan.half[w]
    return found


def group_starts(plan):
    starts, at = [], 0
    for rows in plan.rows:
        starts.append(at)
        at += rows
    return starts, at


def pack_split(plan, where, shards):
    _, total = group_starts(plan)
    wide = plan.chunk // 2

    def body(where_ref, *refs):
        shard_refs, (own_ref, send_ref) = refs[:7], refs[7:]
        core = where_ref[3]
        at = 0
        for group in GROUPS:
            for w in group:
                high = plan.half[w]
                for b in range(plan.chunks[w]):
                    cut = slice(b * wide, (b + 1) * wide)
                    own_ref[at : at + high, :] = shard_refs[w][pl.ds(core * high, high), cut]
                    send_ref[at : at + high, :] = shard_refs[w][
                        pl.ds((1 - core) * high, high), cut
                    ]
                    at += high

    shape = jax.ShapeDtypeStruct((total, wide), BF16)
    return pl.pallas_call(
        body,
        out_shape=(shape, shape),
        in_specs=[SMEM_SPEC] + [VMEM_SPEC] * 7,
        out_specs=(VMEM_SPEC, VMEM_SPEC),
        compiler_params=PARAMS,
        name="pack_split",
    )(where, *shards)


def pack_join(plan, where, own, got):
    starts, total = group_starts(plan)
    wide = plan.chunk // 2

    def body(where_ref, own_ref, got_ref, *unit_refs):
        core = where_ref[3]

        def fill(low_ref, high_ref):
            for g, group in enumerate(GROUPS):
                at = starts[g]
                for w in group:
                    high, count = plan.half[w], plan.chunks[w]
                    for j in range(count):
                        pair = []
                        for b in (2 * j, 2 * j + 1):
                            src = low_ref if b < count else high_ref
                            row = at + (b % count) * high
                            pair.append(src[row : row + high, :])
                        to = at - starts[g] + j * high
                        unit_refs[g][to : to + high, :] = jnp.concatenate(pair, axis=1)
                    at += count * high

        @pl.when(core == 0)
        def _():
            fill(own_ref, got_ref)

        @pl.when(core == 1)
        def _():
            fill(got_ref, own_ref)

    return pl.pallas_call(
        body,
        out_shape=tuple(jax.ShapeDtypeStruct((r, plan.chunk), BF16) for r in plan.rows),
        in_specs=[SMEM_SPEC, VMEM_SPEC, VMEM_SPEC],
        out_specs=(VMEM_SPEC,) * len(GROUPS),
        compiler_params=PARAMS,
        name="pack_join",
    )(where, own, got)


def gather_group(plan, unit):
    stack = jnp.stack([unit] + [send(unit, plan.z_up(k)) for k in range(1, plan.zs)])
    near = send(stack, plan.first())
    side, far = send(stack, plan.second()), send(near, plan.second())
    mine = [stack, near, side, far]
    return mine + [send(part, plan.core()) for part in mine]


def each_piece(plan, group, where_ref, visit):
    z, x, y, core = (where_ref[i] for i in range(4))
    for other in range(2):
        half = core ^ other
        for second in range(2):
            for first in range(2):
                x_at = x ^ jnp.where(half == 0, first, second)
                y_at = y ^ jnp.where(half == 0, second, first)
                for k in range(plan.zs):
                    z_at = lax.rem(z + plan.zs - k, plan.zs)
                    place = (z_at * 2 + x_at) * 2 + half
                    for w, j, row in piece_rows(group, plan):
                        high = plan.half[w]
                        to_row = pl.multiple_of(place * high, 16)
                        to_col = pl.multiple_of(
                            y_at * (plan.full[w][1] // 2) + j * plan.chunk, 128
                        )
                        stack = other * 4 + second * 2 + first
                        visit(stack, k, row, w, to_row, to_col, high)


def assemble(plan, g, where, stacks):
    group = GROUPS[g]

    def body(where_ref, *refs):
        stack_refs, full_refs = refs[:8], dict(zip(group, refs[8:]))

        def visit(stack, k, row, w, to_row, to_col, high):
            full_refs[w][pl.ds(to_row, high), pl.ds(to_col, plan.chunk)] = stack_refs[stack][
                k, row : row + high, :
            ]

        each_piece(plan, group, where_ref, visit)

    return pl.pallas_call(
        body,
        out_shape=tuple(jax.ShapeDtypeStruct(plan.full[w], BF16) for w in group),
        in_specs=[SMEM_SPEC] + [VMEM_SPEC] * 8,
        out_specs=(VMEM_SPEC,) * len(group),
        compiler_params=PARAMS,
        name="assemble",
    )(where, *stacks)


def disassemble(plan, g, where, grads):
    group = GROUPS[g]

    def body(where_ref, *refs):
        full_refs, stack_refs = dict(zip(group, refs[: len(group)])), refs[len(group) :]

        def visit(stack, k, row, w, to_row, to_col, high):
            stack_refs[stack][k, row : row + high, :] = full_refs[w][
                pl.ds(to_row, high), pl.ds(to_col, plan.chunk)
            ]

        each_piece(plan, group, where_ref, visit)

    shape = jax.ShapeDtypeStruct((plan.zs, plan.rows[g], plan.chunk), BF16)
    return pl.pallas_call(
        body,
        out_shape=(shape,) * 8,
        in_specs=[SMEM_SPEC] + [VMEM_SPEC] * len(group),
        out_specs=(VMEM_SPEC,) * 8,
        compiler_params=PARAMS,
        name="disassemble",
    )(where, *grads)


def add_low(one, two):
    return (one.astype(F32) + two.astype(F32)).astype(BF16)


def reduce_group(plan, g, where, stacks):
    got = [send(part, plan.core()) for part in stacks[4:]]
    mine = [add_low(a, b) for a, b in zip(stacks[:4], got)]
    side, far = send(mine[2], plan.second()), send(mine[3], plan.second())
    mine = [add_low(mine[0], side), add_low(mine[1], far)]
    near = send(mine[1], plan.first())
    total = add_low(mine[0], near)
    parts = [total[0]]
    for k in range(1, plan.zs):
        parts.append(send(total[k], plan.z_up(plan.zs - k)))
    own, give = unpack_split(plan, g, where, parts)
    return unpack_join(plan, g, where, own, send(give, plan.core()))


def unpack_split(plan, g, where, parts):
    group, rows, wide = GROUPS[g], plan.rows[g], plan.chunk // 2

    def body(where_ref, *refs):
        part_refs, (own_ref, give_ref) = refs[:-2], refs[-2:]
        core = where_ref[3]

        def fill(low_ref, high_ref):
            at = 0
            for w in group:
                high, count = plan.half[w], plan.chunks[w]
                for j in range(count):
                    row = at + j * high
                    value = sum(p[row : row + high, :].astype(F32) for p in part_refs)
                    for b in (2 * j, 2 * j + 1):
                        dst = low_ref if b < count else high_ref
                        to = at + (b % count) * high
                        cut = (b - 2 * j) * wide
                        dst[to : to + high, :] = value[:, cut : cut + wide]
                at += count * high

        @pl.when(core == 0)
        def _():
            fill(own_ref, give_ref)

        @pl.when(core == 1)
        def _():
            fill(give_ref, own_ref)

    shape = jax.ShapeDtypeStruct((rows, wide), F32)
    return pl.pallas_call(
        body,
        out_shape=(shape, shape),
        in_specs=[SMEM_SPEC] + [VMEM_SPEC] * len(parts),
        out_specs=(VMEM_SPEC, VMEM_SPEC),
        compiler_params=PARAMS,
        name="unpack_split",
    )(where, *parts)


def unpack_join(plan, g, where, own, got):
    group, wide = GROUPS[g], plan.chunk // 2

    def body(where_ref, own_ref, got_ref, *out_refs):
        core = where_ref[3]
        at = 0
        for w, out_ref in zip(group, out_refs):
            high, count = plan.half[w], plan.chunks[w]
            own_rows = pl.ds(pl.multiple_of(core * high, 16), high)
            got_rows = pl.ds(pl.multiple_of((1 - core) * high, 16), high)
            for b in range(count):
                row, cut = at + b * high, slice(b * wide, (b + 1) * wide)
                out_ref[own_rows, cut] = own_ref[row : row + high, :]
                out_ref[got_rows, cut] = got_ref[row : row + high, :]
            at += count * high

    return pl.pallas_call(
        body,
        out_shape=tuple(
            jax.ShapeDtypeStruct((2 * plan.half[w], plan.cols[w]), F32) for w in group
        ),
        in_specs=[SMEM_SPEC, VMEM_SPEC, VMEM_SPEC],
        out_specs=(VMEM_SPEC,) * len(group),
        compiler_params=PARAMS,
        name="unpack_join",
    )(where, own, got)


def gather_small(plan, where, vectors, bias):
    count, part = vectors.shape
    flat = jnp.concatenate([vectors.reshape(-1), bias])
    size = flat.shape[0]
    flat = jnp.pad(flat, (0, -size % 2048)).reshape(-1, 128)
    pair = jnp.stack([flat, send(flat, plan.flip(lambda i: 4))])
    every = jnp.stack([pair] + [send(pair, plan.z_up(k)) for k in range(1, plan.zs)])
    every = every.reshape((plan.dp,) + flat.shape)
    at = jnp.arange(plan.dp, dtype=jnp.int32)
    slot = lax.rem(where[0] - at // 2 + plan.zs, plan.zs) * 2 + ((at % 2) ^ where[1])
    every = jnp.take(every, slot, axis=0).reshape(plan.dp, -1)[:, :size].astype(F32)
    rows = every[:, : count * part].reshape(plan.dp, count, part)
    rows = rows.transpose(1, 0, 2).reshape(count, plan.dp * part)
    return rows, every[:, count * part :].reshape(-1)


def reduce_small(plan, where, rows, bias):
    count, width = rows.shape
    flat = jnp.concatenate([rows.reshape(-1), bias]).astype(F32)
    size = flat.shape[0]
    flat = jnp.pad(flat, (0, -size % 1024)).reshape(-1, 128)
    for bit in (1, 2, 4):
        flat = flat + send(flat, plan.flip(lambda i: bit))
    flat = flat + sum(send(flat, plan.z_up(k)) for k in range(1, plan.zs))
    flat = flat.reshape(-1)
    dp = where[0] * 2 + where[1]
    whole = flat[: count * width].reshape(count, width)
    own = lax.dynamic_slice_in_dim(whole, dp * (width // plan.dp), width // plan.dp, axis=1)
    tail = flat[count * width : size]
    step = bias.shape[0] // plan.dp
    return own, lax.dynamic_slice_in_dim(tail, dp * step, step, axis=0)


def fetch_plain(weights, vectors, bias):
    whole = [
        lax.all_gather(lax.all_gather(w, "dp", axis=0, tiled=True), "patch", axis=1, tiled=True)
        for w in weights
    ]
    rows = lax.all_gather(vectors, "dp", axis=1, tiled=True)
    return whole, rows.astype(F32), lax.all_gather(bias, "dp", axis=0, tiled=True).astype(F32)


def reduce_plain(grads, rows, bias):
    whole = []
    for grad in grads:
        part = lax.psum_scatter(grad, "dp", scatter_dimension=0, tiled=True)
        whole.append(
            lax.psum_scatter(part, "patch", scatter_dimension=1, tiled=True).astype(F32)
        )
    rows = lax.psum(lax.psum_scatter(rows, "dp", scatter_dimension=1, tiled=True), "patch")
    bias = lax.psum(lax.psum_scatter(bias, "dp", scatter_dimension=0, tiled=True), "patch")
    return whole, rows, bias


def norm_forward(total_in, gain_row, shift_row):
    center = total_in - jnp.mean(total_in, -1, keepdims=True)
    spread = lax.rsqrt(jnp.mean(center * center, -1, keepdims=True) + EPS)
    return center * spread * gain_row + shift_row


def exact_gelu(pre_act):
    return jax.nn.gelu(pre_act, approximate=False)


def self_allowed(lengths, length_max):
    positions = jnp.arange(length_max, dtype=jnp.int32)
    key_ok = positions[None, :] < lengths[:, None]
    return jnp.broadcast_to(key_ok[:, None, :], (lengths.shape[0], length_max, length_max))


def cross_allowed(lengths, counts, boxes, length_max):
    positions = jnp.arange(length_max, dtype=jnp.int32)[None, :]
    uses_box = (counts[:, None] > 0) & (positions < lengths[:, None])
    phrase_of = jnp.where(uses_box, positions * counts[:, None] // lengths[:, None], 0)
    phrase_ids = jnp.arange(boxes.shape[1], dtype=jnp.int32)
    chosen = phrase_of[:, :, None] == phrase_ids[None, None, :]
    in_box = jnp.any(chosen[:, :, :, None] & (boxes[:, None] > 0), axis=2)
    grid_ok = jnp.where(uses_box[:, :, None], in_box, True)
    cls_column = jnp.ones(grid_ok.shape[:2] + (1,), dtype=jnp.bool_)
    return jnp.concatenate([cls_column, grid_ok], -1)


def attend_forward(queries, key_in, values, allowed, score_scale):
    scores = (
        jnp.einsum("iqhd,ikhd->ihqk", queries, key_in, preferred_element_type=jnp.float32)
        * score_scale
    )
    scores = jnp.where(allowed[:, None], scores, NEG)
    top_score = jnp.max(scores, -1, keepdims=True)
    exponent = jnp.exp(scores - top_score)
    soft_probs = exponent / jnp.sum(exponent, -1, keepdims=True)
    probs_low = soft_probs.astype(jnp.bfloat16)
    result = jnp.einsum("ihqk,ikhd->iqhd", probs_low, values, preferred_element_type=jnp.float32)
    return (result, soft_probs, probs_low)


def attend_backward(grad_low, queries, key_in, values, soft_probs, probs_low, score_scale):
    grad_probs = jnp.einsum("iqhd,ikhd->ihqk", grad_low, values, preferred_element_type=jnp.float32)
    grad_scores = soft_probs * (grad_probs - jnp.sum(soft_probs * grad_probs, -1, keepdims=True))
    scores_low = grad_scores.astype(jnp.bfloat16)
    grad_query = (
        jnp.einsum("ihqk,ikhd->iqhd", scores_low, key_in, preferred_element_type=jnp.float32)
        * score_scale
    )
    grad_key = (
        jnp.einsum("ihqk,iqhd->ikhd", scores_low, queries, preferred_element_type=jnp.float32)
        * score_scale
    )
    grad_value = jnp.einsum(
        "ihqk,iqhd->ikhd", probs_low, grad_low, preferred_element_type=jnp.float32
    )
    return (grad_query, grad_key, grad_value)


def forward_pass(weights, text_local, patches, lengths, counts, boxes):
    w_qkv, w_out, w_cq, w_ckv, w_cout, w_fin, w_fout, vec_rows, bias_in = weights
    model_width = w_out.shape[0]
    head_count = model_width // HEAD
    item_count = lengths.shape[0]
    seq_len = text_local.shape[0] // item_count
    score_scale = HEAD ** (-0.5)
    zero_row = jnp.zeros((model_width,), jnp.float32)
    qkv_full = jnp.dot(text_local, w_qkv, preferred_element_type=jnp.float32) + jnp.concatenate(
        [vec_rows[0], zero_row, vec_rows[1]]
    )
    qkv_low = qkv_full.astype(jnp.bfloat16).reshape(item_count, seq_len, 3, head_count, HEAD)
    self_q = qkv_low[:, :, 0]
    self_k = qkv_low[:, :, 1]
    self_v = qkv_low[:, :, 2]
    self_res, self_probs, self_plow = attend_forward(
        self_q, self_k, self_v, self_allowed(lengths, seq_len), score_scale
    )
    attn_low = self_res.reshape(-1, model_width).astype(jnp.bfloat16)
    total_one = (
        text_local.astype(jnp.float32)
        + jnp.dot(attn_low, w_out, preferred_element_type=jnp.float32)
        + vec_rows[2]
    )
    hidden_one = norm_forward(total_one, vec_rows[3], vec_rows[4])
    hidden_one_low = hidden_one.astype(jnp.bfloat16)
    cross_query = (
        jnp.dot(hidden_one_low, w_cq, preferred_element_type=jnp.float32) + vec_rows[5]
    ).astype(jnp.bfloat16)
    cross_query = cross_query.reshape(item_count, seq_len, head_count, HEAD)
    kv_bias = jnp.concatenate([zero_row, vec_rows[6]])
    patch_kv = (
        jnp.einsum("ipv,ve->ipe", patches, w_ckv, preferred_element_type=jnp.float32) + kv_bias
    ).astype(jnp.bfloat16)
    patch_count = patch_kv.shape[1]
    cross_key = patch_kv[:, :, :model_width].reshape(item_count, patch_count, head_count, HEAD)
    cross_value = patch_kv[:, :, model_width:].reshape(item_count, patch_count, head_count, HEAD)
    cross_res, cross_probs, cross_plow = attend_forward(
        cross_query,
        cross_key,
        cross_value,
        cross_allowed(lengths, counts, boxes, seq_len),
        score_scale,
    )
    cross_low = cross_res.reshape(-1, model_width).astype(jnp.bfloat16)
    total_two = (
        hidden_one + jnp.dot(cross_low, w_cout, preferred_element_type=jnp.float32) + vec_rows[7]
    )
    hidden_two = norm_forward(total_two, vec_rows[8], vec_rows[9])
    hidden_two_low = hidden_two.astype(jnp.bfloat16)
    pre_act = jnp.dot(hidden_two_low, w_fin, preferred_element_type=jnp.float32) + bias_in
    act_low = exact_gelu(pre_act).astype(jnp.bfloat16)
    total_three = (
        hidden_two + jnp.dot(act_low, w_fout, preferred_element_type=jnp.float32) + vec_rows[10]
    )
    return {
        "text_local": text_local,
        "self_q": self_q,
        "self_k": self_k,
        "self_v": self_v,
        "self_probs": self_probs,
        "self_plow": self_plow,
        "attn_low": attn_low,
        "total_one": total_one,
        "hidden_one_low": hidden_one_low,
        "cross_query": cross_query,
        "cross_key": cross_key,
        "cross_value": cross_value,
        "cross_probs": cross_probs,
        "cross_plow": cross_plow,
        "cross_low": cross_low,
        "total_two": total_two,
        "hidden_two_low": hidden_two_low,
        "pre_act": pre_act,
        "act_low": act_low,
        "total_three": total_three,
        "patches": patches,
    }


def backward_pass(weights, saved, cot_local):
    w_qkv, w_out, w_cq, w_ckv, w_cout, w_fin, w_fout, vec_rows, bias_in = weights
    model_width = w_out.shape[0]
    score_scale = HEAD ** (-0.5)
    item_count = saved["cross_query"].shape[0]
    patch_count = saved["cross_key"].shape[1]
    layer_out, norm_three = jax.vjp(norm_forward, saved["total_three"], vec_rows[11], vec_rows[12])
    grad_three, gain_three, shift_three = norm_three(cot_local.astype(jnp.float32))
    grad_three_low = grad_three.astype(jnp.bfloat16)
    grad_fout = jnp.einsum(
        "rf,rd->fd", saved["act_low"], grad_three_low, preferred_element_type=jnp.float32
    )
    bias_fout = jnp.sum(grad_three_low, 0, dtype=jnp.float32)
    grad_act = jnp.einsum("rd,fd->rf", grad_three_low, w_fout, preferred_element_type=jnp.float32)
    gelu_out, gelu_pull = jax.vjp(exact_gelu, saved["pre_act"])
    grad_pre_low = gelu_pull(grad_act)[0].astype(jnp.bfloat16)
    grad_fin = jnp.einsum(
        "rd,rf->df", saved["hidden_two_low"], grad_pre_low, preferred_element_type=jnp.float32
    )
    bias_fin = jnp.sum(grad_pre_low, 0, dtype=jnp.float32)
    grad_hidden_two = grad_three + jnp.einsum(
        "rf,df->rd", grad_pre_low, w_fin, preferred_element_type=jnp.float32
    )
    hidden_two, norm_two = jax.vjp(norm_forward, saved["total_two"], vec_rows[8], vec_rows[9])
    grad_two, gain_two, shift_two = norm_two(grad_hidden_two)
    grad_two_low = grad_two.astype(jnp.bfloat16)
    grad_cout = jnp.einsum(
        "rd,re->de", saved["cross_low"], grad_two_low, preferred_element_type=jnp.float32
    )
    bias_cout = jnp.sum(grad_two_low, 0, dtype=jnp.float32)
    grad_cross_ctx = jnp.einsum(
        "re,de->rd", grad_two_low, w_cout, preferred_element_type=jnp.float32
    ).astype(jnp.bfloat16)
    grad_cross_ctx = grad_cross_ctx.reshape(saved["cross_query"].shape)
    grad_cq4, grad_ck4, grad_cv4 = attend_backward(
        grad_cross_ctx,
        saved["cross_query"],
        saved["cross_key"],
        saved["cross_value"],
        saved["cross_probs"],
        saved["cross_plow"],
        score_scale,
    )
    grad_cq_low = grad_cq4.reshape(-1, model_width).astype(jnp.bfloat16)
    grad_cq = jnp.einsum(
        "rd,re->de", saved["hidden_one_low"], grad_cq_low, preferred_element_type=jnp.float32
    )
    bias_cq = jnp.sum(grad_cq_low, 0, dtype=jnp.float32)
    grad_hidden_one = grad_two + jnp.einsum(
        "re,de->rd", grad_cq_low, w_cq, preferred_element_type=jnp.float32
    )
    patch_grad = jnp.concatenate(
        [
            grad_ck4.reshape(item_count, patch_count, model_width),
            grad_cv4.reshape(item_count, patch_count, model_width),
        ],
        -1,
    ).astype(jnp.bfloat16)
    bias_cv = jnp.sum(patch_grad[:, :, model_width:], (0, 1), dtype=jnp.float32)
    grad_ckv = jnp.einsum(
        "ipv,ipe->ve", saved["patches"], patch_grad, preferred_element_type=jnp.float32
    )
    patches_grad = jnp.einsum("ipe,ve->ipv", patch_grad, w_ckv, preferred_element_type=jnp.float32)
    hidden_one, norm_one = jax.vjp(norm_forward, saved["total_one"], vec_rows[3], vec_rows[4])
    grad_one, gain_one, shift_one = norm_one(grad_hidden_one)
    grad_one_low = grad_one.astype(jnp.bfloat16)
    grad_out = jnp.einsum(
        "rd,re->de", saved["attn_low"], grad_one_low, preferred_element_type=jnp.float32
    )
    bias_out = jnp.sum(grad_one_low, 0, dtype=jnp.float32)
    grad_self_ctx = jnp.einsum(
        "re,de->rd", grad_one_low, w_out, preferred_element_type=jnp.float32
    ).astype(jnp.bfloat16)
    grad_self_ctx = grad_self_ctx.reshape(saved["self_q"].shape)
    grad_sq, grad_sk, grad_sv = attend_backward(
        grad_self_ctx,
        saved["self_q"],
        saved["self_k"],
        saved["self_v"],
        saved["self_probs"],
        saved["self_plow"],
        score_scale,
    )
    grad_qkv_low = (
        jnp.stack([grad_sq, grad_sk, grad_sv], 2).reshape(-1, 3 * model_width).astype(jnp.bfloat16)
    )
    grad_qkv = jnp.einsum(
        "rd,re->de", saved["text_local"], grad_qkv_low, preferred_element_type=jnp.float32
    )
    bias_q = jnp.sum(grad_qkv_low[:, :model_width], 0, dtype=jnp.float32)
    bias_v = jnp.sum(grad_qkv_low[:, 2 * model_width :], 0, dtype=jnp.float32)
    text_grad = grad_one + jnp.einsum(
        "re,de->rd", grad_qkv_low, w_qkv, preferred_element_type=jnp.float32
    )
    grad_vec = jnp.stack(
        [
            bias_q,
            bias_v,
            bias_out,
            gain_one,
            shift_one,
            bias_cq,
            bias_cv,
            bias_cout,
            gain_two,
            shift_two,
            bias_fout,
            gain_three,
            shift_three,
        ]
    )
    local_grads = (
        grad_qkv,
        grad_out,
        grad_cq,
        grad_ckv,
        grad_cout,
        grad_fin,
        grad_fout,
        grad_vec,
        bias_fin,
    )
    return (layer_out, text_grad, patches_grad, local_grads)


def trade_in(image_grid, count):
    micro, items, own, width = image_grid.shape
    cut = image_grid.reshape(micro, count, items // count, own, width).transpose(1, 0, 2, 3, 4)
    got = lax.all_to_all(cut, "patch", split_axis=0, concat_axis=0, tiled=True)
    return got.transpose(1, 2, 0, 3, 4).reshape(micro * items // count, count * own, width)


def trade_back(grads, micro, count):
    items, patches, width = grads.shape
    cut = grads.reshape(micro, items // micro, count, patches // count, width)
    got = lax.all_to_all(
        cut.transpose(2, 0, 1, 3, 4), "patch", split_axis=0, concat_axis=0, tiled=True
    )
    got = got.transpose(1, 0, 2, 3, 4)
    return got.reshape(micro, items // micro * count, patches // count, width)


def on_device(
    plan,
    text_in,
    image_grid,
    image_cls,
    text_lengths,
    phrase_counts,
    phrase_boxes,
    cotangent,
    *params,
):
    micro, width = text_in.shape[0], text_in.shape[2]
    shards, vectors, ffn_bias = params[:7], params[7], params[8]
    where = coords()
    items = text_lengths.size
    grid = trade_in(image_grid, plan.patch)
    patches = jnp.concatenate([image_cls.reshape(items, 1, -1), grid], axis=1)
    if plan.fast:
        own, give = pack_split(plan, where, shards)
        units = pack_join(plan, where, own, send(give, plan.core()))
        weights = [None] * 7
        for g, group in enumerate(GROUPS):
            full = assemble(plan, g, where, gather_group(plan, units[g]))
            for w, value in zip(group, full):
                weights[w] = value
        rows, bias = gather_small(plan, where, vectors, ffn_bias)
    else:
        weights, rows, bias = fetch_plain(shards, vectors, ffn_bias)
    pack = (*weights, rows, bias)
    saved = forward_pass(
        pack,
        text_in.reshape(-1, width),
        patches,
        text_lengths.reshape(-1),
        phrase_counts.reshape(-1),
        phrase_boxes.reshape((items,) + phrase_boxes.shape[2:]),
    )
    layer_out, text_grad, patches_grad, local = backward_pass(
        pack, saved, cotangent.reshape(-1, width)
    )
    low = [grad.astype(BF16) for grad in local[:7]]
    if plan.fast:
        grads = [None] * 7
        for g in (3, 2, 1, 0):
            stacks = disassemble(plan, g, where, [low[w] for w in GROUPS[g]])
            for w, value in zip(GROUPS[g], reduce_group(plan, g, where, stacks)):
                grads[w] = value
        rows_grad, bias_grad = reduce_small(plan, where, local[7], local[8])
    else:
        grads, rows_grad, bias_grad = reduce_plain(low, local[7], local[8])
    cls_grad = patches_grad[:, 0].reshape(image_cls.shape)
    grid_grad = trade_back(patches_grad[:, 1:].astype(BF16), micro, plan.patch).astype(F32)
    return (
        layer_out.reshape(text_in.shape),
        text_grad.reshape(text_in.shape),
        grid_grad,
        cls_grad,
        *grads,
        rows_grad,
        bias_grad,
    )


def solution(mesh):
    dp, patch = mesh.shape["dp"], mesh.shape["patch"]
    both = P(None, ("dp", "patch"), None)
    weight = P("dp", "patch")

    def run(*args):
        shards = [(w.shape[0] // dp, w.shape[1] // patch) for w in args[7:14]]
        plan = Plan(dp, patch, shards)
        return jax.shard_map(
            functools.partial(on_device, plan),
            mesh=mesh,
            in_specs=(
                both,
                P(None, "dp", "patch", None),
                both,
                P(None, ("dp", "patch")),
                P(None, ("dp", "patch")),
                P(None, ("dp", "patch"), None, None),
                both,
            )
            + (weight,) * 7
            + (P(None, "dp"), P("dp")),
            out_specs=(both, both, P(None, "dp", "patch", None), both)
            + (weight,) * 7
            + (P(None, "dp"), P("dp")),
            check_vma=False,
        )(*args)

    return run
```

```python
import functools

import jax
import jax.numpy as jnp
from jax import lax
from jax.experimental import pallas as pl
from jax.experimental.pallas import tpu as pltpu
from jax.sharding import PartitionSpec as P

HEAD = 64
EPS = 1e-06
NEG = -1e30
BF16 = jnp.bfloat16
F32 = jnp.float32
AXES = ("dp", "patch")
VMEM_SPEC = pl.BlockSpec(memory_space=pltpu.VMEM)
SMEM_SPEC = pl.BlockSpec(memory_space=pltpu.SMEM)
PARAMS = pltpu.CompilerParams(vmem_limit_bytes=62 * 2**20)

QKV, OUT, CQ, CKV, COUT, FIN, FOUT = range(7)
GATHER = ((QKV, OUT), (CQ, CKV, COUT), (FIN,), (FOUT,))
REDUCE = ((QKV,), (CQ, CKV, COUT, OUT), (FIN,), (FOUT,))


class Plan:
    def __init__(self, dp, patch, shards):
        self.dp, self.patch = dp, patch
        self.zs = dp // 2
        self.devices = dp * patch
        self.chunk = shards[OUT][1] * 2
        self.half = [s[0] // 2 for s in shards]
        self.cols = [s[1] for s in shards]
        self.chunks = [s[1] * 2 // self.chunk for s in shards]
        self.full = [(s[0] * dp, s[1] * patch) for s in shards]
        self.fast = (
            dp % 2 == 0
            and patch == 4
            and all(h % 16 == 0 for h in self.half)
            and all(s[1] * 2 % self.chunk == 0 for s in shards)
            and self.chunk % 128 == 0
        )

    def rows(self, group):
        return sum(self.half[w] * self.chunks[w] for w in group)

    def flip(self, pick):
        return [(i, i ^ pick(i)) for i in range(self.devices)]

    def core(self):
        return self.flip(lambda i: 1)

    def first(self):
        return self.flip(lambda i: 4 if i % 2 == 0 else 2)

    def second(self):
        return self.flip(lambda i: 2 if i % 2 == 0 else 4)

    def z_up(self, k):
        return [(i, (i + 8 * k) % self.devices) for i in range(self.devices)]


def send(value, perm):
    return lax.ppermute(value, AXES, perm)


def coords():
    dp, patch = lax.axis_index("dp"), lax.axis_index("patch")
    return jnp.stack([dp // 2, dp % 2, patch // 2, patch % 2]).astype(jnp.int32)


def piece_rows(group, plan):
    at, found = 0, []
    for w in group:
        for j in range(plan.chunks[w]):
            found.append((w, j, at))
            at += plan.half[w]
    return found


def group_starts(plan):
    starts, at = [], 0
    for group in GATHER:
        starts.append(at)
        at += plan.rows(group)
    return starts, at


def pack_split(plan, where, shards):
    _, total = group_starts(plan)
    wide = plan.chunk // 2

    def body(where_ref, *refs):
        shard_refs, (own_ref, send_ref) = refs[:7], refs[7:]
        core = where_ref[3]
        at = 0
        for group in GATHER:
            for w in group:
                high = plan.half[w]
                for b in range(plan.chunks[w]):
                    cut = slice(b * wide, (b + 1) * wide)
                    own_ref[at : at + high, :] = shard_refs[w][pl.ds(core * high, high), cut]
                    send_ref[at : at + high, :] = shard_refs[w][
                        pl.ds((1 - core) * high, high), cut
                    ]
                    at += high

    shape = jax.ShapeDtypeStruct((total, wide), BF16)
    return pl.pallas_call(
        body,
        out_shape=(shape, shape),
        in_specs=[SMEM_SPEC] + [VMEM_SPEC] * 7,
        out_specs=(VMEM_SPEC, VMEM_SPEC),
        compiler_params=PARAMS,
        name="pack_split",
    )(where, *shards)


def pack_join(plan, where, own, got):
    starts, total = group_starts(plan)
    wide = plan.chunk // 2

    def body(where_ref, own_ref, got_ref, *unit_refs):
        core = where_ref[3]

        def fill(low_ref, high_ref):
            for g, group in enumerate(GATHER):
                at = starts[g]
                for w in group:
                    high, count = plan.half[w], plan.chunks[w]
                    for j in range(count):
                        pair = []
                        for b in (2 * j, 2 * j + 1):
                            src = low_ref if b < count else high_ref
                            row = at + (b % count) * high
                            pair.append(src[row : row + high, :])
                        to = at - starts[g] + j * high
                        unit_refs[g][to : to + high, :] = jnp.concatenate(pair, axis=1)
                    at += count * high

        @pl.when(core == 0)
        def _():
            fill(own_ref, got_ref)

        @pl.when(core == 1)
        def _():
            fill(got_ref, own_ref)

    return pl.pallas_call(
        body,
        out_shape=tuple(jax.ShapeDtypeStruct((plan.rows(g), plan.chunk), BF16) for g in GATHER),
        in_specs=[SMEM_SPEC, VMEM_SPEC, VMEM_SPEC],
        out_specs=(VMEM_SPEC,) * len(GATHER),
        compiler_params=PARAMS,
        name="pack_join",
    )(where, own, got)


class Gathering:
    def __init__(self, plan, unit):
        self.plan, self.held, self.step = plan, [unit], 0

    def advance(self):
        plan, held = self.plan, self.held
        if self.step == 0:
            held = held + [send(held[0], plan.z_up(k)) for k in range(1, plan.zs)]
        elif self.step == 1:
            stack = jnp.stack(held)
            held = [stack, send(stack, plan.first()), send(stack, plan.second())]
            held.append(send(stack, plan.core()))
        elif self.step == 2:
            stack, near, side, stack_core = held
            far = send(near, plan.second())
            held = [stack, near, side, far, stack_core]
            held += [send(part, plan.core()) for part in (near, side, far)]
        self.held, self.step = held, self.step + 1


def each_place(plan, group, where_ref, visit):
    z, x, y, core = (where_ref[i] for i in range(4))
    for other in range(2):
        half = core ^ other
        for second in range(2):
            for first in range(2):
                x_at = x ^ jnp.where(half == 0, first, second)
                y_at = y ^ jnp.where(half == 0, second, first)
                for k in range(plan.zs):
                    z_at = lax.rem(z + plan.zs - k, plan.zs)
                    place = (z_at * 2 + x_at) * 2 + half
                    for w, j, row in piece_rows(group, plan):
                        high = plan.half[w]
                        to_row = pl.multiple_of(place * high, 16)
                        stack = other * 4 + second * 2 + first
                        visit(stack, k, row, w, j, to_row, y_at, high)


def assemble(plan, group, where, stacks):

    def body(where_ref, *refs):
        stack_refs, full_refs = refs[:8], dict(zip(group, refs[8:]))

        def visit(stack, k, row, w, j, to_row, to_y, high):
            to_col = pl.multiple_of(to_y * (plan.full[w][1] // 2) + j * plan.chunk, 128)
            full_refs[w][pl.ds(to_row, high), pl.ds(to_col, plan.chunk)] = stack_refs[stack][
                k, row : row + high, :
            ]

        each_place(plan, group, where_ref, visit)

    return pl.pallas_call(
        body,
        out_shape=tuple(jax.ShapeDtypeStruct(plan.full[w], BF16) for w in group),
        in_specs=[SMEM_SPEC] + [VMEM_SPEC] * 8,
        out_specs=(VMEM_SPEC,) * len(group),
        compiler_params=PARAMS,
        name="assemble",
    )(where, *stacks)


def add_low(one, two):
    return (one.astype(F32) + two.astype(F32)).astype(BF16)


class Reducing:
    def __init__(self, plan, group, where, stacks):
        self.plan, self.group, self.where = plan, group, where
        self.held, self.step = list(stacks), 0

    def advance(self):
        plan, held = self.plan, self.held
        if self.step == 0:
            held = held[:4] + [send(part, plan.core()) for part in held[4:]]
        elif self.step == 1:
            mine = [add_low(a, b) for a, b in zip(held[:4], held[4:])]
            held = mine[:2] + [send(part, plan.second()) for part in mine[2:]]
        elif self.step == 2:
            mine = [add_low(held[0], held[2]), add_low(held[1], held[3])]
            held = [mine[0], send(mine[1], plan.first())]
        elif self.step == 3:
            total = add_low(*held)
            parts = [send(total[k], plan.z_up(plan.zs - k)) for k in range(1, plan.zs)]
            held = [total[0]] + parts
        elif self.step == 4:
            own, give = unpack_split(plan, self.group, self.where, held)
            held = [own, send(give, plan.core())]
        elif self.step == 5:
            held = unpack_join(plan, self.group, self.where, *held)
        self.held, self.step = list(held), self.step + 1


def fence(chains, values):
    flat, tree = jax.tree.flatten([values, [chain.held for chain in chains]])
    values, held = jax.tree.unflatten(tree, lax.optimization_barrier(flat))
    for chain, arrays in zip(chains, held):
        chain.held = arrays
    return values


def unpack_split(plan, group, where, parts):
    rows, wide = plan.rows(group), plan.chunk // 2

    def body(where_ref, *refs):
        part_refs, (own_ref, give_ref) = refs[:-2], refs[-2:]
        core = where_ref[3]

        def fill(low_ref, high_ref):
            at = 0
            for w in group:
                high, count = plan.half[w], plan.chunks[w]
                for j in range(count):
                    row = at + j * high
                    value = sum(p[row : row + high, :].astype(F32) for p in part_refs)
                    for b in (2 * j, 2 * j + 1):
                        dst = low_ref if b < count else high_ref
                        to = at + (b % count) * high
                        cut = (b - 2 * j) * wide
                        dst[to : to + high, :] = value[:, cut : cut + wide]
                at += count * high

        @pl.when(core == 0)
        def _():
            fill(own_ref, give_ref)

        @pl.when(core == 1)
        def _():
            fill(give_ref, own_ref)

    shape = jax.ShapeDtypeStruct((rows, wide), F32)
    return pl.pallas_call(
        body,
        out_shape=(shape, shape),
        in_specs=[SMEM_SPEC] + [VMEM_SPEC] * len(parts),
        out_specs=(VMEM_SPEC, VMEM_SPEC),
        compiler_params=PARAMS,
        name="unpack_split",
    )(where, *parts)


def unpack_join(plan, group, where, own, got):
    wide = plan.chunk // 2

    def body(where_ref, own_ref, got_ref, *out_refs):
        core = where_ref[3]
        at = 0
        for w, out_ref in zip(group, out_refs):
            high, count = plan.half[w], plan.chunks[w]
            own_rows = pl.ds(pl.multiple_of(core * high, 16), high)
            got_rows = pl.ds(pl.multiple_of((1 - core) * high, 16), high)
            for b in range(count):
                row, cut = at + b * high, slice(b * wide, (b + 1) * wide)
                out_ref[own_rows, cut] = own_ref[row : row + high, :]
                out_ref[got_rows, cut] = got_ref[row : row + high, :]
            at += count * high

    return pl.pallas_call(
        body,
        out_shape=tuple(
            jax.ShapeDtypeStruct((2 * plan.half[w], plan.cols[w]), F32) for w in group
        ),
        in_specs=[SMEM_SPEC, VMEM_SPEC, VMEM_SPEC],
        out_specs=(VMEM_SPEC,) * len(group),
        compiler_params=PARAMS,
        name="unpack_join",
    )(where, own, got)


def gather_small(plan, where, vectors, bias):
    count, part = vectors.shape
    flat = jnp.concatenate([vectors.reshape(-1), bias])
    size = flat.shape[0]
    flat = jnp.pad(flat, (0, -size % 2048)).reshape(-1, 128)
    pair = jnp.stack([flat, send(flat, plan.flip(lambda i: 4))])
    every = jnp.stack([pair] + [send(pair, plan.z_up(k)) for k in range(1, plan.zs)])
    every = every.reshape((plan.dp,) + flat.shape)
    at = jnp.arange(plan.dp, dtype=jnp.int32)
    slot = lax.rem(where[0] - at // 2 + plan.zs, plan.zs) * 2 + ((at % 2) ^ where[1])
    every = jnp.take(every, slot, axis=0).reshape(plan.dp, -1)[:, :size].astype(F32)
    rows = every[:, : count * part].reshape(plan.dp, count, part)
    rows = rows.transpose(1, 0, 2).reshape(count, plan.dp * part)
    return rows, every[:, count * part :].reshape(-1)


def reduce_small(plan, where, rows, bias):
    count, width = rows.shape
    flat = jnp.concatenate([rows.reshape(-1), bias]).astype(F32)
    size = flat.shape[0]
    flat = jnp.pad(flat, (0, -size % 1024)).reshape(-1, 128)
    for bit in (1, 2, 4):
        flat = flat + send(flat, plan.flip(lambda i: bit))
    flat = flat + sum(send(flat, plan.z_up(k)) for k in range(1, plan.zs))
    flat = flat.reshape(-1)
    dp = where[0] * 2 + where[1]
    whole = flat[: count * width].reshape(count, width)
    own = lax.dynamic_slice_in_dim(whole, dp * (width // plan.dp), width // plan.dp, axis=1)
    tail = flat[count * width : size]
    step = bias.shape[0] // plan.dp
    return own, lax.dynamic_slice_in_dim(tail, dp * step, step, axis=0)


def fetch_plain(weights, vectors, bias):
    whole = [
        lax.all_gather(lax.all_gather(w, "dp", axis=0, tiled=True), "patch", axis=1, tiled=True)
        for w in weights
    ]
    rows = lax.all_gather(vectors, "dp", axis=1, tiled=True)
    return whole, rows.astype(F32), lax.all_gather(bias, "dp", axis=0, tiled=True).astype(F32)


def reduce_plain(grad):
    part = lax.psum_scatter(grad, "dp", scatter_dimension=0, tiled=True)
    return lax.psum_scatter(part, "patch", scatter_dimension=1, tiled=True).astype(F32)


def reduce_small_plain(rows, bias):
    rows = lax.psum_scatter(rows, "dp", scatter_dimension=1, tiled=True)
    bias = lax.psum_scatter(bias, "dp", scatter_dimension=0, tiled=True)
    return lax.psum(rows, "patch"), lax.psum(bias, "patch")


def dot(a, b):
    return lax.dot_general(a, b, (((1,), (0,)), ((), ())), preferred_element_type=F32)


def dot_t(a, b):
    return lax.dot_general(a, b, (((1,), (1,)), ((), ())), preferred_element_type=F32)


def dot_l(a, b):
    return lax.dot_general(a, b, (((0,), (0,)), ((), ())), preferred_element_type=F32)


def norm_parts(total):
    center = total - jnp.mean(total, -1, keepdims=True)
    spread = lax.rsqrt(jnp.mean(center * center, -1, keepdims=True) + EPS)
    return center * spread, spread


def norm_pull(grad, hat, spread, gain):
    scaled = grad * gain
    return spread * (
        scaled
        - jnp.mean(scaled, -1, keepdims=True)
        - hat * jnp.mean(scaled * hat, -1, keepdims=True)
    )


def error_function(x):
    x = jnp.clip(x, -4.0, 4.0)
    s = x * x
    top = jnp.full_like(s, -2.72614225801306e-10)
    for c in (
        2.77068142495902e-08,
        -2.10102402082508e-06,
        -5.69250639462346e-05,
        -7.34990630326855e-04,
        -2.95459980854025e-03,
        -1.60960333262415e-02,
    ):
        top = top * s + c
    low = jnp.full_like(s, -1.45660718464996e-05)
    for c in (
        -2.13374055278905e-04,
        -1.68282697438203e-03,
        -7.37332916720468e-03,
        -1.42647390514189e-02,
    ):
        low = low * s + c
    return x * top / low


def col_sum(value):
    return jnp.sum(value.astype(F32), 0, keepdims=True)


def soft(scores):
    grown = jnp.exp(scores - jnp.max(scores, -1, keepdims=True))
    return grown * (1.0 / jnp.sum(grown, -1, keepdims=True))


def soft_pull(probs, grad):
    return probs * (grad - jnp.sum(probs * grad, -1, keepdims=True))


def lane_masks():
    lane = lax.broadcasted_iota(jnp.int32, (1, 2 * HEAD), 1)
    low = (lane < HEAD).astype(F32)
    return low.astype(BF16), (1.0 - low).astype(BF16), lane < HEAD


def whole(shape):
    return pl.BlockSpec(
        shape, lambda i: (0,) * len(shape), pipeline_mode=pl.Buffered(1)
    )


def summed(shape):
    return pl.BlockSpec(shape, lambda i: (0,) * len(shape))


def tiled(shape):
    return pl.BlockSpec(shape, lambda i: (i,) + (0,) * (len(shape) - 1))


def spec_of(shape, dtype):
    return jax.ShapeDtypeStruct(shape, dtype)


def call(body, name, steps, ins, outs, flops, scratch=()):
    out_shape = tuple(shape for shape, _ in outs)
    moved = sum(a.size * a.dtype.itemsize for a, _ in ins)
    moved += sum(o.size * jnp.dtype(o.dtype).itemsize for o in out_shape)
    return pl.pallas_call(
        body,
        grid=(steps,),
        out_shape=out_shape,
        in_specs=[spec for _, spec in ins],
        out_specs=tuple(spec for _, spec in outs),
        scratch_shapes=list(scratch),
        compiler_params=PARAMS,
        cost_estimate=pl.CostEstimate(
            flops=int(flops), bytes_accessed=int(moved), transcendentals=0
        ),
        name=name,
    )(*[a for a, _ in ins])


def self_forward(dims, text, w_qkv, w_out, rows, lengths):
    d, items, length, group = dims.d, dims.items, dims.length, dims.group
    pairs, tokens, block = d // (2 * HEAD), items * length, group * length
    scale = HEAD ** (-0.5)

    def body(len_ref, x_ref, wqkv_ref, wout_ref, row_ref, qkv_ref, prob_ref, ctx_ref, tot_ref):
        step = pl.program_id(0)
        low, high, _ = lane_masks()
        x = x_ref[...]
        for part, bias in ((0, 0), (1, None), (2, 1)):
            cut = slice(part * d, (part + 1) * d)
            value = dot(x, wqkv_ref[:, cut])
            if bias is not None:
                value = value + row_ref[bias : bias + 1, :]
            qkv_ref[:, cut] = value.astype(BF16)
        place = lax.broadcasted_iota(jnp.int32, (1, length), 1)
        for i in range(group):
            ok = place < len_ref[step * group + i]
            r = slice(i * length, (i + 1) * length)
            for p in range(pairs):
                q, k, v = (
                    qkv_ref[r, part * d + p * 128 : part * d + (p + 1) * 128] for part in range(3)
                )
                scores = dot_t(q, jnp.concatenate([k * low, k * high], 0)) * scale
                probs = jnp.concatenate(
                    [
                        soft(jnp.where(ok, scores[:, h * length : (h + 1) * length], NEG))
                        for h in range(2)
                    ],
                    1,
                ).astype(BF16)
                prob_ref[i, p] = probs
                ctx = dot(probs, jnp.concatenate([v * low, v * high], 0))
                ctx_ref[r, p * 128 : (p + 1) * 128] = ctx.astype(BF16)
        tot_ref[...] = x.astype(F32) + dot(ctx_ref[...], wout_ref[...]) + row_ref[2:3, :]

    return call(
        body,
        "self_forward",
        items // group,
        [
            (lengths, SMEM_SPEC),
            (text, tiled((block, d))),
            (w_qkv, whole((d, 3 * d))),
            (w_out, whole((d, d))),
            (rows, whole(rows.shape)),
        ],
        [
            (spec_of((tokens, 3 * d), BF16), tiled((block, 3 * d))),
            (spec_of((items, pairs, length, 2 * length), BF16), tiled((group, pairs, length, 2 * length))),
            (spec_of((tokens, d), BF16), tiled((block, d))),
            (spec_of((tokens, d), F32), tiled((block, d))),
        ],
        2 * tokens * d * 6 * d,
    )


def cross_forward(dims, total_one, patches, mask, w_cq, w_ckv, w_cout, rows):
    d, items, length, group = dims.d, dims.items, dims.length, dims.group
    pairs, tokens, block = d // (2 * HEAD), items * length, group * length
    count, vis = patches.shape[1], patches.shape[2]
    scale = HEAD ** (-0.5)

    def body(tot_ref, patch_ref, mask_ref, wcq_ref, wckv_ref, wcout_ref, row_ref,
             h_ref, cq_ref, kv_ref, prob_ref, ctx_ref, two_ref):
        low, high, _ = lane_masks()
        hat, _ = norm_parts(tot_ref[...])
        hidden = hat * row_ref[3:4, :] + row_ref[4:5, :]
        h_ref[...] = hidden.astype(BF16)
        cq_ref[...] = (dot(h_ref[...], wcq_ref[...]) + row_ref[5:6, :]).astype(BF16)
        patch = patch_ref[...].reshape(group * count, vis)
        keys = dot(patch, wckv_ref[:, :d]).astype(BF16)
        kv_ref[:, :, :d] = keys.reshape(group, count, d)
        values = (dot(patch, wckv_ref[:, d:]) + row_ref[6:7, :]).astype(BF16)
        kv_ref[:, :, d:] = values.reshape(group, count, d)
        for i in range(group):
            ok = mask_ref[i].astype(F32) > 0.5
            r = slice(i * length, (i + 1) * length)
            for p in range(pairs):
                c = slice(p * 128, (p + 1) * 128)
                q, k, v = cq_ref[r, c], kv_ref[i, :, c], kv_ref[i, :, d + p * 128 : d + (p + 1) * 128]
                ctx = 0.0
                for h, side in enumerate((low, high)):
                    scores = dot_t(q, k * side) * scale
                    probs = soft(jnp.where(ok, scores, NEG)).astype(BF16)
                    prob_ref[i, 2 * p + h] = probs
                    ctx = ctx + dot(probs, v * side)
                ctx_ref[r, c] = ctx.astype(BF16)
        two_ref[...] = hidden + dot(ctx_ref[...], wcout_ref[...]) + row_ref[7:8, :]

    return call(
        body,
        "cross_forward",
        items // group,
        [
            (total_one, tiled((block, d))),
            (patches, tiled((group, count, vis))),
            (mask, tiled((group, length, count))),
            (w_cq, whole((d, d))),
            (w_ckv, whole((vis, 2 * d))),
            (w_cout, whole((d, d))),
            (rows, whole(rows.shape)),
        ],
        [
            (spec_of((tokens, d), BF16), tiled((block, d))),
            (spec_of((tokens, d), BF16), tiled((block, d))),
            (spec_of((items, count, 2 * d), BF16), tiled((group, count, 2 * d))),
            (spec_of((items, 2 * pairs, length, count), BF16), tiled((group, 2 * pairs, length, count))),
            (spec_of((tokens, d), BF16), tiled((block, d))),
            (spec_of((tokens, d), F32), tiled((block, d))),
        ],
        2 * tokens * d * 4 * d + 2 * items * count * vis * 2 * d,
    )


def ffn_forward(dims, total_two, cotangent, w_fin, w_fout, rows, bias):
    d, items, length, group = dims.d, dims.items, dims.length, dims.group
    tokens, block, ff = items * length, group * length, w_fin.shape[1]
    piece = d

    def body(tot_ref, cot_ref, win_ref, wout_ref, row_ref, bias_ref,
             out_ref, h_ref, act_ref, slope_ref, g_ref, glow_ref, sum_ref):
        @pl.when(pl.program_id(0) == 0)
        def _():
            sum_ref[...] = jnp.zeros_like(sum_ref)

        hat, _ = norm_parts(tot_ref[...])
        hidden = hat * row_ref[8:9, :] + row_ref[9:10, :]
        h_ref[...] = hidden.astype(BF16)
        total = hidden + row_ref[10:11, :]
        for at in range(0, ff, piece):
            cut = slice(at, at + piece)
            pre = dot(h_ref[...], win_ref[:, cut]) + bias_ref[:, cut]
            half = 0.5 + 0.5 * error_function(pre * 0.5**0.5)
            act = (pre * half).astype(BF16)
            act_ref[:, cut] = act
            bell = jnp.exp(-0.5 * pre * pre) * 0.3989422804014327
            slope_ref[:, cut] = (half + pre * bell).astype(BF16)
            total = total + dot(act, wout_ref[cut, :])
        hat, spread = norm_parts(total)
        gain = row_ref[11:12, :]
        out_ref[...] = hat * gain + row_ref[12:13, :]
        cot = cot_ref[...].astype(F32)
        grad = norm_pull(cot, hat, spread, gain)
        g_ref[...] = grad
        low = grad.astype(BF16)
        glow_ref[...] = low
        sum_ref[0:1, :] += col_sum(cot * hat)
        sum_ref[1:2, :] += col_sum(cot)
        sum_ref[2:3, :] += col_sum(low)

    return call(
        body,
        "ffn_forward",
        items // group,
        [
            (total_two, tiled((block, d))),
            (cotangent, tiled((block, d))),
            (w_fin, whole((d, ff))),
            (w_fout, whole((ff, d))),
            (rows, whole(rows.shape)),
            (bias, whole(bias.shape)),
        ],
        [
            (spec_of((tokens, d), F32), tiled((block, d))),
            (spec_of((tokens, d), BF16), tiled((block, d))),
            (spec_of((tokens, ff), BF16), tiled((block, ff))),
            (spec_of((tokens, ff), BF16), tiled((block, ff))),
            (spec_of((tokens, d), F32), tiled((block, d))),
            (spec_of((tokens, d), BF16), tiled((block, d))),
            (spec_of((8, d), F32), summed((8, d))),
        ],
        4 * tokens * d * ff,
    )


def ffn_backward(dims, grad_three, grad_low, slope, total_two, w_fin, w_fout, rows):
    d, items, length, group = dims.d, dims.items, dims.length, dims.group
    tokens, block, ff = items * length, group * length, w_fin.shape[1]
    piece = d

    def body(g_ref, glow_ref, slope_ref, tot_ref, win_ref, wout_ref, row_ref,
             pre_ref, two_ref, twolow_ref, sum_ref, bias_ref):
        @pl.when(pl.program_id(0) == 0)
        def _():
            sum_ref[...] = jnp.zeros_like(sum_ref)
            bias_ref[...] = jnp.zeros_like(bias_ref)

        grad = g_ref[...]
        for at in range(0, ff, piece):
            cut = slice(at, at + piece)
            pre = dot_t(glow_ref[...], wout_ref[cut, :]) * slope_ref[:, cut].astype(F32)
            pre = pre.astype(BF16)
            pre_ref[:, cut] = pre
            bias_ref[0:1, cut] += col_sum(pre)
            grad = grad + dot_t(pre, win_ref[:, cut])
        hat, spread = norm_parts(tot_ref[...])
        two = norm_pull(grad, hat, spread, row_ref[8:9, :])
        two_ref[...] = two
        low = two.astype(BF16)
        twolow_ref[...] = low
        sum_ref[0:1, :] += col_sum(grad * hat)
        sum_ref[1:2, :] += col_sum(grad)
        sum_ref[2:3, :] += col_sum(low)

    return call(
        body,
        "ffn_backward",
        items // group,
        [
            (grad_three, tiled((block, d))),
            (grad_low, tiled((block, d))),
            (slope, tiled((block, ff))),
            (total_two, tiled((block, d))),
            (w_fin, whole((d, ff))),
            (w_fout, whole((ff, d))),
            (rows, whole(rows.shape)),
        ],
        [
            (spec_of((tokens, ff), BF16), tiled((block, ff))),
            (spec_of((tokens, d), F32), tiled((block, d))),
            (spec_of((tokens, d), BF16), tiled((block, d))),
            (spec_of((8, d), F32), summed((8, d))),
            (spec_of((8, ff), F32), summed((8, ff))),
        ],
        4 * tokens * d * ff,
    )


def cross_backward(dims, grad_two, grad_low, query, kv, probs, total_one, w_cq, w_ckv, w_cout, rows):
    d, items, length, group = dims.d, dims.items, dims.length, dims.group
    pairs, tokens, block = d // (2 * HEAD), items * length, group * length
    count, vis = kv.shape[1], w_ckv.shape[0]
    scale = HEAD ** (-0.5)

    def body(g_ref, glow_ref, q_ref, kv_ref, prob_ref, tot_ref, wcq_ref, wckv_ref, wcout_ref, row_ref,
             gq_ref, gkv_ref, gp_ref, one_ref, onelow_ref, sum_ref, ctx_ref):
        @pl.when(pl.program_id(0) == 0)
        def _():
            sum_ref[...] = jnp.zeros_like(sum_ref)

        low, high, is_low = lane_masks()
        ctx_ref[...] = dot_t(glow_ref[...], wcout_ref[...]).astype(BF16)
        for i in range(group):
            r = slice(i * length, (i + 1) * length)
            for p in range(pairs):
                c = slice(p * 128, (p + 1) * 128)
                cv = slice(d + p * 128, d + (p + 1) * 128)
                q, k, v, out = q_ref[r, c], kv_ref[i, :, c], kv_ref[i, :, cv], ctx_ref[r, c]
                grad_q, grad_k, grad_v = 0.0, [], []
                for h, side in enumerate((low, high)):
                    soft_low = prob_ref[i, 2 * p + h]
                    score = soft_pull(soft_low.astype(F32), dot_t(out, v * side)).astype(BF16)
                    grad_q = grad_q + dot(score, k * side)
                    grad_k.append(dot_l(score, q))
                    grad_v.append(dot_l(soft_low, out))
                gq_ref[r, c] = (grad_q * scale).astype(BF16)
                gkv_ref[i, :, c] = (jnp.where(is_low, *grad_k) * scale).astype(BF16)
                gkv_ref[i, :, cv] = jnp.where(is_low, *grad_v).astype(BF16)
        grad_kv = gkv_ref[...].reshape(group * count, 2 * d)
        gp_ref[...] = dot_t(grad_kv, wckv_ref[...]).astype(BF16).reshape(group, count, vis)
        grad = g_ref[...] + dot_t(gq_ref[...], wcq_ref[...])
        hat, spread = norm_parts(tot_ref[...])
        one = norm_pull(grad, hat, spread, row_ref[3:4, :])
        one_ref[...] = one
        one_low = one.astype(BF16)
        onelow_ref[...] = one_low
        sum_ref[0:1, :] += col_sum(grad * hat)
        sum_ref[1:2, :] += col_sum(grad)
        sum_ref[2:3, :] += col_sum(one_low)
        sum_ref[3:4, :] += col_sum(gq_ref[...])
        sum_ref[4:5, :] += col_sum(grad_kv[:, d:])

    return call(
        body,
        "cross_backward",
        items // group,
        [
            (grad_two, tiled((block, d))),
            (grad_low, tiled((block, d))),
            (query, tiled((block, d))),
            (kv, tiled((group, count, 2 * d))),
            (probs, tiled((group, 2 * pairs, length, count))),
            (total_one, tiled((block, d))),
            (w_cq, whole((d, d))),
            (w_ckv, whole((vis, 2 * d))),
            (w_cout, whole((d, d))),
            (rows, whole(rows.shape)),
        ],
        [
            (spec_of((tokens, d), BF16), tiled((block, d))),
            (spec_of((items, count, 2 * d), BF16), tiled((group, count, 2 * d))),
            (spec_of((items, count, vis), BF16), tiled((group, count, vis))),
            (spec_of((tokens, d), F32), tiled((block, d))),
            (spec_of((tokens, d), BF16), tiled((block, d))),
            (spec_of((8, d), F32), summed((8, d))),
        ],
        2 * tokens * d * 6 * d + 2 * items * count * vis * 2 * d,
        [pltpu.VMEM((block, d), BF16)],
    )


def self_backward(dims, grad_one, grad_low, qkv, probs, w_qkv, w_out):
    d, items, length, group = dims.d, dims.items, dims.length, dims.group
    pairs, tokens, block = d // (2 * HEAD), items * length, group * length
    scale = HEAD ** (-0.5)

    def body(g_ref, glow_ref, qkv_ref, prob_ref, wqkv_ref, wout_ref, gqkv_ref, text_ref, sum_ref, ctx_ref):
        @pl.when(pl.program_id(0) == 0)
        def _():
            sum_ref[...] = jnp.zeros_like(sum_ref)

        low, high, is_low = lane_masks()
        ctx_ref[...] = dot_t(glow_ref[...], wout_ref[...]).astype(BF16)
        for i in range(group):
            r = slice(i * length, (i + 1) * length)
            for p in range(pairs):
                cuts = [slice(part * d + p * 128, part * d + (p + 1) * 128) for part in range(3)]
                q, k, v = (qkv_ref[r, cut] for cut in cuts)
                out = ctx_ref[r, cuts[0]]
                soft_low = prob_ref[i, p]
                grad = dot_t(out, jnp.concatenate([v * low, v * high], 0))
                score = jnp.concatenate(
                    [
                        soft_pull(
                            soft_low[:, h * length : (h + 1) * length].astype(F32),
                            grad[:, h * length : (h + 1) * length],
                        )
                        for h in range(2)
                    ],
                    1,
                ).astype(BF16)
                grad_q = dot(score, jnp.concatenate([k * low, k * high], 0))
                grad_k = dot_l(score, q)
                grad_v = dot_l(soft_low, out)
                gqkv_ref[r, cuts[0]] = (grad_q * scale).astype(BF16)
                gqkv_ref[r, cuts[1]] = (
                    jnp.where(is_low, grad_k[:length], grad_k[length:]) * scale
                ).astype(BF16)
                gqkv_ref[r, cuts[2]] = jnp.where(is_low, grad_v[:length], grad_v[length:]).astype(BF16)
        text_ref[...] = g_ref[...] + dot_t(gqkv_ref[...], wqkv_ref[...])
        sum_ref[0:1, :] += col_sum(gqkv_ref[:, :d])
        sum_ref[1:2, :] += col_sum(gqkv_ref[:, 2 * d :])

    return call(
        body,
        "self_backward",
        items // group,
        [
            (grad_one, tiled((block, d))),
            (grad_low, tiled((block, d))),
            (qkv, tiled((block, 3 * d))),
            (probs, tiled((group, pairs, length, 2 * length))),
            (w_qkv, whole((d, 3 * d))),
            (w_out, whole((d, d))),
        ],
        [
            (spec_of((tokens, 3 * d), BF16), tiled((block, 3 * d))),
            (spec_of((tokens, d), F32), tiled((block, d))),
            (spec_of((8, d), F32), summed((8, d))),
        ],
        2 * tokens * d * 8 * d,
        [pltpu.VMEM((block, d), BF16)],
    )


def weight_grads(plan, group, where, factors):
    high_rows = max(plan.full[w][0] for w in group)

    def body(where_ref, *refs):
        ins, stack_refs, made = refs[: 2 * len(group)], refs[2 * len(group) : -1], refs[-1]
        for n, w in enumerate(group):
            left, right = ins[2 * n], ins[2 * n + 1]
            rows, half = plan.full[w][0], plan.full[w][1] // 2
            for j in range(plan.chunks[w]):
                for y in range(2):
                    cut = slice(y * half + j * plan.chunk, y * half + (j + 1) * plan.chunk)
                    for at in range(0, rows, 256):
                        value = dot_l(left[:, at : at + 256], right[:, cut])
                        made[y, at : at + 256, :] = value.astype(BF16)

                def visit(stack, k, row, w_at, j_at, to_row, to_y, high):
                    if w_at == w and j_at == j:
                        stack_refs[stack][k, row : row + high, :] = made[
                            to_y, pl.ds(to_row, high), :
                        ]

                each_place(plan, group, where_ref, visit)

    shape = jax.ShapeDtypeStruct((plan.zs, plan.rows(group), plan.chunk), BF16)
    flat = [a for pair in factors for a in pair]
    flops = sum(2 * a.shape[0] * a.shape[1] * b.shape[1] for a, b in factors)
    moved = sum(a.size * 2 for a in flat) + 8 * shape.size * 2
    return pl.pallas_call(
        body,
        out_shape=(shape,) * 8,
        in_specs=[SMEM_SPEC] + [VMEM_SPEC] * len(flat),
        out_specs=(VMEM_SPEC,) * 8,
        scratch_shapes=[pltpu.VMEM((2, high_rows, plan.chunk), BF16)],
        compiler_params=PARAMS,
        cost_estimate=pl.CostEstimate(flops=flops, bytes_accessed=moved, transcendentals=0),
        name="weight_grads",
    )(where, *flat)


class Dims:
    def __init__(self, d, items, length):
        self.d, self.items, self.length = d, items, length
        self.group = 2 if items % 2 == 0 else 1


def cross_mask(lengths, counts, boxes, length, pad):
    place = jnp.arange(length, dtype=jnp.int32)[None, :]
    boxed = (counts[:, None] > 0) & (place < lengths[:, None])
    phrase = jnp.where(boxed, place * counts[:, None] // lengths[:, None], 0)
    chosen = phrase[:, :, None] == jnp.arange(boxes.shape[1], dtype=jnp.int32)
    inside = jnp.einsum(
        "itj,ijp->itp",
        chosen.astype(BF16),
        (boxes > 0).astype(BF16),
        preferred_element_type=F32,
    )
    grid_ok = jnp.where(boxed[:, :, None], inside, 1.0).astype(BF16)
    own = jnp.ones(grid_ok.shape[:2] + (1,), BF16)
    return jnp.concatenate([grid_ok, own, jnp.zeros(grid_ok.shape[:2] + (pad,), BF16)], -1)


def trade_in(image_grid, count):
    micro, items, own, width = image_grid.shape
    cut = image_grid.reshape(micro, count, items // count, own, width).transpose(1, 0, 2, 3, 4)
    got = lax.all_to_all(cut, "patch", split_axis=0, concat_axis=0, tiled=True)
    return got.transpose(1, 2, 0, 3, 4).reshape(micro * items // count, count * own, width)


def trade_back(grads, micro, count):
    items, patches, width = grads.shape
    cut = grads.reshape(micro, items // micro, count, patches // count, width)
    got = lax.all_to_all(
        cut.transpose(2, 0, 1, 3, 4), "patch", split_axis=0, concat_axis=0, tiled=True
    )
    got = got.transpose(1, 0, 2, 3, 4)
    return got.reshape(micro, items // micro * count, patches // count, width)


def on_device(
    plan,
    text_in,
    image_grid,
    image_cls,
    text_lengths,
    phrase_counts,
    phrase_boxes,
    cotangent,
    *params,
):
    micro, width = text_in.shape[0], text_in.shape[2]
    shards, vectors, ffn_bias = params[:7], params[7], params[8]
    where = coords()
    items = text_lengths.size
    text, cot = text_in.reshape(-1, width), cotangent.reshape(-1, width)
    lengths = text_lengths.reshape(-1)
    dims = Dims(width, items, text.shape[0] // items)
    rows, bias = gather_small(plan, where, vectors, ffn_bias)
    rows = jnp.pad(rows, ((0, -rows.shape[0] % 8), (0, 0)))
    own, give = pack_split(plan, where, shards)
    units = pack_join(plan, where, own, send(give, plan.core()))
    grid = trade_in(image_grid, plan.patch)
    real = grid.shape[1]
    pad = -(real + 1) % 16
    patches = jnp.concatenate(
        [
            grid,
            image_cls.reshape(items, 1, -1),
            jnp.zeros((items, pad, grid.shape[2]), BF16),
        ],
        axis=1,
    )
    boxes = phrase_boxes.reshape((items,) + phrase_boxes.shape[2:])
    mask = cross_mask(lengths, phrase_counts.reshape(-1), boxes, dims.length, pad)

    weights = {}

    def ready(g):
        full = assemble(plan, GATHER[g], where, gathers[g].held)
        for w, value in zip(GATHER[g], full):
            weights[w] = value

    gathers = [Gathering(plan, unit) for unit in units]
    gathers[0].advance()
    fence(gathers, [])
    gathers[0].advance()
    gathers[1].advance()
    rows, patches, mask, bias = fence(gathers, [rows, patches, mask, bias])
    gathers[0].advance()
    gathers[1].advance()
    gathers[2].advance()
    fence(gathers, [])
    gathers[1].advance()
    gathers[2].advance()
    gathers[3].advance()
    ready(0)
    qkv, probs, ctx, total_one = self_forward(dims, text, weights[QKV], weights[OUT], rows, lengths)
    total_one = fence(gathers[1:], total_one)
    gathers[2].advance()
    gathers[3].advance()
    ready(1)
    hidden_one, query, kv, cross_probs, cross_ctx, total_two = cross_forward(
        dims, total_one, patches, mask, weights[CQ], weights[CKV], weights[COUT], rows
    )
    total_two = fence(gathers[3:], total_two)
    gathers[3].advance()
    ready(2)
    ready(3)
    layer_out, hidden_two, act, slope, grad_three, low_three, sum_three = ffn_forward(
        dims, total_two, cot, weights[FIN], weights[FOUT], rows, bias[None]
    )
    reduces = {}

    def reduce(g, factors):
        stacks = weight_grads(plan, REDUCE[g], where, factors)
        reduces[g] = Reducing(plan, REDUCE[g], where, stacks)

    def hold(values):
        return fence(list(reduces.values()), values)

    def go(*groups):
        for g in groups:
            reduces[g].advance()

    reduce(3, [(act, low_three)])
    grad_three = hold(grad_three)
    go(3)
    grad_pre, grad_two, low_two, sum_two, sum_pre = ffn_backward(
        dims, grad_three, low_three, slope, total_two, weights[FIN], weights[FOUT], rows
    )
    grad_pre, grad_two = hold([grad_pre, grad_two])
    go(3)
    reduce(2, [(hidden_two, grad_pre)])
    grad_two = hold(grad_two)
    go(3, 2)
    grad_query, grad_kv, grad_patch, grad_one, low_one, sum_one = cross_backward(
        dims, grad_two, low_two, query, kv, cross_probs, total_one,
        weights[CQ], weights[CKV], weights[COUT], rows,
    )
    grad_query, grad_one, grad_patch, low_one = hold([grad_query, grad_one, grad_patch, low_one])
    go(3, 2)
    flat_patches = patches.reshape(-1, patches.shape[2])
    flat_kv = grad_kv.reshape(-1, grad_kv.shape[2])
    reduce(
        1,
        [(hidden_one, grad_query), (flat_patches, flat_kv), (cross_ctx, low_two), (ctx, low_one)],
    )
    grad_one = hold(grad_one)
    go(3, 2, 1)
    grad_qkv, text_grad, sum_self = self_backward(
        dims, grad_one, low_one, qkv, probs, weights[QKV], weights[OUT]
    )
    grad_qkv, sum_self = hold([grad_qkv, sum_self])
    rows_grad = jnp.concatenate(
        [
            sum_self[0:2],
            sum_one[2:3],
            sum_one[0:2],
            sum_one[3:5],
            sum_two[2:3],
            sum_two[0:2],
            sum_three[2:3],
            sum_three[0:2],
        ]
    )
    rows_grad, bias_grad = reduce_small(plan, where, rows_grad, sum_pre[0])
    go(3, 2, 1)
    reduce(0, [(text, grad_qkv)])
    hold([])
    go(2, 1, 0)
    go(2)
    grid_grad = trade_back(grad_patch[:, :real], micro, plan.patch).astype(F32)
    grid_grad = hold(grid_grad)
    go(1, 0)
    hold([])
    go(1, 0)
    go(1)
    hold([])
    go(0)
    hold([])
    go(0)
    go(0)
    grads = [None] * 7
    for g, group in enumerate(REDUCE):
        for w, value in zip(group, reduces[g].held):
            grads[w] = value
    cls_grad = grad_patch[:, real].astype(F32).reshape(image_cls.shape)
    return (
        layer_out.reshape(text_in.shape),
        text_grad.reshape(text_in.shape),
        grid_grad,
        cls_grad,
        *grads,
        rows_grad,
        bias_grad,
    )


def on_device_plain(
    plan,
    text_in,
    image_grid,
    image_cls,
    text_lengths,
    phrase_counts,
    phrase_boxes,
    cotangent,
    *params,
):
    micro, width = text_in.shape[0], text_in.shape[2]
    shards, vectors, ffn_bias = params[:7], params[7], params[8]
    items = text_lengths.size
    text, cot = text_in.reshape(-1, width), cotangent.reshape(-1, width)
    lengths = text_lengths.reshape(-1)
    dims = Dims(width, items, text.shape[0] // items)
    weights, rows, bias = fetch_plain(shards, vectors, ffn_bias)
    rows = jnp.pad(rows, ((0, -rows.shape[0] % 8), (0, 0)))
    grid = trade_in(image_grid, plan.patch)
    real = grid.shape[1]
    pad = -(real + 1) % 16
    patches = jnp.concatenate(
        [
            grid,
            image_cls.reshape(items, 1, -1),
            jnp.zeros((items, pad, grid.shape[2]), BF16),
        ],
        axis=1,
    )
    boxes = phrase_boxes.reshape((items,) + phrase_boxes.shape[2:])
    mask = cross_mask(lengths, phrase_counts.reshape(-1), boxes, dims.length, pad)

    qkv, probs, ctx, total_one = self_forward(dims, text, weights[QKV], weights[OUT], rows, lengths)
    hidden_one, query, kv, cross_probs, cross_ctx, total_two = cross_forward(
        dims, total_one, patches, mask, weights[CQ], weights[CKV], weights[COUT], rows
    )
    layer_out, hidden_two, act, slope, grad_three, low_three, sum_three = ffn_forward(
        dims, total_two, cot, weights[FIN], weights[FOUT], rows, bias[None]
    )
    grads = [None] * 7

    def reduce(g, factors):
        for w, (a, b) in zip(REDUCE[g], factors):
            grads[w] = reduce_plain(dot_l(a, b).astype(BF16))

    reduce(3, [(act, low_three)])
    grad_pre, grad_two, low_two, sum_two, sum_pre = ffn_backward(
        dims, grad_three, low_three, slope, total_two, weights[FIN], weights[FOUT], rows
    )
    reduce(2, [(hidden_two, grad_pre)])
    grad_query, grad_kv, grad_patch, grad_one, low_one, sum_one = cross_backward(
        dims, grad_two, low_two, query, kv, cross_probs, total_one,
        weights[CQ], weights[CKV], weights[COUT], rows,
    )
    flat_patches = patches.reshape(-1, patches.shape[2])
    flat_kv = grad_kv.reshape(-1, grad_kv.shape[2])
    reduce(
        1,
        [(hidden_one, grad_query), (flat_patches, flat_kv), (cross_ctx, low_two), (ctx, low_one)],
    )
    grad_qkv, text_grad, sum_self = self_backward(
        dims, grad_one, low_one, qkv, probs, weights[QKV], weights[OUT]
    )
    reduce(0, [(text, grad_qkv)])
    rows_grad = jnp.concatenate(
        [
            sum_self[0:2],
            sum_one[2:3],
            sum_one[0:2],
            sum_one[3:5],
            sum_two[2:3],
            sum_two[0:2],
            sum_three[2:3],
            sum_three[0:2],
        ]
    )
    rows_grad, bias_grad = reduce_small_plain(rows_grad, sum_pre[0])
    cls_grad = grad_patch[:, real].astype(F32).reshape(image_cls.shape)
    grid_grad = trade_back(grad_patch[:, :real], micro, plan.patch).astype(F32)
    return (
        layer_out.reshape(text_in.shape),
        text_grad.reshape(text_in.shape),
        grid_grad,
        cls_grad,
        *grads,
        rows_grad,
        bias_grad,
    )


def solution(mesh):
    dp, patch = mesh.shape["dp"], mesh.shape["patch"]
    both = P(None, ("dp", "patch"), None)
    weight = P("dp", "patch")

    def run(*args):
        shards = [(w.shape[0] // dp, w.shape[1] // patch) for w in args[7:14]]
        plan = Plan(dp, patch, shards)
        return jax.shard_map(
            functools.partial(on_device if plan.fast else on_device_plain, plan),
            mesh=mesh,
            in_specs=(
                both,
                P(None, "dp", "patch", None),
                both,
                P(None, ("dp", "patch")),
                P(None, ("dp", "patch")),
                P(None, ("dp", "patch"), None, None),
                both,
            )
            + (weight,) * 7
            + (P(None, "dp"), P("dp")),
            out_specs=(both, both, P(None, "dp", "patch", None), both)
            + (weight,) * 7
            + (P(None, "dp"), P("dp")),
            check_vma=False,
        )(*args)

    return run
```

```python
import functools

import jax
import jax.numpy as jnp
from jax import lax
from jax.experimental import pallas as pl
from jax.experimental.pallas import tpu as pltpu
from jax.sharding import PartitionSpec as P

HEAD = 64
EPS = 1e-06
NEG = -1e30
BF16 = jnp.bfloat16
F32 = jnp.float32
AXES = ("dp", "patch")
VMEM_SPEC = pl.BlockSpec(memory_space=pltpu.VMEM)
SMEM_SPEC = pl.BlockSpec(memory_space=pltpu.SMEM)
PARAMS = pltpu.CompilerParams(vmem_limit_bytes=62 * 2**20)

QKV, OUT, CQ, CKV, COUT, FIN, FOUT = range(7)
GATHER = ((QKV, OUT), (CQ, CKV, COUT), (FIN,), (FOUT,))
REDUCE = ((QKV, OUT), (CQ, CKV, COUT), (FIN,), (FOUT,))


class Plan:
    def __init__(self, dp, patch, shards):
        self.dp, self.patch = dp, patch
        self.zs = dp // 2
        self.devices = dp * patch
        self.chunk = shards[OUT][1] * 2
        self.half = [s[0] // 2 for s in shards]
        self.cols = [s[1] for s in shards]
        self.chunks = [s[1] * 2 // self.chunk for s in shards]
        self.full = [(s[0] * dp, s[1] * patch) for s in shards]
        self.fast = (
            dp % 2 == 0
            and patch == 4
            and all(h % 16 == 0 for h in self.half)
            and all(s[1] * 2 % self.chunk == 0 for s in shards)
            and self.chunk % 128 == 0
        )

    def rows(self, group):
        return sum(self.half[w] * self.chunks[w] for w in group)

    def flip(self, pick):
        return [(i, i ^ pick(i)) for i in range(self.devices)]

    def core(self):
        return self.flip(lambda i: 1)

    def first(self):
        return self.flip(lambda i: 4 if i % 2 == 0 else 2)

    def second(self):
        return self.flip(lambda i: 2 if i % 2 == 0 else 4)

    def z_up(self, k):
        return [(i, (i + 8 * k) % self.devices) for i in range(self.devices)]


def send(value, perm):
    return lax.ppermute(value, AXES, perm)


def coords():
    dp, patch = lax.axis_index("dp"), lax.axis_index("patch")
    return jnp.stack([dp // 2, dp % 2, patch // 2, patch % 2]).astype(jnp.int32)


def piece_rows(group, plan):
    at, found = 0, []
    for w in group:
        for j in range(plan.chunks[w]):
            found.append((w, j, at))
            at += plan.half[w]
    return found


def group_starts(plan):
    starts, at = [], 0
    for group in GATHER:
        starts.append(at)
        at += plan.rows(group)
    return starts, at


def pack_split(plan, where, shards):
    _, total = group_starts(plan)
    wide = plan.chunk // 2

    def body(where_ref, *refs):
        shard_refs, (own_ref, send_ref) = refs[:7], refs[7:]
        core = where_ref[3]
        at = 0
        for group in GATHER:
            for w in group:
                high = plan.half[w]
                for b in range(plan.chunks[w]):
                    cut = slice(b * wide, (b + 1) * wide)
                    own_ref[at : at + high, :] = shard_refs[w][pl.ds(core * high, high), cut]
                    send_ref[at : at + high, :] = shard_refs[w][
                        pl.ds((1 - core) * high, high), cut
                    ]
                    at += high

    shape = jax.ShapeDtypeStruct((total, wide), BF16)
    return pl.pallas_call(
        body,
        out_shape=(shape, shape),
        in_specs=[SMEM_SPEC] + [VMEM_SPEC] * 7,
        out_specs=(VMEM_SPEC, VMEM_SPEC),
        compiler_params=PARAMS,
        name="pack_split",
    )(where, *shards)


def pack_join(plan, where, own, got):
    starts, total = group_starts(plan)
    wide = plan.chunk // 2

    def body(where_ref, own_ref, got_ref, *unit_refs):
        core = where_ref[3]

        def fill(low_ref, high_ref):
            for g, group in enumerate(GATHER):
                at = starts[g]
                for w in group:
                    high, count = plan.half[w], plan.chunks[w]
                    for j in range(count):
                        pair = []
                        for b in (2 * j, 2 * j + 1):
                            src = low_ref if b < count else high_ref
                            row = at + (b % count) * high
                            pair.append(src[row : row + high, :])
                        to = at - starts[g] + j * high
                        unit_refs[g][to : to + high, :] = jnp.concatenate(pair, axis=1)
                    at += count * high

        @pl.when(core == 0)
        def _():
            fill(own_ref, got_ref)

        @pl.when(core == 1)
        def _():
            fill(got_ref, own_ref)

    return pl.pallas_call(
        body,
        out_shape=tuple(jax.ShapeDtypeStruct((plan.rows(g), plan.chunk), BF16) for g in GATHER),
        in_specs=[SMEM_SPEC, VMEM_SPEC, VMEM_SPEC],
        out_specs=(VMEM_SPEC,) * len(GATHER),
        compiler_params=PARAMS,
        name="pack_join",
    )(where, own, got)


class Gathering:
    def __init__(self, plan, unit):
        self.plan, self.held, self.step = plan, [unit], 0

    def advance(self):
        plan, held = self.plan, self.held
        if self.step == 0:
            held = held + [send(held[0], plan.z_up(k)) for k in range(1, plan.zs)]
        elif self.step == 1:
            stack = jnp.stack(held)
            held = [stack, send(stack, plan.first()), send(stack, plan.second())]
            held.append(send(stack, plan.core()))
        elif self.step == 2:
            stack, near, side, stack_core = held
            far = send(near, plan.second())
            held = [stack, near, side, far, stack_core]
            held += [send(part, plan.core()) for part in (near, side, far)]
        self.held, self.step = held, self.step + 1


def each_place(plan, group, where_ref, visit):
    z, x, y, core = (where_ref[i] for i in range(4))
    for other in range(2):
        half = core ^ other
        for second in range(2):
            for first in range(2):
                x_at = x ^ jnp.where(half == 0, first, second)
                y_at = y ^ jnp.where(half == 0, second, first)
                for k in range(plan.zs):
                    z_at = lax.rem(z + plan.zs - k, plan.zs)
                    place = (z_at * 2 + x_at) * 2 + half
                    for w, j, row in piece_rows(group, plan):
                        high = plan.half[w]
                        to_row = pl.multiple_of(place * high, 16)
                        stack = other * 4 + second * 2 + first
                        visit(stack, k, row, w, j, to_row, y_at, high)


def assemble(plan, group, where, stacks):

    def body(where_ref, *refs):
        stack_refs, full_refs = refs[:8], dict(zip(group, refs[8:]))

        def visit(stack, k, row, w, j, to_row, to_y, high):
            to_col = pl.multiple_of(to_y * (plan.full[w][1] // 2) + j * plan.chunk, 128)
            full_refs[w][pl.ds(to_row, high), pl.ds(to_col, plan.chunk)] = stack_refs[stack][
                k, row : row + high, :
            ]

        each_place(plan, group, where_ref, visit)

    return pl.pallas_call(
        body,
        out_shape=tuple(jax.ShapeDtypeStruct(plan.full[w], BF16) for w in group),
        in_specs=[SMEM_SPEC] + [VMEM_SPEC] * 8,
        out_specs=(VMEM_SPEC,) * len(group),
        compiler_params=PARAMS,
        name="assemble",
    )(where, *stacks)


def add_low(ones, twos):
    n = len(ones)
    shape = ones[0].shape

    def body(*refs):
        for a, b, out in zip(refs[:n], refs[n : 2 * n], refs[2 * n :]):
            out[...] = (a[...].astype(F32) + b[...].astype(F32)).astype(BF16)

    spec = pl.BlockSpec((1,) + shape[1:], lambda i: (i, 0, 0))
    size = shape[0] * shape[1] * shape[2]
    return pl.pallas_call(
        body,
        grid=(shape[0],),
        out_shape=(jax.ShapeDtypeStruct(shape, BF16),) * n,
        in_specs=[spec] * (2 * n),
        out_specs=(spec,) * n,
        compiler_params=PARAMS,
        cost_estimate=pl.CostEstimate(
            flops=n * size, bytes_accessed=6 * n * size, transcendentals=0
        ),
        name="add_low",
    )(*ones, *twos)


class Reducing:
    def __init__(self, plan, group, where, stacks):
        self.plan, self.group, self.where = plan, group, where
        self.held, self.step = list(stacks), 0

    def advance(self):
        plan, held = self.plan, self.held
        if self.step == 0:
            held = held[:4] + [send(part, plan.core()) for part in held[4:]]
        elif self.step == 1:
            mine = add_low(held[:4], held[4:])
            held = list(mine[:2]) + [send(part, plan.second()) for part in mine[2:]]
        elif self.step == 2:
            mine = add_low(held[:2], held[2:])
            held = [mine[0], send(mine[1], plan.first())]
        elif self.step == 3:
            (total,) = add_low(held[:1], held[1:])
            parts = [send(total[k], plan.z_up(plan.zs - k)) for k in range(1, plan.zs)]
            held = [total[0]] + parts
        elif self.step == 4:
            own, give = unpack_split(plan, self.group, self.where, held)
            held = [own, send(give, plan.core())]
        elif self.step == 5:
            held = unpack_join(plan, self.group, self.where, *held)
        self.held, self.step = list(held), self.step + 1


def fence(chains, values):
    flat, tree = jax.tree.flatten([values, [chain.held for chain in chains]])
    values, held = jax.tree.unflatten(tree, lax.optimization_barrier(flat))
    for chain, arrays in zip(chains, held):
        chain.held = arrays
    return values


def unpack_split(plan, group, where, parts):
    rows, wide = plan.rows(group), plan.chunk // 2

    def body(where_ref, *refs):
        part_refs, (own_ref, give_ref) = refs[:-2], refs[-2:]
        core = where_ref[3]

        def fill(low_ref, high_ref):
            at = 0
            for w in group:
                high, count = plan.half[w], plan.chunks[w]
                for j in range(count):
                    row = at + j * high
                    value = sum(p[row : row + high, :].astype(F32) for p in part_refs)
                    for b in (2 * j, 2 * j + 1):
                        dst = low_ref if b < count else high_ref
                        to = at + (b % count) * high
                        cut = (b - 2 * j) * wide
                        dst[to : to + high, :] = value[:, cut : cut + wide]
                at += count * high

        @pl.when(core == 0)
        def _():
            fill(own_ref, give_ref)

        @pl.when(core == 1)
        def _():
            fill(give_ref, own_ref)

    shape = jax.ShapeDtypeStruct((rows, wide), F32)
    return pl.pallas_call(
        body,
        out_shape=(shape, shape),
        in_specs=[SMEM_SPEC] + [VMEM_SPEC] * len(parts),
        out_specs=(VMEM_SPEC, VMEM_SPEC),
        compiler_params=PARAMS,
        name="unpack_split",
    )(where, *parts)


def unpack_join(plan, group, where, own, got):
    wide = plan.chunk // 2

    def body(where_ref, own_ref, got_ref, *out_refs):
        core = where_ref[3]
        at = 0
        for w, out_ref in zip(group, out_refs):
            high, count = plan.half[w], plan.chunks[w]
            own_rows = pl.ds(pl.multiple_of(core * high, 16), high)
            got_rows = pl.ds(pl.multiple_of((1 - core) * high, 16), high)
            for b in range(count):
                row, cut = at + b * high, slice(b * wide, (b + 1) * wide)
                out_ref[own_rows, cut] = own_ref[row : row + high, :]
                out_ref[got_rows, cut] = got_ref[row : row + high, :]
            at += count * high

    return pl.pallas_call(
        body,
        out_shape=tuple(
            jax.ShapeDtypeStruct((2 * plan.half[w], plan.cols[w]), F32) for w in group
        ),
        in_specs=[SMEM_SPEC, VMEM_SPEC, VMEM_SPEC],
        out_specs=(VMEM_SPEC,) * len(group),
        compiler_params=PARAMS,
        name="unpack_join",
    )(where, own, got)


def gather_small(plan, where, vectors, bias):
    count, part = vectors.shape
    flat = jnp.concatenate([vectors.reshape(-1), bias])
    size = flat.shape[0]
    flat = jnp.pad(flat, (0, -size % 2048)).reshape(-1, 128)
    pair = jnp.stack([flat, send(flat, plan.flip(lambda i: 4))])
    every = jnp.stack([pair] + [send(pair, plan.z_up(k)) for k in range(1, plan.zs)])
    every = every.reshape((plan.dp,) + flat.shape)
    at = jnp.arange(plan.dp, dtype=jnp.int32)
    slot = lax.rem(where[0] - at // 2 + plan.zs, plan.zs) * 2 + ((at % 2) ^ where[1])
    every = jnp.take(every, slot, axis=0).reshape(plan.dp, -1)[:, :size].astype(F32)
    rows = every[:, : count * part].reshape(plan.dp, count, part)
    rows = rows.transpose(1, 0, 2).reshape(count, plan.dp * part)
    return rows, every[:, count * part :].reshape(-1)


class ReducingSmall:
    def __init__(self, plan, where, rows, bias):
        self.plan, self.where, self.shape, self.tail = plan, where, rows.shape, bias.shape[0]
        flat = jnp.concatenate([rows.reshape(-1), bias])
        flat = jnp.pad(flat, (0, -flat.shape[0] % 1024)).reshape(-1, 128)
        self.held, self.step = [flat], 0

    def advance(self):
        plan = self.plan
        flat = sum(self.held)
        if self.step < 3:
            bit = 1 << self.step
            self.held = [flat, send(flat, plan.flip(lambda i: bit))]
        else:
            self.held = [flat] + [send(flat, plan.z_up(k)) for k in range(1, plan.zs)]
        self.step += 1

    def result(self):
        plan, (count, width) = self.plan, self.shape
        flat = sum(self.held).reshape(-1)
        dp = self.where[0] * 2 + self.where[1]
        main = flat[: count * width].reshape(count, width)
        own = lax.dynamic_slice_in_dim(main, dp * (width // plan.dp), width // plan.dp, axis=1)
        tail, step = flat[count * width : count * width + self.tail], self.tail // plan.dp
        return own, lax.dynamic_slice_in_dim(tail, dp * step, step, axis=0)


def fetch_plain(weights, vectors, bias):
    whole = [
        lax.all_gather(lax.all_gather(w, "dp", axis=0, tiled=True), "patch", axis=1, tiled=True)
        for w in weights
    ]
    rows = lax.all_gather(vectors, "dp", axis=1, tiled=True)
    return whole, rows.astype(F32), lax.all_gather(bias, "dp", axis=0, tiled=True).astype(F32)


def reduce_plain(grad):
    part = lax.psum_scatter(grad, "dp", scatter_dimension=0, tiled=True)
    return lax.psum_scatter(part, "patch", scatter_dimension=1, tiled=True).astype(F32)


def reduce_small_plain(rows, bias):
    rows = lax.psum_scatter(rows, "dp", scatter_dimension=1, tiled=True)
    bias = lax.psum_scatter(bias, "dp", scatter_dimension=0, tiled=True)
    return lax.psum(rows, "patch"), lax.psum(bias, "patch")


TAIL = (0.112528827, 0.117839666, 0.0706314405, 0.2046457425, -0.190499398, 0.3478185715, -0.201092832, 0.03812798145)


def dot(a, b):
    return lax.dot_general(a, b, (((1,), (0,)), ((), ())), preferred_element_type=F32)


def dot_t(a, b):
    return lax.dot_general(a, b, (((1,), (1,)), ((), ())), preferred_element_type=F32)


def dot_l(a, b):
    return lax.dot_general(a, b, (((0,), (0,)), ((), ())), preferred_element_type=F32)


def norm_parts(total):
    center = total - jnp.mean(total, -1, keepdims=True)
    spread = lax.rsqrt(jnp.mean(center * center, -1, keepdims=True) + EPS)
    return center * spread, spread


def norm_pull(grad, hat, spread, gain):
    scaled = grad * gain
    return spread * (
        scaled
        - jnp.mean(scaled, -1, keepdims=True)
        - hat * jnp.mean(scaled * hat, -1, keepdims=True)
    )


def gelu_parts(x):
    bell = jnp.exp(-0.5 * (x * x))
    t = 1.0 / (1.0 + (0.4 * 0.5**0.5) * jnp.abs(x))
    tail = jnp.full_like(t, TAIL[-1])
    for c in TAIL[-2::-1]:
        tail = tail * t + c
    tail = tail * (t * bell)
    return jnp.where(x < 0.0, tail, 1.0 - tail), bell


def col_sum(value):
    return jnp.sum(value.astype(F32), 0, keepdims=True)


def soft(scores):
    grown = jnp.exp(scores - jnp.max(scores, 0, keepdims=True))
    return grown * (1.0 / jnp.sum(grown, 0, keepdims=True))


def soft_pull(probs, grad):
    return probs * (grad - jnp.sum(probs * grad, 0, keepdims=True))


def spread_heads(value, low, high):
    return jnp.concatenate([value * low, value * high], 0)


def join_heads(value):
    count = value.shape[1] // 2
    value = jnp.concatenate([value[:HEAD, :count], value[HEAD:, count:]], 0)
    return value.astype(BF16).T


def lane_masks():
    lane = lax.broadcasted_iota(jnp.int32, (1, 2 * HEAD), 1)
    low = (lane < HEAD).astype(F32)
    return low.astype(BF16), (1.0 - low).astype(BF16)


def whole(shape):
    return pl.BlockSpec(
        shape, lambda i: (0,) * len(shape), pipeline_mode=pl.Buffered(1)
    )


def summed(shape):
    return pl.BlockSpec(shape, lambda i: (0,) * len(shape))


def tiled(shape):
    return pl.BlockSpec(shape, lambda i: (i,) + (0,) * (len(shape) - 1))


def spec_of(shape, dtype):
    return jax.ShapeDtypeStruct(shape, dtype)


def call(body, name, steps, ins, outs, flops, scratch=()):
    out_shape = tuple(shape for shape, _ in outs)
    moved = sum(a.size * a.dtype.itemsize for a, _ in ins)
    moved += sum(o.size * jnp.dtype(o.dtype).itemsize for o in out_shape)
    return pl.pallas_call(
        body,
        grid=(steps,),
        out_shape=out_shape,
        in_specs=[spec for _, spec in ins],
        out_specs=tuple(spec for _, spec in outs),
        scratch_shapes=list(scratch),
        compiler_params=PARAMS,
        cost_estimate=pl.CostEstimate(
            flops=int(flops), bytes_accessed=int(moved), transcendentals=0
        ),
        name=name,
    )(*[a for a, _ in ins])


def self_forward(dims, text, w_qkv, w_out, rows, lengths):
    d, items, length, group = dims.d, dims.items, dims.length, dims.group
    pairs, tokens, block = d // (2 * HEAD), items * length, group * length
    scale = HEAD ** (-0.5)

    def body(len_ref, x_ref, wqkv_ref, wout_ref, row_ref, qkv_ref, prob_ref, ctx_ref, tot_ref):
        step = pl.program_id(0)
        low, high = lane_masks()
        x = x_ref[...]
        for part, bias in ((0, 0), (1, None), (2, 1)):
            cut = slice(part * d, (part + 1) * d)
            value = dot(x, wqkv_ref[:, cut])
            if bias is not None:
                value = value + row_ref[bias : bias + 1, :]
            qkv_ref[:, cut] = value.astype(BF16)
        place = lax.broadcasted_iota(jnp.int32, (length, 1), 0)
        for i in range(group):
            ok = place < len_ref[step * group + i]
            r = slice(i * length, (i + 1) * length)
            for p in range(pairs):
                q, k, v = (
                    qkv_ref[r, part * d + p * 128 : part * d + (p + 1) * 128] for part in range(3)
                )
                scores = dot_t(k, spread_heads(q, low, high)) * scale
                probs = soft(jnp.where(ok, scores, NEG)).astype(BF16)
                prob_ref[i, p] = probs
                ctx_ref[r, p * 128 : (p + 1) * 128] = join_heads(dot(v.T, probs))
        tot_ref[...] = x.astype(F32) + dot(ctx_ref[...], wout_ref[...]) + row_ref[2:3, :]

    return call(
        body,
        "self_forward",
        items // group,
        [
            (lengths, SMEM_SPEC),
            (text, tiled((block, d))),
            (w_qkv, whole((d, 3 * d))),
            (w_out, whole((d, d))),
            (rows, whole(rows.shape)),
        ],
        [
            (spec_of((tokens, 3 * d), BF16), tiled((block, 3 * d))),
            (spec_of((items, pairs, length, 2 * length), BF16), tiled((group, pairs, length, 2 * length))),
            (spec_of((tokens, d), BF16), tiled((block, d))),
            (spec_of((tokens, d), F32), tiled((block, d))),
        ],
        2 * tokens * d * 6 * d,
    )


def cross_forward(dims, total_one, grids, cls, mask, w_cq, w_ckv, w_cout, rows):
    d, items, length, group = dims.d, dims.items, dims.length, dims.group
    pairs, tokens, block = d // (2 * HEAD), items * length, group * length
    count, part, vis = mask.shape[1], grids[0].shape[1], cls.shape[2]
    scale = HEAD ** (-0.5)
    parts = len(grids)

    def body(tot_ref, *refs):
        grid_refs = refs[:parts]
        cls_ref, mask_ref, wcq_ref, wckv_ref, wcout_ref, row_ref = refs[parts : parts + 6]
        h_ref, cq_ref, kv_ref, prob_ref, ctx_ref, two_ref, patch_ref = refs[parts + 6 :]
        low, high = lane_masks()
        hat, _ = norm_parts(tot_ref[...])
        hidden = hat * row_ref[3:4, :] + row_ref[4:5, :]
        h_ref[...] = hidden.astype(BF16)
        cq_ref[...] = (dot(h_ref[...], wcq_ref[...]) + row_ref[5:6, :]).astype(BF16)
        for i in range(group):
            for k in range(parts):
                patch_ref[i, k * part : (k + 1) * part, :] = grid_refs[k][i]
            rest = jnp.zeros((count - parts * part - 1, vis), BF16)
            patch_ref[i, parts * part :, :] = jnp.concatenate([cls_ref[i], rest], 0)
        patch = patch_ref[...].reshape(group * count, vis)
        keys = dot(patch, wckv_ref[:, :d]).astype(BF16)
        kv_ref[:, :, :d] = keys.reshape(group, count, d)
        values = (dot(patch, wckv_ref[:, d:]) + row_ref[6:7, :]).astype(BF16)
        kv_ref[:, :, d:] = values.reshape(group, count, d)
        for i in range(group):
            ok = mask_ref[i].astype(F32) > 0.5
            ok = jnp.concatenate([ok, ok], 1)
            r = slice(i * length, (i + 1) * length)
            for p in range(pairs):
                c = slice(p * 128, (p + 1) * 128)
                q, k, v = cq_ref[r, c], kv_ref[i, :, c], kv_ref[i, :, d + p * 128 : d + (p + 1) * 128]
                scores = dot_t(k, spread_heads(q, low, high)) * scale
                probs = soft(jnp.where(ok, scores, NEG)).astype(BF16)
                prob_ref[i, p] = probs
                ctx_ref[r, c] = join_heads(dot(v.T, probs))
        two_ref[...] = hidden + dot(ctx_ref[...], wcout_ref[...]) + row_ref[7:8, :]

    return call(
        body,
        "cross_forward",
        items // group,
        [(total_one, tiled((block, d)))]
        + [(grid, tiled((group, part, vis))) for grid in grids]
        + [
            (cls, tiled((group, 1, vis))),
            (mask, tiled((group, count, length))),
            (w_cq, whole((d, d))),
            (w_ckv, whole((vis, 2 * d))),
            (w_cout, whole((d, d))),
            (rows, whole(rows.shape)),
        ],
        [
            (spec_of((tokens, d), BF16), tiled((block, d))),
            (spec_of((tokens, d), BF16), tiled((block, d))),
            (spec_of((items, count, 2 * d), BF16), tiled((group, count, 2 * d))),
            (spec_of((items, pairs, count, 2 * length), BF16), tiled((group, pairs, count, 2 * length))),
            (spec_of((tokens, d), BF16), tiled((block, d))),
            (spec_of((tokens, d), F32), tiled((block, d))),
            (spec_of((items, count, vis), BF16), tiled((group, count, vis))),
        ],
        2 * tokens * d * 4 * d + 2 * items * count * vis * 2 * d,
    )


def ffn_forward(dims, total_two, cotangent, w_fin, w_fout, rows, bias):
    d, items, length, group = dims.d, dims.items, dims.length, dims.group
    tokens, block, ff = items * length, group * length, w_fin.shape[1]
    piece = d

    def body(tot_ref, cot_ref, win_ref, wout_ref, row_ref, bias_ref,
             out_ref, h_ref, act_ref, slope_ref, g_ref, glow_ref, sum_ref):
        @pl.when(pl.program_id(0) == 0)
        def _():
            sum_ref[...] = jnp.zeros_like(sum_ref)

        hat, _ = norm_parts(tot_ref[...])
        hidden = hat * row_ref[8:9, :] + row_ref[9:10, :]
        h_ref[...] = hidden.astype(BF16)
        total = hidden + row_ref[10:11, :]
        for at in range(0, ff, piece):
            cut = slice(at, at + piece)
            pre = dot(h_ref[...], win_ref[:, cut]) + bias_ref[:, cut]
            under, bell = gelu_parts(pre)
            act = (pre * under).astype(BF16)
            act_ref[:, cut] = act
            slope_ref[:, cut] = (under + (pre * 0.3989422804014327) * bell).astype(BF16)
            total = total + dot(act, wout_ref[cut, :])
        hat, spread = norm_parts(total)
        gain = row_ref[11:12, :]
        out_ref[...] = hat * gain + row_ref[12:13, :]
        cot = cot_ref[...].astype(F32)
        grad = norm_pull(cot, hat, spread, gain)
        g_ref[...] = grad
        low = grad.astype(BF16)
        glow_ref[...] = low
        sum_ref[0:1, :] += col_sum(cot * hat)
        sum_ref[1:2, :] += col_sum(cot)
        sum_ref[2:3, :] += col_sum(low)

    return call(
        body,
        "ffn_forward",
        items // group,
        [
            (total_two, tiled((block, d))),
            (cotangent, tiled((block, d))),
            (w_fin, whole((d, ff))),
            (w_fout, whole((ff, d))),
            (rows, whole(rows.shape)),
            (bias, whole(bias.shape)),
        ],
        [
            (spec_of((tokens, d), F32), tiled((block, d))),
            (spec_of((tokens, d), BF16), tiled((block, d))),
            (spec_of((tokens, ff), BF16), tiled((block, ff))),
            (spec_of((tokens, ff), BF16), tiled((block, ff))),
            (spec_of((tokens, d), F32), tiled((block, d))),
            (spec_of((tokens, d), BF16), tiled((block, d))),
            (spec_of((8, d), F32), summed((8, d))),
        ],
        4 * tokens * d * ff,
    )


def ffn_backward(dims, grad_three, grad_low, slope, total_two, w_fin, w_fout, rows):
    d, items, length, group = dims.d, dims.items, dims.length, dims.group
    tokens, block, ff = items * length, group * length, w_fin.shape[1]
    piece = d

    def body(g_ref, glow_ref, slope_ref, tot_ref, win_ref, wout_ref, row_ref,
             pre_ref, two_ref, twolow_ref, sum_ref, bias_ref):
        @pl.when(pl.program_id(0) == 0)
        def _():
            sum_ref[...] = jnp.zeros_like(sum_ref)
            bias_ref[...] = jnp.zeros_like(bias_ref)

        grad = g_ref[...]
        for at in range(0, ff, piece):
            cut = slice(at, at + piece)
            pre = dot_t(glow_ref[...], wout_ref[cut, :]) * slope_ref[:, cut].astype(F32)
            pre = pre.astype(BF16)
            pre_ref[:, cut] = pre
            bias_ref[0:1, cut] += col_sum(pre)
            grad = grad + dot_t(pre, win_ref[:, cut])
        hat, spread = norm_parts(tot_ref[...])
        two = norm_pull(grad, hat, spread, row_ref[8:9, :])
        two_ref[...] = two
        low = two.astype(BF16)
        twolow_ref[...] = low
        sum_ref[0:1, :] += col_sum(grad * hat)
        sum_ref[1:2, :] += col_sum(grad)
        sum_ref[2:3, :] += col_sum(low)

    return call(
        body,
        "ffn_backward",
        items // group,
        [
            (grad_three, tiled((block, d))),
            (grad_low, tiled((block, d))),
            (slope, tiled((block, ff))),
            (total_two, tiled((block, d))),
            (w_fin, whole((d, ff))),
            (w_fout, whole((ff, d))),
            (rows, whole(rows.shape)),
        ],
        [
            (spec_of((tokens, ff), BF16), tiled((block, ff))),
            (spec_of((tokens, d), F32), tiled((block, d))),
            (spec_of((tokens, d), BF16), tiled((block, d))),
            (spec_of((8, d), F32), summed((8, d))),
            (spec_of((8, ff), F32), summed((8, ff))),
        ],
        4 * tokens * d * ff,
    )


def pair_pull(q, k, v, out, probs, low, high):
    outs = spread_heads(out, low, high)
    score = soft_pull(probs.astype(F32), dot_t(v, outs)).astype(BF16)
    grad_k = dot(score, spread_heads(q, low, high))
    return dot(k.T, score), grad_k, dot(probs, outs)


def cross_attend_back(dims, grad_low, query, kv, probs, w_cout):
    d, items, length, group = dims.d, dims.items, dims.length, dims.group
    pairs, tokens, block = d // (2 * HEAD), items * length, group * length
    count = kv.shape[1]
    scale = HEAD ** (-0.5)

    def body(glow_ref, q_ref, kv_ref, prob_ref, wcout_ref, gq_ref, gkv_ref, sum_ref, ctx_ref):
        @pl.when(pl.program_id(0) == 0)
        def _():
            sum_ref[...] = jnp.zeros_like(sum_ref)

        low, high = lane_masks()
        ctx_ref[...] = dot_t(glow_ref[...], wcout_ref[...]).astype(BF16)
        for i in range(group):
            r = slice(i * length, (i + 1) * length)
            for p in range(pairs):
                c = slice(p * 128, (p + 1) * 128)
                cv = slice(d + p * 128, d + (p + 1) * 128)
                grad_q, grad_k, grad_v = pair_pull(
                    q_ref[r, c], kv_ref[i, :, c], kv_ref[i, :, cv], ctx_ref[r, c], prob_ref[i, p], low, high
                )
                gq_ref[r, c] = join_heads(grad_q * scale)
                gkv_ref[i, :, c] = (grad_k * scale).astype(BF16)
                gkv_ref[i, :, cv] = grad_v.astype(BF16)
        sum_ref[0:1, :] += col_sum(gq_ref[...])
        sum_ref[1:2, :] += col_sum(gkv_ref[:, :, d:].reshape(group * count, d))

    return call(
        body,
        "cross_attend_back",
        items // group,
        [
            (grad_low, tiled((block, d))),
            (query, tiled((block, d))),
            (kv, tiled((group, count, 2 * d))),
            (probs, tiled((group, pairs, count, 2 * length))),
            (w_cout, whole((d, d))),
        ],
        [
            (spec_of((tokens, d), BF16), tiled((block, d))),
            (spec_of((items, count, 2 * d), BF16), tiled((group, count, 2 * d))),
            (spec_of((8, d), F32), summed((8, d))),
        ],
        2 * tokens * d * 4 * d,
        [pltpu.VMEM((block, d), BF16)],
    )


def cross_project_back(dims, grad_two, grad_query, grad_kv, total_one, w_cq, w_ckv, rows, parts, part):
    d, items, length, group = dims.d, dims.items, dims.length, dims.group
    tokens, block = items * length, group * length
    count, vis = grad_kv.shape[1], w_ckv.shape[0]

    def body(g_ref, gq_ref, gkv_ref, tot_ref, wcq_ref, wckv_ref, row_ref, *refs):
        grid_refs, (cls_ref, one_ref, onelow_ref, sum_ref) = refs[:parts], refs[parts:]

        @pl.when(pl.program_id(0) == 0)
        def _():
            sum_ref[...] = jnp.zeros_like(sum_ref)

        for i in range(group):
            value = dot_t(gkv_ref[i], wckv_ref[...])
            for k in range(parts):
                grid_refs[k][i] = value[k * part : (k + 1) * part, :].astype(BF16)
            cls_ref[i] = value[parts * part : parts * part + 1, :]
        grad = g_ref[...] + dot_t(gq_ref[...], wcq_ref[...])
        hat, spread = norm_parts(tot_ref[...])
        one = norm_pull(grad, hat, spread, row_ref[3:4, :])
        one_ref[...] = one
        one_low = one.astype(BF16)
        onelow_ref[...] = one_low
        sum_ref[0:1, :] += col_sum(grad * hat)
        sum_ref[1:2, :] += col_sum(grad)
        sum_ref[2:3, :] += col_sum(one_low)

    return call(
        body,
        "cross_project_back",
        items // group,
        [
            (grad_two, tiled((block, d))),
            (grad_query, tiled((block, d))),
            (grad_kv, tiled((group, count, 2 * d))),
            (total_one, tiled((block, d))),
            (w_cq, whole((d, d))),
            (w_ckv, whole((vis, 2 * d))),
            (rows, whole(rows.shape)),
        ],
        [(spec_of((items, part, vis), BF16), tiled((group, part, vis)))] * parts
        + [
            (spec_of((items, 1, vis), F32), tiled((group, 1, vis))),
            (spec_of((tokens, d), F32), tiled((block, d))),
            (spec_of((tokens, d), BF16), tiled((block, d))),
            (spec_of((8, d), F32), summed((8, d))),
        ],
        2 * tokens * d * d + 2 * items * count * vis * 2 * d,
    )


def self_attend_back(dims, grad_low, qkv, probs, w_out):
    d, items, length, group = dims.d, dims.items, dims.length, dims.group
    pairs, tokens, block = d // (2 * HEAD), items * length, group * length
    scale = HEAD ** (-0.5)

    def body(glow_ref, qkv_ref, prob_ref, wout_ref, gqkv_ref, sum_ref, ctx_ref):
        @pl.when(pl.program_id(0) == 0)
        def _():
            sum_ref[...] = jnp.zeros_like(sum_ref)

        low, high = lane_masks()
        ctx_ref[...] = dot_t(glow_ref[...], wout_ref[...]).astype(BF16)
        for i in range(group):
            r = slice(i * length, (i + 1) * length)
            for p in range(pairs):
                cuts = [slice(part * d + p * 128, part * d + (p + 1) * 128) for part in range(3)]
                q, k, v = (qkv_ref[r, cut] for cut in cuts)
                grad_q, grad_k, grad_v = pair_pull(q, k, v, ctx_ref[r, cuts[0]], prob_ref[i, p], low, high)
                gqkv_ref[r, cuts[0]] = join_heads(grad_q * scale)
                gqkv_ref[r, cuts[1]] = (grad_k * scale).astype(BF16)
                gqkv_ref[r, cuts[2]] = grad_v.astype(BF16)
        sum_ref[0:1, :] += col_sum(gqkv_ref[:, :d])
        sum_ref[1:2, :] += col_sum(gqkv_ref[:, 2 * d :])

    return call(
        body,
        "self_attend_back",
        items // group,
        [
            (grad_low, tiled((block, d))),
            (qkv, tiled((block, 3 * d))),
            (probs, tiled((group, pairs, length, 2 * length))),
            (w_out, whole((d, d))),
        ],
        [
            (spec_of((tokens, 3 * d), BF16), tiled((block, 3 * d))),
            (spec_of((8, d), F32), summed((8, d))),
        ],
        2 * tokens * d * 4 * d,
        [pltpu.VMEM((block, d), BF16)],
    )


def self_project_back(dims, grad_one, grad_qkv, w_qkv):
    d, items, length, group = dims.d, dims.items, dims.length, dims.group
    tokens, block = items * length, group * length

    def body(g_ref, gqkv_ref, wqkv_ref, text_ref):
        text_ref[...] = g_ref[...] + dot_t(gqkv_ref[...], wqkv_ref[...])

    return call(
        body,
        "self_project_back",
        items // group,
        [
            (grad_one, tiled((block, d))),
            (grad_qkv, tiled((block, 3 * d))),
            (w_qkv, whole((d, 3 * d))),
        ],
        [(spec_of((tokens, d), F32), tiled((block, d)))],
        2 * tokens * d * 3 * d,
    )[0]


def place_grids(turn, micro, pieces):
    items, part, vis = pieces[0].shape
    each, parts = items // micro, len(pieces)

    def body(turn_ref, *refs):
        for k in range(parts):
            at = (turn_ref[0] ^ k) * each
            refs[-1][0, pl.ds(at, each)] = refs[k][...].astype(F32)

    return call(
        body,
        "place_grids",
        micro,
        [(turn, SMEM_SPEC)] + [(p, tiled((each, part, vis))) for p in pieces],
        [
            (
                spec_of((micro, each * parts, part, vis), F32),
                tiled((1, each * parts, part, vis)),
            )
        ],
        0,
    )[0]


def weight_grads(plan, group, where, factors):
    high_rows = max(plan.full[w][0] for w in group)

    def body(where_ref, *refs):
        ins, stack_refs, made = refs[: 2 * len(group)], refs[2 * len(group) : -1], refs[-1]
        for n, w in enumerate(group):
            left, right = ins[2 * n], ins[2 * n + 1]
            rows, half = plan.full[w][0], plan.full[w][1] // 2
            for j in range(plan.chunks[w]):
                for y in range(2):
                    cut = slice(y * half + j * plan.chunk, y * half + (j + 1) * plan.chunk)
                    for at in range(0, rows, 256):
                        value = dot_l(left[:, at : at + 256], right[:, cut])
                        made[y, at : at + 256, :] = value.astype(BF16)

                def visit(stack, k, row, w_at, j_at, to_row, to_y, high):
                    if w_at == w and j_at == j:
                        stack_refs[stack][k, row : row + high, :] = made[
                            to_y, pl.ds(to_row, high), :
                        ]

                each_place(plan, group, where_ref, visit)

    shape = jax.ShapeDtypeStruct((plan.zs, plan.rows(group), plan.chunk), BF16)
    flat = [a for pair in factors for a in pair]
    flops = sum(2 * a.shape[0] * a.shape[1] * b.shape[1] for a, b in factors)
    moved = sum(a.size * 2 for a in flat) + 8 * shape.size * 2
    return pl.pallas_call(
        body,
        out_shape=(shape,) * 8,
        in_specs=[SMEM_SPEC] + [VMEM_SPEC] * len(flat),
        out_specs=(VMEM_SPEC,) * 8,
        scratch_shapes=[pltpu.VMEM((2, high_rows, plan.chunk), BF16)],
        compiler_params=PARAMS,
        cost_estimate=pl.CostEstimate(flops=flops, bytes_accessed=moved, transcendentals=0),
        name="weight_grads",
    )(where, *flat)


class Dims:
    def __init__(self, d, items, length):
        self.d, self.items, self.length = d, items, length
        self.group = 2 if items % 2 == 0 else 1


def cross_mask(lengths, counts, boxes, length, count):
    place = jnp.arange(length, dtype=jnp.int32)[None, :]
    boxed = (counts[:, None] > 0) & (place < lengths[:, None])
    phrase = jnp.where(boxed, place * counts[:, None] // lengths[:, None], 0)
    chosen = phrase[:, None, :] == jnp.arange(boxes.shape[1], dtype=jnp.int32)[None, :, None]
    inside = jnp.einsum(
        "ijp,ijt->ipt",
        (boxes > 0).astype(BF16),
        chosen.astype(BF16),
        preferred_element_type=F32,
    )
    grid_ok = jnp.where(boxed[:, None, :], inside, 1.0).astype(BF16)
    items, real = grid_ok.shape[:2]
    own = jnp.ones((items, 1, length), BF16)
    return jnp.concatenate([grid_ok, own, jnp.zeros((items, count - real - 1, length), BF16)], 1)


def trade(pieces, parts):
    return [pieces[0]] + [
        lax.ppermute(pieces[k], "patch", [(i, i ^ k) for i in range(parts)])
        for k in range(1, parts)
    ]


class Work:
    def __init__(self, args, parts):
        (self.text_in, self.image_grid, self.image_cls, lengths, counts, boxes, cot) = args
        self.parts = parts
        self.micro, d = self.text_in.shape[0], self.text_in.shape[2]
        self.items = lengths.size
        self.text, self.cot = self.text_in.reshape(-1, d), cot.reshape(-1, d)
        self.lengths, self.counts = lengths.reshape(-1), counts.reshape(-1)
        self.boxes = boxes.reshape((self.items,) + boxes.shape[2:])
        self.dims = Dims(d, self.items, self.text.shape[0] // self.items)
        self.turn = lax.axis_index("patch").astype(jnp.int32)
        self.part, self.vis = self.image_grid.shape[2:]
        self.each = self.items // self.micro
        self.count = -(-(parts * self.part + 1) // 16) * 16
        self.cls = self.image_cls.reshape(self.items, 1, self.vis)

    def cut_grids(self):
        return [
            lax.dynamic_slice_in_dim(
                self.image_grid, (self.turn ^ k) * self.each, self.each, axis=1
            ).reshape(self.items, self.part, self.vis)
            for k in range(self.parts)
        ]

    def mask(self):
        boxes = self.boxes.reshape(self.items, -1, self.parts, self.part)
        order = jnp.arange(self.parts, dtype=jnp.int32) ^ self.turn
        boxes = jnp.take(boxes, order, axis=2).reshape(self.boxes.shape)
        return cross_mask(self.lengths, self.counts, boxes, self.dims.length, self.count)

    def finish(self, layer_out, text_grad, grids, cls, grads, rows_grad, bias_grad):
        grid_grad = place_grids(self.turn.reshape(1), self.micro, grids)
        return (
            layer_out.reshape(self.text_in.shape),
            text_grad.reshape(self.text_in.shape),
            grid_grad,
            cls.reshape(self.image_cls.shape),
            *grads,
            rows_grad,
            bias_grad,
        )


def rows_of(sum_self, sum_attend, sum_one, sum_two, sum_three):
    return jnp.concatenate(
        [
            sum_self[0:2],
            sum_one[2:3],
            sum_one[0:2],
            sum_attend[0:2],
            sum_two[2:3],
            sum_two[0:2],
            sum_three[2:3],
            sum_three[0:2],
        ]
    )


def on_device(plan, *args):
    work, shards, vectors, ffn_bias = Work(args[:7], plan.patch), args[7:14], args[14], args[15]
    dims, where, parts = work.dims, coords(), plan.patch
    weights = {}

    own, give = pack_split(plan, where, shards)
    units = pack_join(plan, where, own, send(give, plan.core()))
    gathers = [Gathering(plan, unit) for unit in units]
    grids = work.cut_grids()

    def ready(g):
        full = assemble(plan, GATHER[g], where, gathers[g].held)
        for w, value in zip(GATHER[g], full):
            weights[w] = value

    def step(*groups):
        for g in groups:
            gathers[g].advance()

    step(0)
    grids = fence(gathers, grids)
    grids = trade(grids, parts)
    rows, bias = gather_small(plan, where, vectors, ffn_bias)
    rows = jnp.pad(rows, ((0, -rows.shape[0] % 8), (0, 0)))
    step(0, 1)
    rows, bias = fence(gathers, [rows, bias])
    step(0, 2)
    fence(gathers, [])
    step(1, 3)
    ready(0)
    qkv, probs, ctx, total_one = self_forward(
        dims, work.text, weights[QKV], weights[OUT], rows, work.lengths
    )
    mask = work.mask()
    total_one, grids, mask = fence(gathers[1:], [total_one, grids, mask])
    step(1)
    fence(gathers[1:], [])
    step(2, 3)
    ready(1)
    hidden_one, query, kv, cross_probs, cross_ctx, total_two, patches = cross_forward(
        dims, total_one, grids, work.cls, mask, weights[CQ], weights[CKV], weights[COUT], rows
    )
    total_two = fence(gathers[2:], total_two)
    step(2, 3)
    total_two = fence(gathers[2:], total_two)
    ready(2)
    ready(3)
    layer_out, hidden_two, act, slope, grad_three, low_three, sum_three = ffn_forward(
        dims, total_two, work.cot, weights[FIN], weights[FOUT], rows, bias[None]
    )

    reduces = {}

    def reduce(g, factors):
        stacks = weight_grads(plan, REDUCE[g], where, factors)
        reduces[g] = Reducing(plan, REDUCE[g], where, stacks)

    def hold(*values):
        return fence(list(reduces.values()), list(values))

    def go(*groups):
        for g in groups:
            reduces[g].advance()

    reduce(3, [(act, low_three)])
    (grad_three,) = hold(grad_three)
    go(3)
    grad_pre, grad_two, low_two, sum_two, sum_pre = ffn_backward(
        dims, grad_three, low_three, slope, total_two, weights[FIN], weights[FOUT], rows
    )
    grad_pre, grad_two, low_two = hold(grad_pre, grad_two, low_two)
    go(3)
    reduce(2, [(hidden_two, grad_pre)])
    (low_two,) = hold(low_two)
    go(3, 2)
    grad_query, grad_kv, sum_attend = cross_attend_back(
        dims, low_two, query, kv, cross_probs, weights[COUT]
    )
    grad_query, grad_kv = hold(grad_query, grad_kv)
    go(3, 2)
    flat_kv = grad_kv.reshape(-1, grad_kv.shape[2])
    reduce(
        1,
        [
            (hidden_one, grad_query),
            (patches.reshape(-1, work.vis), flat_kv),
            (cross_ctx, low_two),
        ],
    )
    grad_query, grad_kv = hold(grad_query, grad_kv)
    go(3, 2, 1)
    *grids, cls, grad_one, low_one, sum_one = cross_project_back(
        dims, grad_two, grad_query, grad_kv, total_one, weights[CQ], weights[CKV], rows, parts, work.part
    )
    low_one, *grids = hold(low_one, *grids)
    go(3, 2, 1)
    grids = trade(grids, parts)
    grad_qkv, sum_self = self_attend_back(dims, low_one, qkv, probs, weights[OUT])
    grad_qkv, sum_self = hold(grad_qkv, sum_self)
    go(2, 1)
    reduce(0, [(work.text, grad_qkv), (ctx, low_one)])
    reduces["small"] = ReducingSmall(
        plan, where, rows_of(sum_self, sum_attend, sum_one, sum_two, sum_three), sum_pre[0]
    )
    grad_qkv, *grids = hold(grad_qkv, *grids)
    go(2, 1, 0, "small")
    text_grad = self_project_back(dims, grad_one, grad_qkv, weights[QKV])
    hold()
    go(1, 0, "small")
    hold()
    go(1, 0, "small")
    hold()
    go(0, "small")
    hold()
    go(0)
    go(0)
    grads = [None] * 7
    for g, group in enumerate(REDUCE):
        for w, value in zip(group, reduces[g].held):
            grads[w] = value
    return work.finish(layer_out, text_grad, grids, cls, grads, *reduces["small"].result())


def on_device_plain(plan, *args):
    work, parts = Work(args[:7], plan.patch), plan.patch
    dims = work.dims
    weights, rows, bias = fetch_plain(args[7:14], args[14], args[15])
    rows = jnp.pad(rows, ((0, -rows.shape[0] % 8), (0, 0)))
    grids = trade(work.cut_grids(), parts)
    qkv, probs, ctx, total_one = self_forward(
        dims, work.text, weights[QKV], weights[OUT], rows, work.lengths
    )
    hidden_one, query, kv, cross_probs, cross_ctx, total_two, patches = cross_forward(
        dims, total_one, grids, work.cls, work.mask(), weights[CQ], weights[CKV], weights[COUT], rows
    )
    layer_out, hidden_two, act, slope, grad_three, low_three, sum_three = ffn_forward(
        dims, total_two, work.cot, weights[FIN], weights[FOUT], rows, bias[None]
    )
    grad_pre, grad_two, low_two, sum_two, sum_pre = ffn_backward(
        dims, grad_three, low_three, slope, total_two, weights[FIN], weights[FOUT], rows
    )
    grad_query, grad_kv, sum_attend = cross_attend_back(
        dims, low_two, query, kv, cross_probs, weights[COUT]
    )
    *grids, cls, grad_one, low_one, sum_one = cross_project_back(
        dims, grad_two, grad_query, grad_kv, total_one, weights[CQ], weights[CKV], rows, parts, work.part
    )
    grad_qkv, sum_self = self_attend_back(dims, low_one, qkv, probs, weights[OUT])
    text_grad = self_project_back(dims, grad_one, grad_qkv, weights[QKV])
    flat_kv = grad_kv.reshape(-1, grad_kv.shape[2])
    factors = [
        (work.text, grad_qkv),
        (ctx, low_one),
        (hidden_one, grad_query),
        (patches.reshape(-1, work.vis), flat_kv),
        (cross_ctx, low_two),
        (hidden_two, grad_pre),
        (act, low_three),
    ]
    grads = [reduce_plain(dot_l(a, b).astype(BF16)) for a, b in factors]
    small = reduce_small_plain(
        rows_of(sum_self, sum_attend, sum_one, sum_two, sum_three), sum_pre[0]
    )
    return work.finish(layer_out, text_grad, trade(grids, parts), cls, grads, *small)


def solution(mesh):
    dp, patch = mesh.shape["dp"], mesh.shape["patch"]
    both = P(None, ("dp", "patch"), None)
    weight = P("dp", "patch")

    def run(*args):
        shards = [(w.shape[0] // dp, w.shape[1] // patch) for w in args[7:14]]
        plan = Plan(dp, patch, shards)
        return jax.shard_map(
            functools.partial(on_device if plan.fast else on_device_plain, plan),
            mesh=mesh,
            in_specs=(
                both,
                P(None, "dp", "patch", None),
                both,
                P(None, ("dp", "patch")),
                P(None, ("dp", "patch")),
                P(None, ("dp", "patch"), None, None),
                both,
            )
            + (weight,) * 7
            + (P(None, "dp"), P("dp")),
            out_specs=(both, both, P(None, "dp", "patch", None), both)
            + (weight,) * 7
            + (P(None, "dp"), P("dp")),
            check_vma=False,
        )(*args)

    return run
```

```python
import functools

import jax
import jax.numpy as jnp
from jax import lax
from jax.experimental import pallas as pl
from jax.experimental.pallas import tpu as pltpu
from jax.sharding import PartitionSpec as P

HEAD = 64
EPS = 1e-06
NEG = -1e30
BF16 = jnp.bfloat16
F32 = jnp.float32
AXES = ("dp", "patch")
VMEM_SPEC = pl.BlockSpec(memory_space=pltpu.VMEM)
SMEM_SPEC = pl.BlockSpec(memory_space=pltpu.SMEM)
PARAMS = pltpu.CompilerParams(vmem_limit_bytes=62 * 2**20)

QKV, OUT, CQ, CKV, COUT, FIN, FOUT = range(7)
GROUPS = ((QKV, OUT), (CQ, CKV, COUT), (FIN, FOUT))


class Plan:
    def __init__(self, dp, patch, shards):
        self.dp, self.patch = dp, patch
        self.zs = dp // 2
        self.devices = dp * patch
        self.chunk = shards[OUT][1] * 2
        self.half = [s[0] // 2 for s in shards]
        self.cols = [s[1] for s in shards]
        self.chunks = [s[1] * 2 // self.chunk for s in shards]
        self.full = [(s[0] * dp, s[1] * patch) for s in shards]
        self.fast = (
            dp % 2 == 0
            and patch == 4
            and all(h % 16 == 0 for h in self.half)
            and all(s[1] * 2 % self.chunk == 0 for s in shards)
            and self.chunk % 128 == 0
        )

    def rows(self, group):
        return sum(self.half[w] * self.chunks[w] for w in group)

    def flip(self, pick):
        return [(i, i ^ pick(i)) for i in range(self.devices)]

    def core(self):
        return self.flip(lambda i: 1)

    def first(self):
        return self.flip(lambda i: 4 if i % 2 == 0 else 2)

    def second(self):
        return self.flip(lambda i: 2 if i % 2 == 0 else 4)

    def z_up(self, k):
        return [(i, (i + 8 * k) % self.devices) for i in range(self.devices)]


def send(value, perm):
    return lax.ppermute(value, AXES, perm)


def coords():
    dp, patch = lax.axis_index("dp"), lax.axis_index("patch")
    return jnp.stack([dp // 2, dp % 2, patch // 2, patch % 2]).astype(jnp.int32)


def piece_rows(group, plan):
    at, found = 0, []
    for w in group:
        for j in range(plan.chunks[w]):
            found.append((w, j, at))
            at += plan.half[w]
    return found


def group_starts(plan):
    starts, at = [], 0
    for group in GROUPS:
        starts.append(at)
        at += plan.rows(group)
    return starts, at


def pack_split(plan, where, shards):
    _, total = group_starts(plan)
    wide = plan.chunk // 2

    def body(where_ref, *refs):
        shard_refs, (own_ref, send_ref, turned) = list(refs[:7]), refs[7:]
        core = where_ref[3]
        turned[...] = shard_refs[FOUT][...].T
        shard_refs[FOUT] = turned
        at = 0
        for group in GROUPS:
            for w in group:
                high = plan.half[w]
                for b in range(plan.chunks[w]):
                    cut = slice(b * wide, (b + 1) * wide)
                    own_ref[at : at + high, :] = shard_refs[w][pl.ds(core * high, high), cut]
                    send_ref[at : at + high, :] = shard_refs[w][
                        pl.ds((1 - core) * high, high), cut
                    ]
                    at += high

    shape = jax.ShapeDtypeStruct((total, wide), BF16)
    return pl.pallas_call(
        body,
        out_shape=(shape, shape),
        in_specs=[SMEM_SPEC] + [VMEM_SPEC] * 7,
        out_specs=(VMEM_SPEC, VMEM_SPEC),
        scratch_shapes=[pltpu.VMEM(shards[FOUT].shape, BF16)],
        compiler_params=PARAMS,
        name="pack_split",
    )(where, *shards[:FOUT], shards[FOUT].T)


def pack_join(plan, where, own, got):
    starts, total = group_starts(plan)
    wide = plan.chunk // 2

    def body(where_ref, own_ref, got_ref, *unit_refs):
        core = where_ref[3]

        def fill(low_ref, high_ref):
            for g, group in enumerate(GROUPS):
                at = starts[g]
                for w in group:
                    high, count = plan.half[w], plan.chunks[w]
                    for j in range(count):
                        pair = []
                        for b in (2 * j, 2 * j + 1):
                            src = low_ref if b < count else high_ref
                            row = at + (b % count) * high
                            pair.append(src[row : row + high, :])
                        to = at - starts[g] + j * high
                        unit_refs[g][to : to + high, :] = jnp.concatenate(pair, axis=1)
                    at += count * high

        @pl.when(core == 0)
        def _():
            fill(own_ref, got_ref)

        @pl.when(core == 1)
        def _():
            fill(got_ref, own_ref)

    return pl.pallas_call(
        body,
        out_shape=tuple(jax.ShapeDtypeStruct((plan.rows(g), plan.chunk), BF16) for g in GROUPS),
        in_specs=[SMEM_SPEC, VMEM_SPEC, VMEM_SPEC],
        out_specs=(VMEM_SPEC,) * len(GROUPS),
        compiler_params=PARAMS,
        name="pack_join",
    )(where, own, got)


class Gathering:
    def __init__(self, plan, unit):
        self.plan, self.held, self.step = plan, [unit], 0

    def advance(self):
        plan, held = self.plan, self.held
        if self.step == 0:
            held = held + [send(held[0], plan.z_up(k)) for k in range(1, plan.zs)]
        elif self.step == 1:
            stack = jnp.stack(held)
            held = [stack, send(stack, plan.first())]
        elif self.step == 2:
            held = held + [send(part, plan.second()) for part in held]
            held = held + [send(part, plan.core()) for part in held[:2]]
        elif self.step == 3:
            held = held + [send(part, plan.core()) for part in held[2:4]]
        self.held, self.step = held, self.step + 1


def each_place(plan, group, where_ref, visit):
    z, x, y, core = (where_ref[i] for i in range(4))
    for other in range(2):
        half = core ^ other
        for second in range(2):
            for first in range(2):
                x_at = x ^ jnp.where(half == 0, first, second)
                y_at = y ^ jnp.where(half == 0, second, first)
                for k in range(plan.zs):
                    z_at = lax.rem(z + plan.zs - k, plan.zs)
                    place = (z_at * 2 + x_at) * 2 + half
                    for w, j, row in piece_rows(group, plan):
                        high = plan.half[w]
                        to_row = pl.multiple_of(place * high, 16)
                        visit(other, second * 2 + first, k, row, w, j, to_row, y_at, high)


def add_low(ones, twos, widths):
    count, slots, rows, chunk = ones.shape

    def body(one_ref, two_ref, *out_refs):
        at = 0
        for width, out in zip(widths, out_refs):
            for n in range(width):
                out[n] = (one_ref[at].astype(F32) + two_ref[at].astype(F32)).astype(BF16)
                at += 1

    def spec(n):
        return pl.BlockSpec((n, 1, rows, chunk), lambda i: (0, i, 0, 0))

    return pl.pallas_call(
        body,
        grid=(slots,),
        out_shape=tuple(jax.ShapeDtypeStruct((n, slots, rows, chunk), BF16) for n in widths),
        in_specs=[spec(count), spec(count)],
        out_specs=tuple(spec(n) for n in widths),
        compiler_params=PARAMS,
        cost_estimate=pl.CostEstimate(
            flops=ones.size, bytes_accessed=6 * ones.size, transcendentals=0
        ),
        name="add_low",
    )(ones, twos)


def add_slots(ones, twos):
    _, slots, rows, chunk = ones.shape

    def body(one_ref, two_ref, *out_refs):
        for n in range(slots):
            out_refs[n][...] = (one_ref[0, n].astype(F32) + two_ref[0, n].astype(F32)).astype(BF16)

    return pl.pallas_call(
        body,
        out_shape=(jax.ShapeDtypeStruct((rows, chunk), BF16),) * slots,
        in_specs=[VMEM_SPEC, VMEM_SPEC],
        out_specs=(VMEM_SPEC,) * slots,
        compiler_params=PARAMS,
        cost_estimate=pl.CostEstimate(
            flops=ones.size, bytes_accessed=6 * ones.size, transcendentals=0
        ),
        name="add_slots",
    )(ones, twos)


class Reducing:
    def __init__(self, plan, group, where, stacks):
        self.plan, self.group, self.where = plan, group, where
        self.held, self.step = list(stacks), 0

    def advance(self):
        plan, held = self.plan, self.held
        if self.step == 0:
            held = [held[0], send(held[1], plan.core())]
        elif self.step == 1:
            keep, give = add_low(*held, (2, 2))
            held = [keep, send(give, plan.second())]
        elif self.step == 2:
            keep, give = add_low(*held, (1, 1))
            held = [keep, send(give, plan.first())]
        elif self.step == 3:
            slots = add_slots(*held)
            parts = [send(slots[k], plan.z_up(plan.zs - k)) for k in range(1, plan.zs)]
            held = [slots[0]] + parts
        elif self.step == 4:
            own, give = unpack_split(plan, self.group, self.where, held)
            held = [own, send(give, plan.core())]
        elif self.step == 5:
            held = unpack_join(plan, self.group, self.where, *held)
        self.held, self.step = list(held), self.step + 1


def fence(chains, values):
    flat, tree = jax.tree.flatten([values, [chain.held for chain in chains]])
    values, held = jax.tree.unflatten(tree, lax.optimization_barrier(flat))
    for chain, arrays in zip(chains, held):
        chain.held = arrays
    return values


def unpack_split(plan, group, where, parts):
    rows, wide = plan.rows(group), plan.chunk // 2

    def body(where_ref, *refs):
        part_refs, (own_ref, give_ref) = refs[:-2], refs[-2:]
        core = where_ref[3]

        def fill(low_ref, high_ref):
            at = 0
            for w in group:
                high, count = plan.half[w], plan.chunks[w]
                for j in range(count):
                    row = at + j * high
                    value = sum(p[row : row + high, :].astype(F32) for p in part_refs)
                    for b in (2 * j, 2 * j + 1):
                        dst = low_ref if b < count else high_ref
                        to = at + (b % count) * high
                        cut = (b - 2 * j) * wide
                        dst[to : to + high, :] = value[:, cut : cut + wide]
                at += count * high

        @pl.when(core == 0)
        def _():
            fill(own_ref, give_ref)

        @pl.when(core == 1)
        def _():
            fill(give_ref, own_ref)

    shape = jax.ShapeDtypeStruct((rows, wide), F32)
    return pl.pallas_call(
        body,
        out_shape=(shape, shape),
        in_specs=[SMEM_SPEC] + [VMEM_SPEC] * len(parts),
        out_specs=(VMEM_SPEC, VMEM_SPEC),
        compiler_params=PARAMS,
        name="unpack_split",
    )(where, *parts)


def unpack_join(plan, group, where, own, got):
    wide = plan.chunk // 2
    turned = [w == FOUT for w in group]

    def body(where_ref, own_ref, got_ref, *refs):
        core = where_ref[3]
        at = 0
        for n, w in enumerate(group):
            out_ref = refs[-1] if turned[n] else refs[n]
            high, count = plan.half[w], plan.chunks[w]
            own_rows = pl.ds(pl.multiple_of(core * high, 16), high)
            got_rows = pl.ds(pl.multiple_of((1 - core) * high, 16), high)
            for b in range(count):
                row, cut = at + b * high, slice(b * wide, (b + 1) * wide)
                out_ref[own_rows, cut] = own_ref[row : row + high, :]
                out_ref[got_rows, cut] = got_ref[row : row + high, :]
            at += count * high
            if turned[n]:
                refs[n][...] = out_ref[...].T

    shapes = [(2 * plan.half[w], plan.cols[w]) for w in group]
    done = pl.pallas_call(
        body,
        out_shape=tuple(
            jax.ShapeDtypeStruct(shape[::-1] if turn else shape, F32)
            for shape, turn in zip(shapes, turned)
        ),
        in_specs=[SMEM_SPEC, VMEM_SPEC, VMEM_SPEC],
        out_specs=(VMEM_SPEC,) * len(group),
        scratch_shapes=[pltpu.VMEM(shapes[-1], F32)],
        compiler_params=PARAMS,
        name="unpack_join",
    )(where, own, got)
    return [value.T if turn else value for value, turn in zip(done, turned)]


def gather_small(plan, where, vectors, bias):
    count, part = vectors.shape
    flat = jnp.concatenate([vectors.reshape(-1), bias])
    size = flat.shape[0]
    flat = jnp.pad(flat, (0, -size % 2048)).reshape(-1, 128)
    pair = jnp.stack([flat, send(flat, plan.flip(lambda i: 4))])
    every = jnp.stack([pair] + [send(pair, plan.z_up(k)) for k in range(1, plan.zs)])
    every = every.reshape((plan.dp,) + flat.shape)
    at = jnp.arange(plan.dp, dtype=jnp.int32)
    slot = lax.rem(where[0] - at // 2 + plan.zs, plan.zs) * 2 + ((at % 2) ^ where[1])
    every = jnp.take(every, slot, axis=0).reshape(plan.dp, -1)[:, :size].astype(F32)
    rows = every[:, : count * part].reshape(plan.dp, count, part)
    rows = rows.transpose(1, 0, 2).reshape(count, plan.dp * part)
    return rows, every[:, count * part :].reshape(-1)


class ReducingSmall:
    def __init__(self, plan, where, rows, bias):
        self.plan, self.where, self.shape, self.tail = plan, where, rows.shape, bias.shape[0]
        flat = jnp.concatenate([rows.reshape(-1), bias])
        flat = jnp.pad(flat, (0, -flat.shape[0] % 1024)).reshape(-1, 128)
        self.held, self.step = [flat], 0

    def advance(self):
        plan = self.plan
        flat = sum(self.held)
        if self.step < 3:
            bit = 1 << self.step
            self.held = [flat, send(flat, plan.flip(lambda i: bit))]
        else:
            self.held = [flat] + [send(flat, plan.z_up(k)) for k in range(1, plan.zs)]
        self.step += 1

    def result(self):
        plan, (count, width) = self.plan, self.shape
        flat = sum(self.held).reshape(-1)
        dp = self.where[0] * 2 + self.where[1]
        main = flat[: count * width].reshape(count, width)
        own = lax.dynamic_slice_in_dim(main, dp * (width // plan.dp), width // plan.dp, axis=1)
        tail, step = flat[count * width : count * width + self.tail], self.tail // plan.dp
        return own, lax.dynamic_slice_in_dim(tail, dp * step, step, axis=0)


def fetch_plain(weights, vectors, bias):
    whole = [
        lax.all_gather(lax.all_gather(w, "dp", axis=0, tiled=True), "patch", axis=1, tiled=True)
        for w in weights
    ]
    rows = lax.all_gather(vectors, "dp", axis=1, tiled=True)
    return whole, rows.astype(F32), lax.all_gather(bias, "dp", axis=0, tiled=True).astype(F32)


def reduce_plain(grad):
    part = lax.psum_scatter(grad, "dp", scatter_dimension=0, tiled=True)
    return lax.psum_scatter(part, "patch", scatter_dimension=1, tiled=True).astype(F32)


def reduce_small_plain(rows, bias):
    rows = lax.psum_scatter(rows, "dp", scatter_dimension=1, tiled=True)
    bias = lax.psum_scatter(bias, "dp", scatter_dimension=0, tiled=True)
    return lax.psum(rows, "patch"), lax.psum(bias, "patch")


TAIL = (0.112528827, 0.117839666, 0.0706314405, 0.2046457425, -0.190499398, 0.3478185715, -0.201092832, 0.03812798145)


def dot(a, b):
    return lax.dot_general(a, b, (((1,), (0,)), ((), ())), preferred_element_type=F32)


def dot_t(a, b):
    return lax.dot_general(a, b, (((1,), (1,)), ((), ())), preferred_element_type=F32)


def dot_l(a, b):
    return lax.dot_general(a, b, (((0,), (0,)), ((), ())), preferred_element_type=F32)


def norm_parts(total):
    center = total - jnp.mean(total, -1, keepdims=True)
    spread = lax.rsqrt(jnp.mean(center * center, -1, keepdims=True) + EPS)
    return center * spread, spread


def norm_pull(grad, hat, spread, gain):
    scaled = grad * gain
    return spread * (
        scaled
        - jnp.mean(scaled, -1, keepdims=True)
        - hat * jnp.mean(scaled * hat, -1, keepdims=True)
    )


def gelu_parts(x):
    bell = jnp.exp(-0.5 * (x * x))
    t = 1.0 / (1.0 + (0.4 * 0.5**0.5) * jnp.abs(x))
    tail = jnp.full_like(t, TAIL[-1])
    for c in TAIL[-2::-1]:
        tail = tail * t + c
    tail = tail * (t * bell)
    return jnp.where(x < 0.0, tail, 1.0 - tail), bell


def col_sum(value):
    return jnp.sum(value.astype(F32), 0, keepdims=True)


def soft(scores):
    grown = jnp.exp(scores - jnp.max(scores, 0, keepdims=True))
    return grown * (1.0 / jnp.sum(grown, 0, keepdims=True))


def soft_pull(probs, grad):
    return probs * (grad - jnp.sum(probs * grad, 0, keepdims=True))


def spread_heads(value, low, high):
    return jnp.concatenate([value * low, value * high], 0)


def join_heads(value):
    count = value.shape[1] // 2
    value = jnp.concatenate([value[:HEAD, :count], value[HEAD:, count:]], 0)
    return value.astype(BF16).T


def lane_masks():
    lane = lax.broadcasted_iota(jnp.int32, (1, 2 * HEAD), 1)
    low = (lane < HEAD).astype(F32)
    return low.astype(BF16), (1.0 - low).astype(BF16)


def whole(shape):
    return pl.BlockSpec(
        shape, lambda i: (0,) * len(shape), pipeline_mode=pl.Buffered(1)
    )


def summed(shape):
    return pl.BlockSpec(shape, lambda i: (0,) * len(shape))


def tiled(shape):
    return pl.BlockSpec(shape, lambda i: (i,) + (0,) * (len(shape) - 1))


def spec_of(shape, dtype):
    return jax.ShapeDtypeStruct(shape, dtype)


def call(body, name, steps, ins, outs, flops, scratch=()):
    out_shape = tuple(shape for shape, _ in outs)
    moved = sum(a.size * a.dtype.itemsize for a, _ in ins)
    moved += sum(o.size * jnp.dtype(o.dtype).itemsize for o in out_shape)
    return pl.pallas_call(
        body,
        grid=(steps,),
        out_shape=out_shape,
        in_specs=[spec for _, spec in ins],
        out_specs=tuple(spec for _, spec in outs),
        scratch_shapes=list(scratch),
        compiler_params=PARAMS,
        cost_estimate=pl.CostEstimate(
            flops=int(flops), bytes_accessed=int(moved), transcendentals=0
        ),
        name=name,
    )(*[a for a, _ in ins])


class Source:
    def __init__(self, plan, group, where, given):
        self.plan, self.group, self.pieces = plan, group, plan.fast
        if self.pieces:
            self.ins = [(where, SMEM_SPEC)] + [(part, whole(part.shape)) for part in given]
            self.outs = [(spec_of(plan.full[w], BF16), summed(plan.full[w])) for w in group]
        else:
            self.ins = [(w, whole(w.shape)) for w in given]
            self.outs = []
        self.given = given

    def open(self, in_refs, out_refs):
        if not self.pieces:
            return list(in_refs)
        where_ref, parts = in_refs[0], in_refs[1:]
        full = dict(zip(self.group, out_refs))
        plan = self.plan

        def visit(other, stack, k, row, w, j, to_row, to_y, high):
            to_col = pl.multiple_of(to_y * (plan.full[w][1] // 2) + j * plan.chunk, 128)
            part = parts[other * 4 + stack]
            full[w][pl.ds(to_row, high), pl.ds(to_col, plan.chunk)] = part[k, row : row + high, :]

        @pl.when(pl.program_id(0) == 0)
        def _():
            each_place(plan, self.group, where_ref, visit)

        return list(out_refs)

    def split(self, done):
        if not self.pieces:
            return done, self.given
        return done[: -len(self.group)], done[-len(self.group) :]


def self_forward(dims, source, text, rows, lengths):
    d, items, length, group = dims.d, dims.items, dims.length, dims.group
    pairs, tokens, block = d // (2 * HEAD), items * length, group * length
    scale = HEAD ** (-0.5)

    n_in = len(source.ins)

    def body(len_ref, x_ref, row_ref, *refs):
        qkv_ref, prob_ref, ctx_ref, tot_ref = refs[n_in : n_in + 4]
        wqkv_ref, wout_ref = source.open(refs[:n_in], refs[n_in + 4 :])
        step = pl.program_id(0)
        low, high = lane_masks()
        x = x_ref[...]
        for part, bias in ((0, 0), (1, None), (2, 1)):
            cut = slice(part * d, (part + 1) * d)
            value = dot(x, wqkv_ref[:, cut])
            if bias is not None:
                value = value + row_ref[bias : bias + 1, :]
            qkv_ref[:, cut] = value.astype(BF16)
        place = lax.broadcasted_iota(jnp.int32, (length, 1), 0)
        for i in range(group):
            ok = place < len_ref[step * group + i]
            r = slice(i * length, (i + 1) * length)
            for p in range(pairs):
                q, k, v = (
                    qkv_ref[r, part * d + p * 128 : part * d + (p + 1) * 128] for part in range(3)
                )
                scores = dot_t(k, spread_heads(q, low, high)) * scale
                probs = soft(jnp.where(ok, scores, NEG)).astype(BF16)
                prob_ref[i, p] = probs
                ctx_ref[r, p * 128 : (p + 1) * 128] = join_heads(dot(v.T, probs))
        tot_ref[...] = x.astype(F32) + dot(ctx_ref[...], wout_ref[...]) + row_ref[2:3, :]

    done = call(
        body,
        "self_forward",
        items // group,
        [(lengths, SMEM_SPEC), (text, tiled((block, d))), (rows, whole(rows.shape))] + source.ins,
        [
            (spec_of((tokens, 3 * d), BF16), tiled((block, 3 * d))),
            (spec_of((items, pairs, length, 2 * length), BF16), tiled((group, pairs, length, 2 * length))),
            (spec_of((tokens, d), BF16), tiled((block, d))),
            (spec_of((tokens, d), F32), tiled((block, d))),
        ]
        + source.outs,
        2 * tokens * d * 6 * d,
    )
    return source.split(done)


def cross_keys(dims, source, grids, cls, rows, count):
    d, items, group = dims.d, dims.items, dims.group
    part, vis, parts = grids[0].shape[1], cls.shape[2], len(grids)
    n_in = len(source.ins)

    def body(*refs):
        grid_refs, cls_ref, row_ref = refs[:parts], refs[parts], refs[parts + 1]
        refs = refs[parts + 2 :]
        kv_ref, patch_ref = refs[n_in : n_in + 2]
        _, wckv_ref, _ = source.open(refs[:n_in], refs[n_in + 2 :])
        for i in range(group):
            for k in range(parts):
                patch_ref[i, k * part : (k + 1) * part, :] = grid_refs[k][i]
            rest = jnp.zeros((count - parts * part - 1, vis), BF16)
            patch_ref[i, parts * part :, :] = jnp.concatenate([cls_ref[i], rest], 0)
        patch = patch_ref[...].reshape(group * count, vis)
        keys = dot(patch, wckv_ref[:, :d]).astype(BF16)
        kv_ref[:, :, :d] = keys.reshape(group, count, d)
        values = (dot(patch, wckv_ref[:, d:]) + row_ref[6:7, :]).astype(BF16)
        kv_ref[:, :, d:] = values.reshape(group, count, d)

    done = call(
        body,
        "cross_keys",
        items // group,
        [(grid, tiled((group, part, vis))) for grid in grids]
        + [(cls, tiled((group, 1, vis))), (rows, whole(rows.shape))]
        + source.ins,
        [
            (spec_of((items, count, 2 * d), BF16), tiled((group, count, 2 * d))),
            (spec_of((items, count, vis), BF16), tiled((group, count, vis))),
        ]
        + source.outs,
        2 * items * count * vis * 2 * d,
    )
    return source.split(done)


def cross_forward(dims, total_one, kv, mask, w_cq, w_cout, rows):
    d, items, length, group = dims.d, dims.items, dims.length, dims.group
    pairs, tokens, block = d // (2 * HEAD), items * length, group * length
    count = kv.shape[1]
    scale = HEAD ** (-0.5)

    def body(tot_ref, kv_ref, mask_ref, wcq_ref, wcout_ref, row_ref, h_ref, cq_ref, prob_ref, ctx_ref, two_ref):
        low, high = lane_masks()
        hat, _ = norm_parts(tot_ref[...])
        hidden = hat * row_ref[3:4, :] + row_ref[4:5, :]
        h_ref[...] = hidden.astype(BF16)
        cq_ref[...] = (dot(h_ref[...], wcq_ref[...]) + row_ref[5:6, :]).astype(BF16)
        for i in range(group):
            ok = mask_ref[i].astype(F32) > 0.5
            ok = jnp.concatenate([ok, ok], 1)
            r = slice(i * length, (i + 1) * length)
            for p in range(pairs):
                c = slice(p * 128, (p + 1) * 128)
                q, k, v = cq_ref[r, c], kv_ref[i, :, c], kv_ref[i, :, d + p * 128 : d + (p + 1) * 128]
                scores = dot_t(k, spread_heads(q, low, high)) * scale
                probs = soft(jnp.where(ok, scores, NEG)).astype(BF16)
                prob_ref[i, p] = probs
                ctx_ref[r, c] = join_heads(dot(v.T, probs))
        two_ref[...] = hidden + dot(ctx_ref[...], wcout_ref[...]) + row_ref[7:8, :]

    return call(
        body,
        "cross_forward",
        items // group,
        [
            (total_one, tiled((block, d))),
            (kv, tiled((group, count, 2 * d))),
            (mask, tiled((group, count, length))),
            (w_cq, whole((d, d))),
            (w_cout, whole((d, d))),
            (rows, whole(rows.shape)),
        ],
        [
            (spec_of((tokens, d), BF16), tiled((block, d))),
            (spec_of((tokens, d), BF16), tiled((block, d))),
            (spec_of((items, pairs, count, 2 * length), BF16), tiled((group, pairs, count, 2 * length))),
            (spec_of((tokens, d), BF16), tiled((block, d))),
            (spec_of((tokens, d), F32), tiled((block, d))),
        ],
        2 * tokens * d * 6 * d,
    )


def ffn_forward(dims, source, total_two, cotangent, rows, bias):
    d, items, length, group = dims.d, dims.items, dims.length, dims.group
    tokens, block, ff = items * length, group * length, bias.shape[1]
    piece = d
    n_in = len(source.ins)

    def body(tot_ref, cot_ref, row_ref, bias_ref, *refs):
        out_ref, h_ref, act_ref, slope_ref, g_ref, glow_ref, sum_ref = refs[n_in : n_in + 7]
        win_ref, wout_ref = source.open(refs[:n_in], refs[n_in + 7 :])

        @pl.when(pl.program_id(0) == 0)
        def _():
            sum_ref[...] = jnp.zeros_like(sum_ref)

        hat, _ = norm_parts(tot_ref[...])
        hidden = hat * row_ref[8:9, :] + row_ref[9:10, :]
        h_ref[...] = hidden.astype(BF16)
        total = hidden + row_ref[10:11, :]
        for at in range(0, ff, piece):
            cut = slice(at, at + piece)
            pre = dot(h_ref[...], win_ref[:, cut]) + bias_ref[:, cut]
            under, bell = gelu_parts(pre)
            act = (pre * under).astype(BF16)
            act_ref[:, cut] = act
            slope_ref[:, cut] = (under + (pre * 0.3989422804014327) * bell).astype(BF16)
            total = total + dot(act, wout_ref[cut, :])
        hat, spread = norm_parts(total)
        gain = row_ref[11:12, :]
        out_ref[...] = hat * gain + row_ref[12:13, :]
        cot = cot_ref[...].astype(F32)
        grad = norm_pull(cot, hat, spread, gain)
        g_ref[...] = grad
        low = grad.astype(BF16)
        glow_ref[...] = low
        sum_ref[0:1, :] += col_sum(cot * hat)
        sum_ref[1:2, :] += col_sum(cot)
        sum_ref[2:3, :] += col_sum(low)

    done = call(
        body,
        "ffn_forward",
        items // group,
        [
            (total_two, tiled((block, d))),
            (cotangent, tiled((block, d))),
            (rows, whole(rows.shape)),
            (bias, whole(bias.shape)),
        ]
        + source.ins,
        [
            (spec_of((tokens, d), F32), tiled((block, d))),
            (spec_of((tokens, d), BF16), tiled((block, d))),
            (spec_of((tokens, ff), BF16), tiled((block, ff))),
            (spec_of((tokens, ff), BF16), tiled((block, ff))),
            (spec_of((tokens, d), F32), tiled((block, d))),
            (spec_of((tokens, d), BF16), tiled((block, d))),
            (spec_of((8, d), F32), summed((8, d))),
        ]
        + source.outs,
        4 * tokens * d * ff,
    )
    return source.split(done)


def ffn_backward(dims, grad_three, grad_low, slope, total_two, w_fin, w_fout, rows):
    d, items, length, group = dims.d, dims.items, dims.length, dims.group
    tokens, block, ff = items * length, group * length, w_fin.shape[1]
    piece = d

    def body(g_ref, glow_ref, slope_ref, tot_ref, win_ref, wout_ref, row_ref,
             pre_ref, two_ref, twolow_ref, sum_ref, bias_ref):
        @pl.when(pl.program_id(0) == 0)
        def _():
            sum_ref[...] = jnp.zeros_like(sum_ref)
            bias_ref[...] = jnp.zeros_like(bias_ref)

        grad = g_ref[...]
        for at in range(0, ff, piece):
            cut = slice(at, at + piece)
            pre = dot_t(glow_ref[...], wout_ref[cut, :]) * slope_ref[:, cut].astype(F32)
            pre = pre.astype(BF16)
            pre_ref[:, cut] = pre
            bias_ref[0:1, cut] += col_sum(pre)
            grad = grad + dot_t(pre, win_ref[:, cut])
        hat, spread = norm_parts(tot_ref[...])
        two = norm_pull(grad, hat, spread, row_ref[8:9, :])
        two_ref[...] = two
        low = two.astype(BF16)
        twolow_ref[...] = low
        sum_ref[0:1, :] += col_sum(grad * hat)
        sum_ref[1:2, :] += col_sum(grad)
        sum_ref[2:3, :] += col_sum(low)

    return call(
        body,
        "ffn_backward",
        items // group,
        [
            (grad_three, tiled((block, d))),
            (grad_low, tiled((block, d))),
            (slope, tiled((block, ff))),
            (total_two, tiled((block, d))),
            (w_fin, whole((d, ff))),
            (w_fout, whole((ff, d))),
            (rows, whole(rows.shape)),
        ],
        [
            (spec_of((tokens, ff), BF16), tiled((block, ff))),
            (spec_of((tokens, d), F32), tiled((block, d))),
            (spec_of((tokens, d), BF16), tiled((block, d))),
            (spec_of((8, d), F32), summed((8, d))),
            (spec_of((8, ff), F32), summed((8, ff))),
        ],
        4 * tokens * d * ff,
    )


def pair_pull(q, k, v, out, probs, low, high):
    outs = spread_heads(out, low, high)
    score = soft_pull(probs.astype(F32), dot_t(v, outs)).astype(BF16)
    grad_k = dot(score, spread_heads(q, low, high))
    return dot(k.T, score), grad_k, dot(probs, outs)


def cross_attend_back(dims, grad_low, query, kv, probs, w_cout):
    d, items, length, group = dims.d, dims.items, dims.length, dims.group
    pairs, tokens, block = d // (2 * HEAD), items * length, group * length
    count = kv.shape[1]
    scale = HEAD ** (-0.5)

    def body(glow_ref, q_ref, kv_ref, prob_ref, wcout_ref, gq_ref, gkv_ref, sum_ref, ctx_ref):
        @pl.when(pl.program_id(0) == 0)
        def _():
            sum_ref[...] = jnp.zeros_like(sum_ref)

        low, high = lane_masks()
        ctx_ref[...] = dot_t(glow_ref[...], wcout_ref[...]).astype(BF16)
        for i in range(group):
            r = slice(i * length, (i + 1) * length)
            for p in range(pairs):
                c = slice(p * 128, (p + 1) * 128)
                cv = slice(d + p * 128, d + (p + 1) * 128)
                grad_q, grad_k, grad_v = pair_pull(
                    q_ref[r, c], kv_ref[i, :, c], kv_ref[i, :, cv], ctx_ref[r, c], prob_ref[i, p], low, high
                )
                gq_ref[r, c] = join_heads(grad_q * scale)
                gkv_ref[i, :, c] = (grad_k * scale).astype(BF16)
                gkv_ref[i, :, cv] = grad_v.astype(BF16)
        sum_ref[0:1, :] += col_sum(gq_ref[...])
        sum_ref[1:2, :] += col_sum(gkv_ref[:, :, d:].reshape(group * count, d))

    return call(
        body,
        "cross_attend_back",
        items // group,
        [
            (grad_low, tiled((block, d))),
            (query, tiled((block, d))),
            (kv, tiled((group, count, 2 * d))),
            (probs, tiled((group, pairs, count, 2 * length))),
            (w_cout, whole((d, d))),
        ],
        [
            (spec_of((tokens, d), BF16), tiled((block, d))),
            (spec_of((items, count, 2 * d), BF16), tiled((group, count, 2 * d))),
            (spec_of((8, d), F32), summed((8, d))),
        ],
        2 * tokens * d * 4 * d,
        [pltpu.VMEM((block, d), BF16)],
    )


def cross_project_back(dims, grad_two, grad_query, grad_kv, total_one, w_cq, w_ckv, rows, parts, part):
    d, items, length, group = dims.d, dims.items, dims.length, dims.group
    tokens, block = items * length, group * length
    count, vis = grad_kv.shape[1], w_ckv.shape[0]

    def body(g_ref, gq_ref, gkv_ref, tot_ref, wcq_ref, wckv_ref, row_ref, *refs):
        grid_refs, (cls_ref, one_ref, onelow_ref, sum_ref) = refs[:parts], refs[parts:]

        @pl.when(pl.program_id(0) == 0)
        def _():
            sum_ref[...] = jnp.zeros_like(sum_ref)

        for i in range(group):
            value = dot_t(gkv_ref[i], wckv_ref[...])
            for k in range(parts):
                grid_refs[k][i] = value[k * part : (k + 1) * part, :].astype(BF16)
            cls_ref[i] = value[parts * part : parts * part + 1, :]
        grad = g_ref[...] + dot_t(gq_ref[...], wcq_ref[...])
        hat, spread = norm_parts(tot_ref[...])
        one = norm_pull(grad, hat, spread, row_ref[3:4, :])
        one_ref[...] = one
        one_low = one.astype(BF16)
        onelow_ref[...] = one_low
        sum_ref[0:1, :] += col_sum(grad * hat)
        sum_ref[1:2, :] += col_sum(grad)
        sum_ref[2:3, :] += col_sum(one_low)

    return call(
        body,
        "cross_project_back",
        items // group,
        [
            (grad_two, tiled((block, d))),
            (grad_query, tiled((block, d))),
            (grad_kv, tiled((group, count, 2 * d))),
            (total_one, tiled((block, d))),
            (w_cq, whole((d, d))),
            (w_ckv, whole((vis, 2 * d))),
            (rows, whole(rows.shape)),
        ],
        [(spec_of((items, part, vis), BF16), tiled((group, part, vis)))] * parts
        + [
            (spec_of((items, 1, vis), F32), tiled((group, 1, vis))),
            (spec_of((tokens, d), F32), tiled((block, d))),
            (spec_of((tokens, d), BF16), tiled((block, d))),
            (spec_of((8, d), F32), summed((8, d))),
        ],
        2 * tokens * d * d + 2 * items * count * vis * 2 * d,
    )


def self_attend_back(dims, grad_low, qkv, probs, w_out):
    d, items, length, group = dims.d, dims.items, dims.length, dims.group
    pairs, tokens, block = d // (2 * HEAD), items * length, group * length
    scale = HEAD ** (-0.5)

    def body(glow_ref, qkv_ref, prob_ref, wout_ref, gqkv_ref, sum_ref, ctx_ref):
        @pl.when(pl.program_id(0) == 0)
        def _():
            sum_ref[...] = jnp.zeros_like(sum_ref)

        low, high = lane_masks()
        ctx_ref[...] = dot_t(glow_ref[...], wout_ref[...]).astype(BF16)
        for i in range(group):
            r = slice(i * length, (i + 1) * length)
            for p in range(pairs):
                cuts = [slice(part * d + p * 128, part * d + (p + 1) * 128) for part in range(3)]
                q, k, v = (qkv_ref[r, cut] for cut in cuts)
                grad_q, grad_k, grad_v = pair_pull(q, k, v, ctx_ref[r, cuts[0]], prob_ref[i, p], low, high)
                gqkv_ref[r, cuts[0]] = join_heads(grad_q * scale)
                gqkv_ref[r, cuts[1]] = (grad_k * scale).astype(BF16)
                gqkv_ref[r, cuts[2]] = grad_v.astype(BF16)
        sum_ref[0:1, :] += col_sum(gqkv_ref[:, :d])
        sum_ref[1:2, :] += col_sum(gqkv_ref[:, 2 * d :])

    return call(
        body,
        "self_attend_back",
        items // group,
        [
            (grad_low, tiled((block, d))),
            (qkv, tiled((block, 3 * d))),
            (probs, tiled((group, pairs, length, 2 * length))),
            (w_out, whole((d, d))),
        ],
        [
            (spec_of((tokens, 3 * d), BF16), tiled((block, 3 * d))),
            (spec_of((8, d), F32), summed((8, d))),
        ],
        2 * tokens * d * 4 * d,
        [pltpu.VMEM((block, d), BF16)],
    )


def self_project_back(dims, grad_one, grad_qkv, w_qkv):
    d, items, length, group = dims.d, dims.items, dims.length, dims.group
    tokens, block = items * length, group * length

    def body(g_ref, gqkv_ref, wqkv_ref, text_ref):
        text_ref[...] = g_ref[...] + dot_t(gqkv_ref[...], wqkv_ref[...])

    return call(
        body,
        "self_project_back",
        items // group,
        [
            (grad_one, tiled((block, d))),
            (grad_qkv, tiled((block, 3 * d))),
            (w_qkv, whole((d, 3 * d))),
        ],
        [(spec_of((tokens, d), F32), tiled((block, d)))],
        2 * tokens * d * 3 * d,
    )[0]


def cut_grids(turn, image_grid, parts):
    micro, items, part, vis = image_grid.shape
    each = items // parts

    def body(turn_ref, grid_ref, *out_refs):
        def fill(own):
            value = jnp.swapaxes(grid_ref[0], 0, 1)
            for s in range(parts):
                out_refs[s ^ own][...] = value[s * each : (s + 1) * each]

        for own in range(parts):
            pl.when(turn_ref[0] == own)(functools.partial(fill, own))

    return call(
        body,
        "cut_grids",
        micro,
        [
            (turn, SMEM_SPEC),
            (image_grid.transpose(0, 2, 1, 3), tiled((1, part, items, vis))),
        ],
        [(spec_of((micro * each, part, vis), BF16), tiled((each, part, vis)))] * parts,
        0,
    )


def place_grids(turn, micro, pieces):
    items, part, vis = pieces[0].shape
    each, parts = items // micro, len(pieces)

    def body(turn_ref, *refs):
        def fill(own):
            value = jnp.concatenate([refs[s ^ own][...].astype(F32) for s in range(parts)], 0)
            refs[-1][0] = jnp.swapaxes(value, 0, 1)

        for own in range(parts):
            pl.when(turn_ref[0] == own)(functools.partial(fill, own))

    shape = (micro, part, each * parts, vis)
    done = call(
        body,
        "place_grids",
        micro,
        [(turn, SMEM_SPEC)] + [(p, tiled((each, part, vis))) for p in pieces],
        [(spec_of(shape, F32), tiled((1,) + shape[1:]))],
        0,
    )[0]
    return done.transpose(0, 2, 1, 3)


def weight_grads(plan, group, where, factors):
    high_rows = max(plan.full[w][0] for w in group)
    wide = max(plan.full[w][1] for w in group)
    flat = [a for pair in factors for a in pair]
    count = len(flat)

    def body(where_ref, *refs):
        far, stack_refs = refs[:count], refs[count : count + 2]
        near, made, sems = refs[count + 2 : 2 * count + 2], refs[-2], refs[-1]
        copies = [pltpu.make_async_copy(far[n], near[n], sems.at[n]) for n in range(count)]
        for copy in copies:
            copy.start()
        for n, w in enumerate(group):
            left, right = near[2 * n], near[2 * n + 1]
            rows, cols = plan.full[w]
            copies[2 * n].wait()
            copies[2 * n + 1].wait()
            for at in range(0, rows, 256):
                value = dot_l(left[:, at : at + 256], right[...])
                made[at : at + 256, :cols] = value.astype(BF16)

            def visit(other, stack, k, row, w_at, j, to_row, to_y, high):
                if w_at == w:
                    col = pl.multiple_of(to_y * (cols // 2) + j * plan.chunk, 128)
                    stack_refs[other][stack, k, row : row + high, :] = made[
                        pl.ds(to_row, high), pl.ds(col, plan.chunk)
                    ]

            each_place(plan, group, where_ref, visit)

    shape = jax.ShapeDtypeStruct((4, plan.zs, plan.rows(group), plan.chunk), BF16)
    flops = sum(2 * a.shape[0] * a.shape[1] * b.shape[1] for a, b in factors)
    moved = sum(a.size * 2 for a in flat) + 2 * shape.size * 2
    return pl.pallas_call(
        body,
        out_shape=(shape,) * 2,
        in_specs=[SMEM_SPEC] + [pl.BlockSpec(memory_space=pl.ANY)] * count,
        out_specs=(VMEM_SPEC,) * 2,
        scratch_shapes=[pltpu.VMEM(a.shape, BF16) for a in flat]
        + [pltpu.VMEM((high_rows, wide), BF16), pltpu.SemaphoreType.DMA((count,))],
        compiler_params=PARAMS,
        cost_estimate=pl.CostEstimate(flops=flops, bytes_accessed=moved, transcendentals=0),
        name="weight_grads",
    )(where, *flat)


class Dims:
    def __init__(self, d, items, length):
        self.d, self.items, self.length = d, items, length
        self.group = 2 if items % 2 == 0 else 1


def cross_mask(lengths, counts, boxes, length, count):
    place = jnp.arange(length, dtype=jnp.int32)[None, :]
    boxed = (counts[:, None] > 0) & (place < lengths[:, None])
    phrase = jnp.where(boxed, place * counts[:, None] // lengths[:, None], 0)
    chosen = phrase[:, None, :] == jnp.arange(boxes.shape[1], dtype=jnp.int32)[None, :, None]
    inside = jnp.einsum(
        "ijp,ijt->ipt",
        (boxes > 0).astype(BF16),
        chosen.astype(BF16),
        preferred_element_type=F32,
    )
    grid_ok = jnp.where(boxed[:, None, :], inside, 1.0).astype(BF16)
    items, real = grid_ok.shape[:2]
    own = jnp.ones((items, 1, length), BF16)
    return jnp.concatenate([grid_ok, own, jnp.zeros((items, count - real - 1, length), BF16)], 1)


def trade(pieces, parts):
    return [pieces[0]] + [
        lax.ppermute(pieces[k], "patch", [(i, i ^ k) for i in range(parts)])
        for k in range(1, len(pieces))
    ]


class Work:
    def __init__(self, args, parts):
        (self.text_in, self.image_grid, self.image_cls, lengths, counts, boxes, cot) = args
        self.parts = parts
        self.micro, d = self.text_in.shape[0], self.text_in.shape[2]
        self.items = lengths.size
        self.text, self.cot = self.text_in.reshape(-1, d), cot.reshape(-1, d)
        self.lengths, self.counts = lengths.reshape(-1), counts.reshape(-1)
        self.boxes = boxes.reshape((self.items,) + boxes.shape[2:])
        self.dims = Dims(d, self.items, self.text.shape[0] // self.items)
        self.turn = lax.axis_index("patch").astype(jnp.int32).reshape(1)
        self.part, self.vis = self.image_grid.shape[2:]
        self.each = self.items // self.micro
        self.count = -(-(parts * self.part + 1) // 16) * 16
        self.cls = self.image_cls.reshape(self.items, 1, self.vis)

    def mask(self):
        boxes = self.boxes.reshape(self.items, -1, self.parts, self.part)
        order = jnp.arange(self.parts, dtype=jnp.int32) ^ self.turn[0]
        boxes = jnp.take(boxes, order, axis=2).reshape(self.boxes.shape)
        return cross_mask(self.lengths, self.counts, boxes, self.dims.length, self.count)

    def finish(self, layer_out, text_grad, grid_grad, cls, grads, rows_grad, bias_grad):
        return (
            layer_out.reshape(self.text_in.shape),
            text_grad.reshape(self.text_in.shape),
            grid_grad,
            cls.reshape(self.image_cls.shape),
            *grads,
            rows_grad,
            bias_grad,
        )


def rows_of(sum_self, sum_attend, sum_one, sum_two, sum_three):
    return jnp.concatenate(
        [
            sum_self[0:2],
            sum_one[2:3],
            sum_one[0:2],
            sum_attend[0:2],
            sum_two[2:3],
            sum_two[0:2],
            sum_three[2:3],
            sum_three[0:2],
        ]
    )


def on_device(plan, *args):
    work, shards, vectors, ffn_bias = Work(args[:7], plan.patch), args[7:14], args[14], args[15]
    dims, where, parts = work.dims, coords(), plan.patch

    own, give = pack_split(plan, where, shards)
    units = pack_join(plan, where, own, send(give, plan.core()))
    gathers = [Gathering(plan, unit) for unit in units]

    def step(*groups):
        for g in groups:
            gathers[g].advance()

    def source(g):
        return Source(plan, GROUPS[g], where, gathers[g].held)

    image_grid, vectors, ffn_bias = fence(gathers, [work.image_grid, vectors, ffn_bias])
    step(0)
    grids = trade(cut_grids(work.turn, image_grid, parts), parts)
    (vectors, ffn_bias) = fence(gathers, [vectors, ffn_bias])
    step(0, 1)
    rows, bias = gather_small(plan, where, vectors, ffn_bias)
    rows = jnp.pad(rows, ((0, -rows.shape[0] % 8), (0, 0)))
    rows, bias, grids = fence(gathers, [rows, bias, grids])
    step(0, 1, 2)
    fence(gathers[:2], [])
    step(0, 1)
    (qkv, probs, ctx, total_one), (w_qkv, w_out) = self_forward(
        dims, source(0), work.text, rows, work.lengths
    )
    mask = work.mask()
    total_one, grids, mask = fence(gathers[1:], [total_one, grids, mask])
    step(1, 2)
    (kv, patches), (w_cq, w_ckv, w_cout) = cross_keys(
        dims, source(1), grids, work.cls, rows, work.count
    )
    kv, total_one = fence(gathers[2:], [kv, total_one])
    step(2)
    hidden_one, query, cross_probs, cross_ctx, total_two = cross_forward(
        dims, total_one, kv, mask, w_cq, w_cout, rows
    )
    total_two = fence(gathers[2:], total_two)
    step(2)
    (layer_out, hidden_two, act, slope, grad_three, low_three, sum_three), (w_fin, w_fout) = ffn_forward(
        dims, source(2), total_two, work.cot, rows, bias[None]
    )

    reduces = {}

    def reduce(g, factors):
        stacks = weight_grads(plan, GROUPS[g], where, factors)
        reduces[g] = Reducing(plan, GROUPS[g], where, stacks)

    def hold(*values):
        return fence(list(reduces.values()), list(values))

    def go(*groups):
        for g in groups:
            reduces[g].advance()

    grad_pre, grad_two, low_two, sum_two, sum_pre = ffn_backward(
        dims, grad_three, low_three, slope, total_two, w_fin, w_fout, rows
    )
    reduce(2, [(hidden_two, grad_pre), (act, low_three)])
    (low_two,) = hold(low_two)
    go(2)
    grad_query, grad_kv, sum_attend = cross_attend_back(dims, low_two, query, kv, cross_probs, w_cout)
    grad_query, grad_kv = hold(grad_query, grad_kv)
    go(2)
    flat_kv = grad_kv.reshape(-1, grad_kv.shape[2])
    reduce(
        1,
        [
            (hidden_one, grad_query),
            (patches.reshape(-1, work.vis), flat_kv),
            (cross_ctx, low_two),
        ],
    )
    *grids, cls, grad_one, low_one, sum_one = cross_project_back(
        dims, grad_two, grad_query, grad_kv, total_one, w_cq, w_ckv, rows, parts, work.part
    )
    low_one, *grids = hold(low_one, *grids)
    go(2, 1)
    grids[1:3] = trade(grids[:3], parts)[1:]
    grad_qkv, sum_self = self_attend_back(dims, low_one, qkv, probs, w_out)
    grad_qkv, sum_self, *grids = hold(grad_qkv, sum_self, *grids)
    go(2, 1)
    grids[3] = trade(grids, parts)[3]
    reduce(0, [(work.text, grad_qkv), (ctx, low_one)])
    reduces["small"] = ReducingSmall(
        plan, where, rows_of(sum_self, sum_attend, sum_one, sum_two, sum_three), sum_pre[0]
    )
    grad_qkv, *grids = hold(grad_qkv, *grids)
    go(2, 1, 0, "small")
    (grad_qkv,) = hold(grad_qkv)
    go(2, 1, 0, "small")
    text_grad = self_project_back(dims, grad_one, grad_qkv, w_qkv)
    text_grad, *grids = hold(text_grad, *grids)
    go(1, 0, "small")
    grid_grad = place_grids(work.turn, work.micro, grids)
    (grid_grad,) = hold(grid_grad)
    go(1, 0, "small")
    hold()
    go(0)
    go(0)
    grads = [None] * 7
    for g, group in enumerate(GROUPS):
        for w, value in zip(group, reduces[g].held):
            grads[w] = value
    return work.finish(layer_out, text_grad, grid_grad, cls, grads, *reduces["small"].result())


def on_device_plain(plan, *args):
    work, parts = Work(args[:7], plan.patch), plan.patch
    dims = work.dims
    weights, rows, bias = fetch_plain(args[7:14], args[14], args[15])
    rows = jnp.pad(rows, ((0, -rows.shape[0] % 8), (0, 0)))
    grids = trade(cut_grids(work.turn, work.image_grid, parts), parts)

    def source(g):
        return Source(plan, GROUPS[g], None, [weights[w] for w in GROUPS[g]])

    (qkv, probs, ctx, total_one), _ = self_forward(dims, source(0), work.text, rows, work.lengths)
    (kv, patches), _ = cross_keys(dims, source(1), grids, work.cls, rows, work.count)
    hidden_one, query, cross_probs, cross_ctx, total_two = cross_forward(
        dims, total_one, kv, work.mask(), weights[CQ], weights[COUT], rows
    )
    (layer_out, hidden_two, act, slope, grad_three, low_three, sum_three), _ = ffn_forward(
        dims, source(2), total_two, work.cot, rows, bias[None]
    )
    grad_pre, grad_two, low_two, sum_two, sum_pre = ffn_backward(
        dims, grad_three, low_three, slope, total_two, weights[FIN], weights[FOUT], rows
    )
    grad_query, grad_kv, sum_attend = cross_attend_back(
        dims, low_two, query, kv, cross_probs, weights[COUT]
    )
    *grids, cls, grad_one, low_one, sum_one = cross_project_back(
        dims, grad_two, grad_query, grad_kv, total_one, weights[CQ], weights[CKV], rows, parts, work.part
    )
    grad_qkv, sum_self = self_attend_back(dims, low_one, qkv, probs, weights[OUT])
    text_grad = self_project_back(dims, grad_one, grad_qkv, weights[QKV])
    flat_kv = grad_kv.reshape(-1, grad_kv.shape[2])
    factors = [
        (work.text, grad_qkv),
        (ctx, low_one),
        (hidden_one, grad_query),
        (patches.reshape(-1, work.vis), flat_kv),
        (cross_ctx, low_two),
        (hidden_two, grad_pre),
        (act, low_three),
    ]
    grads = [reduce_plain(dot_l(a, b).astype(BF16)) for a, b in factors]
    small = reduce_small_plain(
        rows_of(sum_self, sum_attend, sum_one, sum_two, sum_three), sum_pre[0]
    )
    grid_grad = place_grids(work.turn, work.micro, trade(grids, parts))
    return work.finish(layer_out, text_grad, grid_grad, cls, grads, *small)


def solution(mesh):
    dp, patch = mesh.shape["dp"], mesh.shape["patch"]
    both = P(None, ("dp", "patch"), None)
    weight = P("dp", "patch")

    def run(*args):
        shards = [(w.shape[0] // dp, w.shape[1] // patch) for w in args[7:14]]
        plan = Plan(dp, patch, shards)
        return jax.shard_map(
            functools.partial(on_device if plan.fast else on_device_plain, plan),
            mesh=mesh,
            in_specs=(
                both,
                P(None, "dp", "patch", None),
                both,
                P(None, ("dp", "patch")),
                P(None, ("dp", "patch")),
                P(None, ("dp", "patch"), None, None),
                both,
            )
            + (weight,) * 7
            + (P(None, "dp"), P("dp")),
            out_specs=(both, both, P(None, "dp", "patch", None), both)
            + (weight,) * 7
            + (P(None, "dp"), P("dp")),
            check_vma=False,
        )(*args)

    return run
```

```python
import functools

import jax
import jax.numpy as jnp
from jax import lax
from jax.experimental import pallas as pl
from jax.experimental.pallas import tpu as pltpu
from jax.sharding import PartitionSpec as P

HEAD = 64
EPS = 1e-06
NEG = -1e30
BF16 = jnp.bfloat16
F32 = jnp.float32
AXES = ("dp", "patch")
VMEM_SPEC = pl.BlockSpec(memory_space=pltpu.VMEM)
SMEM_SPEC = pl.BlockSpec(memory_space=pltpu.SMEM)
PARAMS = pltpu.CompilerParams(vmem_limit_bytes=62 * 2**20)

QKV, OUT, CQ, CKV, COUT, FIN, FOUT = range(7)
ROWS = 13
GROUPS = ((QKV,), (OUT, CQ, CKV, COUT), (FIN, FOUT))


class Plan:
    def __init__(self, dp, patch, shards):
        self.dp, self.patch = dp, patch
        self.zs = dp // 2
        self.devices = dp * patch
        self.chunk = shards[OUT][1] * 2
        self.half = [s[0] // 2 for s in shards]
        self.cols = [s[1] for s in shards]
        self.chunks = [s[1] * 2 // self.chunk for s in shards]
        self.full = [(s[0] * dp, s[1] * patch) for s in shards]
        self.fast = (
            dp % 2 == 0
            and self.zs & (self.zs - 1) == 0
            and patch == 4
            and all(h % 16 == 0 for h in self.half)
            and all(s[1] * 2 % self.chunk == 0 for s in shards)
            and self.chunk % 128 == 0
        )

    def rows(self, group):
        return sum(self.half[w] * self.chunks[w] for w in group)

    def flip(self, pick):
        return [(i, i ^ pick(i)) for i in range(self.devices)]

    def core(self):
        return self.flip(lambda i: 1)

    def first(self):
        return self.flip(lambda i: 4 if i % 2 == 0 else 2)

    def second(self):
        return self.flip(lambda i: 2 if i % 2 == 0 else 4)

    def along_z(self, k):
        return self.flip(lambda i: 8 * k)


def send(value, perm):
    return lax.ppermute(value, AXES, perm)


def coords():
    dp, patch = lax.axis_index("dp"), lax.axis_index("patch")
    return jnp.stack([dp // 2, dp % 2, patch // 2, patch % 2]).astype(jnp.int32)


def piece_rows(group, plan):
    at, found = 0, []
    for w in group:
        for j in range(plan.chunks[w]):
            found.append((w, j, at))
            at += plan.half[w]
    return found


def group_starts(plan):
    starts, at = [], 0
    for group in GROUPS:
        starts.append(at)
        at += plan.rows(group)
    return starts, at


def pack_split(plan, where, shards):
    _, total = group_starts(plan)
    wide = plan.chunk // 2

    def body(where_ref, *refs):
        shard_refs, (own_ref, send_ref, turned) = list(refs[:7]), refs[7:]
        core = where_ref[3]
        turned[...] = shard_refs[FOUT][...].T
        shard_refs[FOUT] = turned
        at = 0
        for group in GROUPS:
            for w in group:
                high = plan.half[w]
                for b in range(plan.chunks[w]):
                    cut = slice(b * wide, (b + 1) * wide)
                    own_ref[at : at + high, :] = shard_refs[w][pl.ds(core * high, high), cut]
                    send_ref[at : at + high, :] = shard_refs[w][
                        pl.ds((1 - core) * high, high), cut
                    ]
                    at += high

    shape = jax.ShapeDtypeStruct((total, wide), BF16)
    return pl.pallas_call(
        body,
        out_shape=(shape, shape),
        in_specs=[SMEM_SPEC] + [VMEM_SPEC] * 7,
        out_specs=(VMEM_SPEC, VMEM_SPEC),
        scratch_shapes=[pltpu.VMEM(shards[FOUT].shape, BF16)],
        compiler_params=PARAMS,
        name="pack_split",
    )(where, *shards[:FOUT], shards[FOUT].T)


def pack_join(plan, where, own, got):
    starts, total = group_starts(plan)
    wide = plan.chunk // 2

    def body(where_ref, own_ref, got_ref, *unit_refs):
        core = where_ref[3]

        def fill(low_ref, high_ref):
            for g, group in enumerate(GROUPS):
                at = starts[g]
                for w in group:
                    high, count = plan.half[w], plan.chunks[w]
                    for j in range(count):
                        pair = []
                        for b in (2 * j, 2 * j + 1):
                            src = low_ref if b < count else high_ref
                            row = at + (b % count) * high
                            pair.append(src[row : row + high, :])
                        to = at - starts[g] + j * high
                        unit_refs[g][to : to + high, :] = jnp.concatenate(pair, axis=1)
                    at += count * high

        @pl.when(core == 0)
        def _():
            fill(own_ref, got_ref)

        @pl.when(core == 1)
        def _():
            fill(got_ref, own_ref)

    return pl.pallas_call(
        body,
        out_shape=tuple(jax.ShapeDtypeStruct((plan.rows(g), plan.chunk), BF16) for g in GROUPS),
        in_specs=[SMEM_SPEC, VMEM_SPEC, VMEM_SPEC],
        out_specs=(VMEM_SPEC,) * len(GROUPS),
        compiler_params=PARAMS,
        name="pack_join",
    )(where, own, got)


class Gathering:
    def __init__(self, plan, unit):
        self.plan, self.held, self.step = plan, [unit], 0

    def advance(self):
        plan, held = self.plan, self.held
        if self.step == 0:
            held = held + [send(held[0], plan.along_z(k)) for k in range(1, plan.zs)]
        elif self.step == 1:
            stack = jnp.stack(held)
            held = [stack, send(stack, plan.first())]
        elif self.step == 2:
            near = jnp.stack(held)
            held = [near, send(near, plan.second()), send(near, plan.core())]
        elif self.step == 3:
            held = held + [send(held[1], plan.core())]
        self.held, self.step = held, self.step + 1


def each_place(plan, group, where_ref, visit):
    z, x, y, core = (where_ref[i] for i in range(4))
    for other in range(2):
        half = core ^ other
        for second in range(2):
            for first in range(2):
                x_at = x ^ jnp.where(half == 0, first, second)
                y_at = y ^ jnp.where(half == 0, second, first)
                for k in range(plan.zs):
                    place = ((z ^ k) * 2 + x_at) * 2 + half
                    for w, j, row in piece_rows(group, plan):
                        high = plan.half[w]
                        to_row = pl.multiple_of(place * high, 16)
                        visit(other, second, first, k, row, w, j, to_row, y_at, high)


def add_low(ones, twos, widths):
    count, slots, rows, chunk = ones.shape

    def body(one_ref, two_ref, *out_refs):
        at = 0
        for width, out in zip(widths, out_refs):
            for n in range(width):
                out[n] = (one_ref[at].astype(F32) + two_ref[at].astype(F32)).astype(BF16)
                at += 1

    cuts = 2 if rows % 32 == 0 else 1

    def spec(n):
        return pl.BlockSpec((n, 1, rows // cuts, chunk), lambda i: (0, i // cuts, i % cuts, 0))

    return pl.pallas_call(
        body,
        grid=(slots * cuts,),
        out_shape=tuple(jax.ShapeDtypeStruct((n, slots, rows, chunk), BF16) for n in widths),
        in_specs=[spec(count), spec(count)],
        out_specs=tuple(spec(n) for n in widths),
        compiler_params=PARAMS,
        cost_estimate=pl.CostEstimate(
            flops=ones.size, bytes_accessed=6 * ones.size, transcendentals=0
        ),
        name="add_low",
    )(ones, twos)


def add_slots(ones, twos):
    _, slots, rows, chunk = ones.shape

    def body(one_ref, two_ref, *out_refs):
        for n in range(slots):
            out_refs[n][...] = (one_ref[0, n].astype(F32) + two_ref[0, n].astype(F32)).astype(BF16)

    return pl.pallas_call(
        body,
        out_shape=(jax.ShapeDtypeStruct((rows, chunk), BF16),) * slots,
        in_specs=[VMEM_SPEC, VMEM_SPEC],
        out_specs=(VMEM_SPEC,) * slots,
        compiler_params=PARAMS,
        cost_estimate=pl.CostEstimate(
            flops=ones.size, bytes_accessed=6 * ones.size, transcendentals=0
        ),
        name="add_slots",
    )(ones, twos)


class Reducing:
    def __init__(self, plan, group, where, stacks):
        self.plan, self.group, self.where = plan, group, where
        self.held, self.step = list(stacks), 0

    def advance(self):
        plan, held = self.plan, self.held
        if self.step == 0:
            held = [held[0], send(held[1], plan.core())]
        elif self.step == 1:
            keep, give = add_low(*held, (2, 2))
            held = [keep, send(give, plan.second())]
        elif self.step == 2:
            keep, give = add_low(*held, (1, 1))
            held = [keep, send(give, plan.first())]
        elif self.step == 3:
            slots = add_slots(*held)
            parts = [send(slots[k], plan.along_z(k)) for k in range(1, plan.zs)]
            held = [slots[0]] + parts
        elif self.step == 4:
            own, give = unpack_split(plan, self.group, self.where, held)
            held = [own, send(give, plan.core())]
        elif self.step == 5:
            held = unpack_join(plan, self.group, self.where, *held)
        self.held, self.step = list(held), self.step + 1


def fence(chains, values):
    flat, tree = jax.tree.flatten([values, [chain.held for chain in chains]])
    values, held = jax.tree.unflatten(tree, lax.optimization_barrier(flat))
    for chain, arrays in zip(chains, held):
        chain.held = arrays
    return values


def unpack_split(plan, group, where, parts):
    rows, wide = plan.rows(group), plan.chunk // 2

    def body(where_ref, *refs):
        part_refs, (own_ref, give_ref) = refs[:-2], refs[-2:]
        core = where_ref[3]

        def fill(low_ref, high_ref):
            at = 0
            for w in group:
                high, count = plan.half[w], plan.chunks[w]
                for j in range(count):
                    row = at + j * high
                    value = sum(p[row : row + high, :].astype(F32) for p in part_refs)
                    for b in (2 * j, 2 * j + 1):
                        dst = low_ref if b < count else high_ref
                        to = at + (b % count) * high
                        cut = (b - 2 * j) * wide
                        dst[to : to + high, :] = value[:, cut : cut + wide]
                at += count * high

        @pl.when(core == 0)
        def _():
            fill(own_ref, give_ref)

        @pl.when(core == 1)
        def _():
            fill(give_ref, own_ref)

    shape = jax.ShapeDtypeStruct((rows, wide), F32)
    return pl.pallas_call(
        body,
        out_shape=(shape, shape),
        in_specs=[SMEM_SPEC] + [VMEM_SPEC] * len(parts),
        out_specs=(VMEM_SPEC, VMEM_SPEC),
        compiler_params=PARAMS,
        name="unpack_split",
    )(where, *parts)


def unpack_join(plan, group, where, own, got):
    wide = plan.chunk // 2
    turned = [w == FOUT for w in group]

    def body(where_ref, own_ref, got_ref, *refs):
        core = where_ref[3]
        at = 0
        for n, w in enumerate(group):
            out_ref = refs[-1] if turned[n] else refs[n]
            high, count = plan.half[w], plan.chunks[w]
            own_rows = pl.ds(pl.multiple_of(core * high, 16), high)
            got_rows = pl.ds(pl.multiple_of((1 - core) * high, 16), high)
            for b in range(count):
                row, cut = at + b * high, slice(b * wide, (b + 1) * wide)
                out_ref[own_rows, cut] = own_ref[row : row + high, :]
                out_ref[got_rows, cut] = got_ref[row : row + high, :]
            at += count * high
            if turned[n]:
                refs[n][...] = out_ref[...].T

    shapes = [(2 * plan.half[w], plan.cols[w]) for w in group]
    done = pl.pallas_call(
        body,
        out_shape=tuple(
            jax.ShapeDtypeStruct(shape[::-1] if turn else shape, F32)
            for shape, turn in zip(shapes, turned)
        ),
        in_specs=[SMEM_SPEC, VMEM_SPEC, VMEM_SPEC],
        out_specs=(VMEM_SPEC,) * len(group),
        scratch_shapes=[pltpu.VMEM(shapes[-1], F32)],
        compiler_params=PARAMS,
        name="unpack_join",
    )(where, own, got)
    return [value.T if turn else value for value, turn in zip(done, turned)]


def gather_small(plan, where, vectors, bias):
    count, part = vectors.shape
    flat = jnp.concatenate([vectors.reshape(-1), bias])
    size = flat.shape[0]
    flat = jnp.pad(flat, (0, -size % 2048)).reshape(-1, 128)
    pair = jnp.stack([flat, send(flat, plan.flip(lambda i: 4))])
    every, bit = pair, 1
    while bit < plan.zs:
        every = jnp.concatenate([every, send(every, plan.along_z(bit))])
        bit *= 2
    at = jnp.arange(plan.dp, dtype=jnp.int32)
    slot = at ^ (where[0] * 2 + where[1])
    every = jnp.take(every, slot, axis=0).reshape(plan.dp, -1)[:, :size].astype(F32)
    rows = every[:, : count * part].reshape(plan.dp, count, part)
    rows = rows.transpose(1, 0, 2).reshape(count, plan.dp * part)
    return rows, every[:, count * part :].reshape(-1)


class ReducingSmall:
    def __init__(self, plan, where, sums, bias):
        self.plan, self.where, self.tail = plan, where, bias.shape[1]
        self.held, self.step = [gather_sums(sums, bias)], 0
        bits = [1, 2, 4]
        while 1 << len(bits) < plan.devices:
            bits.append(1 << len(bits))
        self.bits = bits

    def advance(self):
        flat = sum(self.held)
        if self.bits:
            bit = self.bits.pop(0)
            self.held = [flat, send(flat, self.plan.flip(lambda i: bit))]
        else:
            self.held = [flat]

    def result(self):
        plan, flat = self.plan, sum(self.held)
        width = flat.shape[1] // plan.dp
        dp = self.where[0] * 2 + self.where[1]
        own = lax.dynamic_slice_in_dim(flat[:ROWS], dp * width, width, axis=1)
        tail, step = flat[ROWS : ROWS + self.tail // flat.shape[1]].reshape(-1), self.tail // plan.dp
        return own, lax.dynamic_slice_in_dim(tail, dp * step, step, axis=0)


def fetch_plain(weights, vectors, bias):
    whole = [
        lax.all_gather(lax.all_gather(w, "dp", axis=0, tiled=True), "patch", axis=1, tiled=True)
        for w in weights
    ]
    rows = lax.all_gather(vectors, "dp", axis=1, tiled=True)
    return whole, rows.astype(F32), lax.all_gather(bias, "dp", axis=0, tiled=True).astype(F32)


def reduce_plain(grad):
    part = lax.psum_scatter(grad, "dp", scatter_dimension=0, tiled=True)
    return lax.psum_scatter(part, "patch", scatter_dimension=1, tiled=True).astype(F32)


def reduce_small_plain(rows, bias):
    rows = lax.psum_scatter(rows, "dp", scatter_dimension=1, tiled=True)
    bias = lax.psum_scatter(bias, "dp", scatter_dimension=0, tiled=True)
    return lax.psum(rows, "patch"), lax.psum(bias, "patch")


TAIL = (0.112528827, 0.117839666, 0.0706314405, 0.2046457425, -0.190499398, 0.3478185715, -0.201092832, 0.03812798145)


def dot(a, b):
    return lax.dot_general(a, b, (((1,), (0,)), ((), ())), preferred_element_type=F32)


def dot_t(a, b):
    return lax.dot_general(a, b, (((1,), (1,)), ((), ())), preferred_element_type=F32)


def dot_l(a, b):
    return lax.dot_general(a, b, (((0,), (0,)), ((), ())), preferred_element_type=F32)


def norm_parts(total):
    center = total - jnp.mean(total, -1, keepdims=True)
    spread = lax.rsqrt(jnp.mean(center * center, -1, keepdims=True) + EPS)
    return center * spread, spread


def norm_pull(grad, hat, spread, gain):
    scaled = grad * gain
    return spread * (
        scaled
        - jnp.mean(scaled, -1, keepdims=True)
        - hat * jnp.mean(scaled * hat, -1, keepdims=True)
    )


def gelu_parts(x):
    bell = jnp.exp(-0.5 * (x * x))
    t = 1.0 / (1.0 + (0.4 * 0.5**0.5) * jnp.abs(x))
    tail = jnp.full_like(t, TAIL[-1])
    for c in TAIL[-2::-1]:
        tail = tail * t + c
    tail = tail * (t * bell)
    return jnp.where(x < 0.0, tail, 1.0 - tail), bell


def col_sum(value):
    return jnp.sum(value.astype(F32), 0, keepdims=True)


def soft(scores):
    grown = jnp.exp(scores - jnp.max(scores, 0, keepdims=True))
    return grown * (1.0 / jnp.sum(grown, 0, keepdims=True))


def soft_pull(probs, grad):
    return probs * (grad - jnp.sum(probs * grad, 0, keepdims=True))


def spread_heads(value, low, high):
    return jnp.concatenate([value * low, value * high], 0)


def join_heads(value):
    count = value.shape[1] // 2
    value = jnp.concatenate([value[:HEAD, :count], value[HEAD:, count:]], 0)
    return value.astype(BF16).T


def lane_masks():
    lane = lax.broadcasted_iota(jnp.int32, (1, 2 * HEAD), 1)
    low = (lane < HEAD).astype(F32)
    return low.astype(BF16), (1.0 - low).astype(BF16)


def whole(shape):
    return pl.BlockSpec(
        shape, lambda i: (0,) * len(shape), pipeline_mode=pl.Buffered(1)
    )


def summed(shape):
    return pl.BlockSpec(shape, lambda i: (0,) * len(shape))


def tiled(shape):
    return pl.BlockSpec(shape, lambda i: (i,) + (0,) * (len(shape) - 1))


def spec_of(shape, dtype):
    return jax.ShapeDtypeStruct(shape, dtype)


def call(body, name, steps, ins, outs, flops, scratch=()):
    out_shape = tuple(shape for shape, _ in outs)
    moved = sum(a.size * a.dtype.itemsize for a, _ in ins)
    moved += sum(o.size * jnp.dtype(o.dtype).itemsize for o in out_shape)
    return pl.pallas_call(
        body,
        grid=(steps,),
        out_shape=out_shape,
        in_specs=[spec for _, spec in ins],
        out_specs=tuple(spec for _, spec in outs),
        scratch_shapes=list(scratch),
        compiler_params=PARAMS,
        cost_estimate=pl.CostEstimate(
            flops=int(flops), bytes_accessed=int(moved), transcendentals=0
        ),
        name=name,
    )(*[a for a, _ in ins])


class Source:
    def __init__(self, plan, group, where, given):
        self.plan, self.group, self.pieces = plan, group, plan.fast
        if self.pieces:
            self.ins = [(where, SMEM_SPEC)] + [(part, whole(part.shape)) for part in given]
            self.outs = [(spec_of(plan.full[w], BF16), summed(plan.full[w])) for w in group]
        else:
            self.ins = [(w, whole(w.shape)) for w in given]
            self.outs = []
        self.given = given

    def open(self, in_refs, out_refs):
        if not self.pieces:
            return list(in_refs)
        where_ref, parts = in_refs[0], in_refs[1:]
        full = dict(zip(self.group, out_refs))
        plan = self.plan

        def visit(other, second, first, k, row, w, j, to_row, to_y, high):
            to_col = pl.multiple_of(to_y * (plan.full[w][1] // 2) + j * plan.chunk, 128)
            part = parts[other * 2 + second]
            full[w][pl.ds(to_row, high), pl.ds(to_col, plan.chunk)] = part[
                first, k, row : row + high, :
            ]

        @pl.when(pl.program_id(0) == 0)
        def _():
            each_place(plan, self.group, where_ref, visit)

        return list(out_refs)

    def split(self, done):
        if not self.pieces:
            return done, self.given
        return done[: -len(self.group)], done[-len(self.group) :]


def self_forward(dims, source, text, rows, lengths):
    d, items, length, group = dims.d, dims.items, dims.length, dims.group
    pairs, tokens, block = d // (2 * HEAD), items * length, group * length
    scale = HEAD ** (-0.5)

    n_in = len(source.ins)

    def body(len_ref, x_ref, row_ref, *refs):
        qkv_ref, prob_ref, ctx_ref = refs[n_in : n_in + 3]
        (wqkv_ref,) = source.open(refs[:n_in], refs[n_in + 3 :])
        step = pl.program_id(0)
        low, high = lane_masks()
        x = x_ref[...]
        for part, bias in ((0, 0), (1, None), (2, 1)):
            cut = slice(part * d, (part + 1) * d)
            value = dot(x, wqkv_ref[:, cut])
            if bias is not None:
                value = value + row_ref[bias : bias + 1, :]
            qkv_ref[:, cut] = value.astype(BF16)
        place = lax.broadcasted_iota(jnp.int32, (length, 1), 0)
        for i in range(group):
            ok = place < len_ref[step * group + i]
            r = slice(i * length, (i + 1) * length)
            for p in range(pairs):
                q, k, v = (
                    qkv_ref[r, part * d + p * 128 : part * d + (p + 1) * 128] for part in range(3)
                )
                scores = dot_t(k, spread_heads(q, low, high)) * scale
                probs = soft(jnp.where(ok, scores, NEG)).astype(BF16)
                prob_ref[i, p] = probs
                ctx_ref[r, p * 128 : (p + 1) * 128] = join_heads(dot(v.T, probs))
    done = call(
        body,
        "self_forward",
        items // group,
        [(lengths, SMEM_SPEC), (text, tiled((block, d))), (rows, whole(rows.shape))] + source.ins,
        [
            (spec_of((tokens, 3 * d), BF16), tiled((block, 3 * d))),
            (spec_of((items, pairs, length, 2 * length), BF16), tiled((group, pairs, length, 2 * length))),
            (spec_of((tokens, d), BF16), tiled((block, d))),
        ]
        + source.outs,
        2 * tokens * d * 5 * d,
    )
    return source.split(done)


def cross_keys(dims, source, grids, cls, rows, count):
    d, items, group = dims.d, dims.items, dims.group
    part, vis, parts = grids[0].shape[0] // items, cls.shape[2], len(grids)
    n_in = len(source.ins)

    def body(*refs):
        grid_refs, cls_ref, row_ref = refs[:parts], refs[parts], refs[parts + 1]
        refs = refs[parts + 2 :]
        kv_ref, patch_ref = refs[n_in : n_in + 2]
        _, _, wckv_ref, _ = source.open(refs[:n_in], refs[n_in + 2 :])
        for i in range(group):
            for k in range(parts):
                patch_ref[i, k * part : (k + 1) * part, :] = grid_refs[k][i * part : (i + 1) * part, :]
            rest = jnp.zeros((count - parts * part - 1, vis), BF16)
            patch_ref[i, parts * part :, :] = jnp.concatenate([cls_ref[i], rest], 0)
        patch = patch_ref[...].reshape(group * count, vis)
        keys = dot(patch, wckv_ref[:, :d]).astype(BF16)
        kv_ref[:, :, :d] = keys.reshape(group, count, d)
        values = (dot(patch, wckv_ref[:, d:]) + row_ref[6:7, :]).astype(BF16)
        kv_ref[:, :, d:] = values.reshape(group, count, d)

    done = call(
        body,
        "cross_keys",
        items // group,
        [(grid, tiled((group * part, vis))) for grid in grids]
        + [(cls, tiled((group, 1, vis))), (rows, whole(rows.shape))]
        + source.ins,
        [
            (spec_of((items, count, 2 * d), BF16), tiled((group, count, 2 * d))),
            (spec_of((items, count, vis), BF16), tiled((group, count, vis))),
        ]
        + source.outs,
        2 * items * count * vis * 2 * d,
    )
    return source.split(done)


def cross_forward(dims, text, self_ctx, kv, mask, w_out, w_cq, w_cout, rows):
    d, items, length, group = dims.d, dims.items, dims.length, dims.group
    pairs, tokens, block = d // (2 * HEAD), items * length, group * length
    count = kv.shape[1]
    scale = HEAD ** (-0.5)

    def body(x_ref, self_ref, kv_ref, mask_ref, wout_ref, wcq_ref, wcout_ref, row_ref,
             one_ref, h_ref, cq_ref, prob_ref, ctx_ref, two_ref):
        low, high = lane_masks()
        total = x_ref[...].astype(F32) + dot(self_ref[...], wout_ref[...]) + row_ref[2:3, :]
        one_ref[...] = total
        hat, _ = norm_parts(total)
        hidden = hat * row_ref[3:4, :] + row_ref[4:5, :]
        h_ref[...] = hidden.astype(BF16)
        cq_ref[...] = (dot(h_ref[...], wcq_ref[...]) + row_ref[5:6, :]).astype(BF16)
        for i in range(group):
            ok = mask_ref[i].astype(F32) > 0.5
            ok = jnp.concatenate([ok, ok], 1)
            r = slice(i * length, (i + 1) * length)
            for p in range(pairs):
                c = slice(p * 128, (p + 1) * 128)
                q, k, v = cq_ref[r, c], kv_ref[i, :, c], kv_ref[i, :, d + p * 128 : d + (p + 1) * 128]
                scores = dot_t(k, spread_heads(q, low, high)) * scale
                probs = soft(jnp.where(ok, scores, NEG)).astype(BF16)
                prob_ref[i, p] = probs
                ctx_ref[r, c] = join_heads(dot(v.T, probs))
        two_ref[...] = hidden + dot(ctx_ref[...], wcout_ref[...]) + row_ref[7:8, :]

    return call(
        body,
        "cross_forward",
        items // group,
        [
            (text, tiled((block, d))),
            (self_ctx, tiled((block, d))),
            (kv, tiled((group, count, 2 * d))),
            (mask, tiled((group, count, length))),
            (w_out, whole((d, d))),
            (w_cq, whole((d, d))),
            (w_cout, whole((d, d))),
            (rows, whole(rows.shape)),
        ],
        [
            (spec_of((tokens, d), F32), tiled((block, d))),
            (spec_of((tokens, d), BF16), tiled((block, d))),
            (spec_of((tokens, d), BF16), tiled((block, d))),
            (spec_of((items, pairs, count, 2 * length), BF16), tiled((group, pairs, count, 2 * length))),
            (spec_of((tokens, d), BF16), tiled((block, d))),
            (spec_of((tokens, d), F32), tiled((block, d))),
        ],
        2 * tokens * d * 6 * d,
    )


def ffn_forward(dims, source, total_two, cotangent, rows, bias):
    d, items, length, group = dims.d, dims.items, dims.length, dims.group
    tokens, block, ff = items * length, group * length, bias.shape[1]
    piece = d
    n_in = len(source.ins)

    def body(tot_ref, cot_ref, row_ref, bias_ref, *refs):
        out_ref, h_ref, act_ref, slope_ref, g_ref, glow_ref, sum_ref = refs[n_in : n_in + 7]
        win_ref, wout_ref = source.open(refs[:n_in], refs[n_in + 7 :])

        @pl.when(pl.program_id(0) == 0)
        def _():
            sum_ref[...] = jnp.zeros_like(sum_ref)

        hat, _ = norm_parts(tot_ref[...])
        hidden = hat * row_ref[8:9, :] + row_ref[9:10, :]
        h_ref[...] = hidden.astype(BF16)
        total = hidden + row_ref[10:11, :]
        for at in range(0, ff, piece):
            cut = slice(at, at + piece)
            pre = dot(h_ref[...], win_ref[:, cut]) + bias_ref[:, cut]
            under, bell = gelu_parts(pre)
            act = (pre * under).astype(BF16)
            act_ref[:, cut] = act
            slope_ref[:, cut] = (under + (pre * 0.3989422804014327) * bell).astype(BF16)
            total = total + dot(act, wout_ref[cut, :])
        hat, spread = norm_parts(total)
        gain = row_ref[11:12, :]
        out_ref[...] = hat * gain + row_ref[12:13, :]
        cot = cot_ref[...].astype(F32)
        grad = norm_pull(cot, hat, spread, gain)
        g_ref[...] = grad
        low = grad.astype(BF16)
        glow_ref[...] = low
        sum_ref[0:1, :] += col_sum(cot * hat)
        sum_ref[1:2, :] += col_sum(cot)
        sum_ref[2:3, :] += col_sum(low)

    done = call(
        body,
        "ffn_forward",
        items // group,
        [
            (total_two, tiled((block, d))),
            (cotangent, tiled((block, d))),
            (rows, whole(rows.shape)),
            (bias, whole(bias.shape)),
        ]
        + source.ins,
        [
            (spec_of((tokens, d), F32), tiled((block, d))),
            (spec_of((tokens, d), BF16), tiled((block, d))),
            (spec_of((tokens, ff), BF16), tiled((block, ff))),
            (spec_of((tokens, ff), BF16), tiled((block, ff))),
            (spec_of((tokens, d), F32), tiled((block, d))),
            (spec_of((tokens, d), BF16), tiled((block, d))),
            (spec_of((8, d), F32), summed((8, d))),
        ]
        + source.outs,
        4 * tokens * d * ff,
    )
    return source.split(done)


def ffn_backward(dims, grad_three, grad_low, slope, total_two, w_fin, w_fout, rows):
    d, items, length, group = dims.d, dims.items, dims.length, dims.group
    tokens, block, ff = items * length, group * length, w_fin.shape[1]
    piece = d

    def body(g_ref, glow_ref, slope_ref, tot_ref, win_ref, wout_ref, row_ref,
             pre_ref, two_ref, twolow_ref, sum_ref, bias_ref):
        @pl.when(pl.program_id(0) == 0)
        def _():
            sum_ref[...] = jnp.zeros_like(sum_ref)
            bias_ref[...] = jnp.zeros_like(bias_ref)

        grad = g_ref[...]
        for at in range(0, ff, piece):
            cut = slice(at, at + piece)
            pre = dot_t(glow_ref[...], wout_ref[cut, :]) * slope_ref[:, cut].astype(F32)
            pre = pre.astype(BF16)
            pre_ref[:, cut] = pre
            bias_ref[0:1, cut] += col_sum(pre)
            grad = grad + dot_t(pre, win_ref[:, cut])
        hat, spread = norm_parts(tot_ref[...])
        two = norm_pull(grad, hat, spread, row_ref[8:9, :])
        two_ref[...] = two
        low = two.astype(BF16)
        twolow_ref[...] = low
        sum_ref[0:1, :] += col_sum(grad * hat)
        sum_ref[1:2, :] += col_sum(grad)
        sum_ref[2:3, :] += col_sum(low)

    return call(
        body,
        "ffn_backward",
        items // group,
        [
            (grad_three, tiled((block, d))),
            (grad_low, tiled((block, d))),
            (slope, tiled((block, ff))),
            (total_two, tiled((block, d))),
            (w_fin, whole((d, ff))),
            (w_fout, whole((ff, d))),
            (rows, whole(rows.shape)),
        ],
        [
            (spec_of((tokens, ff), BF16), tiled((block, ff))),
            (spec_of((tokens, d), F32), tiled((block, d))),
            (spec_of((tokens, d), BF16), tiled((block, d))),
            (spec_of((8, d), F32), summed((8, d))),
            (spec_of((8, ff), F32), summed((8, ff))),
        ],
        4 * tokens * d * ff,
    )


def pair_pull(q, k, v, out, probs, low, high):
    outs = spread_heads(out, low, high)
    score = soft_pull(probs.astype(F32), dot_t(v, outs)).astype(BF16)
    grad_k = dot(score, spread_heads(q, low, high))
    return dot(k.T, score), grad_k, dot(probs, outs)


def cross_attend_back(dims, grad_low, query, kv, probs, w_cout):
    d, items, length, group = dims.d, dims.items, dims.length, dims.group
    pairs, tokens, block = d // (2 * HEAD), items * length, group * length
    count = kv.shape[1]
    scale = HEAD ** (-0.5)

    def body(glow_ref, q_ref, kv_ref, prob_ref, wcout_ref, gq_ref, gkv_ref, sum_ref, ctx_ref):
        @pl.when(pl.program_id(0) == 0)
        def _():
            sum_ref[...] = jnp.zeros_like(sum_ref)

        low, high = lane_masks()
        ctx_ref[...] = dot_t(glow_ref[...], wcout_ref[...]).astype(BF16)
        for i in range(group):
            r = slice(i * length, (i + 1) * length)
            for p in range(pairs):
                c = slice(p * 128, (p + 1) * 128)
                cv = slice(d + p * 128, d + (p + 1) * 128)
                grad_q, grad_k, grad_v = pair_pull(
                    q_ref[r, c], kv_ref[i, :, c], kv_ref[i, :, cv], ctx_ref[r, c], prob_ref[i, p], low, high
                )
                gq_ref[r, c] = join_heads(grad_q * scale)
                gkv_ref[i, :, c] = (grad_k * scale).astype(BF16)
                gkv_ref[i, :, cv] = grad_v.astype(BF16)
        sum_ref[0:1, :] += col_sum(gq_ref[...])
        sum_ref[1:2, :] += col_sum(gkv_ref[:, :, d:].reshape(group * count, d))

    return call(
        body,
        "cross_attend_back",
        items // group,
        [
            (grad_low, tiled((block, d))),
            (query, tiled((block, d))),
            (kv, tiled((group, count, 2 * d))),
            (probs, tiled((group, pairs, count, 2 * length))),
            (w_cout, whole((d, d))),
        ],
        [
            (spec_of((tokens, d), BF16), tiled((block, d))),
            (spec_of((items, count, 2 * d), BF16), tiled((group, count, 2 * d))),
            (spec_of((8, d), F32), summed((8, d))),
        ],
        2 * tokens * d * 4 * d,
        [pltpu.VMEM((block, d), BF16)],
    )


def cross_project_back(dims, grad_two, grad_query, grad_kv, total_one, w_cq, w_ckv, rows, parts, part):
    d, items, length, group = dims.d, dims.items, dims.length, dims.group
    tokens, block = items * length, group * length
    count, vis = grad_kv.shape[1], w_ckv.shape[0]

    def body(g_ref, gq_ref, gkv_ref, tot_ref, wcq_ref, wckv_ref, row_ref, *refs):
        grid_refs, (cls_ref, one_ref, onelow_ref, sum_ref) = refs[:parts], refs[parts:]

        @pl.when(pl.program_id(0) == 0)
        def _():
            sum_ref[...] = jnp.zeros_like(sum_ref)

        for i in range(group):
            value = dot_t(gkv_ref[i], wckv_ref[...])
            for k in range(parts):
                grid_refs[k][i * part : (i + 1) * part, :] = value[k * part : (k + 1) * part, :].astype(BF16)
            cls_ref[i] = value[parts * part : parts * part + 1, :]
        grad = g_ref[...] + dot_t(gq_ref[...], wcq_ref[...])
        hat, spread = norm_parts(tot_ref[...])
        one = norm_pull(grad, hat, spread, row_ref[3:4, :])
        one_ref[...] = one
        one_low = one.astype(BF16)
        onelow_ref[...] = one_low
        sum_ref[0:1, :] += col_sum(grad * hat)
        sum_ref[1:2, :] += col_sum(grad)
        sum_ref[2:3, :] += col_sum(one_low)

    return call(
        body,
        "cross_project_back",
        items // group,
        [
            (grad_two, tiled((block, d))),
            (grad_query, tiled((block, d))),
            (grad_kv, tiled((group, count, 2 * d))),
            (total_one, tiled((block, d))),
            (w_cq, whole((d, d))),
            (w_ckv, whole((vis, 2 * d))),
            (rows, whole(rows.shape)),
        ],
        [(spec_of((items * part, vis), BF16), tiled((group * part, vis)))] * parts
        + [
            (spec_of((items, 1, vis), F32), tiled((group, 1, vis))),
            (spec_of((tokens, d), F32), tiled((block, d))),
            (spec_of((tokens, d), BF16), tiled((block, d))),
            (spec_of((8, d), F32), summed((8, d))),
        ],
        2 * tokens * d * d + 2 * items * count * vis * 2 * d,
    )


def self_attend_back(dims, grad_low, qkv, probs, w_out):
    d, items, length, group = dims.d, dims.items, dims.length, dims.group
    pairs, tokens, block = d // (2 * HEAD), items * length, group * length
    scale = HEAD ** (-0.5)

    def body(glow_ref, qkv_ref, prob_ref, wout_ref, gqkv_ref, sum_ref, ctx_ref):
        @pl.when(pl.program_id(0) == 0)
        def _():
            sum_ref[...] = jnp.zeros_like(sum_ref)

        low, high = lane_masks()
        ctx_ref[...] = dot_t(glow_ref[...], wout_ref[...]).astype(BF16)
        for i in range(group):
            r = slice(i * length, (i + 1) * length)
            for p in range(pairs):
                cuts = [slice(part * d + p * 128, part * d + (p + 1) * 128) for part in range(3)]
                q, k, v = (qkv_ref[r, cut] for cut in cuts)
                grad_q, grad_k, grad_v = pair_pull(q, k, v, ctx_ref[r, cuts[0]], prob_ref[i, p], low, high)
                gqkv_ref[r, cuts[0]] = join_heads(grad_q * scale)
                gqkv_ref[r, cuts[1]] = (grad_k * scale).astype(BF16)
                gqkv_ref[r, cuts[2]] = grad_v.astype(BF16)
        sum_ref[0:1, :] += col_sum(gqkv_ref[:, :d])
        sum_ref[1:2, :] += col_sum(gqkv_ref[:, 2 * d :])

    return call(
        body,
        "self_attend_back",
        items // group,
        [
            (grad_low, tiled((block, d))),
            (qkv, tiled((block, 3 * d))),
            (probs, tiled((group, pairs, length, 2 * length))),
            (w_out, whole((d, d))),
        ],
        [
            (spec_of((tokens, 3 * d), BF16), tiled((block, 3 * d))),
            (spec_of((8, d), F32), summed((8, d))),
        ],
        2 * tokens * d * 4 * d,
        [pltpu.VMEM((block, d), BF16)],
    )


def self_project_back(dims, grad_one, grad_qkv, w_qkv):
    d, items, length, group = dims.d, dims.items, dims.length, dims.group
    tokens, block = items * length, group * length

    def body(g_ref, gqkv_ref, wqkv_ref, text_ref):
        text_ref[...] = g_ref[...] + dot_t(gqkv_ref[...], wqkv_ref[...])

    return call(
        body,
        "self_project_back",
        items // group,
        [
            (grad_one, tiled((block, d))),
            (grad_qkv, tiled((block, 3 * d))),
            (w_qkv, whole((d, 3 * d))),
        ],
        [(spec_of((tokens, d), F32), tiled((block, d)))],
        2 * tokens * d * 3 * d,
    )[0]


def cut_grids(turn, image_grid, parts):
    micro, items, part, vis = image_grid.shape
    each = items // parts

    def body(turn_ref, grid_ref, *out_refs):
        def fill(own):
            value = jnp.swapaxes(grid_ref[0], 0, 1)
            for s in range(parts):
                mine = value[s * each : (s + 1) * each]
                out_refs[s ^ own][...] = mine.reshape(each * part, vis)

        for own in range(parts):
            pl.when(turn_ref[0] == own)(functools.partial(fill, own))

    return call(
        body,
        "cut_grids",
        micro,
        [
            (turn, SMEM_SPEC),
            (image_grid.transpose(0, 2, 1, 3), tiled((1, part, items, vis))),
        ],
        [(spec_of((micro * each * part, vis), BF16), tiled((each * part, vis)))] * parts,
        0,
    )


def place_grids(turn, micro, items, pieces):
    part, vis = pieces[0].shape[0] // items, pieces[0].shape[1]
    each, parts = items // micro, len(pieces)

    def body(turn_ref, *refs):
        def fill(own):
            value = [
                refs[s ^ own][...].astype(F32).reshape(each, part, vis) for s in range(parts)
            ]
            refs[-1][0] = jnp.swapaxes(jnp.concatenate(value, 0), 0, 1)

        for own in range(parts):
            pl.when(turn_ref[0] == own)(functools.partial(fill, own))

    shape = (micro, part, each * parts, vis)
    done = call(
        body,
        "place_grids",
        micro,
        [(turn, SMEM_SPEC)] + [(p, tiled((each * part, vis))) for p in pieces],
        [(spec_of(shape, F32), tiled((1,) + shape[1:]))],
        0,
    )[0]
    return done.transpose(0, 2, 1, 3)


def gather_sums(sums, bias):
    d, ff = sums[0].shape[1], bias.shape[1]
    high = -(-(ROWS + ff // d) // 8) * 8

    def body(self_ref, attend_ref, one_ref, two_ref, three_ref, bias_ref, out_ref):
        out_ref[...] = jnp.zeros_like(out_ref)
        at = 0
        for ref, row, count in (
            (self_ref, 0, 2),
            (one_ref, 2, 1),
            (one_ref, 0, 2),
            (attend_ref, 0, 2),
            (two_ref, 2, 1),
            (two_ref, 0, 2),
            (three_ref, 2, 1),
            (three_ref, 0, 2),
        ):
            out_ref[at : at + count, :] = ref[row : row + count, :]
            at += count
        for n in range(ff // d):
            out_ref[at + n : at + n + 1, :] = bias_ref[0:1, n * d : (n + 1) * d]

    return pl.pallas_call(
        body,
        out_shape=spec_of((high, d), F32),
        in_specs=[VMEM_SPEC] * 6,
        out_specs=VMEM_SPEC,
        compiler_params=PARAMS,
        name="gather_sums",
    )(*sums, bias)


def weight_grads(plan, group, where, factors):
    high_rows = max(plan.full[w][0] for w in group)
    wide = max(plan.full[w][1] for w in group)
    flat = [a for pair in factors for a in pair]
    count = len(flat)

    def body(where_ref, *refs):
        far, stack_refs = refs[:count], refs[count : count + 2]
        near, made, sems = refs[count + 2 : 2 * count + 2], refs[-2], refs[-1]
        copies = [pltpu.make_async_copy(far[n], near[n], sems.at[n]) for n in range(count)]
        for copy in copies:
            copy.start()
        for n, w in enumerate(group):
            left, right = near[2 * n], near[2 * n + 1]
            rows, cols = plan.full[w]
            copies[2 * n].wait()
            copies[2 * n + 1].wait()
            for at in range(0, rows, 256):
                value = dot_l(left[:, at : at + 256], right[...])
                made[at : at + 256, :cols] = value.astype(BF16)

            def visit(other, second, first, k, row, w_at, j, to_row, to_y, high):
                if w_at == w:
                    col = pl.multiple_of(to_y * (cols // 2) + j * plan.chunk, 128)
                    stack_refs[other][second * 2 + first, k, row : row + high, :] = made[
                        pl.ds(to_row, high), pl.ds(col, plan.chunk)
                    ]

            each_place(plan, group, where_ref, visit)

    shape = jax.ShapeDtypeStruct((4, plan.zs, plan.rows(group), plan.chunk), BF16)
    flops = sum(2 * a.shape[0] * a.shape[1] * b.shape[1] for a, b in factors)
    moved = sum(a.size * 2 for a in flat) + 2 * shape.size * 2
    return pl.pallas_call(
        body,
        out_shape=(shape,) * 2,
        in_specs=[SMEM_SPEC] + [pl.BlockSpec(memory_space=pl.ANY)] * count,
        out_specs=(VMEM_SPEC,) * 2,
        scratch_shapes=[pltpu.VMEM(a.shape, BF16) for a in flat]
        + [pltpu.VMEM((high_rows, wide), BF16), pltpu.SemaphoreType.DMA((count,))],
        compiler_params=PARAMS,
        cost_estimate=pl.CostEstimate(flops=flops, bytes_accessed=moved, transcendentals=0),
        name="weight_grads",
    )(where, *flat)


class Dims:
    def __init__(self, d, items, length):
        self.d, self.items, self.length = d, items, length
        self.group = 2 if items % 2 == 0 else 1


def cross_mask(lengths, counts, boxes, length, count):
    place = jnp.arange(length, dtype=jnp.int32)[None, :]
    boxed = (counts[:, None] > 0) & (place < lengths[:, None])
    phrase = jnp.where(boxed, place * counts[:, None] // lengths[:, None], 0)
    chosen = phrase[:, None, :] == jnp.arange(boxes.shape[1], dtype=jnp.int32)[None, :, None]
    inside = jnp.einsum(
        "ijp,ijt->ipt",
        (boxes > 0).astype(BF16),
        chosen.astype(BF16),
        preferred_element_type=F32,
    )
    grid_ok = jnp.where(boxed[:, None, :], inside, 1.0).astype(BF16)
    items, real = grid_ok.shape[:2]
    own = jnp.ones((items, 1, length), BF16)
    return jnp.concatenate([grid_ok, own, jnp.zeros((items, count - real - 1, length), BF16)], 1)


def trade(pieces):
    parts = lax.axis_size("patch")
    return [pieces[0]] + [
        lax.ppermute(pieces[k], "patch", [(i, i ^ k) for i in range(parts)])
        for k in range(1, len(pieces))
    ]


class Work:
    def __init__(self, args, parts):
        (self.text_in, self.image_grid, self.image_cls, lengths, counts, boxes, cot) = args
        self.parts = parts
        self.micro, d = self.text_in.shape[0], self.text_in.shape[2]
        self.items = lengths.size
        self.text, self.cot = self.text_in.reshape(-1, d), cot.reshape(-1, d)
        self.lengths, self.counts = lengths.reshape(-1), counts.reshape(-1)
        self.boxes = boxes.reshape((self.items,) + boxes.shape[2:])
        self.dims = Dims(d, self.items, self.text.shape[0] // self.items)
        self.turn = lax.axis_index("patch").astype(jnp.int32).reshape(1)
        self.part, self.vis = self.image_grid.shape[2:]
        self.each = self.items // self.micro
        self.count = -(-(parts * self.part + 1) // 16) * 16
        self.cls = self.image_cls.reshape(self.items, 1, self.vis)

    def mask(self):
        boxes = self.boxes.reshape(self.items, -1, self.parts, self.part)
        order = jnp.arange(self.parts, dtype=jnp.int32) ^ self.turn[0]
        boxes = jnp.take(boxes, order, axis=2).reshape(self.boxes.shape)
        return cross_mask(self.lengths, self.counts, boxes, self.dims.length, self.count)

    def finish(self, layer_out, text_grad, grid_grad, cls, grads, rows_grad, bias_grad):
        return (
            layer_out.reshape(self.text_in.shape),
            text_grad.reshape(self.text_in.shape),
            grid_grad,
            cls.reshape(self.image_cls.shape),
            *grads,
            rows_grad,
            bias_grad,
        )


def on_device(plan, *args):
    work, shards, vectors, ffn_bias = Work(args[:7], plan.patch), args[7:14], args[14], args[15]
    dims, where, parts = work.dims, coords(), plan.patch

    own, give = pack_split(plan, where, shards)
    units = pack_join(plan, where, own, send(give, plan.core()))
    grids = cut_grids(work.turn, work.image_grid, parts)
    gathers = [Gathering(plan, unit) for unit in units]

    def step(*groups):
        for g in groups:
            gathers[g].advance()

    def source(g):
        return Source(plan, GROUPS[g], where, gathers[g].held)

    vectors, ffn_bias, *grids = fence(gathers, [vectors, ffn_bias, *grids])
    step(0)
    grids[1:3] = trade(grids[:3])[1:]
    vectors, ffn_bias, grids[3] = fence(gathers[:1], [vectors, ffn_bias, grids[3]])
    step(0, 1)
    rows, bias = gather_small(plan, where, vectors, ffn_bias)
    rows = jnp.pad(rows, ((0, -rows.shape[0] % 8), (0, 0)))
    rows, bias = fence(gathers[:1], [rows, bias])
    step(0)
    fence(gathers[:2], [])
    step(0, 1)
    mask = work.mask()
    rows, mask = fence(gathers[:2], [rows, mask])
    step(1, 2)
    (qkv, probs, ctx), (w_qkv,) = self_forward(dims, source(0), work.text, rows, work.lengths)
    ctx, grids = fence(gathers[1:], [ctx, grids])
    step(1, 2)
    grids[3] = trade(grids)[3]
    (kv, patches), (w_out, w_cq, w_ckv, w_cout) = cross_keys(
        dims, source(1), grids, work.cls, rows, work.count
    )
    kv, ctx = fence(gathers[2:], [kv, ctx])
    step(2)
    total_one, hidden_one, query, cross_probs, cross_ctx, total_two = cross_forward(
        dims, work.text, ctx, kv, mask, w_out, w_cq, w_cout, rows
    )
    total_two = fence(gathers[2:], total_two)
    step(2)
    (layer_out, hidden_two, act, slope, grad_three, low_three, sum_three), (w_fin, w_fout) = ffn_forward(
        dims, source(2), total_two, work.cot, rows, bias[None]
    )

    reduces = {}

    def reduce(g, factors):
        stacks = weight_grads(plan, GROUPS[g], where, factors)
        reduces[g] = Reducing(plan, GROUPS[g], where, stacks)

    def hold(*values, on=None):
        chains = [reduces[g] for g in (reduces if on is None else on)]
        return fence(chains, list(values))

    def go(*groups):
        for g in groups:
            reduces[g].advance()

    grad_pre, grad_two, low_two, sum_two, sum_pre = ffn_backward(
        dims, grad_three, low_three, slope, total_two, w_fin, w_fout, rows
    )
    reduce(2, [(hidden_two, grad_pre), (act, low_three)])
    (low_two,) = hold(low_two)
    go(2)
    grad_query, grad_kv, sum_attend = cross_attend_back(dims, low_two, query, kv, cross_probs, w_cout)
    grad_query, grad_kv = hold(grad_query, grad_kv)
    go(2)
    *grids, cls, grad_one, low_one, sum_one = cross_project_back(
        dims, grad_two, grad_query, grad_kv, total_one, w_cq, w_ckv, rows, parts, work.part
    )
    reduce(
        1,
        [
            (ctx, low_one),
            (hidden_one, grad_query),
            (patches.reshape(-1, work.vis), grad_kv.reshape(-1, grad_kv.shape[2])),
            (cross_ctx, low_two),
        ],
    )
    low_one, *grids = hold(low_one, *grids)
    go(2, 1)
    grids[1] = trade(grids[:2])[1]
    grad_qkv, sum_self = self_attend_back(dims, low_one, qkv, probs, w_out)
    grad_qkv, sum_self = hold(grad_qkv, sum_self)
    go(2, 1)
    reduce(0, [(work.text, grad_qkv)])
    text_grad = self_project_back(dims, grad_one, grad_qkv, w_qkv)
    sums = [sum_self, sum_attend, sum_one, sum_two, sum_three]
    reduces["small"] = ReducingSmall(plan, where, sums, sum_pre)
    text_grad, *grids = hold(text_grad, *grids)
    go(2, 1, 0, "small")
    grids[2] = trade(grids[:3])[2]
    hold(on=[0, 1, 2, "small"])
    go(2, 1, 0, "small")
    hold(on=[0, 2, "small"])
    go(0, "small")
    grids[3] = trade(grids)[3]
    hold(on=[0, 1, "small"])
    go(1, 0, "small")
    grids = hold(*grids)
    grid_grad = place_grids(work.turn, work.micro, work.items, grids)
    go(1, 0, "small")
    go(0)
    grads = [None] * 7
    for g, group in enumerate(GROUPS):
        for w, value in zip(group, reduces[g].held):
            grads[w] = value
    return work.finish(layer_out, text_grad, grid_grad, cls, grads, *reduces["small"].result())


def on_device_plain(plan, *args):
    work, parts = Work(args[:7], plan.patch), plan.patch
    dims = work.dims
    weights, rows, bias = fetch_plain(args[7:14], args[14], args[15])
    rows = jnp.pad(rows, ((0, -rows.shape[0] % 8), (0, 0)))
    grids = trade(cut_grids(work.turn, work.image_grid, parts))

    def source(g):
        return Source(plan, GROUPS[g], None, [weights[w] for w in GROUPS[g]])

    (qkv, probs, ctx), _ = self_forward(dims, source(0), work.text, rows, work.lengths)
    (kv, patches), _ = cross_keys(dims, source(1), grids, work.cls, rows, work.count)
    total_one, hidden_one, query, cross_probs, cross_ctx, total_two = cross_forward(
        dims, work.text, ctx, kv, work.mask(), weights[OUT], weights[CQ], weights[COUT], rows
    )
    (layer_out, hidden_two, act, slope, grad_three, low_three, sum_three), _ = ffn_forward(
        dims, source(2), total_two, work.cot, rows, bias[None]
    )
    grad_pre, grad_two, low_two, sum_two, sum_pre = ffn_backward(
        dims, grad_three, low_three, slope, total_two, weights[FIN], weights[FOUT], rows
    )
    grad_query, grad_kv, sum_attend = cross_attend_back(
        dims, low_two, query, kv, cross_probs, weights[COUT]
    )
    *grids, cls, grad_one, low_one, sum_one = cross_project_back(
        dims, grad_two, grad_query, grad_kv, total_one, weights[CQ], weights[CKV], rows, parts, work.part
    )
    grad_qkv, sum_self = self_attend_back(dims, low_one, qkv, probs, weights[OUT])
    text_grad = self_project_back(dims, grad_one, grad_qkv, weights[QKV])
    flat_kv = grad_kv.reshape(-1, grad_kv.shape[2])
    factors = [
        (work.text, grad_qkv),
        (ctx, low_one),
        (hidden_one, grad_query),
        (patches.reshape(-1, work.vis), flat_kv),
        (cross_ctx, low_two),
        (hidden_two, grad_pre),
        (act, low_three),
    ]
    grads = [reduce_plain(dot_l(a, b).astype(BF16)) for a, b in factors]
    sums = gather_sums([sum_self, sum_attend, sum_one, sum_two, sum_three], sum_pre)
    small = reduce_small_plain(sums[:ROWS], sum_pre[0])
    grid_grad = place_grids(work.turn, work.micro, work.items, trade(grids))
    return work.finish(layer_out, text_grad, grid_grad, cls, grads, *small)


def solution(mesh):
    dp, patch = mesh.shape["dp"], mesh.shape["patch"]
    both = P(None, ("dp", "patch"), None)
    weight = P("dp", "patch")

    def run(*args):
        shards = [(w.shape[0] // dp, w.shape[1] // patch) for w in args[7:14]]
        plan = Plan(dp, patch, shards)
        return jax.shard_map(
            functools.partial(on_device if plan.fast else on_device_plain, plan),
            mesh=mesh,
            in_specs=(
                both,
                P(None, "dp", "patch", None),
                both,
                P(None, ("dp", "patch")),
                P(None, ("dp", "patch")),
                P(None, ("dp", "patch"), None, None),
                both,
            )
            + (weight,) * 7
            + (P(None, "dp"), P("dp")),
            out_specs=(both, both, P(None, "dp", "patch", None), both)
            + (weight,) * 7
            + (P(None, "dp"), P("dp")),
            check_vma=False,
        )(*args)

    return run
```

```python
import functools

import jax
import jax.numpy as jnp
from jax import lax
from jax.experimental import pallas as pl
from jax.experimental.pallas import tpu as pltpu
from jax.sharding import PartitionSpec as P

HEAD = 64
EPS = 1e-06
NEG = -1e30
BF16 = jnp.bfloat16
F32 = jnp.float32
AXES = ("dp", "patch")
VMEM_SPEC = pl.BlockSpec(memory_space=pltpu.VMEM)
SMEM_SPEC = pl.BlockSpec(memory_space=pltpu.SMEM)
PARAMS = pltpu.CompilerParams(vmem_limit_bytes=62 * 2**20)

QKV, OUT, CQ, CKV, COUT, FIN, FOUT = range(7)
ROWS = 13
GROUPS = ((QKV,), (OUT, CQ, CKV, COUT), (FIN, FOUT))


class Plan:
    def __init__(self, dp, patch, shards):
        self.dp, self.patch = dp, patch
        self.zs = dp // 2
        self.devices = dp * patch
        self.chunk = shards[OUT][1] * 2
        self.half = [s[0] // 2 for s in shards]
        self.cols = [s[1] for s in shards]
        self.chunks = [s[1] * 2 // self.chunk for s in shards]
        self.full = [(s[0] * dp, s[1] * patch) for s in shards]
        self.fast = (
            dp % 2 == 0
            and self.zs & (self.zs - 1) == 0
            and patch == 4
            and all(h % 16 == 0 for h in self.half)
            and all(s[1] * 2 % self.chunk == 0 for s in shards)
            and self.chunk % 128 == 0
        )

    def rows(self, group):
        return sum(self.half[w] * self.chunks[w] for w in group)

    def flip(self, pick):
        return [(i, i ^ pick(i)) for i in range(self.devices)]

    def core(self):
        return self.flip(lambda i: 1)

    def first(self):
        return self.flip(lambda i: 4 if i % 2 == 0 else 2)

    def second(self):
        return self.flip(lambda i: 2 if i % 2 == 0 else 4)

    def along_z(self, k):
        return self.flip(lambda i: 8 * k)


def send(value, perm):
    return lax.ppermute(value, AXES, perm)


def coords():
    dp, patch = lax.axis_index("dp"), lax.axis_index("patch")
    return jnp.stack([dp // 2, dp % 2, patch // 2, patch % 2]).astype(jnp.int32)


def piece_rows(group, plan):
    at, found = 0, []
    for w in group:
        for j in range(plan.chunks[w]):
            found.append((w, j, at))
            at += plan.half[w]
    return found


def group_starts(plan):
    starts, at = [], 0
    for group in GROUPS:
        starts.append(at)
        at += plan.rows(group)
    return starts, at


def pack_split(plan, where, shards):
    _, total = group_starts(plan)
    wide = plan.chunk // 2

    def body(where_ref, *refs):
        shard_refs, (own_ref, send_ref, turned) = list(refs[:7]), refs[7:]
        core = where_ref[3]
        turned[...] = shard_refs[FOUT][...].T
        shard_refs[FOUT] = turned
        at = 0
        for group in GROUPS:
            for w in group:
                high = plan.half[w]
                for b in range(plan.chunks[w]):
                    cut = slice(b * wide, (b + 1) * wide)
                    own_ref[at : at + high, :] = shard_refs[w][pl.ds(core * high, high), cut]
                    send_ref[at : at + high, :] = shard_refs[w][
                        pl.ds((1 - core) * high, high), cut
                    ]
                    at += high

    shape = jax.ShapeDtypeStruct((total, wide), BF16)
    return pl.pallas_call(
        body,
        out_shape=(shape, shape),
        in_specs=[SMEM_SPEC] + [VMEM_SPEC] * 7,
        out_specs=(VMEM_SPEC, VMEM_SPEC),
        scratch_shapes=[pltpu.VMEM(shards[FOUT].shape, BF16)],
        compiler_params=PARAMS,
        name="pack_split",
    )(where, *shards[:FOUT], shards[FOUT].T)


def pack_join(plan, where, own, got):
    starts, total = group_starts(plan)
    wide = plan.chunk // 2

    def body(where_ref, own_ref, got_ref, *unit_refs):
        core = where_ref[3]

        def fill(low_ref, high_ref):
            for g, group in enumerate(GROUPS):
                at = starts[g]
                for w in group:
                    high, count = plan.half[w], plan.chunks[w]
                    for j in range(count):
                        pair = []
                        for b in (2 * j, 2 * j + 1):
                            src = low_ref if b < count else high_ref
                            row = at + (b % count) * high
                            pair.append(src[row : row + high, :])
                        to = at - starts[g] + j * high
                        unit_refs[g][to : to + high, :] = jnp.concatenate(pair, axis=1)
                    at += count * high

        @pl.when(core == 0)
        def _():
            fill(own_ref, got_ref)

        @pl.when(core == 1)
        def _():
            fill(got_ref, own_ref)

    return pl.pallas_call(
        body,
        out_shape=tuple(jax.ShapeDtypeStruct((plan.rows(g), plan.chunk), BF16) for g in GROUPS),
        in_specs=[SMEM_SPEC, VMEM_SPEC, VMEM_SPEC],
        out_specs=(VMEM_SPEC,) * len(GROUPS),
        compiler_params=PARAMS,
        name="pack_join",
    )(where, own, got)


class Gathering:
    def __init__(self, plan, unit):
        self.plan, self.held = plan, [unit]

    def along_z(self, *steps):
        self.held += [send(self.held[0], self.plan.along_z(k)) for k in steps]

    def first(self):
        stack = jnp.stack(self.held)
        self.held = [stack, send(stack, self.plan.first())]

    def second(self):
        near = jnp.stack(self.held)
        self.held = [near, send(near, self.plan.second()), send(near, self.plan.core())]

    def core(self):
        self.held.append(send(self.held[1], self.plan.core()))


def each_place(plan, group, where_ref, visit):
    z, x, y, core = (where_ref[i] for i in range(4))
    for other in range(2):
        half = core ^ other
        for second in range(2):
            for first in range(2):
                x_at = x ^ jnp.where(half == 0, first, second)
                y_at = y ^ jnp.where(half == 0, second, first)
                for k in range(plan.zs):
                    place = ((z ^ k) * 2 + x_at) * 2 + half
                    for w, j, row in piece_rows(group, plan):
                        high = plan.half[w]
                        to_row = pl.multiple_of(place * high, 16)
                        visit(other, second, first, k, row, w, j, to_row, y_at, high)


def add_low(ones, twos, widths):
    count, slots, rows, chunk = ones.shape

    def body(one_ref, two_ref, *out_refs):
        at = 0
        for width, out in zip(widths, out_refs):
            for n in range(width):
                out[n] = (one_ref[at].astype(F32) + two_ref[at].astype(F32)).astype(BF16)
                at += 1

    cuts = 2 if rows % 32 == 0 else 1

    def spec(n):
        return pl.BlockSpec((n, 1, rows // cuts, chunk), lambda i: (0, i // cuts, i % cuts, 0))

    return pl.pallas_call(
        body,
        grid=(slots * cuts,),
        out_shape=tuple(jax.ShapeDtypeStruct((n, slots, rows, chunk), BF16) for n in widths),
        in_specs=[spec(count), spec(count)],
        out_specs=tuple(spec(n) for n in widths),
        compiler_params=PARAMS,
        cost_estimate=pl.CostEstimate(
            flops=ones.size, bytes_accessed=6 * ones.size, transcendentals=0
        ),
        name="add_low",
    )(ones, twos)


def add_slots(ones, twos):
    _, slots, rows, chunk = ones.shape

    def body(one_ref, two_ref, *out_refs):
        for n in range(slots):
            out_refs[n][...] = (one_ref[0, n].astype(F32) + two_ref[0, n].astype(F32)).astype(BF16)

    return pl.pallas_call(
        body,
        out_shape=(jax.ShapeDtypeStruct((rows, chunk), BF16),) * slots,
        in_specs=[VMEM_SPEC, VMEM_SPEC],
        out_specs=(VMEM_SPEC,) * slots,
        compiler_params=PARAMS,
        cost_estimate=pl.CostEstimate(
            flops=ones.size, bytes_accessed=6 * ones.size, transcendentals=0
        ),
        name="add_slots",
    )(ones, twos)


class Reducing:
    def __init__(self, plan, group, where, stacks):
        self.plan, self.group, self.where = plan, group, where
        self.held, self.step = list(stacks), 0

    def advance(self):
        plan, held = self.plan, self.held
        if self.step == 0:
            held = [held[0], send(held[1], plan.core())]
        elif self.step == 1:
            keep, give = add_low(*held, (2, 2))
            held = [keep, send(give, plan.second())]
        elif self.step == 2:
            keep, give = add_low(*held, (1, 1))
            held = [keep, send(give, plan.first())]
        elif self.step == 3:
            slots = add_slots(*held)
            near = plan.zs // 2 + 1
            held = [slots[0]] + [send(slots[k], plan.along_z(k)) for k in range(1, near)]
            held += slots[near:]
        elif self.step == 4:
            near = plan.zs // 2 + 1
            held = held[:near] + [send(held[k], plan.along_z(k)) for k in range(near, plan.zs)]
        elif self.step == 5:
            own, give = unpack_split(plan, self.group, self.where, held)
            held = [own, send(give, plan.core())]
        elif self.step == 6:
            held = unpack_join(plan, self.group, self.where, *held)
        self.held, self.step = list(held), self.step + 1


def fence(chains, values):
    flat, tree = jax.tree.flatten([values, [chain.held for chain in chains]])
    values, held = jax.tree.unflatten(tree, lax.optimization_barrier(flat))
    for chain, arrays in zip(chains, held):
        chain.held = arrays
    return values


def unpack_split(plan, group, where, parts):
    rows, wide = plan.rows(group), plan.chunk // 2

    def body(where_ref, *refs):
        part_refs, (own_ref, give_ref) = refs[:-2], refs[-2:]
        core = where_ref[3]

        def fill(low_ref, high_ref):
            at = 0
            for w in group:
                high, count = plan.half[w], plan.chunks[w]
                for j in range(count):
                    row = at + j * high
                    value = sum(p[row : row + high, :].astype(F32) for p in part_refs)
                    for b in (2 * j, 2 * j + 1):
                        dst = low_ref if b < count else high_ref
                        to = at + (b % count) * high
                        cut = (b - 2 * j) * wide
                        dst[to : to + high, :] = value[:, cut : cut + wide]
                at += count * high

        @pl.when(core == 0)
        def _():
            fill(own_ref, give_ref)

        @pl.when(core == 1)
        def _():
            fill(give_ref, own_ref)

    shape = jax.ShapeDtypeStruct((rows, wide), F32)
    return pl.pallas_call(
        body,
        out_shape=(shape, shape),
        in_specs=[SMEM_SPEC] + [VMEM_SPEC] * len(parts),
        out_specs=(VMEM_SPEC, VMEM_SPEC),
        compiler_params=PARAMS,
        name="unpack_split",
    )(where, *parts)


def unpack_join(plan, group, where, own, got):
    wide = plan.chunk // 2
    turned = [w == FOUT for w in group]

    def body(where_ref, own_ref, got_ref, *refs):
        core = where_ref[3]
        at = 0
        for n, w in enumerate(group):
            out_ref = refs[-1] if turned[n] else refs[n]
            high, count = plan.half[w], plan.chunks[w]
            own_rows = pl.ds(pl.multiple_of(core * high, 16), high)
            got_rows = pl.ds(pl.multiple_of((1 - core) * high, 16), high)
            for b in range(count):
                row, cut = at + b * high, slice(b * wide, (b + 1) * wide)
                out_ref[own_rows, cut] = own_ref[row : row + high, :]
                out_ref[got_rows, cut] = got_ref[row : row + high, :]
            at += count * high
            if turned[n]:
                refs[n][...] = out_ref[...].T

    shapes = [(2 * plan.half[w], plan.cols[w]) for w in group]
    done = pl.pallas_call(
        body,
        out_shape=tuple(
            jax.ShapeDtypeStruct(shape[::-1] if turn else shape, F32)
            for shape, turn in zip(shapes, turned)
        ),
        in_specs=[SMEM_SPEC, VMEM_SPEC, VMEM_SPEC],
        out_specs=(VMEM_SPEC,) * len(group),
        scratch_shapes=[pltpu.VMEM(shapes[-1], F32)],
        compiler_params=PARAMS,
        name="unpack_join",
    )(where, own, got)
    return [value.T if turn else value for value, turn in zip(done, turned)]


class GatheringSmall:
    def __init__(self, plan, where, vectors, bias):
        self.plan, self.where, self.shape = plan, where, vectors.shape
        flat = jnp.concatenate([vectors.reshape(-1), bias])
        self.size = flat.shape[0]
        self.held, self.bit = [jnp.pad(flat, (0, -self.size % 2048)).reshape(1, -1, 128)], 4

    def advance(self):
        every = jnp.concatenate(self.held)
        self.held = [every, send(every, self.plan.flip(lambda i: self.bit))]
        self.bit *= 2

    def result(self):
        plan, (count, part) = self.plan, self.shape
        while self.bit < plan.devices:
            self.advance()
        every = jnp.concatenate(self.held).reshape(plan.dp, -1)
        slot = jnp.arange(plan.dp, dtype=jnp.int32) ^ (self.where[0] * 2 + self.where[1])
        every = jnp.take(every, slot, axis=0)[:, : self.size].astype(F32)
        rows = every[:, : count * part].reshape(plan.dp, count, part)
        rows = rows.transpose(1, 0, 2).reshape(count, plan.dp * part)
        bias = every[:, count * part :].reshape(1, -1)
        return jnp.pad(rows, ((0, -count % 8), (0, 0))), bias


class ReducingSmall:
    def __init__(self, plan, where, sums, bias):
        self.plan, self.where, self.tail = plan, where, bias.shape[1]
        self.held, self.step = [gather_sums(sums, bias)], 0
        bits = [1, 2, 4]
        while 1 << len(bits) < plan.devices:
            bits.append(1 << len(bits))
        self.bits = bits

    def advance(self):
        flat = sum(self.held)
        if self.bits:
            bit = self.bits.pop(0)
            self.held = [flat, send(flat, self.plan.flip(lambda i: bit))]
        else:
            self.held = [flat]

    def result(self):
        plan, flat = self.plan, sum(self.held)
        width = flat.shape[1] // plan.dp
        dp = self.where[0] * 2 + self.where[1]
        own = lax.dynamic_slice_in_dim(flat[:ROWS], dp * width, width, axis=1)
        tail, step = flat[ROWS : ROWS + self.tail // flat.shape[1]].reshape(-1), self.tail // plan.dp
        return own, lax.dynamic_slice_in_dim(tail, dp * step, step, axis=0)


def fetch_plain(weights, vectors, bias):
    whole = [
        lax.all_gather(lax.all_gather(w, "dp", axis=0, tiled=True), "patch", axis=1, tiled=True)
        for w in weights
    ]
    rows = lax.all_gather(vectors, "dp", axis=1, tiled=True)
    return whole, rows.astype(F32), lax.all_gather(bias, "dp", axis=0, tiled=True).astype(F32)


def reduce_plain(grad):
    part = lax.psum_scatter(grad, "dp", scatter_dimension=0, tiled=True)
    return lax.psum_scatter(part, "patch", scatter_dimension=1, tiled=True).astype(F32)


def reduce_small_plain(rows, bias):
    rows = lax.psum_scatter(rows, "dp", scatter_dimension=1, tiled=True)
    bias = lax.psum_scatter(bias, "dp", scatter_dimension=0, tiled=True)
    return lax.psum(rows, "patch"), lax.psum(bias, "patch")


TAIL = (0.112528827, 0.117839666, 0.0706314405, 0.2046457425, -0.190499398, 0.3478185715, -0.201092832, 0.03812798145)


def dot(a, b):
    return lax.dot_general(a, b, (((1,), (0,)), ((), ())), preferred_element_type=F32)


def dot_t(a, b):
    return lax.dot_general(a, b, (((1,), (1,)), ((), ())), preferred_element_type=F32)


def dot_l(a, b):
    return lax.dot_general(a, b, (((0,), (0,)), ((), ())), preferred_element_type=F32)


def norm_parts(total):
    center = total - jnp.mean(total, -1, keepdims=True)
    spread = lax.rsqrt(jnp.mean(center * center, -1, keepdims=True) + EPS)
    return center * spread, spread


def norm_pull(grad, hat, spread, gain):
    scaled = grad * gain
    return spread * (
        scaled
        - jnp.mean(scaled, -1, keepdims=True)
        - hat * jnp.mean(scaled * hat, -1, keepdims=True)
    )


def gelu_parts(x):
    bell = jnp.exp(-0.5 * (x * x))
    t = 1.0 / (1.0 + (0.4 * 0.5**0.5) * jnp.abs(x))
    tail = jnp.full_like(t, TAIL[-1])
    for c in TAIL[-2::-1]:
        tail = tail * t + c
    tail = tail * (t * bell)
    return jnp.where(x < 0.0, tail, 1.0 - tail), bell


def col_sum(value):
    return jnp.sum(value.astype(F32), 0, keepdims=True)


def soft(scores):
    grown = jnp.exp(scores - jnp.max(scores, 0, keepdims=True))
    return grown * (1.0 / jnp.sum(grown, 0, keepdims=True))


def soft_pull(probs, grad):
    return probs * (grad - jnp.sum(probs * grad, 0, keepdims=True))


def spread_heads(value, low, high):
    return jnp.concatenate([value * low, value * high], 0)


def join_heads(value):
    count = value.shape[1] // 2
    value = jnp.concatenate([value[:HEAD, :count], value[HEAD:, count:]], 0)
    return value.astype(BF16).T


def lane_masks():
    lane = lax.broadcasted_iota(jnp.int32, (1, 2 * HEAD), 1)
    low = (lane < HEAD).astype(F32)
    return low.astype(BF16), (1.0 - low).astype(BF16)


def whole(shape):
    return pl.BlockSpec(
        shape, lambda i: (0,) * len(shape), pipeline_mode=pl.Buffered(1)
    )


def summed(shape):
    return pl.BlockSpec(shape, lambda i: (0,) * len(shape))


def tiled(shape):
    return pl.BlockSpec(shape, lambda i: (i,) + (0,) * (len(shape) - 1))


def spec_of(shape, dtype):
    return jax.ShapeDtypeStruct(shape, dtype)


def call(body, name, steps, ins, outs, flops, scratch=()):
    out_shape = tuple(shape for shape, _ in outs)
    moved = sum(a.size * a.dtype.itemsize for a, _ in ins)
    moved += sum(o.size * jnp.dtype(o.dtype).itemsize for o in out_shape)
    return pl.pallas_call(
        body,
        grid=(steps,),
        out_shape=out_shape,
        in_specs=[spec for _, spec in ins],
        out_specs=tuple(spec for _, spec in outs),
        scratch_shapes=list(scratch),
        compiler_params=PARAMS,
        cost_estimate=pl.CostEstimate(
            flops=int(flops), bytes_accessed=int(moved), transcendentals=0
        ),
        name=name,
    )(*[a for a, _ in ins])


class Source:
    def __init__(self, plan, group, where, given):
        self.plan, self.group, self.pieces = plan, group, plan.fast
        if self.pieces:
            self.ins = [(where, SMEM_SPEC)] + [(part, whole(part.shape)) for part in given]
            self.outs = [(spec_of(plan.full[w], BF16), summed(plan.full[w])) for w in group]
        else:
            self.ins = [(w, whole(w.shape)) for w in given]
            self.outs = []
        self.given = given

    def open(self, in_refs, out_refs):
        if not self.pieces:
            return list(in_refs)
        where_ref, parts = in_refs[0], in_refs[1:]
        full = dict(zip(self.group, out_refs))
        plan = self.plan

        def visit(other, second, first, k, row, w, j, to_row, to_y, high):
            to_col = pl.multiple_of(to_y * (plan.full[w][1] // 2) + j * plan.chunk, 128)
            part = parts[other * 2 + second]
            full[w][pl.ds(to_row, high), pl.ds(to_col, plan.chunk)] = part[
                first, k, row : row + high, :
            ]

        @pl.when(pl.program_id(0) == 0)
        def _():
            each_place(plan, self.group, where_ref, visit)

        return list(out_refs)

    def split(self, done):
        if not self.pieces:
            return done, self.given
        return done[: -len(self.group)], done[-len(self.group) :]


def self_forward(dims, source, text, rows, lengths):
    d, items, length, group = dims.d, dims.items, dims.length, dims.group
    pairs, tokens, block = d // (2 * HEAD), items * length, group * length
    scale = HEAD ** (-0.5)

    n_in = len(source.ins)

    def body(len_ref, x_ref, row_ref, *refs):
        qkv_ref, prob_ref, ctx_ref = refs[n_in : n_in + 3]
        (wqkv_ref,) = source.open(refs[:n_in], refs[n_in + 3 :])
        step = pl.program_id(0)
        low, high = lane_masks()
        x = x_ref[...]
        for part, bias in ((0, 0), (1, None), (2, 1)):
            cut = slice(part * d, (part + 1) * d)
            value = dot(x, wqkv_ref[:, cut])
            if bias is not None:
                value = value + row_ref[bias : bias + 1, :]
            qkv_ref[:, cut] = value.astype(BF16)
        place = lax.broadcasted_iota(jnp.int32, (length, 1), 0)
        for i in range(group):
            ok = place < len_ref[step * group + i]
            r = slice(i * length, (i + 1) * length)
            for p in range(pairs):
                q, k, v = (
                    qkv_ref[r, part * d + p * 128 : part * d + (p + 1) * 128] for part in range(3)
                )
                scores = dot_t(k, spread_heads(q, low, high)) * scale
                probs = soft(jnp.where(ok, scores, NEG)).astype(BF16)
                prob_ref[i, p] = probs
                ctx_ref[r, p * 128 : (p + 1) * 128] = join_heads(dot(v.T, probs))
    done = call(
        body,
        "self_forward",
        items // group,
        [(lengths, SMEM_SPEC), (text, tiled((block, d))), (rows, whole(rows.shape))] + source.ins,
        [
            (spec_of((tokens, 3 * d), BF16), tiled((block, 3 * d))),
            (spec_of((items, pairs, length, 2 * length), BF16), tiled((group, pairs, length, 2 * length))),
            (spec_of((tokens, d), BF16), tiled((block, d))),
        ]
        + source.outs,
        2 * tokens * d * 5 * d,
    )
    return source.split(done)


def cross_keys(dims, source, grids, cls, rows, count):
    d, items, group = dims.d, dims.items, dims.group
    part, vis, parts = grids[0].shape[0] // items, cls.shape[2], len(grids)
    n_in = len(source.ins)

    def body(*refs):
        grid_refs, cls_ref, row_ref = refs[:parts], refs[parts], refs[parts + 1]
        refs = refs[parts + 2 :]
        kv_ref, patch_ref = refs[n_in : n_in + 2]
        _, _, wckv_ref, _ = source.open(refs[:n_in], refs[n_in + 2 :])
        for i in range(group):
            for k in range(parts):
                patch_ref[i, k * part : (k + 1) * part, :] = grid_refs[k][i * part : (i + 1) * part, :]
            rest = jnp.zeros((count - parts * part - 1, vis), BF16)
            patch_ref[i, parts * part :, :] = jnp.concatenate([cls_ref[i], rest], 0)
        patch = patch_ref[...].reshape(group * count, vis)
        keys = dot(patch, wckv_ref[:, :d]).astype(BF16)
        kv_ref[:, :, :d] = keys.reshape(group, count, d)
        values = (dot(patch, wckv_ref[:, d:]) + row_ref[6:7, :]).astype(BF16)
        kv_ref[:, :, d:] = values.reshape(group, count, d)

    done = call(
        body,
        "cross_keys",
        items // group,
        [(grid, tiled((group * part, vis))) for grid in grids]
        + [(cls, tiled((group, 1, vis))), (rows, whole(rows.shape))]
        + source.ins,
        [
            (spec_of((items, count, 2 * d), BF16), tiled((group, count, 2 * d))),
            (spec_of((items, count, vis), BF16), tiled((group, count, vis))),
        ]
        + source.outs,
        2 * items * count * vis * 2 * d,
    )
    return source.split(done)


def cross_forward(dims, text, self_ctx, kv, mask, w_out, w_cq, w_cout, rows):
    d, items, length, group = dims.d, dims.items, dims.length, dims.group
    pairs, tokens, block = d // (2 * HEAD), items * length, group * length
    count = kv.shape[1]
    scale = HEAD ** (-0.5)

    def body(x_ref, self_ref, kv_ref, mask_ref, wout_ref, wcq_ref, wcout_ref, row_ref,
             one_ref, h_ref, cq_ref, prob_ref, ctx_ref, two_ref):
        low, high = lane_masks()
        total = x_ref[...].astype(F32) + dot(self_ref[...], wout_ref[...]) + row_ref[2:3, :]
        one_ref[...] = total
        hat, _ = norm_parts(total)
        hidden = hat * row_ref[3:4, :] + row_ref[4:5, :]
        h_ref[...] = hidden.astype(BF16)
        cq_ref[...] = (dot(h_ref[...], wcq_ref[...]) + row_ref[5:6, :]).astype(BF16)
        for i in range(group):
            ok = mask_ref[i].astype(F32) > 0.5
            ok = jnp.concatenate([ok, ok], 1)
            r = slice(i * length, (i + 1) * length)
            for p in range(pairs):
                c = slice(p * 128, (p + 1) * 128)
                q, k, v = cq_ref[r, c], kv_ref[i, :, c], kv_ref[i, :, d + p * 128 : d + (p + 1) * 128]
                scores = dot_t(k, spread_heads(q, low, high)) * scale
                probs = soft(jnp.where(ok, scores, NEG)).astype(BF16)
                prob_ref[i, p] = probs
                ctx_ref[r, c] = join_heads(dot(v.T, probs))
        two_ref[...] = hidden + dot(ctx_ref[...], wcout_ref[...]) + row_ref[7:8, :]

    return call(
        body,
        "cross_forward",
        items // group,
        [
            (text, tiled((block, d))),
            (self_ctx, tiled((block, d))),
            (kv, tiled((group, count, 2 * d))),
            (mask, tiled((group, count, length))),
            (w_out, whole((d, d))),
            (w_cq, whole((d, d))),
            (w_cout, whole((d, d))),
            (rows, whole(rows.shape)),
        ],
        [
            (spec_of((tokens, d), F32), tiled((block, d))),
            (spec_of((tokens, d), BF16), tiled((block, d))),
            (spec_of((tokens, d), BF16), tiled((block, d))),
            (spec_of((items, pairs, count, 2 * length), BF16), tiled((group, pairs, count, 2 * length))),
            (spec_of((tokens, d), BF16), tiled((block, d))),
            (spec_of((tokens, d), F32), tiled((block, d))),
        ],
        2 * tokens * d * 6 * d,
    )


def ffn_forward(dims, source, total_two, cotangent, rows, bias):
    d, items, length, group = dims.d, dims.items, dims.length, dims.group
    tokens, block, ff = items * length, group * length, bias.shape[1]
    piece = d
    n_in = len(source.ins)

    def body(tot_ref, cot_ref, row_ref, bias_ref, *refs):
        out_ref, h_ref, act_ref, slope_ref, g_ref, glow_ref, sum_ref = refs[n_in : n_in + 7]
        win_ref, wout_ref = source.open(refs[:n_in], refs[n_in + 7 :])

        @pl.when(pl.program_id(0) == 0)
        def _():
            sum_ref[...] = jnp.zeros_like(sum_ref)

        hat, _ = norm_parts(tot_ref[...])
        hidden = hat * row_ref[8:9, :] + row_ref[9:10, :]
        h_ref[...] = hidden.astype(BF16)
        total = hidden + row_ref[10:11, :]
        for at in range(0, ff, piece):
            cut = slice(at, at + piece)
            pre = dot(h_ref[...], win_ref[:, cut]) + bias_ref[:, cut]
            under, bell = gelu_parts(pre)
            act = (pre * under).astype(BF16)
            act_ref[:, cut] = act
            slope_ref[:, cut] = (under + (pre * 0.3989422804014327) * bell).astype(BF16)
            total = total + dot(act, wout_ref[cut, :])
        hat, spread = norm_parts(total)
        gain = row_ref[11:12, :]
        out_ref[...] = hat * gain + row_ref[12:13, :]
        cot = cot_ref[...].astype(F32)
        grad = norm_pull(cot, hat, spread, gain)
        g_ref[...] = grad
        low = grad.astype(BF16)
        glow_ref[...] = low
        sum_ref[0:1, :] += col_sum(cot * hat)
        sum_ref[1:2, :] += col_sum(cot)
        sum_ref[2:3, :] += col_sum(low)

    done = call(
        body,
        "ffn_forward",
        items // group,
        [
            (total_two, tiled((block, d))),
            (cotangent, tiled((block, d))),
            (rows, whole(rows.shape)),
            (bias, whole(bias.shape)),
        ]
        + source.ins,
        [
            (spec_of((tokens, d), F32), tiled((block, d))),
            (spec_of((tokens, d), BF16), tiled((block, d))),
            (spec_of((tokens, ff), BF16), tiled((block, ff))),
            (spec_of((tokens, ff), BF16), tiled((block, ff))),
            (spec_of((tokens, d), F32), tiled((block, d))),
            (spec_of((tokens, d), BF16), tiled((block, d))),
            (spec_of((8, d), F32), summed((8, d))),
        ]
        + source.outs,
        4 * tokens * d * ff,
    )
    return source.split(done)


def ffn_backward(dims, grad_three, grad_low, slope, total_two, w_fin, w_fout, rows):
    d, items, length, group = dims.d, dims.items, dims.length, dims.group
    tokens, block, ff = items * length, group * length, w_fin.shape[1]
    piece = d

    def body(g_ref, glow_ref, slope_ref, tot_ref, win_ref, wout_ref, row_ref,
             pre_ref, two_ref, twolow_ref, sum_ref, bias_ref):
        @pl.when(pl.program_id(0) == 0)
        def _():
            sum_ref[...] = jnp.zeros_like(sum_ref)
            bias_ref[...] = jnp.zeros_like(bias_ref)

        grad = g_ref[...]
        for at in range(0, ff, piece):
            cut = slice(at, at + piece)
            pre = dot_t(glow_ref[...], wout_ref[cut, :]) * slope_ref[:, cut].astype(F32)
            pre = pre.astype(BF16)
            pre_ref[:, cut] = pre
            bias_ref[0:1, cut] += col_sum(pre)
            grad = grad + dot_t(pre, win_ref[:, cut])
        hat, spread = norm_parts(tot_ref[...])
        two = norm_pull(grad, hat, spread, row_ref[8:9, :])
        two_ref[...] = two
        low = two.astype(BF16)
        twolow_ref[...] = low
        sum_ref[0:1, :] += col_sum(grad * hat)
        sum_ref[1:2, :] += col_sum(grad)
        sum_ref[2:3, :] += col_sum(low)

    return call(
        body,
        "ffn_backward",
        items // group,
        [
            (grad_three, tiled((block, d))),
            (grad_low, tiled((block, d))),
            (slope, tiled((block, ff))),
            (total_two, tiled((block, d))),
            (w_fin, whole((d, ff))),
            (w_fout, whole((ff, d))),
            (rows, whole(rows.shape)),
        ],
        [
            (spec_of((tokens, ff), BF16), tiled((block, ff))),
            (spec_of((tokens, d), F32), tiled((block, d))),
            (spec_of((tokens, d), BF16), tiled((block, d))),
            (spec_of((8, d), F32), summed((8, d))),
            (spec_of((8, ff), F32), summed((8, ff))),
        ],
        4 * tokens * d * ff,
    )


def pair_pull(q, k, v, out, probs, low, high):
    outs = spread_heads(out, low, high)
    score = soft_pull(probs.astype(F32), dot_t(v, outs)).astype(BF16)
    grad_k = dot(score, spread_heads(q, low, high))
    return dot(k.T, score), grad_k, dot(probs, outs)


def cross_attend_back(dims, grad_low, query, kv, probs, w_cout):
    d, items, length, group = dims.d, dims.items, dims.length, dims.group
    pairs, tokens, block = d // (2 * HEAD), items * length, group * length
    count = kv.shape[1]
    scale = HEAD ** (-0.5)

    def body(glow_ref, q_ref, kv_ref, prob_ref, wcout_ref, gq_ref, gkv_ref, sum_ref, ctx_ref):
        @pl.when(pl.program_id(0) == 0)
        def _():
            sum_ref[...] = jnp.zeros_like(sum_ref)

        low, high = lane_masks()
        ctx_ref[...] = dot_t(glow_ref[...], wcout_ref[...]).astype(BF16)
        for i in range(group):
            r = slice(i * length, (i + 1) * length)
            for p in range(pairs):
                c = slice(p * 128, (p + 1) * 128)
                cv = slice(d + p * 128, d + (p + 1) * 128)
                grad_q, grad_k, grad_v = pair_pull(
                    q_ref[r, c], kv_ref[i, :, c], kv_ref[i, :, cv], ctx_ref[r, c], prob_ref[i, p], low, high
                )
                gq_ref[r, c] = join_heads(grad_q * scale)
                gkv_ref[i, :, c] = (grad_k * scale).astype(BF16)
                gkv_ref[i, :, cv] = grad_v.astype(BF16)
        sum_ref[0:1, :] += col_sum(gq_ref[...])
        sum_ref[1:2, :] += col_sum(gkv_ref[:, :, d:].reshape(group * count, d))

    return call(
        body,
        "cross_attend_back",
        items // group,
        [
            (grad_low, tiled((block, d))),
            (query, tiled((block, d))),
            (kv, tiled((group, count, 2 * d))),
            (probs, tiled((group, pairs, count, 2 * length))),
            (w_cout, whole((d, d))),
        ],
        [
            (spec_of((tokens, d), BF16), tiled((block, d))),
            (spec_of((items, count, 2 * d), BF16), tiled((group, count, 2 * d))),
            (spec_of((8, d), F32), summed((8, d))),
        ],
        2 * tokens * d * 4 * d,
        [pltpu.VMEM((block, d), BF16)],
    )


def cross_project_back(dims, grad_two, grad_query, grad_kv, total_one, w_cq, w_ckv, rows, parts, part):
    d, items, length, group = dims.d, dims.items, dims.length, dims.group
    tokens, block = items * length, group * length
    count, vis = grad_kv.shape[1], w_ckv.shape[0]

    def body(g_ref, gq_ref, gkv_ref, tot_ref, wcq_ref, wckv_ref, row_ref, *refs):
        grid_refs, (cls_ref, one_ref, onelow_ref, sum_ref) = refs[:parts], refs[parts:]

        @pl.when(pl.program_id(0) == 0)
        def _():
            sum_ref[...] = jnp.zeros_like(sum_ref)

        for i in range(group):
            value = dot_t(gkv_ref[i], wckv_ref[...])
            for k in range(parts):
                grid_refs[k][i * part : (i + 1) * part, :] = value[k * part : (k + 1) * part, :].astype(BF16)
            cls_ref[i] = value[parts * part : parts * part + 1, :]
        grad = g_ref[...] + dot_t(gq_ref[...], wcq_ref[...])
        hat, spread = norm_parts(tot_ref[...])
        one = norm_pull(grad, hat, spread, row_ref[3:4, :])
        one_ref[...] = one
        one_low = one.astype(BF16)
        onelow_ref[...] = one_low
        sum_ref[0:1, :] += col_sum(grad * hat)
        sum_ref[1:2, :] += col_sum(grad)
        sum_ref[2:3, :] += col_sum(one_low)

    return call(
        body,
        "cross_project_back",
        items // group,
        [
            (grad_two, tiled((block, d))),
            (grad_query, tiled((block, d))),
            (grad_kv, tiled((group, count, 2 * d))),
            (total_one, tiled((block, d))),
            (w_cq, whole((d, d))),
            (w_ckv, whole((vis, 2 * d))),
            (rows, whole(rows.shape)),
        ],
        [(spec_of((items * part, vis), BF16), tiled((group * part, vis)))] * parts
        + [
            (spec_of((items, 1, vis), F32), tiled((group, 1, vis))),
            (spec_of((tokens, d), F32), tiled((block, d))),
            (spec_of((tokens, d), BF16), tiled((block, d))),
            (spec_of((8, d), F32), summed((8, d))),
        ],
        2 * tokens * d * d + 2 * items * count * vis * 2 * d,
    )


def self_attend_back(dims, grad_low, qkv, probs, w_out):
    d, items, length, group = dims.d, dims.items, dims.length, dims.group
    pairs, tokens, block = d // (2 * HEAD), items * length, group * length
    scale = HEAD ** (-0.5)

    def body(glow_ref, qkv_ref, prob_ref, wout_ref, gqkv_ref, sum_ref, ctx_ref):
        @pl.when(pl.program_id(0) == 0)
        def _():
            sum_ref[...] = jnp.zeros_like(sum_ref)

        low, high = lane_masks()
        ctx_ref[...] = dot_t(glow_ref[...], wout_ref[...]).astype(BF16)
        for i in range(group):
            r = slice(i * length, (i + 1) * length)
            for p in range(pairs):
                cuts = [slice(part * d + p * 128, part * d + (p + 1) * 128) for part in range(3)]
                q, k, v = (qkv_ref[r, cut] for cut in cuts)
                grad_q, grad_k, grad_v = pair_pull(q, k, v, ctx_ref[r, cuts[0]], prob_ref[i, p], low, high)
                gqkv_ref[r, cuts[0]] = join_heads(grad_q * scale)
                gqkv_ref[r, cuts[1]] = (grad_k * scale).astype(BF16)
                gqkv_ref[r, cuts[2]] = grad_v.astype(BF16)
        sum_ref[0:1, :] += col_sum(gqkv_ref[:, :d])
        sum_ref[1:2, :] += col_sum(gqkv_ref[:, 2 * d :])

    return call(
        body,
        "self_attend_back",
        items // group,
        [
            (grad_low, tiled((block, d))),
            (qkv, tiled((block, 3 * d))),
            (probs, tiled((group, pairs, length, 2 * length))),
            (w_out, whole((d, d))),
        ],
        [
            (spec_of((tokens, 3 * d), BF16), tiled((block, 3 * d))),
            (spec_of((8, d), F32), summed((8, d))),
        ],
        2 * tokens * d * 4 * d,
        [pltpu.VMEM((block, d), BF16)],
    )


def self_project_back(dims, grad_one, grad_qkv, w_qkv):
    d, items, length, group = dims.d, dims.items, dims.length, dims.group
    tokens, block = items * length, group * length

    def body(g_ref, gqkv_ref, wqkv_ref, text_ref):
        text_ref[...] = g_ref[...] + dot_t(gqkv_ref[...], wqkv_ref[...])

    return call(
        body,
        "self_project_back",
        items // group,
        [
            (grad_one, tiled((block, d))),
            (grad_qkv, tiled((block, 3 * d))),
            (w_qkv, whole((d, 3 * d))),
        ],
        [(spec_of((tokens, d), F32), tiled((block, d)))],
        2 * tokens * d * 3 * d,
    )[0]


def cut_grids(turn, image_grid, parts):
    micro, items, part, vis = image_grid.shape
    each = items // parts

    def body(turn_ref, grid_ref, *out_refs):
        def fill(own):
            value = jnp.swapaxes(grid_ref[0], 0, 1)
            for s in range(parts):
                mine = value[s * each : (s + 1) * each]
                out_refs[s ^ own][...] = mine.reshape(each * part, vis)

        for own in range(parts):
            pl.when(turn_ref[0] == own)(functools.partial(fill, own))

    return call(
        body,
        "cut_grids",
        micro,
        [
            (turn, SMEM_SPEC),
            (image_grid.transpose(0, 2, 1, 3), tiled((1, part, items, vis))),
        ],
        [(spec_of((micro * each * part, vis), BF16), tiled((each * part, vis)))] * parts,
        0,
    )


def place_grids(turn, micro, items, pieces):
    part, vis = pieces[0].shape[0] // items, pieces[0].shape[1]
    each, parts = items // micro, len(pieces)

    def body(turn_ref, *refs):
        def fill(own):
            value = [
                refs[s ^ own][...].astype(F32).reshape(each, part, vis) for s in range(parts)
            ]
            refs[-1][0] = jnp.swapaxes(jnp.concatenate(value, 0), 0, 1)

        for own in range(parts):
            pl.when(turn_ref[0] == own)(functools.partial(fill, own))

    shape = (micro, part, each * parts, vis)
    done = call(
        body,
        "place_grids",
        micro,
        [(turn, SMEM_SPEC)] + [(p, tiled((each * part, vis))) for p in pieces],
        [(spec_of(shape, F32), tiled((1,) + shape[1:]))],
        0,
    )[0]
    return done.transpose(0, 2, 1, 3)


def gather_sums(sums, bias):
    d, ff = sums[0].shape[1], bias.shape[1]
    high = -(-(ROWS + ff // d) // 8) * 8

    def body(self_ref, attend_ref, one_ref, two_ref, three_ref, bias_ref, out_ref):
        out_ref[...] = jnp.zeros_like(out_ref)
        at = 0
        for ref, row, count in (
            (self_ref, 0, 2),
            (one_ref, 2, 1),
            (one_ref, 0, 2),
            (attend_ref, 0, 2),
            (two_ref, 2, 1),
            (two_ref, 0, 2),
            (three_ref, 2, 1),
            (three_ref, 0, 2),
        ):
            out_ref[at : at + count, :] = ref[row : row + count, :]
            at += count
        for n in range(ff // d):
            out_ref[at + n : at + n + 1, :] = bias_ref[0:1, n * d : (n + 1) * d]

    return pl.pallas_call(
        body,
        out_shape=spec_of((high, d), F32),
        in_specs=[VMEM_SPEC] * 6,
        out_specs=VMEM_SPEC,
        compiler_params=PARAMS,
        name="gather_sums",
    )(*sums, bias)


def weight_grads(plan, group, where, factors):
    high_rows = max(plan.full[w][0] for w in group)
    wide = max(plan.full[w][1] for w in group)
    flat = [a for pair in factors for a in pair]
    count = len(flat)

    def body(where_ref, *refs):
        far, stack_refs = refs[:count], refs[count : count + 2]
        near, made, sems = refs[count + 2 : 2 * count + 2], refs[-2], refs[-1]
        copies = [pltpu.make_async_copy(far[n], near[n], sems.at[n]) for n in range(count)]
        for copy in copies:
            copy.start()
        for n, w in enumerate(group):
            left, right = near[2 * n], near[2 * n + 1]
            rows, cols = plan.full[w]
            copies[2 * n].wait()
            copies[2 * n + 1].wait()
            for at in range(0, rows, 256):
                value = dot_l(left[:, at : at + 256], right[...])
                made[at : at + 256, :cols] = value.astype(BF16)

            def visit(other, second, first, k, row, w_at, j, to_row, to_y, high):
                if w_at == w:
                    col = pl.multiple_of(to_y * (cols // 2) + j * plan.chunk, 128)
                    stack_refs[other][second * 2 + first, k, row : row + high, :] = made[
                        pl.ds(to_row, high), pl.ds(col, plan.chunk)
                    ]

            each_place(plan, group, where_ref, visit)

    shape = jax.ShapeDtypeStruct((4, plan.zs, plan.rows(group), plan.chunk), BF16)
    flops = sum(2 * a.shape[0] * a.shape[1] * b.shape[1] for a, b in factors)
    moved = sum(a.size * 2 for a in flat) + 2 * shape.size * 2
    return pl.pallas_call(
        body,
        out_shape=(shape,) * 2,
        in_specs=[SMEM_SPEC] + [pl.BlockSpec(memory_space=pl.ANY)] * count,
        out_specs=(VMEM_SPEC,) * 2,
        scratch_shapes=[pltpu.VMEM(a.shape, BF16) for a in flat]
        + [pltpu.VMEM((high_rows, wide), BF16), pltpu.SemaphoreType.DMA((count,))],
        compiler_params=PARAMS,
        cost_estimate=pl.CostEstimate(flops=flops, bytes_accessed=moved, transcendentals=0),
        name="weight_grads",
    )(where, *flat)


class Dims:
    def __init__(self, d, items, length):
        self.d, self.items, self.length = d, items, length
        self.group = 2 if items % 2 == 0 else 1


def cross_mask(lengths, counts, boxes, length, count):
    place = jnp.arange(length, dtype=jnp.int32)[None, :]
    boxed = (counts[:, None] > 0) & (place < lengths[:, None])
    phrase = jnp.where(boxed, place * counts[:, None] // lengths[:, None], 0)
    chosen = phrase[:, None, :] == jnp.arange(boxes.shape[1], dtype=jnp.int32)[None, :, None]
    inside = jnp.einsum(
        "ijp,ijt->ipt",
        (boxes > 0).astype(BF16),
        chosen.astype(BF16),
        preferred_element_type=F32,
    )
    grid_ok = jnp.where(boxed[:, None, :], inside, 1.0).astype(BF16)
    items, real = grid_ok.shape[:2]
    own = jnp.ones((items, 1, length), BF16)
    return jnp.concatenate([grid_ok, own, jnp.zeros((items, count - real - 1, length), BF16)], 1)


def trade(pieces):
    parts = lax.axis_size("patch")
    return [pieces[0]] + [
        lax.ppermute(pieces[k], "patch", [(i, i ^ k) for i in range(parts)])
        for k in range(1, len(pieces))
    ]


class Work:
    def __init__(self, args, parts):
        (self.text_in, self.image_grid, self.image_cls, lengths, counts, boxes, cot) = args
        self.parts = parts
        self.micro, d = self.text_in.shape[0], self.text_in.shape[2]
        self.items = lengths.size
        self.text, self.cot = self.text_in.reshape(-1, d), cot.reshape(-1, d)
        self.lengths, self.counts = lengths.reshape(-1), counts.reshape(-1)
        self.boxes = boxes.reshape((self.items,) + boxes.shape[2:])
        self.dims = Dims(d, self.items, self.text.shape[0] // self.items)
        self.turn = lax.axis_index("patch").astype(jnp.int32).reshape(1)
        self.part, self.vis = self.image_grid.shape[2:]
        self.each = self.items // self.micro
        self.count = -(-(parts * self.part + 1) // 16) * 16
        self.cls = self.image_cls.reshape(self.items, 1, self.vis)

    def mask(self):
        boxes = self.boxes.reshape(self.items, -1, self.parts, self.part)
        order = jnp.arange(self.parts, dtype=jnp.int32) ^ self.turn[0]
        boxes = jnp.take(boxes, order, axis=2).reshape(self.boxes.shape)
        return cross_mask(self.lengths, self.counts, boxes, self.dims.length, self.count)

    def finish(self, layer_out, text_grad, grid_grad, cls, grads, rows_grad, bias_grad):
        return (
            layer_out.reshape(self.text_in.shape),
            text_grad.reshape(self.text_in.shape),
            grid_grad,
            cls.reshape(self.image_cls.shape),
            *grads,
            rows_grad,
            bias_grad,
        )


def on_device(plan, *args):
    work, shards, vectors, ffn_bias = Work(args[:7], plan.patch), args[7:14], args[14], args[15]
    dims, where, parts = work.dims, coords(), plan.patch

    own, give = pack_split(plan, where, shards)
    units = pack_join(plan, where, own, send(give, plan.core()))
    grids = list(cut_grids(work.turn, work.image_grid, parts))
    vectors, bias, grids, units = lax.optimization_barrier((vectors, ffn_bias, grids, units))
    one, two, three = (Gathering(plan, unit) for unit in units)
    small = GatheringSmall(plan, where, vectors, bias)

    def source(g, gather):
        return Source(plan, GROUPS[g], where, gather.held)

    one.along_z(*range(1, plan.zs))
    grids[2] = trade(grids[:3])[2]
    small.advance()
    grids = fence([one, two, small], grids)
    one.first()
    two.along_z(*range(1, plan.zs // 2 + 1))
    grids[3] = trade(grids)[3]
    small.advance()
    fence([one, two, three, small], [])
    one.second()
    two.along_z(*range(plan.zs // 2 + 1, plan.zs))
    rows, bias = small.result()
    rows, bias, grids = fence([one, two, three], [rows, bias, grids])
    one.core()
    two.first()
    three.along_z(*range(1, plan.zs // 2 + 1))
    mask = work.mask()
    mask = fence([one, two, three], mask)
    two.second()
    three.along_z(*range(plan.zs // 2 + 1, plan.zs))
    grids[1] = trade(grids[:2])[1]
    (qkv, probs, ctx), (w_qkv,) = self_forward(dims, source(0, one), work.text, rows, work.lengths)
    ctx, grids = fence([two, three], [ctx, grids])
    two.core()
    three.first()
    (kv, patches), (w_out, w_cq, w_ckv, w_cout) = cross_keys(
        dims, source(1, two), grids, work.cls, rows, work.count
    )
    kv, ctx = fence([three], [kv, ctx])
    three.second()
    total_one, hidden_one, query, cross_probs, cross_ctx, total_two = cross_forward(
        dims, work.text, ctx, kv, mask, w_out, w_cq, w_cout, rows
    )
    total_two = fence([three], total_two)
    three.core()
    (layer_out, hidden_two, act, slope, grad_three, low_three, sum_three), (w_fin, w_fout) = ffn_forward(
        dims, source(2, three), total_two, work.cot, rows, bias
    )

    reduces = {}

    def reduce(g, factors):
        stacks = weight_grads(plan, GROUPS[g], where, factors)
        reduces[g] = Reducing(plan, GROUPS[g], where, stacks)

    def hold(*values, on=None):
        chains = [reduces[g] for g in (reduces if on is None else on)]
        return fence(chains, list(values))

    def go(*groups):
        for g in groups:
            reduces[g].advance()

    grad_pre, grad_two, low_two, sum_two, sum_pre = ffn_backward(
        dims, grad_three, low_three, slope, total_two, w_fin, w_fout, rows
    )
    reduce(2, [(hidden_two, grad_pre), (act, low_three)])
    (low_two,) = hold(low_two)
    go(2)
    grad_query, grad_kv, sum_attend = cross_attend_back(dims, low_two, query, kv, cross_probs, w_cout)
    grad_query, grad_kv = hold(grad_query, grad_kv)
    go(2)
    *grids, cls, grad_one, low_one, sum_one = cross_project_back(
        dims, grad_two, grad_query, grad_kv, total_one, w_cq, w_ckv, rows, parts, work.part
    )
    reduce(
        1,
        [
            (ctx, low_one),
            (hidden_one, grad_query),
            (patches.reshape(-1, work.vis), grad_kv.reshape(-1, grad_kv.shape[2])),
            (cross_ctx, low_two),
        ],
    )
    low_one, *grids = hold(low_one, *grids)
    go(2, 1)
    grids[1] = trade(grids[:2])[1]
    grad_qkv, sum_self = self_attend_back(dims, low_one, qkv, probs, w_out)
    grad_qkv, sum_self, *grids = hold(grad_qkv, sum_self, *grids)
    go(1, 2)
    reduce(0, [(work.text, grad_qkv)])
    text_grad = self_project_back(dims, grad_one, grad_qkv, w_qkv)
    sums = [sum_self, sum_attend, sum_one, sum_two, sum_three]
    reduces["small"] = ReducingSmall(plan, where, sums, sum_pre)
    (text_grad,) = hold(text_grad)
    go(0, 1, 2, "small")
    hold()
    go(0, 1, 2, "small")
    grids = hold(*grids)
    go(0, 1, 2, "small")
    grids[2] = trade(grids[:3])[2]
    grids = hold(*grids)
    go(0, 0, 1, "small")
    grids[3] = trade(grids)[3]
    grids = hold(*grids)
    go(0, 1, "small")
    grid_grad = place_grids(work.turn, work.micro, work.items, grids)
    go(0)
    grads = [None] * 7
    for g, group in enumerate(GROUPS):
        for w, value in zip(group, reduces[g].held):
            grads[w] = value
    return work.finish(layer_out, text_grad, grid_grad, cls, grads, *reduces["small"].result())


def on_device_plain(plan, *args):
    work, parts = Work(args[:7], plan.patch), plan.patch
    dims = work.dims
    weights, rows, bias = fetch_plain(args[7:14], args[14], args[15])
    rows = jnp.pad(rows, ((0, -rows.shape[0] % 8), (0, 0)))
    grids = trade(cut_grids(work.turn, work.image_grid, parts))

    def source(g):
        return Source(plan, GROUPS[g], None, [weights[w] for w in GROUPS[g]])

    (qkv, probs, ctx), _ = self_forward(dims, source(0), work.text, rows, work.lengths)
    (kv, patches), _ = cross_keys(dims, source(1), grids, work.cls, rows, work.count)
    total_one, hidden_one, query, cross_probs, cross_ctx, total_two = cross_forward(
        dims, work.text, ctx, kv, work.mask(), weights[OUT], weights[CQ], weights[COUT], rows
    )
    (layer_out, hidden_two, act, slope, grad_three, low_three, sum_three), _ = ffn_forward(
        dims, source(2), total_two, work.cot, rows, bias[None]
    )
    grad_pre, grad_two, low_two, sum_two, sum_pre = ffn_backward(
        dims, grad_three, low_three, slope, total_two, weights[FIN], weights[FOUT], rows
    )
    grad_query, grad_kv, sum_attend = cross_attend_back(
        dims, low_two, query, kv, cross_probs, weights[COUT]
    )
    *grids, cls, grad_one, low_one, sum_one = cross_project_back(
        dims, grad_two, grad_query, grad_kv, total_one, weights[CQ], weights[CKV], rows, parts, work.part
    )
    grad_qkv, sum_self = self_attend_back(dims, low_one, qkv, probs, weights[OUT])
    text_grad = self_project_back(dims, grad_one, grad_qkv, weights[QKV])
    flat_kv = grad_kv.reshape(-1, grad_kv.shape[2])
    factors = [
        (work.text, grad_qkv),
        (ctx, low_one),
        (hidden_one, grad_query),
        (patches.reshape(-1, work.vis), flat_kv),
        (cross_ctx, low_two),
        (hidden_two, grad_pre),
        (act, low_three),
    ]
    grads = [reduce_plain(dot_l(a, b).astype(BF16)) for a, b in factors]
    sums = gather_sums([sum_self, sum_attend, sum_one, sum_two, sum_three], sum_pre)
    small = reduce_small_plain(sums[:ROWS], sum_pre[0])
    grid_grad = place_grids(work.turn, work.micro, work.items, trade(grids))
    return work.finish(layer_out, text_grad, grid_grad, cls, grads, *small)


def solution(mesh):
    dp, patch = mesh.shape["dp"], mesh.shape["patch"]
    both = P(None, ("dp", "patch"), None)
    weight = P("dp", "patch")

    def run(*args):
        shards = [(w.shape[0] // dp, w.shape[1] // patch) for w in args[7:14]]
        plan = Plan(dp, patch, shards)
        return jax.shard_map(
            functools.partial(on_device if plan.fast else on_device_plain, plan),
            mesh=mesh,
            in_specs=(
                both,
                P(None, "dp", "patch", None),
                both,
                P(None, ("dp", "patch")),
                P(None, ("dp", "patch")),
                P(None, ("dp", "patch"), None, None),
                both,
            )
            + (weight,) * 7
            + (P(None, "dp"), P("dp")),
            out_specs=(both, both, P(None, "dp", "patch", None), both)
            + (weight,) * 7
            + (P(None, "dp"), P("dp")),
            check_vma=False,
        )(*args)

    return run
```

```python
import functools

import jax
import jax.numpy as jnp
from jax import lax
from jax.experimental import pallas as pl
from jax.experimental.pallas import tpu as pltpu
from jax.sharding import PartitionSpec as P

HEAD = 64
EPS = 1e-06
NEG = -1e30
BF16 = jnp.bfloat16
F32 = jnp.float32
AXES = ("dp", "patch")
VMEM_SPEC = pl.BlockSpec(memory_space=pltpu.VMEM)
SMEM_SPEC = pl.BlockSpec(memory_space=pltpu.SMEM)
PARAMS = pltpu.CompilerParams(vmem_limit_bytes=62 * 2**20)

QKV, OUT, CQ, CKV, COUT, FIN, FOUT = range(7)
ROWS = 13
GATHER = ((QKV,), (OUT, CQ, CKV, COUT), (FIN, FOUT))
REDUCE = ((QKV, OUT), (CQ, CKV, COUT), (FIN,), (FOUT,))


class Plan:
    def __init__(self, dp, patch, shards):
        self.dp, self.patch = dp, patch
        self.zs = dp // 2
        self.devices = dp * patch
        self.chunk = shards[OUT][1] * 2
        self.half = [s[0] // 2 for s in shards]
        self.cols = [s[1] for s in shards]
        self.chunks = [s[1] * 2 // self.chunk for s in shards]
        self.full = [(s[0] * dp, s[1] * patch) for s in shards]
        self.fast = (
            dp % 2 == 0
            and self.zs & (self.zs - 1) == 0
            and patch == 4
            and all(h % 16 == 0 for h in self.half)
            and all(s[1] * 2 % self.chunk == 0 for s in shards)
            and self.chunk % 128 == 0
        )

    def rows(self, group):
        return sum(self.half[w] * self.chunks[w] for w in group)

    def flip(self, pick):
        return [(i, i ^ pick(i)) for i in range(self.devices)]

    def core(self):
        return self.flip(lambda i: 1)

    def first(self):
        return self.flip(lambda i: 4 if i % 2 == 0 else 2)

    def second(self):
        return self.flip(lambda i: 2 if i % 2 == 0 else 4)

    def along_z(self, k):
        return self.flip(lambda i: 8 * k)


def send(value, perm):
    return lax.ppermute(value, AXES, perm)


def coords():
    dp, patch = lax.axis_index("dp"), lax.axis_index("patch")
    return jnp.stack([dp // 2, dp % 2, patch // 2, patch % 2]).astype(jnp.int32)


def piece_rows(group, plan):
    at, found = 0, []
    for w in group:
        for j in range(plan.chunks[w]):
            found.append((w, j, at))
            at += plan.half[w]
    return found


def group_starts(plan):
    starts, at = [], 0
    for group in GATHER:
        starts.append(at)
        at += plan.rows(group)
    return starts, at


def pack_split(plan, where, shards):
    _, total = group_starts(plan)
    wide = plan.chunk // 2

    def body(where_ref, *refs):
        shard_refs, (own_ref, send_ref, turned) = list(refs[:7]), refs[7:]
        core = where_ref[3]
        turned[...] = shard_refs[FOUT][...].T
        shard_refs[FOUT] = turned
        at = 0
        for group in GATHER:
            for w in group:
                high = plan.half[w]
                for b in range(plan.chunks[w]):
                    cut = slice(b * wide, (b + 1) * wide)
                    own_ref[at : at + high, :] = shard_refs[w][pl.ds(core * high, high), cut]
                    send_ref[at : at + high, :] = shard_refs[w][
                        pl.ds((1 - core) * high, high), cut
                    ]
                    at += high

    shape = jax.ShapeDtypeStruct((total, wide), BF16)
    return pl.pallas_call(
        body,
        out_shape=(shape, shape),
        in_specs=[SMEM_SPEC] + [VMEM_SPEC] * 7,
        out_specs=(VMEM_SPEC, VMEM_SPEC),
        scratch_shapes=[pltpu.VMEM(shards[FOUT].shape, BF16)],
        compiler_params=PARAMS,
        name="pack_split",
    )(where, *shards[:FOUT], shards[FOUT].T)


def pack_join(plan, where, own, got):
    starts, total = group_starts(plan)
    wide = plan.chunk // 2

    def body(where_ref, own_ref, got_ref, *unit_refs):
        core = where_ref[3]

        def fill(low_ref, high_ref):
            for g, group in enumerate(GATHER):
                at = starts[g]
                for w in group:
                    high, count = plan.half[w], plan.chunks[w]
                    for j in range(count):
                        pair = []
                        for b in (2 * j, 2 * j + 1):
                            src = low_ref if b < count else high_ref
                            row = at + (b % count) * high
                            pair.append(src[row : row + high, :])
                        to = at - starts[g] + j * high
                        unit_refs[g][to : to + high, :] = jnp.concatenate(pair, axis=1)
                    at += count * high

        @pl.when(core == 0)
        def _():
            fill(own_ref, got_ref)

        @pl.when(core == 1)
        def _():
            fill(got_ref, own_ref)

    return pl.pallas_call(
        body,
        out_shape=tuple(jax.ShapeDtypeStruct((plan.rows(g), plan.chunk), BF16) for g in GATHER),
        in_specs=[SMEM_SPEC, VMEM_SPEC, VMEM_SPEC],
        out_specs=(VMEM_SPEC,) * len(GATHER),
        compiler_params=PARAMS,
        name="pack_join",
    )(where, own, got)


class Gathering:
    def __init__(self, plan, unit):
        self.plan, self.held = plan, [unit]

    def along_z(self, *steps):
        self.held += [send(self.held[0], self.plan.along_z(k)) for k in steps]

    def first(self):
        stack = jnp.stack(self.held)
        self.held = [stack, send(stack, self.plan.first())]

    def second(self):
        near = jnp.stack(self.held)
        self.held = [near, send(near, self.plan.second()), send(near, self.plan.core())]

    def core(self):
        self.held.append(send(self.held[1], self.plan.core()))


def each_place(plan, group, where_ref, visit):
    z, x, y, core = (where_ref[i] for i in range(4))
    for other in range(2):
        half = core ^ other
        for second in range(2):
            for first in range(2):
                x_at = x ^ jnp.where(half == 0, first, second)
                y_at = y ^ jnp.where(half == 0, second, first)
                for k in range(plan.zs):
                    place = ((z ^ k) * 2 + x_at) * 2 + half
                    for w, j, row in piece_rows(group, plan):
                        high = plan.half[w]
                        to_row = pl.multiple_of(place * high, 16)
                        visit(other, second, first, k, row, w, j, to_row, y_at, high)


def add_low(ones, twos, widths):
    count, slots, rows, chunk = ones.shape

    def body(one_ref, two_ref, *out_refs):
        at = 0
        for width, out in zip(widths, out_refs):
            for n in range(width):
                out[n] = (one_ref[at].astype(F32) + two_ref[at].astype(F32)).astype(BF16)
                at += 1

    def spec(n):
        return pl.BlockSpec((n, 1, rows, chunk), lambda i: (0, i, 0, 0))

    return pl.pallas_call(
        body,
        grid=(slots,),
        out_shape=tuple(jax.ShapeDtypeStruct((n, slots, rows, chunk), BF16) for n in widths),
        in_specs=[spec(count), spec(count)],
        out_specs=tuple(spec(n) for n in widths),
        compiler_params=PARAMS,
        cost_estimate=pl.CostEstimate(
            flops=ones.size, bytes_accessed=6 * ones.size, transcendentals=0
        ),
        name="add_low",
    )(ones, twos)


def add_slots(ones, twos):
    _, slots, rows, chunk = ones.shape

    def body(one_ref, two_ref, *out_refs):
        for n in range(slots):
            out_refs[n][...] = (one_ref[0, n].astype(F32) + two_ref[0, n].astype(F32)).astype(BF16)

    return pl.pallas_call(
        body,
        out_shape=(jax.ShapeDtypeStruct((rows, chunk), BF16),) * slots,
        in_specs=[VMEM_SPEC, VMEM_SPEC],
        out_specs=(VMEM_SPEC,) * slots,
        compiler_params=PARAMS,
        cost_estimate=pl.CostEstimate(
            flops=ones.size, bytes_accessed=6 * ones.size, transcendentals=0
        ),
        name="add_slots",
    )(ones, twos)


class Reducing:
    def __init__(self, plan, group, where, stacks):
        self.plan, self.group, self.where = plan, group, where
        self.held, self.step = list(stacks), 0

    def advance(self):
        plan, held = self.plan, self.held
        if self.step == 0:
            held = [held[0], send(held[1], plan.core())]
        elif self.step == 1:
            keep, give = add_low(*held, (2, 2))
            held = [keep, send(give, plan.second())]
        elif self.step == 2:
            keep, give = add_low(*held, (1, 1))
            held = [keep, send(give, plan.first())]
        elif self.step == 3:
            slots = add_slots(*held)
            near = plan.zs // 2 + 1
            held = [slots[0]] + [send(slots[k], plan.along_z(k)) for k in range(1, near)]
            held += slots[near:]
        elif self.step == 4:
            near = plan.zs // 2 + 1
            held = held[:near] + [send(held[k], plan.along_z(k)) for k in range(near, plan.zs)]
        elif self.step == 5:
            own, give = unpack_split(plan, self.group, self.where, held)
            held = [own, send(give, plan.core())]
        elif self.step == 6:
            held = unpack_join(plan, self.group, self.where, *held)
        self.held, self.step = list(held), self.step + 1


def fence(chains, values):
    flat, tree = jax.tree.flatten([values, [chain.held for chain in chains]])
    values, held = jax.tree.unflatten(tree, lax.optimization_barrier(flat))
    for chain, arrays in zip(chains, held):
        chain.held = arrays
    return values


def unpack_split(plan, group, where, parts):
    rows, wide = plan.rows(group), plan.chunk // 2

    def body(where_ref, *refs):
        part_refs, (own_ref, give_ref) = refs[:-2], refs[-2:]
        core = where_ref[3]

        def fill(low_ref, high_ref):
            at = 0
            for w in group:
                high, count = plan.half[w], plan.chunks[w]
                for j in range(count):
                    row = at + j * high
                    value = sum(p[row : row + high, :].astype(F32) for p in part_refs)
                    for b in (2 * j, 2 * j + 1):
                        dst = low_ref if b < count else high_ref
                        to = at + (b % count) * high
                        cut = (b - 2 * j) * wide
                        dst[to : to + high, :] = value[:, cut : cut + wide]
                at += count * high

        @pl.when(core == 0)
        def _():
            fill(own_ref, give_ref)

        @pl.when(core == 1)
        def _():
            fill(give_ref, own_ref)

    shape = jax.ShapeDtypeStruct((rows, wide), F32)
    return pl.pallas_call(
        body,
        out_shape=(shape, shape),
        in_specs=[SMEM_SPEC] + [VMEM_SPEC] * len(parts),
        out_specs=(VMEM_SPEC, VMEM_SPEC),
        compiler_params=PARAMS,
        name="unpack_split",
    )(where, *parts)


def unpack_join(plan, group, where, own, got):
    wide = plan.chunk // 2
    turned = [w == FOUT for w in group]

    def body(where_ref, own_ref, got_ref, *refs):
        core = where_ref[3]
        at = 0
        for n, w in enumerate(group):
            out_ref = refs[-1] if turned[n] else refs[n]
            high, count = plan.half[w], plan.chunks[w]
            own_rows = pl.ds(pl.multiple_of(core * high, 16), high)
            got_rows = pl.ds(pl.multiple_of((1 - core) * high, 16), high)
            for b in range(count):
                row, cut = at + b * high, slice(b * wide, (b + 1) * wide)
                out_ref[own_rows, cut] = own_ref[row : row + high, :]
                out_ref[got_rows, cut] = got_ref[row : row + high, :]
            at += count * high
            if turned[n]:
                refs[n][...] = out_ref[...].T

    shapes = [(2 * plan.half[w], plan.cols[w]) for w in group]
    done = pl.pallas_call(
        body,
        out_shape=tuple(
            jax.ShapeDtypeStruct(shape[::-1] if turn else shape, F32)
            for shape, turn in zip(shapes, turned)
        ),
        in_specs=[SMEM_SPEC, VMEM_SPEC, VMEM_SPEC],
        out_specs=(VMEM_SPEC,) * len(group),
        scratch_shapes=[pltpu.VMEM(shapes[-1], F32)],
        compiler_params=PARAMS,
        name="unpack_join",
    )(where, own, got)
    return [value.T if turn else value for value, turn in zip(done, turned)]


class GatheringSmall:
    def __init__(self, plan, where, vectors, bias):
        self.plan, self.where, self.shape = plan, where, vectors.shape
        flat = jnp.concatenate([vectors.reshape(-1), bias])
        self.size = flat.shape[0]
        self.held, self.bit = [jnp.pad(flat, (0, -self.size % 2048)).reshape(1, -1, 128)], 4

    def advance(self):
        every = jnp.concatenate(self.held)
        self.held = [every, send(every, self.plan.flip(lambda i: self.bit))]
        self.bit *= 2

    def result(self):
        plan, (count, part) = self.plan, self.shape
        while self.bit < plan.devices:
            self.advance()
        every = jnp.concatenate(self.held).reshape(plan.dp, -1)
        slot = jnp.arange(plan.dp, dtype=jnp.int32) ^ (self.where[0] * 2 + self.where[1])
        every = jnp.take(every, slot, axis=0)[:, : self.size].astype(F32)
        rows = every[:, : count * part].reshape(plan.dp, count, part)
        rows = rows.transpose(1, 0, 2).reshape(count, plan.dp * part)
        bias = every[:, count * part :].reshape(1, -1)
        return jnp.pad(rows, ((0, -count % 8), (0, 0))), bias


class ReducingSmall:
    def __init__(self, plan, where, sums, bias):
        self.plan, self.where, self.tail = plan, where, bias.shape[1]
        self.held, self.step = [gather_sums(sums, bias)], 0
        bits = [1, 2, 4]
        while 1 << len(bits) < plan.devices:
            bits.append(1 << len(bits))
        self.bits = bits

    def advance(self):
        flat = sum(self.held)
        if self.bits:
            bit = self.bits.pop(0)
            self.held = [flat, send(flat, self.plan.flip(lambda i: bit))]
        else:
            self.held = [flat]

    def result(self):
        plan, flat = self.plan, sum(self.held)
        width = flat.shape[1] // plan.dp
        dp = self.where[0] * 2 + self.where[1]
        own = lax.dynamic_slice_in_dim(flat[:ROWS], dp * width, width, axis=1)
        tail, step = flat[ROWS : ROWS + self.tail // flat.shape[1]].reshape(-1), self.tail // plan.dp
        return own, lax.dynamic_slice_in_dim(tail, dp * step, step, axis=0)


def fetch_plain(weights, vectors, bias):
    whole = [
        lax.all_gather(lax.all_gather(w, "dp", axis=0, tiled=True), "patch", axis=1, tiled=True)
        for w in weights
    ]
    rows = lax.all_gather(vectors, "dp", axis=1, tiled=True)
    return whole, rows.astype(F32), lax.all_gather(bias, "dp", axis=0, tiled=True).astype(F32)


def reduce_plain(grad):
    part = lax.psum_scatter(grad, "dp", scatter_dimension=0, tiled=True)
    return lax.psum_scatter(part, "patch", scatter_dimension=1, tiled=True).astype(F32)


def reduce_small_plain(rows, bias):
    rows = lax.psum_scatter(rows, "dp", scatter_dimension=1, tiled=True)
    bias = lax.psum_scatter(bias, "dp", scatter_dimension=0, tiled=True)
    return lax.psum(rows, "patch"), lax.psum(bias, "patch")


TAIL = (0.112528827, 0.117839666, 0.0706314405, 0.2046457425, -0.190499398, 0.3478185715, -0.201092832, 0.03812798145)


def dot(a, b):
    return lax.dot_general(a, b, (((1,), (0,)), ((), ())), preferred_element_type=F32)


def dot_t(a, b):
    return lax.dot_general(a, b, (((1,), (1,)), ((), ())), preferred_element_type=F32)


def dot_l(a, b):
    return lax.dot_general(a, b, (((0,), (0,)), ((), ())), preferred_element_type=F32)


def norm_parts(total):
    center = total - jnp.mean(total, -1, keepdims=True)
    spread = lax.rsqrt(jnp.mean(center * center, -1, keepdims=True) + EPS)
    return center * spread, spread


def norm_pull(grad, hat, spread, gain):
    scaled = grad * gain
    return spread * (
        scaled
        - jnp.mean(scaled, -1, keepdims=True)
        - hat * jnp.mean(scaled * hat, -1, keepdims=True)
    )


def gelu_parts(x):
    bell = jnp.exp(-0.5 * (x * x))
    t = 1.0 / (1.0 + (0.4 * 0.5**0.5) * jnp.abs(x))
    tail = jnp.full_like(t, TAIL[-1])
    for c in TAIL[-2::-1]:
        tail = tail * t + c
    tail = tail * (t * bell)
    return jnp.where(x < 0.0, tail, 1.0 - tail), bell


def col_sum(value):
    return jnp.sum(value.astype(F32), 0, keepdims=True)


def soft(scores):
    grown = jnp.exp(scores - jnp.max(scores, 0, keepdims=True))
    return grown * (1.0 / jnp.sum(grown, 0, keepdims=True))


def soft_pull(probs, grad):
    return probs * (grad - jnp.sum(probs * grad, 0, keepdims=True))


def spread_heads(value, low, high):
    return jnp.concatenate([value * low, value * high], 0)


def join_heads(value):
    count = value.shape[1] // 2
    value = jnp.concatenate([value[:HEAD, :count], value[HEAD:, count:]], 0)
    return value.astype(BF16).T


def lane_masks():
    lane = lax.broadcasted_iota(jnp.int32, (1, 2 * HEAD), 1)
    low = (lane < HEAD).astype(F32)
    return low.astype(BF16), (1.0 - low).astype(BF16)


def whole(shape):
    return pl.BlockSpec(
        shape, lambda i: (0,) * len(shape), pipeline_mode=pl.Buffered(1)
    )


def summed(shape):
    return pl.BlockSpec(shape, lambda i: (0,) * len(shape))


def tiled(shape):
    return pl.BlockSpec(shape, lambda i: (i,) + (0,) * (len(shape) - 1))


def spec_of(shape, dtype):
    return jax.ShapeDtypeStruct(shape, dtype)


def call(body, name, steps, ins, outs, flops, scratch=()):
    out_shape = tuple(shape for shape, _ in outs)
    moved = sum(a.size * a.dtype.itemsize for a, _ in ins)
    moved += sum(o.size * jnp.dtype(o.dtype).itemsize for o in out_shape)
    return pl.pallas_call(
        body,
        grid=(steps,),
        out_shape=out_shape,
        in_specs=[spec for _, spec in ins],
        out_specs=tuple(spec for _, spec in outs),
        scratch_shapes=list(scratch),
        compiler_params=PARAMS,
        cost_estimate=pl.CostEstimate(
            flops=int(flops), bytes_accessed=int(moved), transcendentals=0
        ),
        name=name,
    )(*[a for a, _ in ins])


class Source:
    def __init__(self, plan, group, where, given):
        self.plan, self.group, self.pieces = plan, group, plan.fast
        if self.pieces:
            self.ins = [(where, SMEM_SPEC)] + [(part, whole(part.shape)) for part in given]
            self.outs = [(spec_of(plan.full[w], BF16), summed(plan.full[w])) for w in group]
        else:
            self.ins = [(w, whole(w.shape)) for w in given]
            self.outs = []
        self.given = given

    def open(self, in_refs, out_refs):
        if not self.pieces:
            return list(in_refs)
        where_ref, parts = in_refs[0], in_refs[1:]
        full = dict(zip(self.group, out_refs))
        plan = self.plan

        def visit(other, second, first, k, row, w, j, to_row, to_y, high):
            to_col = pl.multiple_of(to_y * (plan.full[w][1] // 2) + j * plan.chunk, 128)
            part = parts[other * 2 + second]
            full[w][pl.ds(to_row, high), pl.ds(to_col, plan.chunk)] = part[
                first, k, row : row + high, :
            ]

        @pl.when(pl.program_id(0) == 0)
        def _():
            each_place(plan, self.group, where_ref, visit)

        return list(out_refs)

    def split(self, done):
        if not self.pieces:
            return done, self.given
        return done[: -len(self.group)], done[-len(self.group) :]


def self_forward(dims, source, text, rows, lengths):
    d, items, length, group = dims.d, dims.items, dims.length, dims.group
    pairs, tokens, block = d // (2 * HEAD), items * length, group * length
    scale = HEAD ** (-0.5)

    n_in = len(source.ins)

    def body(len_ref, x_ref, row_ref, *refs):
        qkv_ref, prob_ref, ctx_ref = refs[n_in : n_in + 3]
        (wqkv_ref,) = source.open(refs[:n_in], refs[n_in + 3 :])
        step = pl.program_id(0)
        low, high = lane_masks()
        x = x_ref[...]
        for part, bias in ((0, 0), (1, None), (2, 1)):
            cut = slice(part * d, (part + 1) * d)
            value = dot(x, wqkv_ref[:, cut])
            if bias is not None:
                value = value + row_ref[bias : bias + 1, :]
            qkv_ref[:, cut] = value.astype(BF16)
        place = lax.broadcasted_iota(jnp.int32, (length, 1), 0)
        for i in range(group):
            ok = place < len_ref[step * group + i]
            r = slice(i * length, (i + 1) * length)
            for p in range(pairs):
                q, k, v = (
                    qkv_ref[r, part * d + p * 128 : part * d + (p + 1) * 128] for part in range(3)
                )
                scores = dot_t(k, spread_heads(q, low, high)) * scale
                probs = soft(jnp.where(ok, scores, NEG)).astype(BF16)
                prob_ref[i, p] = probs
                ctx_ref[r, p * 128 : (p + 1) * 128] = join_heads(dot(v.T, probs))
    done = call(
        body,
        "self_forward",
        items // group,
        [(lengths, SMEM_SPEC), (text, tiled((block, d))), (rows, whole(rows.shape))] + source.ins,
        [
            (spec_of((tokens, 3 * d), BF16), tiled((block, 3 * d))),
            (spec_of((items, pairs, length, 2 * length), BF16), tiled((group, pairs, length, 2 * length))),
            (spec_of((tokens, d), BF16), tiled((block, d))),
        ]
        + source.outs,
        2 * tokens * d * 5 * d,
    )
    return source.split(done)


def cross_keys(dims, source, grids, cls, rows, count):
    d, items, group = dims.d, dims.items, dims.group
    part, vis, parts = grids[0].shape[0] // items, cls.shape[2], len(grids)
    n_in = len(source.ins)

    def body(*refs):
        grid_refs, cls_ref, row_ref = refs[:parts], refs[parts], refs[parts + 1]
        refs = refs[parts + 2 :]
        kv_ref, patch_ref = refs[n_in : n_in + 2]
        _, _, wckv_ref, _ = source.open(refs[:n_in], refs[n_in + 2 :])
        for i in range(group):
            for k in range(parts):
                patch_ref[i, k * part : (k + 1) * part, :] = grid_refs[k][i * part : (i + 1) * part, :]
            rest = jnp.zeros((count - parts * part - 1, vis), BF16)
            patch_ref[i, parts * part :, :] = jnp.concatenate([cls_ref[i], rest], 0)
        patch = patch_ref[...].reshape(group * count, vis)
        keys = dot(patch, wckv_ref[:, :d]).astype(BF16)
        kv_ref[:, :, :d] = keys.reshape(group, count, d)
        values = (dot(patch, wckv_ref[:, d:]) + row_ref[6:7, :]).astype(BF16)
        kv_ref[:, :, d:] = values.reshape(group, count, d)

    done = call(
        body,
        "cross_keys",
        items // group,
        [(grid, tiled((group * part, vis))) for grid in grids]
        + [(cls, tiled((group, 1, vis))), (rows, whole(rows.shape))]
        + source.ins,
        [
            (spec_of((items, count, 2 * d), BF16), tiled((group, count, 2 * d))),
            (spec_of((items, count, vis), BF16), tiled((group, count, vis))),
        ]
        + source.outs,
        2 * items * count * vis * 2 * d,
    )
    return source.split(done)


def cross_forward(dims, text, self_ctx, kv, mask, w_out, w_cq, w_cout, rows):
    d, items, length, group = dims.d, dims.items, dims.length, dims.group
    pairs, tokens, block = d // (2 * HEAD), items * length, group * length
    count = kv.shape[1]
    scale = HEAD ** (-0.5)

    def body(x_ref, self_ref, kv_ref, mask_ref, wout_ref, wcq_ref, wcout_ref, row_ref,
             one_ref, h_ref, cq_ref, prob_ref, ctx_ref, two_ref):
        low, high = lane_masks()
        total = x_ref[...].astype(F32) + dot(self_ref[...], wout_ref[...]) + row_ref[2:3, :]
        one_ref[...] = total
        hat, _ = norm_parts(total)
        hidden = hat * row_ref[3:4, :] + row_ref[4:5, :]
        h_ref[...] = hidden.astype(BF16)
        cq_ref[...] = (dot(h_ref[...], wcq_ref[...]) + row_ref[5:6, :]).astype(BF16)
        for i in range(group):
            ok = mask_ref[i].astype(F32) > 0.5
            ok = jnp.concatenate([ok, ok], 1)
            r = slice(i * length, (i + 1) * length)
            for p in range(pairs):
                c = slice(p * 128, (p + 1) * 128)
                q, k, v = cq_ref[r, c], kv_ref[i, :, c], kv_ref[i, :, d + p * 128 : d + (p + 1) * 128]
                scores = dot_t(k, spread_heads(q, low, high)) * scale
                probs = soft(jnp.where(ok, scores, NEG)).astype(BF16)
                prob_ref[i, p] = probs
                ctx_ref[r, c] = join_heads(dot(v.T, probs))
        two_ref[...] = hidden + dot(ctx_ref[...], wcout_ref[...]) + row_ref[7:8, :]

    return call(
        body,
        "cross_forward",
        items // group,
        [
            (text, tiled((block, d))),
            (self_ctx, tiled((block, d))),
            (kv, tiled((group, count, 2 * d))),
            (mask, tiled((group, count, length))),
            (w_out, whole((d, d))),
            (w_cq, whole((d, d))),
            (w_cout, whole((d, d))),
            (rows, whole(rows.shape)),
        ],
        [
            (spec_of((tokens, d), F32), tiled((block, d))),
            (spec_of((tokens, d), BF16), tiled((block, d))),
            (spec_of((tokens, d), BF16), tiled((block, d))),
            (spec_of((items, pairs, count, 2 * length), BF16), tiled((group, pairs, count, 2 * length))),
            (spec_of((tokens, d), BF16), tiled((block, d))),
            (spec_of((tokens, d), F32), tiled((block, d))),
        ],
        2 * tokens * d * 6 * d,
    )


def ffn_forward(dims, source, total_two, cotangent, rows, bias):
    d, items, length, group = dims.d, dims.items, dims.length, dims.group
    tokens, block, ff = items * length, group * length, bias.shape[1]
    piece = d
    n_in = len(source.ins)

    def body(tot_ref, cot_ref, row_ref, bias_ref, *refs):
        out_ref, h_ref, act_ref, slope_ref, g_ref, glow_ref, sum_ref = refs[n_in : n_in + 7]
        win_ref, wout_ref = source.open(refs[:n_in], refs[n_in + 7 :])

        @pl.when(pl.program_id(0) == 0)
        def _():
            sum_ref[...] = jnp.zeros_like(sum_ref)

        hat, _ = norm_parts(tot_ref[...])
        hidden = hat * row_ref[8:9, :] + row_ref[9:10, :]
        h_ref[...] = hidden.astype(BF16)
        total = hidden + row_ref[10:11, :]
        for at in range(0, ff, piece):
            cut = slice(at, at + piece)
            pre = dot(h_ref[...], win_ref[:, cut]) + bias_ref[:, cut]
            under, bell = gelu_parts(pre)
            act = (pre * under).astype(BF16)
            act_ref[:, cut] = act
            slope_ref[:, cut] = (under + (pre * 0.3989422804014327) * bell).astype(BF16)
            total = total + dot(act, wout_ref[cut, :])
        hat, spread = norm_parts(total)
        gain = row_ref[11:12, :]
        out_ref[...] = hat * gain + row_ref[12:13, :]
        cot = cot_ref[...].astype(F32)
        grad = norm_pull(cot, hat, spread, gain)
        g_ref[...] = grad
        low = grad.astype(BF16)
        glow_ref[...] = low
        sum_ref[0:1, :] += col_sum(cot * hat)
        sum_ref[1:2, :] += col_sum(cot)
        sum_ref[2:3, :] += col_sum(low)

    done = call(
        body,
        "ffn_forward",
        items // group,
        [
            (total_two, tiled((block, d))),
            (cotangent, tiled((block, d))),
            (rows, whole(rows.shape)),
            (bias, whole(bias.shape)),
        ]
        + source.ins,
        [
            (spec_of((tokens, d), F32), tiled((block, d))),
            (spec_of((tokens, d), BF16), tiled((block, d))),
            (spec_of((tokens, ff), BF16), tiled((block, ff))),
            (spec_of((tokens, ff), BF16), tiled((block, ff))),
            (spec_of((tokens, d), F32), tiled((block, d))),
            (spec_of((tokens, d), BF16), tiled((block, d))),
            (spec_of((8, d), F32), summed((8, d))),
        ]
        + source.outs,
        4 * tokens * d * ff,
    )
    return source.split(done)


def ffn_backward(dims, grad_three, grad_low, slope, total_two, w_fin, w_fout, rows):
    d, items, length, group = dims.d, dims.items, dims.length, dims.group
    tokens, block, ff = items * length, group * length, w_fin.shape[1]
    piece = d

    def body(g_ref, glow_ref, slope_ref, tot_ref, win_ref, wout_ref, row_ref,
             pre_ref, two_ref, twolow_ref, sum_ref, bias_ref):
        @pl.when(pl.program_id(0) == 0)
        def _():
            sum_ref[...] = jnp.zeros_like(sum_ref)
            bias_ref[...] = jnp.zeros_like(bias_ref)

        grad = g_ref[...]
        for at in range(0, ff, piece):
            cut = slice(at, at + piece)
            pre = dot_t(glow_ref[...], wout_ref[cut, :]) * slope_ref[:, cut].astype(F32)
            pre = pre.astype(BF16)
            pre_ref[:, cut] = pre
            bias_ref[0:1, cut] += col_sum(pre)
            grad = grad + dot_t(pre, win_ref[:, cut])
        hat, spread = norm_parts(tot_ref[...])
        two = norm_pull(grad, hat, spread, row_ref[8:9, :])
        two_ref[...] = two
        low = two.astype(BF16)
        twolow_ref[...] = low
        sum_ref[0:1, :] += col_sum(grad * hat)
        sum_ref[1:2, :] += col_sum(grad)
        sum_ref[2:3, :] += col_sum(low)

    return call(
        body,
        "ffn_backward",
        items // group,
        [
            (grad_three, tiled((block, d))),
            (grad_low, tiled((block, d))),
            (slope, tiled((block, ff))),
            (total_two, tiled((block, d))),
            (w_fin, whole((d, ff))),
            (w_fout, whole((ff, d))),
            (rows, whole(rows.shape)),
        ],
        [
            (spec_of((tokens, ff), BF16), tiled((block, ff))),
            (spec_of((tokens, d), F32), tiled((block, d))),
            (spec_of((tokens, d), BF16), tiled((block, d))),
            (spec_of((8, d), F32), summed((8, d))),
            (spec_of((8, ff), F32), summed((8, ff))),
        ],
        4 * tokens * d * ff,
    )


def pair_pull(q, k, v, out, probs, low, high):
    outs = spread_heads(out, low, high)
    score = soft_pull(probs.astype(F32), dot_t(v, outs)).astype(BF16)
    grad_k = dot(score, spread_heads(q, low, high))
    return dot(k.T, score), grad_k, dot(probs, outs)


def cross_attend_back(dims, grad_low, query, kv, probs, w_cout):
    d, items, length, group = dims.d, dims.items, dims.length, dims.group
    pairs, tokens, block = d // (2 * HEAD), items * length, group * length
    count = kv.shape[1]
    scale = HEAD ** (-0.5)

    def body(glow_ref, q_ref, kv_ref, prob_ref, wcout_ref, gq_ref, gkv_ref, sum_ref, ctx_ref):
        @pl.when(pl.program_id(0) == 0)
        def _():
            sum_ref[...] = jnp.zeros_like(sum_ref)

        low, high = lane_masks()
        ctx_ref[...] = dot_t(glow_ref[...], wcout_ref[...]).astype(BF16)
        for i in range(group):
            r = slice(i * length, (i + 1) * length)
            for p in range(pairs):
                c = slice(p * 128, (p + 1) * 128)
                cv = slice(d + p * 128, d + (p + 1) * 128)
                grad_q, grad_k, grad_v = pair_pull(
                    q_ref[r, c], kv_ref[i, :, c], kv_ref[i, :, cv], ctx_ref[r, c], prob_ref[i, p], low, high
                )
                gq_ref[r, c] = join_heads(grad_q * scale)
                gkv_ref[i, :, c] = (grad_k * scale).astype(BF16)
                gkv_ref[i, :, cv] = grad_v.astype(BF16)
        sum_ref[0:1, :] += col_sum(gq_ref[...])
        sum_ref[1:2, :] += col_sum(gkv_ref[:, :, d:].reshape(group * count, d))

    return call(
        body,
        "cross_attend_back",
        items // group,
        [
            (grad_low, tiled((block, d))),
            (query, tiled((block, d))),
            (kv, tiled((group, count, 2 * d))),
            (probs, tiled((group, pairs, count, 2 * length))),
            (w_cout, whole((d, d))),
        ],
        [
            (spec_of((tokens, d), BF16), tiled((block, d))),
            (spec_of((items, count, 2 * d), BF16), tiled((group, count, 2 * d))),
            (spec_of((8, d), F32), summed((8, d))),
        ],
        2 * tokens * d * 4 * d,
        [pltpu.VMEM((block, d), BF16)],
    )


def cross_project_back(dims, grad_two, grad_query, grad_kv, total_one, w_cq, w_ckv, rows, parts, part):
    d, items, length, group = dims.d, dims.items, dims.length, dims.group
    tokens, block = items * length, group * length
    count, vis = grad_kv.shape[1], w_ckv.shape[0]

    def body(g_ref, gq_ref, gkv_ref, tot_ref, wcq_ref, wckv_ref, row_ref, *refs):
        grid_refs, (cls_ref, one_ref, onelow_ref, sum_ref) = refs[:parts], refs[parts:]

        @pl.when(pl.program_id(0) == 0)
        def _():
            sum_ref[...] = jnp.zeros_like(sum_ref)

        for i in range(group):
            value = dot_t(gkv_ref[i], wckv_ref[...])
            for k in range(parts):
                grid_refs[k][i * part : (i + 1) * part, :] = value[k * part : (k + 1) * part, :].astype(BF16)
            cls_ref[i] = value[parts * part : parts * part + 1, :]
        grad = g_ref[...] + dot_t(gq_ref[...], wcq_ref[...])
        hat, spread = norm_parts(tot_ref[...])
        one = norm_pull(grad, hat, spread, row_ref[3:4, :])
        one_ref[...] = one
        one_low = one.astype(BF16)
        onelow_ref[...] = one_low
        sum_ref[0:1, :] += col_sum(grad * hat)
        sum_ref[1:2, :] += col_sum(grad)
        sum_ref[2:3, :] += col_sum(one_low)

    return call(
        body,
        "cross_project_back",
        items // group,
        [
            (grad_two, tiled((block, d))),
            (grad_query, tiled((block, d))),
            (grad_kv, tiled((group, count, 2 * d))),
            (total_one, tiled((block, d))),
            (w_cq, whole((d, d))),
            (w_ckv, whole((vis, 2 * d))),
            (rows, whole(rows.shape)),
        ],
        [(spec_of((items * part, vis), BF16), tiled((group * part, vis)))] * parts
        + [
            (spec_of((items, 1, vis), F32), tiled((group, 1, vis))),
            (spec_of((tokens, d), F32), tiled((block, d))),
            (spec_of((tokens, d), BF16), tiled((block, d))),
            (spec_of((8, d), F32), summed((8, d))),
        ],
        2 * tokens * d * d + 2 * items * count * vis * 2 * d,
    )


def self_attend_back(dims, grad_low, qkv, probs, w_out):
    d, items, length, group = dims.d, dims.items, dims.length, dims.group
    pairs, tokens, block = d // (2 * HEAD), items * length, group * length
    scale = HEAD ** (-0.5)

    def body(glow_ref, qkv_ref, prob_ref, wout_ref, gqkv_ref, sum_ref, ctx_ref):
        @pl.when(pl.program_id(0) == 0)
        def _():
            sum_ref[...] = jnp.zeros_like(sum_ref)

        low, high = lane_masks()
        ctx_ref[...] = dot_t(glow_ref[...], wout_ref[...]).astype(BF16)
        for i in range(group):
            r = slice(i * length, (i + 1) * length)
            for p in range(pairs):
                cuts = [slice(part * d + p * 128, part * d + (p + 1) * 128) for part in range(3)]
                q, k, v = (qkv_ref[r, cut] for cut in cuts)
                grad_q, grad_k, grad_v = pair_pull(q, k, v, ctx_ref[r, cuts[0]], prob_ref[i, p], low, high)
                gqkv_ref[r, cuts[0]] = join_heads(grad_q * scale)
                gqkv_ref[r, cuts[1]] = (grad_k * scale).astype(BF16)
                gqkv_ref[r, cuts[2]] = grad_v.astype(BF16)
        sum_ref[0:1, :] += col_sum(gqkv_ref[:, :d])
        sum_ref[1:2, :] += col_sum(gqkv_ref[:, 2 * d :])

    return call(
        body,
        "self_attend_back",
        items // group,
        [
            (grad_low, tiled((block, d))),
            (qkv, tiled((block, 3 * d))),
            (probs, tiled((group, pairs, length, 2 * length))),
            (w_out, whole((d, d))),
        ],
        [
            (spec_of((tokens, 3 * d), BF16), tiled((block, 3 * d))),
            (spec_of((8, d), F32), summed((8, d))),
        ],
        2 * tokens * d * 4 * d,
        [pltpu.VMEM((block, d), BF16)],
    )


def self_project_back(dims, grad_one, grad_qkv, w_qkv):
    d, items, length, group = dims.d, dims.items, dims.length, dims.group
    tokens, block = items * length, group * length

    def body(g_ref, gqkv_ref, wqkv_ref, text_ref):
        text_ref[...] = g_ref[...] + dot_t(gqkv_ref[...], wqkv_ref[...])

    return call(
        body,
        "self_project_back",
        items // group,
        [
            (grad_one, tiled((block, d))),
            (grad_qkv, tiled((block, 3 * d))),
            (w_qkv, whole((d, 3 * d))),
        ],
        [(spec_of((tokens, d), F32), tiled((block, d)))],
        2 * tokens * d * 3 * d,
    )[0]


def cut_grids(turn, image_grid, parts):
    micro, items, part, vis = image_grid.shape
    each = items // parts

    def body(turn_ref, grid_ref, *out_refs):
        def fill(own):
            value = jnp.swapaxes(grid_ref[0], 0, 1)
            for s in range(parts):
                mine = value[s * each : (s + 1) * each]
                out_refs[s ^ own][...] = mine.reshape(each * part, vis)

        for own in range(parts):
            pl.when(turn_ref[0] == own)(functools.partial(fill, own))

    return call(
        body,
        "cut_grids",
        micro,
        [
            (turn, SMEM_SPEC),
            (image_grid.transpose(0, 2, 1, 3), tiled((1, part, items, vis))),
        ],
        [(spec_of((micro * each * part, vis), BF16), tiled((each * part, vis)))] * parts,
        0,
    )


def place_grids(turn, micro, items, pieces):
    part, vis = pieces[0].shape[0] // items, pieces[0].shape[1]
    each, parts = items // micro, len(pieces)

    def body(turn_ref, *refs):
        def fill(own):
            value = [
                refs[s ^ own][...].astype(F32).reshape(each, part, vis) for s in range(parts)
            ]
            refs[-1][0] = jnp.swapaxes(jnp.concatenate(value, 0), 0, 1)

        for own in range(parts):
            pl.when(turn_ref[0] == own)(functools.partial(fill, own))

    shape = (micro, part, each * parts, vis)
    done = call(
        body,
        "place_grids",
        micro,
        [(turn, SMEM_SPEC)] + [(p, tiled((each * part, vis))) for p in pieces],
        [(spec_of(shape, F32), tiled((1,) + shape[1:]))],
        0,
    )[0]
    return done.transpose(0, 2, 1, 3)


def gather_sums(sums, bias):
    d, ff = sums[0].shape[1], bias.shape[1]
    high = -(-(ROWS + ff // d) // 8) * 8

    def body(self_ref, attend_ref, one_ref, two_ref, three_ref, bias_ref, out_ref):
        out_ref[...] = jnp.zeros_like(out_ref)
        at = 0
        for ref, row, count in (
            (self_ref, 0, 2),
            (one_ref, 2, 1),
            (one_ref, 0, 2),
            (attend_ref, 0, 2),
            (two_ref, 2, 1),
            (two_ref, 0, 2),
            (three_ref, 2, 1),
            (three_ref, 0, 2),
        ):
            out_ref[at : at + count, :] = ref[row : row + count, :]
            at += count
        for n in range(ff // d):
            out_ref[at + n : at + n + 1, :] = bias_ref[0:1, n * d : (n + 1) * d]

    return pl.pallas_call(
        body,
        out_shape=spec_of((high, d), F32),
        in_specs=[VMEM_SPEC] * 6,
        out_specs=VMEM_SPEC,
        compiler_params=PARAMS,
        name="gather_sums",
    )(*sums, bias)


def weight_grads(plan, group, where, factors):
    high_rows = max(plan.full[w][0] for w in group)
    wide = max(plan.full[w][1] for w in group)
    flat = [a for pair in factors for a in pair]
    count = len(flat)

    def body(where_ref, *refs):
        far, stack_refs = refs[:count], refs[count : count + 2]
        near, made, sems = refs[count + 2 : 2 * count + 2], refs[-2], refs[-1]
        copies = [pltpu.make_async_copy(far[n], near[n], sems.at[n]) for n in range(count)]
        for copy in copies:
            copy.start()
        for n, w in enumerate(group):
            left, right = near[2 * n], near[2 * n + 1]
            rows, cols = plan.full[w]
            copies[2 * n].wait()
            copies[2 * n + 1].wait()
            for at in range(0, rows, 256):
                value = dot_l(left[:, at : at + 256], right[...])
                made[at : at + 256, :cols] = value.astype(BF16)

            def visit(other, second, first, k, row, w_at, j, to_row, to_y, high):
                if w_at == w:
                    col = pl.multiple_of(to_y * (cols // 2) + j * plan.chunk, 128)
                    stack_refs[other][second * 2 + first, k, row : row + high, :] = made[
                        pl.ds(to_row, high), pl.ds(col, plan.chunk)
                    ]

            each_place(plan, group, where_ref, visit)

    shape = jax.ShapeDtypeStruct((4, plan.zs, plan.rows(group), plan.chunk), BF16)
    flops = sum(2 * a.shape[0] * a.shape[1] * b.shape[1] for a, b in factors)
    moved = sum(a.size * 2 for a in flat) + 2 * shape.size * 2
    return pl.pallas_call(
        body,
        out_shape=(shape,) * 2,
        in_specs=[SMEM_SPEC] + [pl.BlockSpec(memory_space=pl.ANY)] * count,
        out_specs=(VMEM_SPEC,) * 2,
        scratch_shapes=[pltpu.VMEM(a.shape, BF16) for a in flat]
        + [pltpu.VMEM((high_rows, wide), BF16), pltpu.SemaphoreType.DMA((count,))],
        compiler_params=PARAMS,
        cost_estimate=pl.CostEstimate(flops=flops, bytes_accessed=moved, transcendentals=0),
        name="weight_grads",
    )(where, *flat)


class Dims:
    def __init__(self, d, items, length):
        self.d, self.items, self.length = d, items, length
        self.group = 2 if items % 2 == 0 else 1


def cross_mask(lengths, counts, boxes, length, count):
    place = jnp.arange(length, dtype=jnp.int32)[None, :]
    boxed = (counts[:, None] > 0) & (place < lengths[:, None])
    phrase = jnp.where(boxed, place * counts[:, None] // lengths[:, None], 0)
    chosen = phrase[:, None, :] == jnp.arange(boxes.shape[1], dtype=jnp.int32)[None, :, None]
    inside = jnp.einsum(
        "ijp,ijt->ipt",
        (boxes > 0).astype(BF16),
        chosen.astype(BF16),
        preferred_element_type=F32,
    )
    grid_ok = jnp.where(boxed[:, None, :], inside, 1.0).astype(BF16)
    items, real = grid_ok.shape[:2]
    own = jnp.ones((items, 1, length), BF16)
    return jnp.concatenate([grid_ok, own, jnp.zeros((items, count - real - 1, length), BF16)], 1)


def trade(pieces):
    parts = lax.axis_size("patch")
    return [pieces[0]] + [
        lax.ppermute(pieces[k], "patch", [(i, i ^ k) for i in range(parts)])
        for k in range(1, len(pieces))
    ]


class Work:
    def __init__(self, args, parts):
        (self.text_in, self.image_grid, self.image_cls, lengths, counts, boxes, cot) = args
        self.parts = parts
        self.micro, d = self.text_in.shape[0], self.text_in.shape[2]
        self.items = lengths.size
        self.text, self.cot = self.text_in.reshape(-1, d), cot.reshape(-1, d)
        self.lengths, self.counts = lengths.reshape(-1), counts.reshape(-1)
        self.boxes = boxes.reshape((self.items,) + boxes.shape[2:])
        self.dims = Dims(d, self.items, self.text.shape[0] // self.items)
        self.turn = lax.axis_index("patch").astype(jnp.int32).reshape(1)
        self.part, self.vis = self.image_grid.shape[2:]
        self.each = self.items // self.micro
        self.count = -(-(parts * self.part + 1) // 16) * 16
        self.cls = self.image_cls.reshape(self.items, 1, self.vis)

    def mask(self):
        boxes = self.boxes.reshape(self.items, -1, self.parts, self.part)
        order = jnp.arange(self.parts, dtype=jnp.int32) ^ self.turn[0]
        boxes = jnp.take(boxes, order, axis=2).reshape(self.boxes.shape)
        return cross_mask(self.lengths, self.counts, boxes, self.dims.length, self.count)

    def finish(self, layer_out, text_grad, grid_grad, cls, grads, rows_grad, bias_grad):
        return (
            layer_out.reshape(self.text_in.shape),
            text_grad.reshape(self.text_in.shape),
            grid_grad,
            cls.reshape(self.image_cls.shape),
            *grads,
            rows_grad,
            bias_grad,
        )


def on_device(plan, *args):
    work, shards, vectors, ffn_bias = Work(args[:7], plan.patch), args[7:14], args[14], args[15]
    dims, where, parts = work.dims, coords(), plan.patch

    own, give = pack_split(plan, where, shards)
    units = pack_join(plan, where, own, send(give, plan.core()))
    grids = list(cut_grids(work.turn, work.image_grid, parts))
    vectors, bias, grids, units = lax.optimization_barrier((vectors, ffn_bias, grids, units))
    one, two, three = (Gathering(plan, unit) for unit in units)
    small = GatheringSmall(plan, where, vectors, bias)

    def source(g, gather):
        return Source(plan, GATHER[g], where, gather.held)

    one.along_z(*range(1, plan.zs))
    grids[2] = trade(grids[:3])[2]
    small.advance()
    grids = fence([one, two, small], grids)
    one.first()
    two.along_z(*range(1, plan.zs // 2 + 1))
    grids[3] = trade(grids)[3]
    small.advance()
    grids = fence([one, two, three, small], grids)
    one.second()
    two.along_z(*range(plan.zs // 2 + 1, plan.zs))
    rows, bias = small.result()
    rows, bias, grids = fence([one, two, three], [rows, bias, grids])
    one.core()
    two.first()
    three.along_z(*range(1, plan.zs // 2 + 1))
    (qkv, probs, ctx), (w_qkv,) = self_forward(dims, source(0, one), work.text, rows, work.lengths)
    (ctx,) = fence([two, three], [ctx])
    two.second()
    three.along_z(*range(plan.zs // 2 + 1, plan.zs))
    grids[1] = trade(grids[:2])[1]
    mask = work.mask()
    ctx, grids, mask = fence([two, three], [ctx, grids, mask])
    two.core()
    three.first()
    (kv, patches), (w_out, w_cq, w_ckv, w_cout) = cross_keys(
        dims, source(1, two), grids, work.cls, rows, work.count
    )
    kv, ctx = fence([three], [kv, ctx])
    three.second()
    total_one, hidden_one, query, cross_probs, cross_ctx, total_two = cross_forward(
        dims, work.text, ctx, kv, mask, w_out, w_cq, w_cout, rows
    )
    total_two = fence([three], total_two)
    three.core()
    (layer_out, hidden_two, act, slope, grad_three, low_three, sum_three), (w_fin, w_fout) = ffn_forward(
        dims, source(2, three), total_two, work.cot, rows, bias
    )

    reduces = {}

    def reduce(g, factors):
        stacks = weight_grads(plan, REDUCE[g], where, factors)
        reduces[g] = Reducing(plan, REDUCE[g], where, stacks)

    def hold(*values, on=None):
        chains = [reduces[g] for g in (reduces if on is None else on)]
        return fence(chains, list(values))

    def go(*groups):
        for g in groups:
            reduces[g].advance()

    reduce(3, [(act, low_three)])
    (grad_three,) = hold(grad_three)
    go(3)
    grad_pre, grad_two, low_two, sum_two, sum_pre = ffn_backward(
        dims, grad_three, low_three, slope, total_two, w_fin, w_fout, rows
    )
    grad_pre, low_two = hold(grad_pre, low_two)
    go(3)
    reduce(2, [(hidden_two, grad_pre)])
    (low_two,) = hold(low_two)
    go(3, 2)
    grad_query, grad_kv, sum_attend = cross_attend_back(dims, low_two, query, kv, cross_probs, w_cout)
    grad_query, grad_kv = hold(grad_query, grad_kv)
    go(2, 3)
    reduce(
        1,
        [
            (hidden_one, grad_query),
            (patches.reshape(-1, work.vis), grad_kv.reshape(-1, grad_kv.shape[2])),
            (cross_ctx, low_two),
        ],
    )
    grad_query, grad_kv = hold(grad_query, grad_kv)
    go(2, 3, 1)
    *grids, cls, grad_one, low_one, sum_one = cross_project_back(
        dims, grad_two, grad_query, grad_kv, total_one, w_cq, w_ckv, rows, parts, work.part
    )
    low_one, *grids = hold(low_one, *grids)
    go(1, 3, 2)
    grids[1] = trade(grids[:2])[1]
    grad_qkv, sum_self = self_attend_back(dims, low_one, qkv, probs, w_out)
    grad_qkv, sum_self, *grids = hold(grad_qkv, sum_self, *grids)
    go(1, 2, 3)
    grids[2] = trade(grids[:3])[2]
    reduce(0, [(work.text, grad_qkv), (ctx, low_one)])
    sums = [sum_self, sum_attend, sum_one, sum_two, sum_three]
    reduces["small"] = ReducingSmall(plan, where, sums, sum_pre)
    grad_qkv, *grids = hold(grad_qkv, *grids)
    go(0, 1, 2, "small")
    text_grad = self_project_back(dims, grad_one, grad_qkv, w_qkv)
    (text_grad,) = hold(text_grad)
    go(0, 1, 2, "small")
    hold()
    go(0, 1, "small")
    hold()
    go(0, 0, 1, "small")
    grids[3] = trade(grids)[3]
    grids = hold(*grids)
    go(0, "small")
    grid_grad = place_grids(work.turn, work.micro, work.items, grids)
    go(0)
    grads = [None] * 7
    for g, group in enumerate(REDUCE):
        for w, value in zip(group, reduces[g].held):
            grads[w] = value
    return work.finish(layer_out, text_grad, grid_grad, cls, grads, *reduces["small"].result())


def on_device_plain(plan, *args):
    work, parts = Work(args[:7], plan.patch), plan.patch
    dims = work.dims
    weights, rows, bias = fetch_plain(args[7:14], args[14], args[15])
    rows = jnp.pad(rows, ((0, -rows.shape[0] % 8), (0, 0)))
    grids = trade(cut_grids(work.turn, work.image_grid, parts))

    def source(g):
        return Source(plan, GATHER[g], None, [weights[w] for w in GATHER[g]])

    (qkv, probs, ctx), _ = self_forward(dims, source(0), work.text, rows, work.lengths)
    (kv, patches), _ = cross_keys(dims, source(1), grids, work.cls, rows, work.count)
    total_one, hidden_one, query, cross_probs, cross_ctx, total_two = cross_forward(
        dims, work.text, ctx, kv, work.mask(), weights[OUT], weights[CQ], weights[COUT], rows
    )
    (layer_out, hidden_two, act, slope, grad_three, low_three, sum_three), _ = ffn_forward(
        dims, source(2), total_two, work.cot, rows, bias[None]
    )
    grad_pre, grad_two, low_two, sum_two, sum_pre = ffn_backward(
        dims, grad_three, low_three, slope, total_two, weights[FIN], weights[FOUT], rows
    )
    grad_query, grad_kv, sum_attend = cross_attend_back(
        dims, low_two, query, kv, cross_probs, weights[COUT]
    )
    *grids, cls, grad_one, low_one, sum_one = cross_project_back(
        dims, grad_two, grad_query, grad_kv, total_one, weights[CQ], weights[CKV], rows, parts, work.part
    )
    grad_qkv, sum_self = self_attend_back(dims, low_one, qkv, probs, weights[OUT])
    text_grad = self_project_back(dims, grad_one, grad_qkv, weights[QKV])
    flat_kv = grad_kv.reshape(-1, grad_kv.shape[2])
    factors = [
        (work.text, grad_qkv),
        (ctx, low_one),
        (hidden_one, grad_query),
        (patches.reshape(-1, work.vis), flat_kv),
        (cross_ctx, low_two),
        (hidden_two, grad_pre),
        (act, low_three),
    ]
    grads = [reduce_plain(dot_l(a, b).astype(BF16)) for a, b in factors]
    sums = gather_sums([sum_self, sum_attend, sum_one, sum_two, sum_three], sum_pre)
    small = reduce_small_plain(sums[:ROWS], sum_pre[0])
    grid_grad = place_grids(work.turn, work.micro, work.items, trade(grids))
    return work.finish(layer_out, text_grad, grid_grad, cls, grads, *small)


def solution(mesh):
    dp, patch = mesh.shape["dp"], mesh.shape["patch"]
    both = P(None, ("dp", "patch"), None)
    weight = P("dp", "patch")

    def run(*args):
        shards = [(w.shape[0] // dp, w.shape[1] // patch) for w in args[7:14]]
        plan = Plan(dp, patch, shards)
        return jax.shard_map(
            functools.partial(on_device if plan.fast else on_device_plain, plan),
            mesh=mesh,
            in_specs=(
                both,
                P(None, "dp", "patch", None),
                both,
                P(None, ("dp", "patch")),
                P(None, ("dp", "patch")),
                P(None, ("dp", "patch"), None, None),
                both,
            )
            + (weight,) * 7
            + (P(None, "dp"), P("dp")),
            out_specs=(both, both, P(None, "dp", "patch", None), both)
            + (weight,) * 7
            + (P(None, "dp"), P("dp")),
            check_vma=False,
        )(*args)

    return run
```

```python
import functools

import jax
import jax.numpy as jnp
from jax import lax
from jax.experimental import pallas as pl
from jax.experimental.pallas import tpu as pltpu
from jax.sharding import PartitionSpec as P

HEAD = 64
EPS = 1e-06
NEG = -1e30
BF16 = jnp.bfloat16
F32 = jnp.float32
AXES = ("dp", "patch")
VMEM_SPEC = pl.BlockSpec(memory_space=pltpu.VMEM)
SMEM_SPEC = pl.BlockSpec(memory_space=pltpu.SMEM)
PARAMS = pltpu.CompilerParams(vmem_limit_bytes=62 * 2**20)

QKV, OUT, CQ, CKV, COUT, FIN, FOUT = range(7)
ROWS = 13
GATHER = ((QKV,), (OUT, CQ, CKV, COUT), (FIN, FOUT))
REDUCE = ((QKV, OUT), (CQ, CKV, COUT), (FIN, FOUT))


class Plan:
    def __init__(self, dp, patch, shards):
        self.dp, self.patch = dp, patch
        self.zs = dp // 2
        self.devices = dp * patch
        self.chunk = shards[OUT][1] * 2
        self.half = [s[0] // 2 for s in shards]
        self.cols = [s[1] for s in shards]
        self.chunks = [s[1] * 2 // self.chunk for s in shards]
        self.full = [(s[0] * dp, s[1] * patch) for s in shards]
        self.fast = (
            dp % 2 == 0
            and self.zs & (self.zs - 1) == 0
            and patch == 4
            and all(h % 16 == 0 for h in self.half)
            and all(s[1] * 2 % self.chunk == 0 for s in shards)
            and self.chunk % 128 == 0
        )

    def rows(self, group):
        return sum(self.half[w] * self.chunks[w] for w in group)

    def flip(self, pick):
        return [(i, i ^ pick(i)) for i in range(self.devices)]

    def core(self):
        return self.flip(lambda i: 1)

    def first(self):
        return self.flip(lambda i: 4 if i % 2 == 0 else 2)

    def second(self):
        return self.flip(lambda i: 2 if i % 2 == 0 else 4)

    def along_z(self, k):
        return self.flip(lambda i: 8 * k)


def send(value, perm):
    return lax.ppermute(value, AXES, perm)


def coords():
    dp, patch = lax.axis_index("dp"), lax.axis_index("patch")
    return jnp.stack([dp // 2, dp % 2, patch // 2, patch % 2]).astype(jnp.int32)


def piece_rows(group, plan):
    at, found = 0, []
    for w in group:
        for j in range(plan.chunks[w]):
            found.append((w, j, at))
            at += plan.half[w]
    return found


def group_starts(plan):
    starts, at = [], 0
    for group in GATHER:
        starts.append(at)
        at += plan.rows(group)
    return starts, at


def pack_split(plan, where, shards):
    _, total = group_starts(plan)
    wide = plan.chunk // 2

    def body(where_ref, *refs):
        shard_refs, (own_ref, send_ref, turned) = list(refs[:7]), refs[7:]
        core = where_ref[3]
        turned[...] = shard_refs[FOUT][...].T
        shard_refs[FOUT] = turned
        at = 0
        for group in GATHER:
            for w in group:
                high = plan.half[w]
                for b in range(plan.chunks[w]):
                    cut = slice(b * wide, (b + 1) * wide)
                    own_ref[at : at + high, :] = shard_refs[w][pl.ds(core * high, high), cut]
                    send_ref[at : at + high, :] = shard_refs[w][
                        pl.ds((1 - core) * high, high), cut
                    ]
                    at += high

    shape = jax.ShapeDtypeStruct((total, wide), BF16)
    return pl.pallas_call(
        body,
        out_shape=(shape, shape),
        in_specs=[SMEM_SPEC] + [VMEM_SPEC] * 7,
        out_specs=(VMEM_SPEC, VMEM_SPEC),
        scratch_shapes=[pltpu.VMEM(shards[FOUT].shape, BF16)],
        compiler_params=PARAMS,
        name="pack_split",
    )(where, *shards[:FOUT], shards[FOUT].T)


def pack_join(plan, where, own, got):
    starts, total = group_starts(plan)
    wide = plan.chunk // 2

    def body(where_ref, own_ref, got_ref, *unit_refs):
        core = where_ref[3]

        def fill(low_ref, high_ref):
            for g, group in enumerate(GATHER):
                at = starts[g]
                for w in group:
                    high, count = plan.half[w], plan.chunks[w]
                    for j in range(count):
                        pair = []
                        for b in (2 * j, 2 * j + 1):
                            src = low_ref if b < count else high_ref
                            row = at + (b % count) * high
                            pair.append(src[row : row + high, :])
                        to = at - starts[g] + j * high
                        unit_refs[g][to : to + high, :] = jnp.concatenate(pair, axis=1)
                    at += count * high

        @pl.when(core == 0)
        def _():
            fill(own_ref, got_ref)

        @pl.when(core == 1)
        def _():
            fill(got_ref, own_ref)

    return pl.pallas_call(
        body,
        out_shape=tuple(jax.ShapeDtypeStruct((plan.rows(g), plan.chunk), BF16) for g in GATHER),
        in_specs=[SMEM_SPEC, VMEM_SPEC, VMEM_SPEC],
        out_specs=(VMEM_SPEC,) * len(GATHER),
        compiler_params=PARAMS,
        name="pack_join",
    )(where, own, got)


class Gathering:
    def __init__(self, plan, unit):
        self.plan, self.held = plan, [unit]

    def along_z(self, *steps):
        self.held += [send(self.held[0], self.plan.along_z(k)) for k in steps]

    def first(self):
        stack = jnp.stack(self.held)
        self.held = [stack, send(stack, self.plan.first())]

    def second(self):
        near = jnp.stack(self.held)
        self.held = [near, send(near, self.plan.second()), send(near, self.plan.core())]

    def core(self):
        self.held.append(send(self.held[1], self.plan.core()))


def each_place(plan, group, where_ref, visit):
    z, x, y, core = (where_ref[i] for i in range(4))
    for other in range(2):
        half = core ^ other
        for second in range(2):
            for first in range(2):
                x_at = x ^ jnp.where(half == 0, first, second)
                y_at = y ^ jnp.where(half == 0, second, first)
                for k in range(plan.zs):
                    place = ((z ^ k) * 2 + x_at) * 2 + half
                    for w, j, row in piece_rows(group, plan):
                        high = plan.half[w]
                        to_row = pl.multiple_of(place * high, 16)
                        visit(other, second, first, k, row, w, j, to_row, y_at, high)


def add_low(ones, twos, widths):
    count, slots, rows, chunk = ones.shape
    parts = [two.shape[0] for two in twos]

    def body(one_ref, *refs):
        two_refs, out_refs = refs[: len(parts)], refs[len(parts) :]
        twice = [ref.at[n] for ref, part in zip(two_refs, parts) for n in range(part)]
        outs = [ref.at[n] for ref, width in zip(out_refs, widths) for n in range(width)]
        for n in range(count):
            outs[n][...] = (one_ref[n].astype(F32) + twice[n][...].astype(F32)).astype(BF16)

    def spec(n):
        return pl.BlockSpec((n, 1, rows, chunk), lambda i: (0, i, 0, 0))

    return pl.pallas_call(
        body,
        grid=(slots,),
        out_shape=tuple(jax.ShapeDtypeStruct((n, slots, rows, chunk), BF16) for n in widths),
        in_specs=[spec(count)] + [spec(n) for n in parts],
        out_specs=tuple(spec(n) for n in widths),
        compiler_params=PARAMS,
        cost_estimate=pl.CostEstimate(
            flops=ones.size, bytes_accessed=6 * ones.size, transcendentals=0
        ),
        name="add_low",
    )(ones, *twos)


def add_slots(ones, twos):
    _, slots, rows, chunk = ones.shape

    def body(one_ref, two_ref, *out_refs):
        for n in range(slots):
            out_refs[n][...] = (one_ref[0, n].astype(F32) + two_ref[0, n].astype(F32)).astype(BF16)

    return pl.pallas_call(
        body,
        out_shape=(jax.ShapeDtypeStruct((rows, chunk), BF16),) * slots,
        in_specs=[VMEM_SPEC, VMEM_SPEC],
        out_specs=(VMEM_SPEC,) * slots,
        compiler_params=PARAMS,
        cost_estimate=pl.CostEstimate(
            flops=ones.size, bytes_accessed=6 * ones.size, transcendentals=0
        ),
        name="add_slots",
    )(ones, twos)


class Reducing:
    def __init__(self, plan, group, where, stacks, twice=False):
        self.plan, self.group, self.where, self.twice = plan, group, where, twice
        self.held = list(stacks)
        self.steps = [self.core, self.second] + [self.again] * twice
        self.steps += [self.first, self.near_z, self.far_z, self.split, self.join]

    def advance(self):
        self.held = list(self.steps.pop(0)(*self.held))

    def core(self, keep, give):
        return keep, send(give, self.plan.core())

    def second(self, keep, got):
        keep, give, *rest = add_low(keep, [got], (2, 1, 1) if self.twice else (2, 2))
        return keep, send(give, self.plan.second()), *rest

    def again(self, keep, got, give):
        return keep, got, send(give, self.plan.second())

    def first(self, keep, *got):
        keep, give = add_low(keep, got, (1, 1))
        return keep, send(give, self.plan.first())

    def near_z(self, keep, got):
        plan, slots = self.plan, list(add_slots(keep, got))
        for k in range(1, plan.zs // 2 + 1):
            slots[k] = send(slots[k], plan.along_z(k))
        return slots

    def far_z(self, *slots):
        plan, slots = self.plan, list(slots)
        for k in range(plan.zs // 2 + 1, plan.zs):
            slots[k] = send(slots[k], plan.along_z(k))
        return slots

    def split(self, *parts):
        own, give = unpack_split(self.plan, self.group, self.where, parts)
        return own, send(give, self.plan.core())

    def join(self, own, got):
        return unpack_join(self.plan, self.group, self.where, own, got)


def fence(chains, values):
    flat, tree = jax.tree.flatten([values, [chain.held for chain in chains]])
    values, held = jax.tree.unflatten(tree, lax.optimization_barrier(flat))
    for chain, arrays in zip(chains, held):
        chain.held = arrays
    return values


def unpack_split(plan, group, where, parts):
    rows, wide = plan.rows(group), plan.chunk // 2

    def body(where_ref, *refs):
        part_refs, (own_ref, give_ref) = refs[:-2], refs[-2:]
        core = where_ref[3]

        def fill(low_ref, high_ref):
            at = 0
            for w in group:
                high, count = plan.half[w], plan.chunks[w]
                for j in range(count):
                    row = at + j * high
                    value = sum(p[row : row + high, :].astype(F32) for p in part_refs)
                    for b in (2 * j, 2 * j + 1):
                        dst = low_ref if b < count else high_ref
                        to = at + (b % count) * high
                        cut = (b - 2 * j) * wide
                        dst[to : to + high, :] = value[:, cut : cut + wide]
                at += count * high

        @pl.when(core == 0)
        def _():
            fill(own_ref, give_ref)

        @pl.when(core == 1)
        def _():
            fill(give_ref, own_ref)

    shape = jax.ShapeDtypeStruct((rows, wide), F32)
    return pl.pallas_call(
        body,
        out_shape=(shape, shape),
        in_specs=[SMEM_SPEC] + [VMEM_SPEC] * len(parts),
        out_specs=(VMEM_SPEC, VMEM_SPEC),
        compiler_params=PARAMS,
        name="unpack_split",
    )(where, *parts)


def unpack_join(plan, group, where, own, got):
    wide = plan.chunk // 2
    turned = [w == FOUT for w in group]

    def body(where_ref, own_ref, got_ref, *refs):
        core = where_ref[3]
        at = 0
        for n, w in enumerate(group):
            out_ref = refs[-1] if turned[n] else refs[n]
            high, count = plan.half[w], plan.chunks[w]
            own_rows = pl.ds(pl.multiple_of(core * high, 16), high)
            got_rows = pl.ds(pl.multiple_of((1 - core) * high, 16), high)
            for b in range(count):
                row, cut = at + b * high, slice(b * wide, (b + 1) * wide)
                out_ref[own_rows, cut] = own_ref[row : row + high, :]
                out_ref[got_rows, cut] = got_ref[row : row + high, :]
            at += count * high
            if turned[n]:
                refs[n][...] = out_ref[...].T

    shapes = [(2 * plan.half[w], plan.cols[w]) for w in group]
    done = pl.pallas_call(
        body,
        out_shape=tuple(
            jax.ShapeDtypeStruct(shape[::-1] if turn else shape, F32)
            for shape, turn in zip(shapes, turned)
        ),
        in_specs=[SMEM_SPEC, VMEM_SPEC, VMEM_SPEC],
        out_specs=(VMEM_SPEC,) * len(group),
        scratch_shapes=[pltpu.VMEM(shapes[-1], F32)],
        compiler_params=PARAMS,
        name="unpack_join",
    )(where, own, got)
    return [value.T if turn else value for value, turn in zip(done, turned)]


class GatheringSmall:
    def __init__(self, plan, where, vectors, bias):
        self.plan, self.where, self.shape = plan, where, vectors.shape
        flat = jnp.concatenate([vectors.reshape(-1), bias])
        self.size = flat.shape[0]
        self.held, self.bit = [jnp.pad(flat, (0, -self.size % 2048)).reshape(1, -1, 128)], 4

    def advance(self):
        every = jnp.concatenate(self.held)
        self.held = [every, send(every, self.plan.flip(lambda i: self.bit))]
        self.bit *= 2

    def result(self):
        plan, (count, part) = self.plan, self.shape
        while self.bit < plan.devices:
            self.advance()
        every = jnp.concatenate(self.held).reshape(plan.dp, -1)
        slot = jnp.arange(plan.dp, dtype=jnp.int32) ^ (self.where[0] * 2 + self.where[1])
        every = jnp.take(every, slot, axis=0)[:, : self.size].astype(F32)
        rows = every[:, : count * part].reshape(plan.dp, count, part)
        rows = rows.transpose(1, 0, 2).reshape(count, plan.dp * part)
        bias = every[:, count * part :].reshape(1, -1)
        return jnp.pad(rows, ((0, -count % 8), (0, 0))), bias


class ReducingSmall:
    def __init__(self, plan, where, sums, bias):
        self.plan, self.where, self.tail = plan, where, bias.shape[1]
        self.held, self.step = [gather_sums(sums, bias)], 0
        bits = [1, 2, 4]
        while 1 << len(bits) < plan.devices:
            bits.append(1 << len(bits))
        self.bits = bits

    def advance(self):
        flat = sum(self.held)
        if self.bits:
            bit = self.bits.pop(0)
            self.held = [flat, send(flat, self.plan.flip(lambda i: bit))]
        else:
            self.held = [flat]

    def result(self):
        plan, flat = self.plan, sum(self.held)
        width = flat.shape[1] // plan.dp
        dp = self.where[0] * 2 + self.where[1]
        own = lax.dynamic_slice_in_dim(flat[:ROWS], dp * width, width, axis=1)
        tail, step = flat[ROWS : ROWS + self.tail // flat.shape[1]].reshape(-1), self.tail // plan.dp
        return own, lax.dynamic_slice_in_dim(tail, dp * step, step, axis=0)


def fetch_plain(weights, vectors, bias):
    whole = [
        lax.all_gather(lax.all_gather(w, "dp", axis=0, tiled=True), "patch", axis=1, tiled=True)
        for w in weights
    ]
    rows = lax.all_gather(vectors, "dp", axis=1, tiled=True)
    return whole, rows.astype(F32), lax.all_gather(bias, "dp", axis=0, tiled=True).astype(F32)


def reduce_plain(grad):
    part = lax.psum_scatter(grad, "dp", scatter_dimension=0, tiled=True)
    return lax.psum_scatter(part, "patch", scatter_dimension=1, tiled=True).astype(F32)


def reduce_small_plain(rows, bias):
    rows = lax.psum_scatter(rows, "dp", scatter_dimension=1, tiled=True)
    bias = lax.psum_scatter(bias, "dp", scatter_dimension=0, tiled=True)
    return lax.psum(rows, "patch"), lax.psum(bias, "patch")


TAIL = (0.112528827, 0.117839666, 0.0706314405, 0.2046457425, -0.190499398, 0.3478185715, -0.201092832, 0.03812798145)


def dot(a, b):
    return lax.dot_general(a, b, (((1,), (0,)), ((), ())), preferred_element_type=F32)


def dot_t(a, b):
    return lax.dot_general(a, b, (((1,), (1,)), ((), ())), preferred_element_type=F32)


def dot_l(a, b):
    return lax.dot_general(a, b, (((0,), (0,)), ((), ())), preferred_element_type=F32)


def norm_parts(total):
    center = total - jnp.mean(total, -1, keepdims=True)
    spread = lax.rsqrt(jnp.mean(center * center, -1, keepdims=True) + EPS)
    return center * spread, spread


def norm_pull(grad, hat, spread, gain):
    scaled = grad * gain
    return spread * (
        scaled
        - jnp.mean(scaled, -1, keepdims=True)
        - hat * jnp.mean(scaled * hat, -1, keepdims=True)
    )


def gelu_parts(x):
    bell = jnp.exp(-0.5 * (x * x))
    t = 1.0 / (1.0 + (0.4 * 0.5**0.5) * jnp.abs(x))
    tail = jnp.full_like(t, TAIL[-1])
    for c in TAIL[-2::-1]:
        tail = tail * t + c
    tail = tail * (t * bell)
    return jnp.where(x < 0.0, tail, 1.0 - tail), bell


def col_sum(value):
    return jnp.sum(value.astype(F32), 0, keepdims=True)


def soft(scores):
    grown = jnp.exp(scores - jnp.max(scores, 0, keepdims=True))
    return grown * (1.0 / jnp.sum(grown, 0, keepdims=True))


def soft_pull(probs, grad):
    return probs * (grad - jnp.sum(probs * grad, 0, keepdims=True))


def spread_heads(value, low, high):
    return jnp.concatenate([value * low, value * high], 0)


def join_heads(value):
    count = value.shape[1] // 2
    value = jnp.concatenate([value[:HEAD, :count], value[HEAD:, count:]], 0)
    return value.astype(BF16).T


def lane_masks():
    lane = lax.broadcasted_iota(jnp.int32, (1, 2 * HEAD), 1)
    low = (lane < HEAD).astype(F32)
    return low.astype(BF16), (1.0 - low).astype(BF16)


def whole(shape):
    return pl.BlockSpec(
        shape, lambda i: (0,) * len(shape), pipeline_mode=pl.Buffered(1)
    )


def summed(shape):
    return pl.BlockSpec(shape, lambda i: (0,) * len(shape))


def tiled(shape):
    return pl.BlockSpec(shape, lambda i: (i,) + (0,) * (len(shape) - 1))


def spec_of(shape, dtype):
    return jax.ShapeDtypeStruct(shape, dtype)


def call(body, name, steps, ins, outs, flops, scratch=()):
    out_shape = tuple(shape for shape, _ in outs)
    moved = sum(a.size * a.dtype.itemsize for a, _ in ins)
    moved += sum(o.size * jnp.dtype(o.dtype).itemsize for o in out_shape)
    return pl.pallas_call(
        body,
        grid=(steps,),
        out_shape=out_shape,
        in_specs=[spec for _, spec in ins],
        out_specs=tuple(spec for _, spec in outs),
        scratch_shapes=list(scratch),
        compiler_params=PARAMS,
        cost_estimate=pl.CostEstimate(
            flops=int(flops), bytes_accessed=int(moved), transcendentals=0
        ),
        name=name,
    )(*[a for a, _ in ins])


class Source:
    def __init__(self, plan, group, where, given, kept=True):
        self.plan, self.group, self.pieces, self.given = plan, group, plan.fast, given
        self.outs, self.scratch = [], []
        if not self.pieces:
            self.ins = [(w, whole(w.shape)) for w in given]
            return
        self.ins = [(where, SMEM_SPEC)] + [(part, whole(part.shape)) for part in given]
        if kept:
            self.outs = [(spec_of(plan.full[w], BF16), summed(plan.full[w])) for w in group]
        else:
            self.scratch = [pltpu.VMEM(plan.full[w], BF16) for w in group]

    def open(self, in_refs, out_refs):
        if not self.pieces:
            return list(in_refs)
        where_ref, parts = in_refs[0], in_refs[1:]
        full = dict(zip(self.group, out_refs))
        plan = self.plan

        def visit(other, second, first, k, row, w, j, to_row, to_y, high):
            to_col = pl.multiple_of(to_y * (plan.full[w][1] // 2) + j * plan.chunk, 128)
            part = parts[other * 2 + second]
            full[w][pl.ds(to_row, high), pl.ds(to_col, plan.chunk)] = part[
                first, k, row : row + high, :
            ]

        @pl.when(pl.program_id(0) == 0)
        def _():
            each_place(plan, self.group, where_ref, visit)

        return list(out_refs)

    def split(self, done):
        if not self.pieces:
            return done, self.given
        return done[: -len(self.group)], done[-len(self.group) :]


def self_forward(dims, source, text, rows, lengths):
    d, items, length, group = dims.d, dims.items, dims.length, dims.group
    pairs, tokens, block = d // (2 * HEAD), items * length, group * length
    scale = HEAD ** (-0.5)

    n_in = len(source.ins)

    def body(len_ref, x_ref, row_ref, *refs):
        qkv_ref, prob_ref, ctx_ref = refs[n_in : n_in + 3]
        (wqkv_ref,) = source.open(refs[:n_in], refs[n_in + 3 :])
        step = pl.program_id(0)
        low, high = lane_masks()
        x = x_ref[...]
        for part, bias in ((0, 0), (1, None), (2, 1)):
            cut = slice(part * d, (part + 1) * d)
            value = dot(x, wqkv_ref[:, cut])
            if bias is not None:
                value = value + row_ref[bias : bias + 1, :]
            qkv_ref[:, cut] = value.astype(BF16)
        place = lax.broadcasted_iota(jnp.int32, (length, 1), 0)
        for i in range(group):
            ok = place < len_ref[step * group + i]
            r = slice(i * length, (i + 1) * length)
            for p in range(pairs):
                q, k, v = (
                    qkv_ref[r, part * d + p * 128 : part * d + (p + 1) * 128] for part in range(3)
                )
                scores = dot_t(k, spread_heads(q, low, high)) * scale
                probs = soft(jnp.where(ok, scores, NEG)).astype(BF16)
                prob_ref[i, p] = probs
                ctx_ref[r, p * 128 : (p + 1) * 128] = join_heads(dot(v.T, probs))
    done = call(
        body,
        "self_forward",
        items // group,
        [(lengths, SMEM_SPEC), (text, tiled((block, d))), (rows, whole(rows.shape))] + source.ins,
        [
            (spec_of((tokens, 3 * d), BF16), tiled((block, 3 * d))),
            (spec_of((items, pairs, length, 2 * length), BF16), tiled((group, pairs, length, 2 * length))),
            (spec_of((tokens, d), BF16), tiled((block, d))),
        ]
        + source.outs,
        2 * tokens * d * 5 * d,
    )
    return source.split(done)


def cross_keys(dims, source, grids, cls, rows, count):
    d, items, group = dims.d, dims.items, dims.group
    part, vis, parts = grids[0].shape[0] // items, cls.shape[2], len(grids)
    n_in = len(source.ins)

    def body(*refs):
        grid_refs, cls_ref, row_ref = refs[:parts], refs[parts], refs[parts + 1]
        refs = refs[parts + 2 :]
        kv_ref, patch_ref = refs[n_in : n_in + 2]
        _, _, wckv_ref, _ = source.open(refs[:n_in], refs[n_in + 2 :])
        for i in range(group):
            for k in range(parts):
                patch_ref[i, k * part : (k + 1) * part, :] = grid_refs[k][i * part : (i + 1) * part, :]
            rest = jnp.zeros((count - parts * part - 1, vis), BF16)
            patch_ref[i, parts * part :, :] = jnp.concatenate([cls_ref[i], rest], 0)
        patch = patch_ref[...].reshape(group * count, vis)
        keys = dot(patch, wckv_ref[:, :d]).astype(BF16)
        kv_ref[:, :, :d] = keys.reshape(group, count, d)
        values = (dot(patch, wckv_ref[:, d:]) + row_ref[6:7, :]).astype(BF16)
        kv_ref[:, :, d:] = values.reshape(group, count, d)

    done = call(
        body,
        "cross_keys",
        items // group,
        [(grid, tiled((group * part, vis))) for grid in grids]
        + [(cls, tiled((group, 1, vis))), (rows, whole(rows.shape))]
        + source.ins,
        [
            (spec_of((items, count, 2 * d), BF16), tiled((group, count, 2 * d))),
            (spec_of((items, count, vis), BF16), tiled((group, count, vis))),
        ]
        + source.outs,
        2 * items * count * vis * 2 * d,
    )
    return source.split(done)


def cross_forward(dims, text, self_ctx, kv, mask, w_out, w_cq, w_cout, rows):
    d, items, length, group = dims.d, dims.items, dims.length, dims.group
    pairs, tokens, block = d // (2 * HEAD), items * length, group * length
    count = kv.shape[1]
    scale = HEAD ** (-0.5)

    def body(x_ref, self_ref, kv_ref, mask_ref, wout_ref, wcq_ref, wcout_ref, row_ref,
             one_ref, h_ref, cq_ref, prob_ref, ctx_ref, two_ref):
        low, high = lane_masks()
        total = x_ref[...].astype(F32) + dot(self_ref[...], wout_ref[...]) + row_ref[2:3, :]
        one_ref[...] = total
        hat, _ = norm_parts(total)
        hidden = hat * row_ref[3:4, :] + row_ref[4:5, :]
        h_ref[...] = hidden.astype(BF16)
        cq_ref[...] = (dot(h_ref[...], wcq_ref[...]) + row_ref[5:6, :]).astype(BF16)
        for i in range(group):
            ok = mask_ref[i].astype(F32) > 0.5
            ok = jnp.concatenate([ok, ok], 1)
            r = slice(i * length, (i + 1) * length)
            for p in range(pairs):
                c = slice(p * 128, (p + 1) * 128)
                q, k, v = cq_ref[r, c], kv_ref[i, :, c], kv_ref[i, :, d + p * 128 : d + (p + 1) * 128]
                scores = dot_t(k, spread_heads(q, low, high)) * scale
                probs = soft(jnp.where(ok, scores, NEG)).astype(BF16)
                prob_ref[i, p] = probs
                ctx_ref[r, c] = join_heads(dot(v.T, probs))
        two_ref[...] = hidden + dot(ctx_ref[...], wcout_ref[...]) + row_ref[7:8, :]

    return call(
        body,
        "cross_forward",
        items // group,
        [
            (text, tiled((block, d))),
            (self_ctx, tiled((block, d))),
            (kv, tiled((group, count, 2 * d))),
            (mask, tiled((group, count, length))),
            (w_out, whole((d, d))),
            (w_cq, whole((d, d))),
            (w_cout, whole((d, d))),
            (rows, whole(rows.shape)),
        ],
        [
            (spec_of((tokens, d), F32), tiled((block, d))),
            (spec_of((tokens, d), BF16), tiled((block, d))),
            (spec_of((tokens, d), BF16), tiled((block, d))),
            (spec_of((items, pairs, count, 2 * length), BF16), tiled((group, pairs, count, 2 * length))),
            (spec_of((tokens, d), BF16), tiled((block, d))),
            (spec_of((tokens, d), F32), tiled((block, d))),
        ],
        2 * tokens * d * 6 * d,
    )


def ffn_both(dims, source, total_two, cotangent, rows, bias):
    d, items, length, group = dims.d, dims.items, dims.length, dims.group
    tokens, block, ff = items * length, group * length, bias.shape[1]
    piece = d
    n_in = len(source.ins)

    def body(tot_ref, cot_ref, row_ref, bias_ref, *refs):
        (out_ref, h_ref, act_ref, glow_ref, pre_ref, two_ref, twolow_ref, sum_ref, bsum_ref) = refs[
            n_in : n_in + 9
        ]
        slope_ref = refs[n_in + 9]
        win_ref, wout_ref = source.open(refs[:n_in], refs[n_in + 10 :])

        @pl.when(pl.program_id(0) == 0)
        def _():
            sum_ref[...] = jnp.zeros_like(sum_ref)
            bsum_ref[...] = jnp.zeros_like(bsum_ref)

        hat_two, spread_two = norm_parts(tot_ref[...])
        hidden = hat_two * row_ref[8:9, :] + row_ref[9:10, :]
        h_ref[...] = hidden.astype(BF16)
        total = hidden + row_ref[10:11, :]
        cuts = [slice(at, at + piece) for at in range(0, ff, piece)]

        def into(cut):
            return dot(h_ref[...], win_ref[:, cut]) + bias_ref[:, cut]

        def middle(pre, cut):
            under, bell = gelu_parts(pre)
            act_ref[:, cut] = (pre * under).astype(BF16)
            slope_ref[:, cut] = under + (pre * 0.3989422804014327) * bell

        for cut in cuts:
            middle(into(cut), cut)
            total = total + dot(act_ref[:, cut], wout_ref[cut, :])
        hat, spread = norm_parts(total)
        gain = row_ref[11:12, :]
        out_ref[...] = hat * gain + row_ref[12:13, :]
        cot = cot_ref[...].astype(F32)
        grad = norm_pull(cot, hat, spread, gain)
        glow_ref[...] = grad.astype(BF16)
        sum_ref[0:1, :] += col_sum(cot * hat)
        sum_ref[1:2, :] += col_sum(cot)
        sum_ref[2:3, :] += col_sum(glow_ref[...])
        for cut in cuts:
            pre = (dot_t(glow_ref[...], wout_ref[cut, :]) * slope_ref[:, cut]).astype(BF16)
            pre_ref[:, cut] = pre
            bsum_ref[0:1, cut] += col_sum(pre)
            grad = grad + dot_t(pre, win_ref[:, cut])
        two = norm_pull(grad, hat_two, spread_two, row_ref[8:9, :])
        two_ref[...] = two
        low = two.astype(BF16)
        twolow_ref[...] = low
        sum_ref[3:4, :] += col_sum(grad * hat_two)
        sum_ref[4:5, :] += col_sum(grad)
        sum_ref[5:6, :] += col_sum(low)

    return call(
        body,
        "ffn_both",
        items // group,
        [
            (total_two, tiled((block, d))),
            (cotangent, tiled((block, d))),
            (rows, whole(rows.shape)),
            (bias, whole(bias.shape)),
        ]
        + source.ins,
        [
            (spec_of((tokens, d), F32), tiled((block, d))),
            (spec_of((tokens, d), BF16), tiled((block, d))),
            (spec_of((tokens, ff), BF16), tiled((block, ff))),
            (spec_of((tokens, d), BF16), tiled((block, d))),
            (spec_of((tokens, ff), BF16), tiled((block, ff))),
            (spec_of((tokens, d), F32), tiled((block, d))),
            (spec_of((tokens, d), BF16), tiled((block, d))),
            (spec_of((8, d), F32), summed((8, d))),
            (spec_of((8, ff), F32), summed((8, ff))),
        ],
        8 * tokens * d * ff,
        [pltpu.VMEM((block, ff), F32)] + source.scratch,
    )


def pair_pull(q, k, v, out, probs, low, high):
    outs = spread_heads(out, low, high)
    score = soft_pull(probs.astype(F32), dot_t(v, outs)).astype(BF16)
    grad_k = dot(score, spread_heads(q, low, high))
    return dot(k.T, score), grad_k, dot(probs, outs)


def cross_attend_back(dims, grad_low, query, kv, probs, w_cout):
    d, items, length, group = dims.d, dims.items, dims.length, dims.group
    pairs, tokens, block = d // (2 * HEAD), items * length, group * length
    count = kv.shape[1]
    scale = HEAD ** (-0.5)

    def body(glow_ref, q_ref, kv_ref, prob_ref, wcout_ref, gq_ref, gkv_ref, sum_ref, ctx_ref):
        @pl.when(pl.program_id(0) == 0)
        def _():
            sum_ref[...] = jnp.zeros_like(sum_ref)

        low, high = lane_masks()
        ctx_ref[...] = dot_t(glow_ref[...], wcout_ref[...]).astype(BF16)
        for i in range(group):
            r = slice(i * length, (i + 1) * length)
            for p in range(pairs):
                c = slice(p * 128, (p + 1) * 128)
                cv = slice(d + p * 128, d + (p + 1) * 128)
                grad_q, grad_k, grad_v = pair_pull(
                    q_ref[r, c], kv_ref[i, :, c], kv_ref[i, :, cv], ctx_ref[r, c], prob_ref[i, p], low, high
                )
                gq_ref[r, c] = join_heads(grad_q * scale)
                gkv_ref[i, :, c] = (grad_k * scale).astype(BF16)
                gkv_ref[i, :, cv] = grad_v.astype(BF16)
        sum_ref[0:1, :] += col_sum(gq_ref[...])
        sum_ref[1:2, :] += col_sum(gkv_ref[:, :, d:].reshape(group * count, d))

    return call(
        body,
        "cross_attend_back",
        items // group,
        [
            (grad_low, tiled((block, d))),
            (query, tiled((block, d))),
            (kv, tiled((group, count, 2 * d))),
            (probs, tiled((group, pairs, count, 2 * length))),
            (w_cout, whole((d, d))),
        ],
        [
            (spec_of((tokens, d), BF16), tiled((block, d))),
            (spec_of((items, count, 2 * d), BF16), tiled((group, count, 2 * d))),
            (spec_of((8, d), F32), summed((8, d))),
        ],
        2 * tokens * d * 4 * d,
        [pltpu.VMEM((block, d), BF16)],
    )


def cross_project_back(dims, grad_two, grad_query, grad_kv, total_one, w_cq, w_ckv, rows, parts, part):
    d, items, length, group = dims.d, dims.items, dims.length, dims.group
    tokens, block = items * length, group * length
    count, vis = grad_kv.shape[1], w_ckv.shape[0]

    def body(g_ref, gq_ref, gkv_ref, tot_ref, wcq_ref, wckv_ref, row_ref, *refs):
        grid_refs, (cls_ref, one_ref, onelow_ref, sum_ref) = refs[:parts], refs[parts:]

        @pl.when(pl.program_id(0) == 0)
        def _():
            sum_ref[...] = jnp.zeros_like(sum_ref)

        for i in range(group):
            value = dot_t(gkv_ref[i], wckv_ref[...])
            for k in range(parts):
                grid_refs[k][i * part : (i + 1) * part, :] = value[k * part : (k + 1) * part, :].astype(BF16)
            cls_ref[i] = value[parts * part : parts * part + 1, :]
        grad = g_ref[...] + dot_t(gq_ref[...], wcq_ref[...])
        hat, spread = norm_parts(tot_ref[...])
        one = norm_pull(grad, hat, spread, row_ref[3:4, :])
        one_ref[...] = one
        one_low = one.astype(BF16)
        onelow_ref[...] = one_low
        sum_ref[0:1, :] += col_sum(grad * hat)
        sum_ref[1:2, :] += col_sum(grad)
        sum_ref[2:3, :] += col_sum(one_low)

    return call(
        body,
        "cross_project_back",
        items // group,
        [
            (grad_two, tiled((block, d))),
            (grad_query, tiled((block, d))),
            (grad_kv, tiled((group, count, 2 * d))),
            (total_one, tiled((block, d))),
            (w_cq, whole((d, d))),
            (w_ckv, whole((vis, 2 * d))),
            (rows, whole(rows.shape)),
        ],
        [(spec_of((items * part, vis), BF16), tiled((group * part, vis)))] * parts
        + [
            (spec_of((items, 1, vis), F32), tiled((group, 1, vis))),
            (spec_of((tokens, d), F32), tiled((block, d))),
            (spec_of((tokens, d), BF16), tiled((block, d))),
            (spec_of((8, d), F32), summed((8, d))),
        ],
        2 * tokens * d * d + 2 * items * count * vis * 2 * d,
    )


def self_attend_back(dims, grad_low, qkv, probs, w_out):
    d, items, length, group = dims.d, dims.items, dims.length, dims.group
    pairs, tokens, block = d // (2 * HEAD), items * length, group * length
    scale = HEAD ** (-0.5)

    def body(glow_ref, qkv_ref, prob_ref, wout_ref, gqkv_ref, sum_ref, ctx_ref):
        @pl.when(pl.program_id(0) == 0)
        def _():
            sum_ref[...] = jnp.zeros_like(sum_ref)

        low, high = lane_masks()
        ctx_ref[...] = dot_t(glow_ref[...], wout_ref[...]).astype(BF16)
        for i in range(group):
            r = slice(i * length, (i + 1) * length)
            for p in range(pairs):
                cuts = [slice(part * d + p * 128, part * d + (p + 1) * 128) for part in range(3)]
                q, k, v = (qkv_ref[r, cut] for cut in cuts)
                grad_q, grad_k, grad_v = pair_pull(q, k, v, ctx_ref[r, cuts[0]], prob_ref[i, p], low, high)
                gqkv_ref[r, cuts[0]] = join_heads(grad_q * scale)
                gqkv_ref[r, cuts[1]] = (grad_k * scale).astype(BF16)
                gqkv_ref[r, cuts[2]] = grad_v.astype(BF16)
        sum_ref[0:1, :] += col_sum(gqkv_ref[:, :d])
        sum_ref[1:2, :] += col_sum(gqkv_ref[:, 2 * d :])

    return call(
        body,
        "self_attend_back",
        items // group,
        [
            (grad_low, tiled((block, d))),
            (qkv, tiled((block, 3 * d))),
            (probs, tiled((group, pairs, length, 2 * length))),
            (w_out, whole((d, d))),
        ],
        [
            (spec_of((tokens, 3 * d), BF16), tiled((block, 3 * d))),
            (spec_of((8, d), F32), summed((8, d))),
        ],
        2 * tokens * d * 4 * d,
        [pltpu.VMEM((block, d), BF16)],
    )


def self_project_back(dims, grad_one, grad_qkv, w_qkv):
    d, items, length, group = dims.d, dims.items, dims.length, dims.group
    tokens, block = items * length, group * length

    def body(g_ref, gqkv_ref, wqkv_ref, text_ref):
        text_ref[...] = g_ref[...] + dot_t(gqkv_ref[...], wqkv_ref[...])

    return call(
        body,
        "self_project_back",
        items // group,
        [
            (grad_one, tiled((block, d))),
            (grad_qkv, tiled((block, 3 * d))),
            (w_qkv, whole((d, 3 * d))),
        ],
        [(spec_of((tokens, d), F32), tiled((block, d)))],
        2 * tokens * d * 3 * d,
    )[0]


def cut_grids(turn, image_grid, parts):
    micro, items, part, vis = image_grid.shape
    each = items // parts

    def body(turn_ref, grid_ref, *out_refs):
        def fill(own):
            value = jnp.swapaxes(grid_ref[0], 0, 1)
            for s in range(parts):
                mine = value[s * each : (s + 1) * each]
                out_refs[s ^ own][...] = mine.reshape(each * part, vis)

        for own in range(parts):
            pl.when(turn_ref[0] == own)(functools.partial(fill, own))

    return call(
        body,
        "cut_grids",
        micro,
        [
            (turn, SMEM_SPEC),
            (image_grid.transpose(0, 2, 1, 3), tiled((1, part, items, vis))),
        ],
        [(spec_of((micro * each * part, vis), BF16), tiled((each * part, vis)))] * parts,
        0,
    )


def place_grids(turn, micro, items, pieces):
    part, vis = pieces[0].shape[0] // items, pieces[0].shape[1]
    each, parts = items // micro, len(pieces)

    def body(turn_ref, *refs):
        def fill(own):
            value = [
                refs[s ^ own][...].astype(F32).reshape(each, part, vis) for s in range(parts)
            ]
            refs[-1][0] = jnp.swapaxes(jnp.concatenate(value, 0), 0, 1)

        for own in range(parts):
            pl.when(turn_ref[0] == own)(functools.partial(fill, own))

    shape = (micro, part, each * parts, vis)
    done = call(
        body,
        "place_grids",
        micro,
        [(turn, SMEM_SPEC)] + [(p, tiled((each * part, vis))) for p in pieces],
        [(spec_of(shape, F32), tiled((1,) + shape[1:]))],
        0,
    )[0]
    return done.transpose(0, 2, 1, 3)


def gather_sums(sums, bias):
    d, ff = sums[0].shape[1], bias.shape[1]
    high = -(-(ROWS + ff // d) // 8) * 8

    def body(self_ref, attend_ref, one_ref, ffn_ref, bias_ref, out_ref):
        out_ref[...] = jnp.zeros_like(out_ref)
        at = 0
        for ref, row, count in (
            (self_ref, 0, 2),
            (one_ref, 2, 1),
            (one_ref, 0, 2),
            (attend_ref, 0, 2),
            (ffn_ref, 5, 1),
            (ffn_ref, 3, 2),
            (ffn_ref, 2, 1),
            (ffn_ref, 0, 2),
        ):
            out_ref[at : at + count, :] = ref[row : row + count, :]
            at += count
        for n in range(ff // d):
            out_ref[at + n : at + n + 1, :] = bias_ref[0:1, n * d : (n + 1) * d]

    return pl.pallas_call(
        body,
        out_shape=spec_of((high, d), F32),
        in_specs=[VMEM_SPEC] * 5,
        out_specs=VMEM_SPEC,
        compiler_params=PARAMS,
        name="gather_sums",
    )(*sums, bias)


def weight_grads(plan, group, where, factors):
    high_rows = max(plan.full[w][0] for w in group)
    wide = max(plan.full[w][1] for w in group)
    flat = [a for pair in factors for a in pair]
    count = len(flat)

    def body(where_ref, *refs):
        far, stack_refs = refs[:count], refs[count : count + 2]
        near, made, sems = refs[count + 2 : 2 * count + 2], refs[-2], refs[-1]
        copies = [pltpu.make_async_copy(far[n], near[n], sems.at[n]) for n in range(count)]
        for copy in copies:
            copy.start()
        for n, w in enumerate(group):
            left, right = near[2 * n], near[2 * n + 1]
            rows, cols = plan.full[w]
            copies[2 * n].wait()
            copies[2 * n + 1].wait()
            for at in range(0, rows, 256):
                value = dot_l(left[:, at : at + 256], right[...])
                made[at : at + 256, :cols] = value.astype(BF16)

            def visit(other, second, first, k, row, w_at, j, to_row, to_y, high):
                if w_at == w:
                    col = pl.multiple_of(to_y * (cols // 2) + j * plan.chunk, 128)
                    stack_refs[other][second * 2 + first, k, row : row + high, :] = made[
                        pl.ds(to_row, high), pl.ds(col, plan.chunk)
                    ]

            each_place(plan, group, where_ref, visit)

    shape = jax.ShapeDtypeStruct((4, plan.zs, plan.rows(group), plan.chunk), BF16)
    flops = sum(2 * a.shape[0] * a.shape[1] * b.shape[1] for a, b in factors)
    moved = sum(a.size * 2 for a in flat) + 2 * shape.size * 2
    return pl.pallas_call(
        body,
        out_shape=(shape,) * 2,
        in_specs=[SMEM_SPEC] + [pl.BlockSpec(memory_space=pl.ANY)] * count,
        out_specs=(VMEM_SPEC,) * 2,
        scratch_shapes=[pltpu.VMEM(a.shape, BF16) for a in flat]
        + [pltpu.VMEM((high_rows, wide), BF16), pltpu.SemaphoreType.DMA((count,))],
        compiler_params=PARAMS,
        cost_estimate=pl.CostEstimate(flops=flops, bytes_accessed=moved, transcendentals=0),
        name="weight_grads",
    )(where, *flat)


class Dims:
    def __init__(self, d, items, length):
        self.d, self.items, self.length = d, items, length
        self.group = 2 if items % 2 == 0 else 1


def cross_mask(lengths, counts, boxes, length, count):
    place = jnp.arange(length, dtype=jnp.int32)[None, :]
    boxed = (counts[:, None] > 0) & (place < lengths[:, None])
    phrase = jnp.where(boxed, place * counts[:, None] // lengths[:, None], 0)
    chosen = phrase[:, None, :] == jnp.arange(boxes.shape[1], dtype=jnp.int32)[None, :, None]
    inside = jnp.einsum(
        "ijp,ijt->ipt",
        (boxes > 0).astype(BF16),
        chosen.astype(BF16),
        preferred_element_type=F32,
    )
    grid_ok = jnp.where(boxed[:, None, :], inside, 1.0).astype(BF16)
    items, real = grid_ok.shape[:2]
    own = jnp.ones((items, 1, length), BF16)
    return jnp.concatenate([grid_ok, own, jnp.zeros((items, count - real - 1, length), BF16)], 1)


def trade(pieces):
    parts = lax.axis_size("patch")
    return [pieces[0]] + [
        lax.ppermute(pieces[k], "patch", [(i, i ^ k) for i in range(parts)])
        for k in range(1, len(pieces))
    ]


class Work:
    def __init__(self, args, parts):
        (self.text_in, self.image_grid, self.image_cls, lengths, counts, boxes, cot) = args
        self.parts = parts
        self.micro, d = self.text_in.shape[0], self.text_in.shape[2]
        self.items = lengths.size
        self.text, self.cot = self.text_in.reshape(-1, d), cot.reshape(-1, d)
        self.lengths, self.counts = lengths.reshape(-1), counts.reshape(-1)
        self.boxes = boxes.reshape((self.items,) + boxes.shape[2:])
        self.dims = Dims(d, self.items, self.text.shape[0] // self.items)
        self.turn = lax.axis_index("patch").astype(jnp.int32).reshape(1)
        self.part, self.vis = self.image_grid.shape[2:]
        self.each = self.items // self.micro
        self.count = -(-(parts * self.part + 1) // 16) * 16
        self.cls = self.image_cls.reshape(self.items, 1, self.vis)

    def mask(self):
        boxes = self.boxes.reshape(self.items, -1, self.parts, self.part)
        order = jnp.arange(self.parts, dtype=jnp.int32) ^ self.turn[0]
        boxes = jnp.take(boxes, order, axis=2).reshape(self.boxes.shape)
        return cross_mask(self.lengths, self.counts, boxes, self.dims.length, self.count)

    def finish(self, layer_out, text_grad, grid_grad, cls, grads, rows_grad, bias_grad):
        return (
            layer_out.reshape(self.text_in.shape),
            text_grad.reshape(self.text_in.shape),
            grid_grad,
            cls.reshape(self.image_cls.shape),
            *grads,
            rows_grad,
            bias_grad,
        )


def on_device(plan, *args):
    work, shards, vectors, ffn_bias = Work(args[:7], plan.patch), args[7:14], args[14], args[15]
    dims, where, parts = work.dims, coords(), plan.patch

    own, give = pack_split(plan, where, shards)
    units = pack_join(plan, where, own, send(give, plan.core()))
    grids = list(cut_grids(work.turn, work.image_grid, parts))
    vectors, bias, grids, units = lax.optimization_barrier((vectors, ffn_bias, grids, units))
    one, two, three = (Gathering(plan, unit) for unit in units)
    small = GatheringSmall(plan, where, vectors, bias)

    def source(g, gather, kept=True):
        return Source(plan, GATHER[g], where, gather.held, kept)

    one.along_z(*range(1, plan.zs))
    grids[2] = trade(grids[:3])[2]
    small.advance()
    grids = fence([one, two, small], grids)
    one.first()
    two.along_z(*range(1, plan.zs // 2 + 1))
    grids[3] = trade(grids)[3]
    small.advance()
    grids = fence([one, two, three, small], grids)
    one.second()
    two.along_z(*range(plan.zs // 2 + 1, plan.zs))
    rows, bias = small.result()
    rows, bias, grids = fence([one, two, three], [rows, bias, grids])
    one.core()
    two.first()
    three.along_z(*range(1, plan.zs // 2 + 1))
    (qkv, probs, ctx), (w_qkv,) = self_forward(dims, source(0, one), work.text, rows, work.lengths)
    (ctx,) = fence([two, three], [ctx])
    two.second()
    three.along_z(*range(plan.zs // 2 + 1, plan.zs))
    grids[1] = trade(grids[:2])[1]
    mask = work.mask()
    ctx, grids, mask = fence([two, three], [ctx, grids, mask])
    two.core()
    three.first()
    (kv, patches), (w_out, w_cq, w_ckv, w_cout) = cross_keys(
        dims, source(1, two), grids, work.cls, rows, work.count
    )
    kv, ctx = fence([three], [kv, ctx])
    three.second()
    total_one, hidden_one, query, cross_probs, cross_ctx, total_two = cross_forward(
        dims, work.text, ctx, kv, mask, w_out, w_cq, w_cout, rows
    )
    total_two = fence([three], total_two)
    three.core()
    layer_out, hidden_two, act, low_three, grad_pre, grad_two, low_two, sum_ffn, sum_pre = ffn_both(
        dims, source(2, three, kept=False), total_two, work.cot, rows, bias
    )

    reduces = {}

    def reduce(g, factors, twice=False):
        stacks = weight_grads(plan, REDUCE[g], where, factors)
        reduces[g] = Reducing(plan, REDUCE[g], where, stacks, twice)

    def hold(*values, on=None):
        chains = [reduces[g] for g in (reduces if on is None else on)]
        return fence(chains, list(values))

    def go(*groups):
        for g in groups:
            reduces[g].advance()

    reduce(2, [(hidden_two, grad_pre), (act, low_three)], twice=True)
    (low_two,) = hold(low_two)
    go(2)
    grad_query, grad_kv, sum_attend = cross_attend_back(dims, low_two, query, kv, cross_probs, w_cout)
    grad_query, grad_kv = hold(grad_query, grad_kv)
    go(2)
    reduces[2].held[0], grad_query, grad_kv = lax.optimization_barrier(
        (reduces[2].held[0], grad_query, grad_kv)
    )
    reduce(
        1,
        [
            (hidden_one, grad_query),
            (patches.reshape(-1, work.vis), grad_kv.reshape(-1, grad_kv.shape[2])),
            (cross_ctx, low_two),
        ],
    )
    grad_query, grad_kv = hold(grad_query, grad_kv)
    go(2, 1)
    *grids, cls, grad_one, low_one, sum_one = cross_project_back(
        dims, grad_two, grad_query, grad_kv, total_one, w_cq, w_ckv, rows, parts, work.part
    )
    low_one, *grids = hold(low_one, *grids)
    go(2, 1)
    grids[1] = trade(grids[:2])[1]
    grad_qkv, sum_self = self_attend_back(dims, low_one, qkv, probs, w_out)
    reduce(0, [(work.text, grad_qkv), (ctx, low_one)])
    sums = [sum_self, sum_attend, sum_one, sum_ffn]
    reduces["small"] = ReducingSmall(plan, where, sums, sum_pre)
    grad_qkv, *grids = hold(grad_qkv, *grids)
    go(0, 1, 2, "small")
    text_grad = self_project_back(dims, grad_one, grad_qkv, w_qkv)
    (text_grad,) = hold(text_grad)
    go(0, 2, "small")
    grids = hold(*grids)
    go(0, 1, 1, 2, "small")
    grids[2] = trade(grids[:3])[2]
    grids = hold(*grids)
    go(0, 0, 1, 2, "small")
    grids[3] = trade(grids)[3]
    grids = hold(*grids)
    go(0, 1, "small")
    grid_grad = place_grids(work.turn, work.micro, work.items, grids)
    go(0)
    grads = [None] * 7
    for g, group in enumerate(REDUCE):
        for w, value in zip(group, reduces[g].held):
            grads[w] = value
    return work.finish(layer_out, text_grad, grid_grad, cls, grads, *reduces["small"].result())


def on_device_plain(plan, *args):
    work, parts = Work(args[:7], plan.patch), plan.patch
    dims = work.dims
    weights, rows, bias = fetch_plain(args[7:14], args[14], args[15])
    rows = jnp.pad(rows, ((0, -rows.shape[0] % 8), (0, 0)))
    grids = trade(cut_grids(work.turn, work.image_grid, parts))

    def source(g):
        return Source(plan, GATHER[g], None, [weights[w] for w in GATHER[g]])

    (qkv, probs, ctx), _ = self_forward(dims, source(0), work.text, rows, work.lengths)
    (kv, patches), _ = cross_keys(dims, source(1), grids, work.cls, rows, work.count)
    total_one, hidden_one, query, cross_probs, cross_ctx, total_two = cross_forward(
        dims, work.text, ctx, kv, work.mask(), weights[OUT], weights[CQ], weights[COUT], rows
    )
    layer_out, hidden_two, act, low_three, grad_pre, grad_two, low_two, sum_ffn, sum_pre = ffn_both(
        dims, source(2), total_two, work.cot, rows, bias[None]
    )
    grad_query, grad_kv, sum_attend = cross_attend_back(
        dims, low_two, query, kv, cross_probs, weights[COUT]
    )
    *grids, cls, grad_one, low_one, sum_one = cross_project_back(
        dims, grad_two, grad_query, grad_kv, total_one, weights[CQ], weights[CKV], rows, parts, work.part
    )
    grad_qkv, sum_self = self_attend_back(dims, low_one, qkv, probs, weights[OUT])
    text_grad = self_project_back(dims, grad_one, grad_qkv, weights[QKV])
    flat_kv = grad_kv.reshape(-1, grad_kv.shape[2])
    factors = [
        (work.text, grad_qkv),
        (ctx, low_one),
        (hidden_one, grad_query),
        (patches.reshape(-1, work.vis), flat_kv),
        (cross_ctx, low_two),
        (hidden_two, grad_pre),
        (act, low_three),
    ]
    grads = [reduce_plain(dot_l(a, b).astype(BF16)) for a, b in factors]
    sums = gather_sums([sum_self, sum_attend, sum_one, sum_ffn], sum_pre)
    small = reduce_small_plain(sums[:ROWS], sum_pre[0])
    grid_grad = place_grids(work.turn, work.micro, work.items, trade(grids))
    return work.finish(layer_out, text_grad, grid_grad, cls, grads, *small)


def solution(mesh):
    dp, patch = mesh.shape["dp"], mesh.shape["patch"]
    both = P(None, ("dp", "patch"), None)
    weight = P("dp", "patch")

    def run(*args):
        shards = [(w.shape[0] // dp, w.shape[1] // patch) for w in args[7:14]]
        plan = Plan(dp, patch, shards)
        return jax.shard_map(
            functools.partial(on_device if plan.fast else on_device_plain, plan),
            mesh=mesh,
            in_specs=(
                both,
                P(None, "dp", "patch", None),
                both,
                P(None, ("dp", "patch")),
                P(None, ("dp", "patch")),
                P(None, ("dp", "patch"), None, None),
                both,
            )
            + (weight,) * 7
            + (P(None, "dp"), P("dp")),
            out_specs=(both, both, P(None, "dp", "patch", None), both)
            + (weight,) * 7
            + (P(None, "dp"), P("dp")),
            check_vma=False,
        )(*args)

    return run
```

```python
import functools

import jax
import jax.numpy as jnp
from jax import lax
from jax.experimental import pallas as pl
from jax.experimental.pallas import tpu as pltpu
from jax.sharding import PartitionSpec as P

HEAD = 64
EPS = 1e-06
NEG = -1e30
BF16 = jnp.bfloat16
F32 = jnp.float32
AXES = ("dp", "patch")
VMEM_SPEC = pl.BlockSpec(memory_space=pltpu.VMEM)
SMEM_SPEC = pl.BlockSpec(memory_space=pltpu.SMEM)
PARAMS = pltpu.CompilerParams(vmem_limit_bytes=62 * 2**20)

QKV, OUT, CQ, CKV, COUT, FIN, FOUT = range(7)
ROWS = 13
EXTRA = 16
GATHER = ((QKV,), (OUT, CQ, CKV, COUT), (FIN, FOUT))
REDUCE = ((QKV, OUT), (CQ, CKV, COUT), (FIN, FOUT))


class Plan:
    def __init__(self, dp, patch, shards):
        self.dp, self.patch = dp, patch
        self.zs = dp // 2
        self.devices = dp * patch
        self.chunk = shards[OUT][1] * 2
        self.half = [s[0] // 2 for s in shards]
        self.cols = [s[1] for s in shards]
        self.chunks = [s[1] * 2 // self.chunk for s in shards]
        self.full = [(s[0] * dp, s[1] * patch) for s in shards]
        self.fast = (
            dp % 2 == 0
            and self.zs & (self.zs - 1) == 0
            and patch == 4
            and all(h % 16 == 0 for h in self.half)
            and all(s[1] * 2 % self.chunk == 0 for s in shards)
            and self.chunk % 128 == 0
            and shards[FIN][1] * patch // dp <= self.chunk
        )

    def rows(self, group):
        return sum(self.half[w] * self.chunks[w] for w in group)

    def flip(self, pick):
        return [(i, i ^ pick(i)) for i in range(self.devices)]

    def core(self):
        return self.flip(lambda i: 1)

    def first(self):
        return self.flip(lambda i: 4 if i % 2 == 0 else 2)

    def second(self):
        return self.flip(lambda i: 2 if i % 2 == 0 else 4)

    def along_z(self, k):
        return self.flip(lambda i: 8 * k)


def send(value, perm):
    return lax.ppermute(value, AXES, perm)


def coords():
    dp, patch = lax.axis_index("dp"), lax.axis_index("patch")
    return jnp.stack([dp // 2, dp % 2, patch // 2, patch % 2]).astype(jnp.int32)


def piece_rows(group, plan):
    at, found = 0, []
    for w in group:
        for j in range(plan.chunks[w]):
            found.append((w, j, at))
            at += plan.half[w]
    return found


def group_starts(plan):
    starts, at = [], 0
    for group in GATHER:
        starts.append(at)
        at += plan.rows(group)
    return starts, at


def pack_split(plan, where, shards):
    _, total = group_starts(plan)
    wide = plan.chunk // 2

    def body(where_ref, *refs):
        shard_refs, (own_ref, send_ref, turned) = list(refs[:7]), refs[7:]
        core = where_ref[3]
        turned[...] = shard_refs[FOUT][...].T
        shard_refs[FOUT] = turned
        at = 0
        for group in GATHER:
            for w in group:
                high = plan.half[w]
                for b in range(plan.chunks[w]):
                    cut = slice(b * wide, (b + 1) * wide)
                    own_ref[at : at + high, :] = shard_refs[w][pl.ds(core * high, high), cut]
                    send_ref[at : at + high, :] = shard_refs[w][
                        pl.ds((1 - core) * high, high), cut
                    ]
                    at += high

    shape = jax.ShapeDtypeStruct((total, wide), BF16)
    return pl.pallas_call(
        body,
        out_shape=(shape, shape),
        in_specs=[SMEM_SPEC] + [VMEM_SPEC] * 7,
        out_specs=(VMEM_SPEC, VMEM_SPEC),
        scratch_shapes=[pltpu.VMEM(shards[FOUT].shape, BF16)],
        compiler_params=PARAMS,
        name="pack_split",
    )(where, *shards[:FOUT], shards[FOUT].T)


def pack_join(plan, where, own, got):
    starts, total = group_starts(plan)
    wide = plan.chunk // 2

    def body(where_ref, own_ref, got_ref, *unit_refs):
        core = where_ref[3]

        def fill(low_ref, high_ref):
            for g, group in enumerate(GATHER):
                at = starts[g]
                for w in group:
                    high, count = plan.half[w], plan.chunks[w]
                    for j in range(count):
                        pair = []
                        for b in (2 * j, 2 * j + 1):
                            src = low_ref if b < count else high_ref
                            row = at + (b % count) * high
                            pair.append(src[row : row + high, :])
                        to = at - starts[g] + j * high
                        unit_refs[g][to : to + high, :] = jnp.concatenate(pair, axis=1)
                    at += count * high

        @pl.when(core == 0)
        def _():
            fill(own_ref, got_ref)

        @pl.when(core == 1)
        def _():
            fill(got_ref, own_ref)

    return pl.pallas_call(
        body,
        out_shape=tuple(jax.ShapeDtypeStruct((plan.rows(g), plan.chunk), BF16) for g in GATHER),
        in_specs=[SMEM_SPEC, VMEM_SPEC, VMEM_SPEC],
        out_specs=(VMEM_SPEC,) * len(GATHER),
        compiler_params=PARAMS,
        name="pack_join",
    )(where, own, got)


class Gathering:
    def __init__(self, plan, unit):
        self.plan, self.held = plan, [unit]

    def along_z(self, *steps):
        self.held += [send(self.held[0], self.plan.along_z(k)) for k in steps]

    def first(self):
        stack = jnp.stack(self.held)
        self.held = [stack, send(stack, self.plan.first())]

    def second(self):
        near = jnp.stack(self.held)
        self.held = [near, send(near, self.plan.second()), send(near, self.plan.core())]

    def core(self):
        self.held.append(send(self.held[1], self.plan.core()))


def each_place(plan, group, where_ref, visit):
    z, x, y, core = (where_ref[i] for i in range(4))
    for other in range(2):
        half = core ^ other
        for second in range(2):
            for first in range(2):
                x_at = x ^ jnp.where(half == 0, first, second)
                y_at = y ^ jnp.where(half == 0, second, first)
                for k in range(plan.zs):
                    place = ((z ^ k) * 2 + x_at) * 2 + half
                    for w, j, row in piece_rows(group, plan):
                        high = plan.half[w]
                        to_row = pl.multiple_of(place * high, 16)
                        visit(other, second, first, k, row, w, j, to_row, y_at, high)


def add_low(ones, twos, widths):
    count, slots, rows, chunk = ones.shape
    parts = [two.shape[0] for two in twos]

    def body(one_ref, *refs):
        two_refs, out_refs = refs[: len(parts)], refs[len(parts) :]
        twice = [ref.at[n] for ref, part in zip(two_refs, parts) for n in range(part)]
        outs = [ref.at[n] for ref, width in zip(out_refs, widths) for n in range(width)]
        for n in range(count):
            outs[n][...] = (one_ref[n].astype(F32) + twice[n][...].astype(F32)).astype(BF16)

    def spec(n):
        return pl.BlockSpec((n, 1, rows, chunk), lambda i: (0, i, 0, 0))

    return pl.pallas_call(
        body,
        grid=(slots,),
        out_shape=tuple(jax.ShapeDtypeStruct((n, slots, rows, chunk), BF16) for n in widths),
        in_specs=[spec(count)] + [spec(n) for n in parts],
        out_specs=tuple(spec(n) for n in widths),
        compiler_params=PARAMS,
        cost_estimate=pl.CostEstimate(
            flops=ones.size, bytes_accessed=6 * ones.size, transcendentals=0
        ),
        name="add_low",
    )(ones, *twos)


def add_slots(ones, twos):
    _, slots, rows, chunk = ones.shape

    def body(one_ref, two_ref, *out_refs):
        for n in range(slots):
            out_refs[n][...] = (one_ref[0, n].astype(F32) + two_ref[0, n].astype(F32)).astype(BF16)

    return pl.pallas_call(
        body,
        out_shape=(jax.ShapeDtypeStruct((rows, chunk), BF16),) * slots,
        in_specs=[VMEM_SPEC, VMEM_SPEC],
        out_specs=(VMEM_SPEC,) * slots,
        compiler_params=PARAMS,
        cost_estimate=pl.CostEstimate(
            flops=ones.size, bytes_accessed=6 * ones.size, transcendentals=0
        ),
        name="add_slots",
    )(ones, twos)


class Reducing:
    def __init__(self, plan, group, where, stacks, twice=False, extra=False):
        self.plan, self.group, self.where = plan, group, where
        self.twice, self.extra = twice, extra
        self.held = list(stacks)
        self.steps = [self.core, self.second] + [self.again] * twice
        self.steps += [self.first, self.near_z, self.far_z, self.split, self.join]

    def advance(self):
        self.held = list(self.steps.pop(0)(*self.held))

    def core(self, keep, give):
        return keep, send(give, self.plan.core())

    def second(self, keep, got):
        keep, give, *rest = add_low(keep, [got], (2, 1, 1) if self.twice else (2, 2))
        return keep, send(give, self.plan.second()), *rest

    def again(self, keep, got, give):
        return keep, got, send(give, self.plan.second())

    def first(self, keep, *got):
        keep, give = add_low(keep, got, (1, 1))
        return keep, send(give, self.plan.first())

    def near_z(self, keep, got):
        plan, slots = self.plan, list(add_slots(keep, got))
        for k in range(1, plan.zs // 2 + 1):
            slots[k] = send(slots[k], plan.along_z(k))
        return slots

    def far_z(self, *slots):
        plan, slots = self.plan, list(slots)
        for k in range(plan.zs // 2 + 1, plan.zs):
            slots[k] = send(slots[k], plan.along_z(k))
        return slots

    def split(self, *parts):
        own, give, *rest = unpack_split(self.plan, self.group, self.where, parts, self.extra)
        return own, send(give, self.plan.core()), *rest

    def join(self, own, got, *rest):
        return *unpack_join(self.plan, self.group, self.where, own, got), *rest


def fence(chains, values):
    flat, tree = jax.tree.flatten([values, [chain.held for chain in chains]])
    values, held = jax.tree.unflatten(tree, lax.optimization_barrier(flat))
    for chain, arrays in zip(chains, held):
        chain.held = arrays
    return values


def unpack_split(plan, group, where, parts, extra):
    rows, wide = plan.rows(group), plan.chunk // 2
    count = len(parts)

    def body(where_ref, *refs):
        part_refs, (own_ref, give_ref) = refs[:count], refs[count : count + 2]
        core = where_ref[3]
        if extra:
            refs[-1][...] = sum(p[rows : rows + EXTRA, :].astype(F32) for p in part_refs)

        def fill(low_ref, high_ref):
            at = 0
            for w in group:
                high, count = plan.half[w], plan.chunks[w]
                for j in range(count):
                    row = at + j * high
                    value = sum(p[row : row + high, :].astype(F32) for p in part_refs)
                    for b in (2 * j, 2 * j + 1):
                        dst = low_ref if b < count else high_ref
                        to = at + (b % count) * high
                        cut = (b - 2 * j) * wide
                        dst[to : to + high, :] = value[:, cut : cut + wide]
                at += count * high

        @pl.when(core == 0)
        def _():
            fill(own_ref, give_ref)

        @pl.when(core == 1)
        def _():
            fill(give_ref, own_ref)

    shape = jax.ShapeDtypeStruct((rows, wide), F32)
    return pl.pallas_call(
        body,
        out_shape=(shape, shape) + (jax.ShapeDtypeStruct((EXTRA, plan.chunk), F32),) * extra,
        in_specs=[SMEM_SPEC] + [VMEM_SPEC] * len(parts),
        out_specs=(VMEM_SPEC,) * (2 + extra),
        compiler_params=PARAMS,
        name="unpack_split",
    )(where, *parts)


def unpack_join(plan, group, where, own, got):
    wide = plan.chunk // 2
    turned = [w == FOUT for w in group]

    def body(where_ref, own_ref, got_ref, *refs):
        core = where_ref[3]
        at = 0
        for n, w in enumerate(group):
            out_ref = refs[-1] if turned[n] else refs[n]
            high, count = plan.half[w], plan.chunks[w]
            own_rows = pl.ds(pl.multiple_of(core * high, 16), high)
            got_rows = pl.ds(pl.multiple_of((1 - core) * high, 16), high)
            for b in range(count):
                row, cut = at + b * high, slice(b * wide, (b + 1) * wide)
                out_ref[own_rows, cut] = own_ref[row : row + high, :]
                out_ref[got_rows, cut] = got_ref[row : row + high, :]
            at += count * high
            if turned[n]:
                refs[n][...] = out_ref[...].T

    shapes = [(2 * plan.half[w], plan.cols[w]) for w in group]
    done = pl.pallas_call(
        body,
        out_shape=tuple(
            jax.ShapeDtypeStruct(shape[::-1] if turn else shape, F32)
            for shape, turn in zip(shapes, turned)
        ),
        in_specs=[SMEM_SPEC, VMEM_SPEC, VMEM_SPEC],
        out_specs=(VMEM_SPEC,) * len(group),
        scratch_shapes=[pltpu.VMEM(shapes[-1], F32)],
        compiler_params=PARAMS,
        name="unpack_join",
    )(where, own, got)
    return [value.T if turn else value for value, turn in zip(done, turned)]


class GatheringSmall:
    def __init__(self, plan, where, vectors, bias):
        self.plan, self.where, self.shape = plan, where, vectors.shape
        flat = jnp.concatenate([vectors.reshape(-1), bias])
        self.size = flat.shape[0]
        self.held, self.bit = [jnp.pad(flat, (0, -self.size % 2048)).reshape(1, -1, 128)], 4

    def advance(self):
        every = jnp.concatenate(self.held)
        self.held = [every, send(every, self.plan.flip(lambda i: self.bit))]
        self.bit *= 2

    def result(self):
        plan, (count, part) = self.plan, self.shape
        while self.bit < plan.devices:
            self.advance()
        every = jnp.concatenate(self.held).reshape(plan.dp, -1)
        slot = jnp.arange(plan.dp, dtype=jnp.int32) ^ (self.where[0] * 2 + self.where[1])
        every = jnp.take(every, slot, axis=0)[:, : self.size].astype(F32)
        rows = every[:, : count * part].reshape(plan.dp, count, part)
        rows = rows.transpose(1, 0, 2).reshape(count, plan.dp * part)
        bias = every[:, count * part :].reshape(1, -1)
        return jnp.pad(rows, ((0, -count % 8), (0, 0))), bias


def fetch_plain(weights, vectors, bias):
    whole = [
        lax.all_gather(lax.all_gather(w, "dp", axis=0, tiled=True), "patch", axis=1, tiled=True)
        for w in weights
    ]
    rows = lax.all_gather(vectors, "dp", axis=1, tiled=True)
    return whole, rows.astype(F32), lax.all_gather(bias, "dp", axis=0, tiled=True).astype(F32)


def reduce_plain(grad):
    part = lax.psum_scatter(grad, "dp", scatter_dimension=0, tiled=True)
    return lax.psum_scatter(part, "patch", scatter_dimension=1, tiled=True).astype(F32)


def reduce_small_plain(rows, bias):
    rows = lax.psum_scatter(rows, "dp", scatter_dimension=1, tiled=True)
    bias = lax.psum_scatter(bias, "dp", scatter_dimension=0, tiled=True)
    return lax.psum(rows, "patch"), lax.psum(bias, "patch")


TAIL = (0.112528827, 0.117839666, 0.0706314405, 0.2046457425, -0.190499398, 0.3478185715, -0.201092832, 0.03812798145)


def dot(a, b):
    return lax.dot_general(a, b, (((1,), (0,)), ((), ())), preferred_element_type=F32)


def dot_t(a, b):
    return lax.dot_general(a, b, (((1,), (1,)), ((), ())), preferred_element_type=F32)


def dot_l(a, b):
    return lax.dot_general(a, b, (((0,), (0,)), ((), ())), preferred_element_type=F32)


def norm_parts(total):
    center = total - jnp.mean(total, -1, keepdims=True)
    spread = lax.rsqrt(jnp.mean(center * center, -1, keepdims=True) + EPS)
    return center * spread, spread


def norm_pull(grad, hat, spread, gain):
    scaled = grad * gain
    return spread * (
        scaled
        - jnp.mean(scaled, -1, keepdims=True)
        - hat * jnp.mean(scaled * hat, -1, keepdims=True)
    )


def gelu_parts(x):
    bell = jnp.exp(-0.5 * (x * x))
    t = 1.0 / (1.0 + (0.4 * 0.5**0.5) * jnp.abs(x))
    tail = jnp.full_like(t, TAIL[-1])
    for c in TAIL[-2::-1]:
        tail = tail * t + c
    tail = tail * (t * bell)
    return jnp.where(x < 0.0, tail, 1.0 - tail), bell


def col_sum(value):
    return jnp.sum(value.astype(F32), 0, keepdims=True)


def soft(scores):
    grown = jnp.exp(scores - jnp.max(scores, 0, keepdims=True))
    return grown * (1.0 / jnp.sum(grown, 0, keepdims=True))


def soft_pull(probs, grad):
    return probs * (grad - jnp.sum(probs * grad, 0, keepdims=True))


def spread_heads(value, low, high):
    return jnp.concatenate([value * low, value * high], 0)


def join_heads(value):
    count = value.shape[1] // 2
    value = jnp.concatenate([value[:HEAD, :count], value[HEAD:, count:]], 0)
    return value.astype(BF16).T


def lane_masks():
    lane = lax.broadcasted_iota(jnp.int32, (1, 2 * HEAD), 1)
    low = (lane < HEAD).astype(F32)
    return low.astype(BF16), (1.0 - low).astype(BF16)


def whole(shape):
    return pl.BlockSpec(
        shape, lambda i: (0,) * len(shape), pipeline_mode=pl.Buffered(1)
    )


def summed(shape):
    return pl.BlockSpec(shape, lambda i: (0,) * len(shape))


def tiled(shape):
    return pl.BlockSpec(shape, lambda i: (i,) + (0,) * (len(shape) - 1))


def spec_of(shape, dtype):
    return jax.ShapeDtypeStruct(shape, dtype)


def call(body, name, steps, ins, outs, flops, scratch=()):
    out_shape = tuple(shape for shape, _ in outs)
    moved = sum(a.size * a.dtype.itemsize for a, _ in ins)
    moved += sum(o.size * jnp.dtype(o.dtype).itemsize for o in out_shape)
    return pl.pallas_call(
        body,
        grid=(steps,),
        out_shape=out_shape,
        in_specs=[spec for _, spec in ins],
        out_specs=tuple(spec for _, spec in outs),
        scratch_shapes=list(scratch),
        compiler_params=PARAMS,
        cost_estimate=pl.CostEstimate(
            flops=int(flops), bytes_accessed=int(moved), transcendentals=0
        ),
        name=name,
    )(*[a for a, _ in ins])


class Source:
    def __init__(self, plan, group, where, given, kept=True):
        self.plan, self.group, self.pieces, self.given = plan, group, plan.fast, given
        self.outs, self.scratch = [], []
        if not self.pieces:
            self.ins = [(w, whole(w.shape)) for w in given]
            return
        self.ins = [(where, SMEM_SPEC)] + [(part, whole(part.shape)) for part in given]
        if kept:
            self.outs = [(spec_of(plan.full[w], BF16), summed(plan.full[w])) for w in group]
        else:
            self.scratch = [pltpu.VMEM(plan.full[w], BF16) for w in group]

    def open(self, in_refs, out_refs):
        if not self.pieces:
            return list(in_refs)
        where_ref, parts = in_refs[0], in_refs[1:]
        full = dict(zip(self.group, out_refs))
        plan = self.plan

        def visit(other, second, first, k, row, w, j, to_row, to_y, high):
            to_col = pl.multiple_of(to_y * (plan.full[w][1] // 2) + j * plan.chunk, 128)
            part = parts[other * 2 + second]
            full[w][pl.ds(to_row, high), pl.ds(to_col, plan.chunk)] = part[
                first, k, row : row + high, :
            ]

        @pl.when(pl.program_id(0) == 0)
        def _():
            each_place(plan, self.group, where_ref, visit)

        return list(out_refs)

    def split(self, done):
        if not self.pieces:
            return done, self.given
        return done[: -len(self.group)], done[-len(self.group) :]


def self_forward(dims, source, text, rows, lengths):
    d, items, length, group = dims.d, dims.items, dims.length, dims.group
    pairs, tokens, block = d // (2 * HEAD), items * length, group * length
    scale = HEAD ** (-0.5)

    n_in = len(source.ins)

    def body(len_ref, x_ref, row_ref, *refs):
        qkv_ref, prob_ref, ctx_ref = refs[n_in : n_in + 3]
        (wqkv_ref,) = source.open(refs[:n_in], refs[n_in + 3 :])
        step = pl.program_id(0)
        low, high = lane_masks()
        x = x_ref[...]
        for part, bias in ((0, 0), (1, None), (2, 1)):
            cut = slice(part * d, (part + 1) * d)
            value = dot(x, wqkv_ref[:, cut])
            if bias is not None:
                value = value + row_ref[bias : bias + 1, :]
            qkv_ref[:, cut] = value.astype(BF16)
        place = lax.broadcasted_iota(jnp.int32, (length, 1), 0)
        for i in range(group):
            ok = place < len_ref[step * group + i]
            r = slice(i * length, (i + 1) * length)
            for p in range(pairs):
                q, k, v = (
                    qkv_ref[r, part * d + p * 128 : part * d + (p + 1) * 128] for part in range(3)
                )
                scores = dot_t(k, spread_heads(q, low, high)) * scale
                probs = soft(jnp.where(ok, scores, NEG)).astype(BF16)
                prob_ref[i, p] = probs
                ctx_ref[r, p * 128 : (p + 1) * 128] = join_heads(dot(v.T, probs))
    done = call(
        body,
        "self_forward",
        items // group,
        [(lengths, SMEM_SPEC), (text, tiled((block, d))), (rows, whole(rows.shape))] + source.ins,
        [
            (spec_of((tokens, 3 * d), BF16), tiled((block, 3 * d))),
            (spec_of((items, pairs, length, 2 * length), BF16), tiled((group, pairs, length, 2 * length))),
            (spec_of((tokens, d), BF16), tiled((block, d))),
        ]
        + source.outs,
        2 * tokens * d * 5 * d,
    )
    return source.split(done)


def cross_keys(dims, source, grids, cls, rows, count):
    d, items, group = dims.d, dims.items, dims.group
    part, vis, parts = grids[0].shape[0] // items, cls.shape[2], len(grids)
    n_in = len(source.ins)

    def body(*refs):
        grid_refs, cls_ref, row_ref = refs[:parts], refs[parts], refs[parts + 1]
        refs = refs[parts + 2 :]
        kv_ref, patch_ref = refs[n_in : n_in + 2]
        _, _, wckv_ref, _ = source.open(refs[:n_in], refs[n_in + 2 :])
        for i in range(group):
            for k in range(parts):
                patch_ref[i, k * part : (k + 1) * part, :] = grid_refs[k][i * part : (i + 1) * part, :]
            rest = jnp.zeros((count - parts * part - 1, vis), BF16)
            patch_ref[i, parts * part :, :] = jnp.concatenate([cls_ref[i], rest], 0)
        patch = patch_ref[...].reshape(group * count, vis)
        keys = dot(patch, wckv_ref[:, :d]).astype(BF16)
        kv_ref[:, :, :d] = keys.reshape(group, count, d)
        values = (dot(patch, wckv_ref[:, d:]) + row_ref[6:7, :]).astype(BF16)
        kv_ref[:, :, d:] = values.reshape(group, count, d)

    done = call(
        body,
        "cross_keys",
        items // group,
        [(grid, tiled((group * part, vis))) for grid in grids]
        + [(cls, tiled((group, 1, vis))), (rows, whole(rows.shape))]
        + source.ins,
        [
            (spec_of((items, count, 2 * d), BF16), tiled((group, count, 2 * d))),
            (spec_of((items, count, vis), BF16), tiled((group, count, vis))),
        ]
        + source.outs,
        2 * items * count * vis * 2 * d,
    )
    return source.split(done)


def cross_forward(dims, text, self_ctx, kv, mask, w_out, w_cq, w_cout, rows):
    d, items, length, group = dims.d, dims.items, dims.length, dims.group
    pairs, tokens, block = d // (2 * HEAD), items * length, group * length
    count = kv.shape[1]
    scale = HEAD ** (-0.5)

    def body(x_ref, self_ref, kv_ref, mask_ref, wout_ref, wcq_ref, wcout_ref, row_ref,
             one_ref, h_ref, cq_ref, prob_ref, ctx_ref, two_ref):
        low, high = lane_masks()
        total = x_ref[...].astype(F32) + dot(self_ref[...], wout_ref[...]) + row_ref[2:3, :]
        one_ref[...] = total
        hat, _ = norm_parts(total)
        hidden = hat * row_ref[3:4, :] + row_ref[4:5, :]
        h_ref[...] = hidden.astype(BF16)
        cq_ref[...] = (dot(h_ref[...], wcq_ref[...]) + row_ref[5:6, :]).astype(BF16)
        for i in range(group):
            ok = mask_ref[i].astype(F32) > 0.5
            ok = jnp.concatenate([ok, ok], 1)
            r = slice(i * length, (i + 1) * length)
            for p in range(pairs):
                c = slice(p * 128, (p + 1) * 128)
                q, k, v = cq_ref[r, c], kv_ref[i, :, c], kv_ref[i, :, d + p * 128 : d + (p + 1) * 128]
                scores = dot_t(k, spread_heads(q, low, high)) * scale
                probs = soft(jnp.where(ok, scores, NEG)).astype(BF16)
                prob_ref[i, p] = probs
                ctx_ref[r, c] = join_heads(dot(v.T, probs))
        two_ref[...] = hidden + dot(ctx_ref[...], wcout_ref[...]) + row_ref[7:8, :]

    return call(
        body,
        "cross_forward",
        items // group,
        [
            (text, tiled((block, d))),
            (self_ctx, tiled((block, d))),
            (kv, tiled((group, count, 2 * d))),
            (mask, tiled((group, count, length))),
            (w_out, whole((d, d))),
            (w_cq, whole((d, d))),
            (w_cout, whole((d, d))),
            (rows, whole(rows.shape)),
        ],
        [
            (spec_of((tokens, d), F32), tiled((block, d))),
            (spec_of((tokens, d), BF16), tiled((block, d))),
            (spec_of((tokens, d), BF16), tiled((block, d))),
            (spec_of((items, pairs, count, 2 * length), BF16), tiled((group, pairs, count, 2 * length))),
            (spec_of((tokens, d), BF16), tiled((block, d))),
            (spec_of((tokens, d), F32), tiled((block, d))),
        ],
        2 * tokens * d * 6 * d,
    )


def ffn_both(dims, source, total_two, cotangent, rows, bias):
    d, items, length, group = dims.d, dims.items, dims.length, dims.group
    tokens, block, ff = items * length, group * length, bias.shape[1]
    piece = d
    n_in = len(source.ins)

    def body(tot_ref, cot_ref, row_ref, bias_ref, *refs):
        (out_ref, h_ref, act_ref, glow_ref, pre_ref, two_ref, twolow_ref, sum_ref, bsum_ref) = refs[
            n_in : n_in + 9
        ]
        slope_ref = refs[n_in + 9]
        win_ref, wout_ref = source.open(refs[:n_in], refs[n_in + 10 :])

        @pl.when(pl.program_id(0) == 0)
        def _():
            sum_ref[...] = jnp.zeros_like(sum_ref)
            bsum_ref[...] = jnp.zeros_like(bsum_ref)

        hat_two, spread_two = norm_parts(tot_ref[...])
        hidden = hat_two * row_ref[8:9, :] + row_ref[9:10, :]
        h_ref[...] = hidden.astype(BF16)
        total = hidden + row_ref[10:11, :]
        cuts = [slice(at, at + piece) for at in range(0, ff, piece)]

        def into(cut):
            return dot(h_ref[...], win_ref[:, cut]) + bias_ref[:, cut]

        def middle(pre, cut):
            under, bell = gelu_parts(pre)
            act_ref[:, cut] = (pre * under).astype(BF16)
            slope_ref[:, cut] = under + (pre * 0.3989422804014327) * bell

        for cut in cuts:
            middle(into(cut), cut)
            total = total + dot(act_ref[:, cut], wout_ref[cut, :])
        hat, spread = norm_parts(total)
        gain = row_ref[11:12, :]
        out_ref[...] = hat * gain + row_ref[12:13, :]
        cot = cot_ref[...].astype(F32)
        grad = norm_pull(cot, hat, spread, gain)
        glow_ref[...] = grad.astype(BF16)
        sum_ref[0:1, :] += col_sum(cot * hat)
        sum_ref[1:2, :] += col_sum(cot)
        sum_ref[2:3, :] += col_sum(glow_ref[...])
        for cut in cuts:
            pre = (dot_t(glow_ref[...], wout_ref[cut, :]) * slope_ref[:, cut]).astype(BF16)
            pre_ref[:, cut] = pre
            bsum_ref[0:1, cut] += col_sum(pre)
            grad = grad + dot_t(pre, win_ref[:, cut])
        two = norm_pull(grad, hat_two, spread_two, row_ref[8:9, :])
        two_ref[...] = two
        low = two.astype(BF16)
        twolow_ref[...] = low
        sum_ref[3:4, :] += col_sum(grad * hat_two)
        sum_ref[4:5, :] += col_sum(grad)
        sum_ref[5:6, :] += col_sum(low)

    return call(
        body,
        "ffn_both",
        items // group,
        [
            (total_two, tiled((block, d))),
            (cotangent, tiled((block, d))),
            (rows, whole(rows.shape)),
            (bias, whole(bias.shape)),
        ]
        + source.ins,
        [
            (spec_of((tokens, d), F32), tiled((block, d))),
            (spec_of((tokens, d), BF16), tiled((block, d))),
            (spec_of((tokens, ff), BF16), tiled((block, ff))),
            (spec_of((tokens, d), BF16), tiled((block, d))),
            (spec_of((tokens, ff), BF16), tiled((block, ff))),
            (spec_of((tokens, d), F32), tiled((block, d))),
            (spec_of((tokens, d), BF16), tiled((block, d))),
            (spec_of((8, d), F32), summed((8, d))),
            (spec_of((8, ff), F32), summed((8, ff))),
        ],
        8 * tokens * d * ff,
        [pltpu.VMEM((block, ff), F32)] + source.scratch,
    )


def pair_pull(q, k, v, out, probs, low, high):
    outs = spread_heads(out, low, high)
    score = soft_pull(probs.astype(F32), dot_t(v, outs)).astype(BF16)
    grad_k = dot(score, spread_heads(q, low, high))
    return dot(k.T, score), grad_k, dot(probs, outs)


def cross_attend_back(dims, grad_low, query, kv, probs, w_cout):
    d, items, length, group = dims.d, dims.items, dims.length, dims.group
    pairs, tokens, block = d // (2 * HEAD), items * length, group * length
    count = kv.shape[1]
    scale = HEAD ** (-0.5)

    def body(glow_ref, q_ref, kv_ref, prob_ref, wcout_ref, gq_ref, gkv_ref, sum_ref, ctx_ref):
        @pl.when(pl.program_id(0) == 0)
        def _():
            sum_ref[...] = jnp.zeros_like(sum_ref)

        low, high = lane_masks()
        ctx_ref[...] = dot_t(glow_ref[...], wcout_ref[...]).astype(BF16)
        for i in range(group):
            r = slice(i * length, (i + 1) * length)
            for p in range(pairs):
                c = slice(p * 128, (p + 1) * 128)
                cv = slice(d + p * 128, d + (p + 1) * 128)
                grad_q, grad_k, grad_v = pair_pull(
                    q_ref[r, c], kv_ref[i, :, c], kv_ref[i, :, cv], ctx_ref[r, c], prob_ref[i, p], low, high
                )
                gq_ref[r, c] = join_heads(grad_q * scale)
                gkv_ref[i, :, c] = (grad_k * scale).astype(BF16)
                gkv_ref[i, :, cv] = grad_v.astype(BF16)
        sum_ref[0:1, :] += col_sum(gq_ref[...])
        sum_ref[1:2, :] += col_sum(gkv_ref[:, :, d:].reshape(group * count, d))

    return call(
        body,
        "cross_attend_back",
        items // group,
        [
            (grad_low, tiled((block, d))),
            (query, tiled((block, d))),
            (kv, tiled((group, count, 2 * d))),
            (probs, tiled((group, pairs, count, 2 * length))),
            (w_cout, whole((d, d))),
        ],
        [
            (spec_of((tokens, d), BF16), tiled((block, d))),
            (spec_of((items, count, 2 * d), BF16), tiled((group, count, 2 * d))),
            (spec_of((8, d), F32), summed((8, d))),
        ],
        2 * tokens * d * 4 * d,
        [pltpu.VMEM((block, d), BF16)],
    )


def cross_project_back(dims, grad_two, grad_query, grad_kv, total_one, w_cq, w_ckv, rows, parts, part):
    d, items, length, group = dims.d, dims.items, dims.length, dims.group
    tokens, block = items * length, group * length
    count, vis = grad_kv.shape[1], w_ckv.shape[0]

    def body(g_ref, gq_ref, gkv_ref, tot_ref, wcq_ref, wckv_ref, row_ref, *refs):
        grid_refs, (cls_ref, one_ref, onelow_ref, sum_ref) = refs[:parts], refs[parts:]

        @pl.when(pl.program_id(0) == 0)
        def _():
            sum_ref[...] = jnp.zeros_like(sum_ref)

        for i in range(group):
            value = dot_t(gkv_ref[i], wckv_ref[...])
            for k in range(parts):
                grid_refs[k][i * part : (i + 1) * part, :] = value[k * part : (k + 1) * part, :].astype(BF16)
            cls_ref[i] = value[parts * part : parts * part + 1, :]
        grad = g_ref[...] + dot_t(gq_ref[...], wcq_ref[...])
        hat, spread = norm_parts(tot_ref[...])
        one = norm_pull(grad, hat, spread, row_ref[3:4, :])
        one_ref[...] = one
        one_low = one.astype(BF16)
        onelow_ref[...] = one_low
        sum_ref[0:1, :] += col_sum(grad * hat)
        sum_ref[1:2, :] += col_sum(grad)
        sum_ref[2:3, :] += col_sum(one_low)

    return call(
        body,
        "cross_project_back",
        items // group,
        [
            (grad_two, tiled((block, d))),
            (grad_query, tiled((block, d))),
            (grad_kv, tiled((group, count, 2 * d))),
            (total_one, tiled((block, d))),
            (w_cq, whole((d, d))),
            (w_ckv, whole((vis, 2 * d))),
            (rows, whole(rows.shape)),
        ],
        [(spec_of((items * part, vis), BF16), tiled((group * part, vis)))] * parts
        + [
            (spec_of((items, 1, vis), F32), tiled((group, 1, vis))),
            (spec_of((tokens, d), F32), tiled((block, d))),
            (spec_of((tokens, d), BF16), tiled((block, d))),
            (spec_of((8, d), F32), summed((8, d))),
        ],
        2 * tokens * d * d + 2 * items * count * vis * 2 * d,
    )


def self_attend_back(dims, grad_low, qkv, probs, w_out):
    d, items, length, group = dims.d, dims.items, dims.length, dims.group
    pairs, tokens, block = d // (2 * HEAD), items * length, group * length
    scale = HEAD ** (-0.5)

    def body(glow_ref, qkv_ref, prob_ref, wout_ref, gqkv_ref, sum_ref, ctx_ref):
        @pl.when(pl.program_id(0) == 0)
        def _():
            sum_ref[...] = jnp.zeros_like(sum_ref)

        low, high = lane_masks()
        ctx_ref[...] = dot_t(glow_ref[...], wout_ref[...]).astype(BF16)
        for i in range(group):
            r = slice(i * length, (i + 1) * length)
            for p in range(pairs):
                cuts = [slice(part * d + p * 128, part * d + (p + 1) * 128) for part in range(3)]
                q, k, v = (qkv_ref[r, cut] for cut in cuts)
                grad_q, grad_k, grad_v = pair_pull(q, k, v, ctx_ref[r, cuts[0]], prob_ref[i, p], low, high)
                gqkv_ref[r, cuts[0]] = join_heads(grad_q * scale)
                gqkv_ref[r, cuts[1]] = (grad_k * scale).astype(BF16)
                gqkv_ref[r, cuts[2]] = grad_v.astype(BF16)
        sum_ref[0:1, :] += col_sum(gqkv_ref[:, :d])
        sum_ref[1:2, :] += col_sum(gqkv_ref[:, 2 * d :])

    return call(
        body,
        "self_attend_back",
        items // group,
        [
            (grad_low, tiled((block, d))),
            (qkv, tiled((block, 3 * d))),
            (probs, tiled((group, pairs, length, 2 * length))),
            (w_out, whole((d, d))),
        ],
        [
            (spec_of((tokens, 3 * d), BF16), tiled((block, 3 * d))),
            (spec_of((8, d), F32), summed((8, d))),
        ],
        2 * tokens * d * 4 * d,
        [pltpu.VMEM((block, d), BF16)],
    )


def self_project_back(dims, grad_one, grad_qkv, w_qkv):
    d, items, length, group = dims.d, dims.items, dims.length, dims.group
    tokens, block = items * length, group * length

    def body(g_ref, gqkv_ref, wqkv_ref, text_ref):
        text_ref[...] = g_ref[...] + dot_t(gqkv_ref[...], wqkv_ref[...])

    return call(
        body,
        "self_project_back",
        items // group,
        [
            (grad_one, tiled((block, d))),
            (grad_qkv, tiled((block, 3 * d))),
            (w_qkv, whole((d, 3 * d))),
        ],
        [(spec_of((tokens, d), F32), tiled((block, d)))],
        2 * tokens * d * 3 * d,
    )[0]


def cut_grids(turn, image_grid, parts):
    micro, items, part, vis = image_grid.shape
    each = items // parts

    def body(turn_ref, grid_ref, *out_refs):
        def fill(own):
            value = jnp.swapaxes(grid_ref[0], 0, 1)
            for s in range(parts):
                mine = value[s * each : (s + 1) * each]
                out_refs[s ^ own][...] = mine.reshape(each * part, vis)

        for own in range(parts):
            pl.when(turn_ref[0] == own)(functools.partial(fill, own))

    return call(
        body,
        "cut_grids",
        micro,
        [
            (turn, SMEM_SPEC),
            (image_grid.transpose(0, 2, 1, 3), tiled((1, part, items, vis))),
        ],
        [(spec_of((micro * each * part, vis), BF16), tiled((each * part, vis)))] * parts,
        0,
    )


def place_grids(turn, micro, items, pieces):
    part, vis = pieces[0].shape[0] // items, pieces[0].shape[1]
    each, parts = items // micro, len(pieces)

    def body(turn_ref, *refs):
        def fill(own):
            value = [
                refs[s ^ own][...].astype(F32).reshape(each, part, vis) for s in range(parts)
            ]
            refs[-1][0] = jnp.swapaxes(jnp.concatenate(value, 0), 0, 1)

        for own in range(parts):
            pl.when(turn_ref[0] == own)(functools.partial(fill, own))

    shape = (micro, part, each * parts, vis)
    done = call(
        body,
        "place_grids",
        micro,
        [(turn, SMEM_SPEC)] + [(p, tiled((each * part, vis))) for p in pieces],
        [(spec_of(shape, F32), tiled((1,) + shape[1:]))],
        0,
    )[0]
    return done.transpose(0, 2, 1, 3)


def gather_sums(sums, bias):
    d, ff = sums[0].shape[1], bias.shape[1]
    high = -(-(ROWS + ff // d) // 8) * 8

    def body(self_ref, attend_ref, one_ref, ffn_ref, bias_ref, out_ref):
        out_ref[...] = jnp.zeros_like(out_ref)
        at = 0
        for ref, row, count in (
            (self_ref, 0, 2),
            (one_ref, 2, 1),
            (one_ref, 0, 2),
            (attend_ref, 0, 2),
            (ffn_ref, 5, 1),
            (ffn_ref, 3, 2),
            (ffn_ref, 2, 1),
            (ffn_ref, 0, 2),
        ):
            out_ref[at : at + count, :] = ref[row : row + count, :]
            at += count
        for n in range(ff // d):
            out_ref[at + n : at + n + 1, :] = bias_ref[0:1, n * d : (n + 1) * d]

    return pl.pallas_call(
        body,
        out_shape=spec_of((high, d), F32),
        in_specs=[VMEM_SPEC] * 5,
        out_specs=VMEM_SPEC,
        compiler_params=PARAMS,
        name="gather_sums",
    )(*sums, bias)


def weight_grads(plan, group, where, factors, extra=()):
    high_rows = max(plan.full[w][0] for w in group)
    wide = max(plan.full[w][1] for w in group)
    flat = [a for pair in factors for a in pair]
    count, base = len(flat), plan.rows(group)

    def body(where_ref, *refs):
        far, (own_ref, other_ref) = refs[:count], refs[count + len(extra) : count + len(extra) + 2]
        stack_refs = (own_ref, other_ref)
        near, (made, sems) = refs[-count - 2 - len(extra) : -2 - len(extra)], refs[-2 - len(extra) :][:2]
        copies = [pltpu.make_async_copy(far[n], near[n], sems.at[n]) for n in range(count)]
        for copy in copies:
            copy.start()
        if extra:
            add_extra(where_ref, refs[count], stack_refs, refs[-1])
        for n, w in enumerate(group):
            left, right = near[2 * n], near[2 * n + 1]
            rows, cols = plan.full[w]
            copies[2 * n].wait()
            copies[2 * n + 1].wait()
            for at in range(0, rows, 256):
                value = dot_l(left[:, at : at + 256], right[...])
                made[at : at + 256, :cols] = value.astype(BF16)

            def visit(other, second, first, k, row, w_at, j, to_row, to_y, high):
                if w_at == w:
                    col = pl.multiple_of(to_y * (cols // 2) + j * plan.chunk, 128)
                    stack_refs[other][second * 2 + first, k, row : row + high, :] = made[
                        pl.ds(to_row, high), pl.ds(col, plan.chunk)
                    ]

            each_place(plan, group, where_ref, visit)

    def add_extra(where_ref, sum_ref, stack_refs, table):
        width, d = sum_ref.shape[1] // plan.dp, sum_ref.shape[1]
        step = plan.full[FIN][1] // plan.dp
        table[...] = jnp.zeros_like(table)
        for n in range(plan.dp):
            table[n, :ROWS, :width] = sum_ref[:ROWS, n * width : (n + 1) * width]
            row, at = divmod(n * step, d)
            table[n, ROWS : ROWS + 1, :step] = sum_ref[ROWS + row : ROWS + row + 1, at : at + step]
        z, x, _, core = (where_ref[i] for i in range(4))
        for other in range(2):
            for second in range(2):
                for first in range(2):
                    x_at = x ^ jnp.where((core ^ other) == 0, first, second)
                    for k in range(plan.zs):
                        value = table[(z ^ k) * 2 + x_at].astype(BF16)
                        stack_refs[other][second * 2 + first, k, base : base + EXTRA, :] = value

    high = base + EXTRA * len(extra)
    shape = jax.ShapeDtypeStruct((4, plan.zs, high, plan.chunk), BF16)
    flops = sum(2 * a.shape[0] * a.shape[1] * b.shape[1] for a, b in factors)
    moved = sum(a.size * 2 for a in flat) + 2 * shape.size * 2
    table = [pltpu.VMEM((plan.dp, EXTRA, plan.chunk), F32)] * len(extra)
    return pl.pallas_call(
        body,
        out_shape=(shape,) * 2,
        in_specs=[SMEM_SPEC]
        + [pl.BlockSpec(memory_space=pl.ANY)] * count
        + [VMEM_SPEC] * len(extra),
        out_specs=(VMEM_SPEC,) * 2,
        scratch_shapes=[pltpu.VMEM(a.shape, BF16) for a in flat]
        + [pltpu.VMEM((high_rows, wide), BF16), pltpu.SemaphoreType.DMA((count,))]
        + table,
        compiler_params=PARAMS,
        cost_estimate=pl.CostEstimate(flops=flops, bytes_accessed=moved, transcendentals=0),
        name="weight_grads",
    )(where, *flat, *extra)


class Dims:
    def __init__(self, d, items, length):
        self.d, self.items, self.length = d, items, length
        self.group = 2 if items % 2 == 0 else 1


def cross_mask(lengths, counts, boxes, length, count):
    place = jnp.arange(length, dtype=jnp.int32)[None, :]
    boxed = (counts[:, None] > 0) & (place < lengths[:, None])
    phrase = jnp.where(boxed, place * counts[:, None] // lengths[:, None], 0)
    chosen = phrase[:, None, :] == jnp.arange(boxes.shape[1], dtype=jnp.int32)[None, :, None]
    inside = jnp.einsum(
        "ijp,ijt->ipt",
        (boxes > 0).astype(BF16),
        chosen.astype(BF16),
        preferred_element_type=F32,
    )
    grid_ok = jnp.where(boxed[:, None, :], inside, 1.0).astype(BF16)
    items, real = grid_ok.shape[:2]
    own = jnp.ones((items, 1, length), BF16)
    return jnp.concatenate([grid_ok, own, jnp.zeros((items, count - real - 1, length), BF16)], 1)


def trade(pieces):
    parts = lax.axis_size("patch")
    return [pieces[0]] + [
        lax.ppermute(pieces[k], "patch", [(i, i ^ k) for i in range(parts)])
        for k in range(1, len(pieces))
    ]


class Work:
    def __init__(self, args, parts):
        (self.text_in, self.image_grid, self.image_cls, lengths, counts, boxes, cot) = args
        self.parts = parts
        self.micro, d = self.text_in.shape[0], self.text_in.shape[2]
        self.items = lengths.size
        self.text, self.cot = self.text_in.reshape(-1, d), cot.reshape(-1, d)
        self.lengths, self.counts = lengths.reshape(-1), counts.reshape(-1)
        self.boxes = boxes.reshape((self.items,) + boxes.shape[2:])
        self.dims = Dims(d, self.items, self.text.shape[0] // self.items)
        self.turn = lax.axis_index("patch").astype(jnp.int32).reshape(1)
        self.part, self.vis = self.image_grid.shape[2:]
        self.each = self.items // self.micro
        self.count = -(-(parts * self.part + 1) // 16) * 16
        self.cls = self.image_cls.reshape(self.items, 1, self.vis)

    def mask(self):
        boxes = self.boxes.reshape(self.items, -1, self.parts, self.part)
        order = jnp.arange(self.parts, dtype=jnp.int32) ^ self.turn[0]
        boxes = jnp.take(boxes, order, axis=2).reshape(self.boxes.shape)
        return cross_mask(self.lengths, self.counts, boxes, self.dims.length, self.count)

    def finish(self, layer_out, text_grad, grid_grad, cls, grads, rows_grad, bias_grad):
        return (
            layer_out.reshape(self.text_in.shape),
            text_grad.reshape(self.text_in.shape),
            grid_grad,
            cls.reshape(self.image_cls.shape),
            *grads,
            rows_grad,
            bias_grad,
        )


def on_device(plan, *args):
    work, shards, vectors, ffn_bias = Work(args[:7], plan.patch), args[7:14], args[14], args[15]
    dims, where, parts = work.dims, coords(), plan.patch

    own, give = pack_split(plan, where, shards)
    units = pack_join(plan, where, own, send(give, plan.core()))
    grids = list(cut_grids(work.turn, work.image_grid, parts))
    vectors, bias, grids, units = lax.optimization_barrier((vectors, ffn_bias, grids, units))
    one, two, three = (Gathering(plan, unit) for unit in units)
    small = GatheringSmall(plan, where, vectors, bias)

    def source(g, gather, kept=True):
        return Source(plan, GATHER[g], where, gather.held, kept)

    one.along_z(*range(1, plan.zs))
    grids[2] = trade(grids[:3])[2]
    small.advance()
    grids = fence([one, two, small], grids)
    one.first()
    two.along_z(*range(1, plan.zs // 2 + 1))
    grids[3] = trade(grids)[3]
    small.advance()
    grids = fence([one, two, three, small], grids)
    one.second()
    two.along_z(*range(plan.zs // 2 + 1, plan.zs))
    rows, bias = small.result()
    rows, bias, grids = fence([one, two, three], [rows, bias, grids])
    one.core()
    two.first()
    three.along_z(*range(1, plan.zs // 2 + 1))
    (qkv, probs, ctx), (w_qkv,) = self_forward(dims, source(0, one), work.text, rows, work.lengths)
    (ctx,) = fence([two, three], [ctx])
    two.second()
    three.along_z(*range(plan.zs // 2 + 1, plan.zs))
    grids[1] = trade(grids[:2])[1]
    mask = work.mask()
    ctx, grids, mask = fence([two, three], [ctx, grids, mask])
    two.core()
    three.first()
    (kv, patches), (w_out, w_cq, w_ckv, w_cout) = cross_keys(
        dims, source(1, two), grids, work.cls, rows, work.count
    )
    kv, ctx = fence([three], [kv, ctx])
    three.second()
    total_one, hidden_one, query, cross_probs, cross_ctx, total_two = cross_forward(
        dims, work.text, ctx, kv, mask, w_out, w_cq, w_cout, rows
    )
    total_two = fence([three], total_two)
    three.core()
    layer_out, hidden_two, act, low_three, grad_pre, grad_two, low_two, sum_ffn, sum_pre = ffn_both(
        dims, source(2, three, kept=False), total_two, work.cot, rows, bias
    )

    reduces = {}

    def reduce(g, factors, twice=False, extra=()):
        stacks = weight_grads(plan, REDUCE[g], where, factors, extra)
        reduces[g] = Reducing(plan, REDUCE[g], where, stacks, twice, len(extra))

    def hold(*values, on=None):
        chains = [reduces[g] for g in (reduces if on is None else on)]
        return fence(chains, list(values))

    def go(*groups):
        for g in groups:
            reduces[g].advance()

    reduce(2, [(hidden_two, grad_pre), (act, low_three)], twice=True)
    (low_two,) = hold(low_two)
    go(2)
    grad_query, grad_kv, sum_attend = cross_attend_back(dims, low_two, query, kv, cross_probs, w_cout)
    grad_query, grad_kv = hold(grad_query, grad_kv)
    go(2)
    reduces[2].held[0], grad_query, grad_kv = lax.optimization_barrier(
        (reduces[2].held[0], grad_query, grad_kv)
    )
    reduce(
        1,
        [
            (hidden_one, grad_query),
            (patches.reshape(-1, work.vis), grad_kv.reshape(-1, grad_kv.shape[2])),
            (cross_ctx, low_two),
        ],
    )
    grad_query, grad_kv = hold(grad_query, grad_kv)
    go(2, 1)
    *grids, cls, grad_one, low_one, sum_one = cross_project_back(
        dims, grad_two, grad_query, grad_kv, total_one, w_cq, w_ckv, rows, parts, work.part
    )
    low_one, *grids = hold(low_one, *grids)
    go(2, 1)
    grids[1] = trade(grids[:2])[1]
    grad_qkv, sum_self = self_attend_back(dims, low_one, qkv, probs, w_out)
    sums = gather_sums([sum_self, sum_attend, sum_one, sum_ffn], sum_pre)
    reduce(0, [(work.text, grad_qkv), (ctx, low_one)], extra=(sums,))
    grad_qkv, *grids = hold(grad_qkv, *grids)
    go(0, 1, 2)
    grids[2] = trade(grids[:3])[2]
    text_grad = self_project_back(dims, grad_one, grad_qkv, w_qkv)
    text_grad, *grids = hold(text_grad, *grids)
    go(0, 2)
    hold()
    go(0, 1, 1)
    grids[3] = trade(grids)[3]
    grids = hold(*grids)
    go(0, 0, 2, 1)
    grid_grad = place_grids(work.turn, work.micro, work.items, grids)
    (grid_grad,) = hold(grid_grad)
    go(0, 2, 1)
    go(0)
    *done, extra = reduces[0].held
    grads = [None] * 7
    for g, group in enumerate(REDUCE):
        for w, value in zip(group, done if g == 0 else reduces[g].held):
            grads[w] = value
    small = extra[:ROWS, : vectors.shape[1]], extra[ROWS, : ffn_bias.shape[0]]
    return work.finish(layer_out, text_grad, grid_grad, cls, grads, *small)


def on_device_plain(plan, *args):
    work, parts = Work(args[:7], plan.patch), plan.patch
    dims = work.dims
    weights, rows, bias = fetch_plain(args[7:14], args[14], args[15])
    rows = jnp.pad(rows, ((0, -rows.shape[0] % 8), (0, 0)))
    grids = trade(cut_grids(work.turn, work.image_grid, parts))

    def source(g):
        return Source(plan, GATHER[g], None, [weights[w] for w in GATHER[g]])

    (qkv, probs, ctx), _ = self_forward(dims, source(0), work.text, rows, work.lengths)
    (kv, patches), _ = cross_keys(dims, source(1), grids, work.cls, rows, work.count)
    total_one, hidden_one, query, cross_probs, cross_ctx, total_two = cross_forward(
        dims, work.text, ctx, kv, work.mask(), weights[OUT], weights[CQ], weights[COUT], rows
    )
    layer_out, hidden_two, act, low_three, grad_pre, grad_two, low_two, sum_ffn, sum_pre = ffn_both(
        dims, source(2), total_two, work.cot, rows, bias[None]
    )
    grad_query, grad_kv, sum_attend = cross_attend_back(
        dims, low_two, query, kv, cross_probs, weights[COUT]
    )
    *grids, cls, grad_one, low_one, sum_one = cross_project_back(
        dims, grad_two, grad_query, grad_kv, total_one, weights[CQ], weights[CKV], rows, parts, work.part
    )
    grad_qkv, sum_self = self_attend_back(dims, low_one, qkv, probs, weights[OUT])
    text_grad = self_project_back(dims, grad_one, grad_qkv, weights[QKV])
    flat_kv = grad_kv.reshape(-1, grad_kv.shape[2])
    factors = [
        (work.text, grad_qkv),
        (ctx, low_one),
        (hidden_one, grad_query),
        (patches.reshape(-1, work.vis), flat_kv),
        (cross_ctx, low_two),
        (hidden_two, grad_pre),
        (act, low_three),
    ]
    grads = [reduce_plain(dot_l(a, b).astype(BF16)) for a, b in factors]
    sums = gather_sums([sum_self, sum_attend, sum_one, sum_ffn], sum_pre)
    small = reduce_small_plain(sums[:ROWS], sum_pre[0])
    grid_grad = place_grids(work.turn, work.micro, work.items, trade(grids))
    return work.finish(layer_out, text_grad, grid_grad, cls, grads, *small)


def solution(mesh):
    dp, patch = mesh.shape["dp"], mesh.shape["patch"]
    both = P(None, ("dp", "patch"), None)
    weight = P("dp", "patch")

    def run(*args):
        shards = [(w.shape[0] // dp, w.shape[1] // patch) for w in args[7:14]]
        plan = Plan(dp, patch, shards)
        return jax.shard_map(
            functools.partial(on_device if plan.fast else on_device_plain, plan),
            mesh=mesh,
            in_specs=(
                both,
                P(None, "dp", "patch", None),
                both,
                P(None, ("dp", "patch")),
                P(None, ("dp", "patch")),
                P(None, ("dp", "patch"), None, None),
                both,
            )
            + (weight,) * 7
            + (P(None, "dp"), P("dp")),
            out_specs=(both, both, P(None, "dp", "patch", None), both)
            + (weight,) * 7
            + (P(None, "dp"), P("dp")),
            check_vma=False,
        )(*args)

    return run
```

```python
import functools

import jax
import jax.numpy as jnp
from jax import lax
from jax.experimental import pallas as pl
from jax.experimental.pallas import tpu as pltpu
from jax.sharding import PartitionSpec as P

HEAD = 64
EPS = 1e-06
NEG = -1e30
BF16 = jnp.bfloat16
F32 = jnp.float32
AXES = ("dp", "patch")
VMEM_SPEC = pl.BlockSpec(memory_space=pltpu.VMEM)
SMEM_SPEC = pl.BlockSpec(memory_space=pltpu.SMEM)
PARAMS = pltpu.CompilerParams(vmem_limit_bytes=62 * 2**20)

QKV, OUT, CQ, CKV, COUT, FIN, FOUT = range(7)
ROWS = 13
EXTRA = 16
GATHER = ((QKV,), (OUT, CQ, CKV, COUT), (FIN, FOUT))
REDUCE = ((QKV, OUT), (CQ, CKV, COUT), (FIN, FOUT))


class Plan:
    def __init__(self, dp, patch, shards):
        self.dp, self.patch = dp, patch
        self.zs = dp // 2
        self.devices = dp * patch
        self.chunk = shards[OUT][1] * 2
        self.half = [s[0] // 2 for s in shards]
        self.cols = [s[1] for s in shards]
        self.chunks = [s[1] * 2 // self.chunk for s in shards]
        self.full = [(s[0] * dp, s[1] * patch) for s in shards]
        self.fast = (
            dp % 2 == 0
            and self.zs & (self.zs - 1) == 0
            and patch == 4
            and all(h % 16 == 0 for h in self.half)
            and all(s[1] * 2 % self.chunk == 0 for s in shards)
            and self.chunk % 128 == 0
            and shards[FIN][1] * patch // dp <= self.chunk
        )

    def rows(self, group):
        return sum(self.half[w] * self.chunks[w] for w in group)

    def flip(self, pick):
        return [(i, i ^ pick(i)) for i in range(self.devices)]

    def core(self):
        return self.flip(lambda i: 1)

    def first(self):
        return self.flip(lambda i: 4 if i % 2 == 0 else 2)

    def second(self):
        return self.flip(lambda i: 2 if i % 2 == 0 else 4)

    def along_z(self, k):
        return self.flip(lambda i: 8 * k)


def send(value, perm):
    return lax.ppermute(value, AXES, perm)


def coords():
    dp, patch = lax.axis_index("dp"), lax.axis_index("patch")
    return jnp.stack([dp // 2, dp % 2, patch // 2, patch % 2]).astype(jnp.int32)


def piece_rows(group, plan):
    at, found = 0, []
    for w in group:
        for j in range(plan.chunks[w]):
            found.append((w, j, at))
            at += plan.half[w]
    return found


def group_starts(plan):
    starts, at = [], 0
    for group in GATHER:
        starts.append(at)
        at += plan.rows(group)
    return starts, at


def pack_split(plan, where, shards):
    _, total = group_starts(plan)
    wide = plan.chunk // 2

    def body(where_ref, *refs):
        shard_refs, (own_ref, send_ref, turned) = list(refs[:7]), refs[7:]
        core = where_ref[3]
        turned[...] = shard_refs[FOUT][...].T
        shard_refs[FOUT] = turned
        at = 0
        for group in GATHER:
            for w in group:
                high = plan.half[w]
                for b in range(plan.chunks[w]):
                    cut = slice(b * wide, (b + 1) * wide)
                    own_ref[at : at + high, :] = shard_refs[w][pl.ds(core * high, high), cut]
                    send_ref[at : at + high, :] = shard_refs[w][
                        pl.ds((1 - core) * high, high), cut
                    ]
                    at += high

    shape = jax.ShapeDtypeStruct((total, wide), BF16)
    return pl.pallas_call(
        body,
        out_shape=(shape, shape),
        in_specs=[SMEM_SPEC] + [VMEM_SPEC] * 7,
        out_specs=(VMEM_SPEC, VMEM_SPEC),
        scratch_shapes=[pltpu.VMEM(shards[FOUT].shape, BF16)],
        compiler_params=PARAMS,
        name="pack_split",
    )(where, *shards[:FOUT], shards[FOUT].T)


def pack_join(plan, where, own, got):
    starts, total = group_starts(plan)
    wide = plan.chunk // 2

    def body(where_ref, own_ref, got_ref, *unit_refs):
        core = where_ref[3]

        def fill(low_ref, high_ref):
            for g, group in enumerate(GATHER):
                at = starts[g]
                for w in group:
                    high, count = plan.half[w], plan.chunks[w]
                    for j in range(count):
                        pair = []
                        for b in (2 * j, 2 * j + 1):
                            src = low_ref if b < count else high_ref
                            row = at + (b % count) * high
                            pair.append(src[row : row + high, :])
                        to = at - starts[g] + j * high
                        unit_refs[g][to : to + high, :] = jnp.concatenate(pair, axis=1)
                    at += count * high

        @pl.when(core == 0)
        def _():
            fill(own_ref, got_ref)

        @pl.when(core == 1)
        def _():
            fill(got_ref, own_ref)

    return pl.pallas_call(
        body,
        out_shape=tuple(jax.ShapeDtypeStruct((plan.rows(g), plan.chunk), BF16) for g in GATHER),
        in_specs=[SMEM_SPEC, VMEM_SPEC, VMEM_SPEC],
        out_specs=(VMEM_SPEC,) * len(GATHER),
        compiler_params=PARAMS,
        name="pack_join",
    )(where, own, got)


class Gathering:
    def __init__(self, plan, unit):
        self.plan, self.held = plan, [unit]

    def along_z(self, *steps):
        self.held += [send(self.held[0], self.plan.along_z(k)) for k in steps]

    def first(self):
        stack = jnp.stack(self.held)
        self.held = [stack, send(stack, self.plan.first())]

    def second(self):
        side = [send(part, self.plan.second()) for part in self.held]
        self.held += side + [send(part, self.plan.core()) for part in self.held]

    def core(self):
        self.held += [send(part, self.plan.core()) for part in self.held[2:4]]


def each_place(plan, group, where_ref, visit):
    z, x, y, core = (where_ref[i] for i in range(4))
    for other in range(2):
        half = core ^ other
        for second in range(2):
            for first in range(2):
                x_at = x ^ jnp.where(half == 0, first, second)
                y_at = y ^ jnp.where(half == 0, second, first)
                for k in range(plan.zs):
                    place = ((z ^ k) * 2 + x_at) * 2 + half
                    for w, j, row in piece_rows(group, plan):
                        high = plan.half[w]
                        to_row = pl.multiple_of(place * high, 16)
                        visit(other, second, first, k, row, w, j, to_row, y_at, high)


def add_low(one, two):
    return (one.astype(F32) + two.astype(F32)).astype(BF16)


class Reducing:
    def __init__(self, plan, group, where, stacks, twice=False, extra=0):
        self.plan, self.group, self.where = plan, group, where
        self.twice, self.extra = twice, extra
        self.held = list(stacks)
        self.steps = [self.core, self.second] + [self.again] * twice
        self.steps += [self.first, self.near_z, self.far_z, self.split, self.join]

    def advance(self):
        self.held = list(self.steps.pop(0)(*self.held))

    def core(self, keep, give):
        return keep, send(give, self.plan.core())

    def second(self, keep, got):
        ends = (2, 3, 4) if self.twice else (2, 4)
        gives = [add_low(keep[a:b], got[a:b]) for a, b in zip(ends, ends[1:])]
        gives[0] = send(gives[0], self.plan.second())
        return add_low(keep[:2], got[:2]), *gives

    def again(self, keep, got, give):
        return keep, got, send(give, self.plan.second())

    def first(self, keep, *got):
        near, far = (got[0], got[1][0]) if self.twice else (got[0][:1], got[0][1])
        give = add_low(keep[1], far)
        return add_low(keep[0], near[0]), send(give, self.plan.first())

    def near_z(self, keep, got):
        plan, slots = self.plan, [add_low(keep[k], got[k]) for k in range(self.plan.zs)]
        for k in range(1, plan.zs // 2 + 1):
            slots[k] = send(slots[k], plan.along_z(k))
        return slots

    def far_z(self, *slots):
        plan, slots = self.plan, list(slots)
        for k in range(plan.zs // 2 + 1, plan.zs):
            slots[k] = send(slots[k], plan.along_z(k))
        return slots

    def split(self, *parts):
        own, give, *rest = unpack_split(self.plan, self.group, self.where, parts, self.extra)
        return own, send(give, self.plan.core()), *rest

    def join(self, own, got, *rest):
        return *unpack_join(self.plan, self.group, self.where, own, got), *rest


def fence(chains, values):
    flat, tree = jax.tree.flatten([values, [chain.held for chain in chains]])
    values, held = jax.tree.unflatten(tree, lax.optimization_barrier(flat))
    for chain, arrays in zip(chains, held):
        chain.held = arrays
    return values


def unpack_split(plan, group, where, parts, extra):
    rows, wide = plan.rows(group), plan.chunk // 2
    count = len(parts)

    def body(where_ref, *refs):
        part_refs, (own_ref, give_ref) = refs[:count], refs[count : count + 2]
        core = where_ref[3]
        if extra:
            value = sum(p[rows : rows + EXTRA, :].astype(F32) for p in part_refs)
            refs[-2][...] = value[:ROWS, : refs[-2].shape[1]]
            refs[-1][...] = value[ROWS : ROWS + 1, : refs[-1].shape[1]]

        def fill(low_ref, high_ref):
            at = 0
            for w in group:
                high, count = plan.half[w], plan.chunks[w]
                for j in range(count):
                    row = at + j * high
                    value = sum(p[row : row + high, :].astype(F32) for p in part_refs)
                    for b in (2 * j, 2 * j + 1):
                        dst = low_ref if b < count else high_ref
                        to = at + (b % count) * high
                        cut = (b - 2 * j) * wide
                        dst[to : to + high, :] = value[:, cut : cut + wide]
                at += count * high

        @pl.when(core == 0)
        def _():
            fill(own_ref, give_ref)

        @pl.when(core == 1)
        def _():
            fill(give_ref, own_ref)

    shape = jax.ShapeDtypeStruct((rows, wide), F32)
    return pl.pallas_call(
        body,
        out_shape=(shape, shape)
        + (
            jax.ShapeDtypeStruct((ROWS, plan.full[OUT][1] // plan.dp), F32),
            jax.ShapeDtypeStruct((1, plan.full[FIN][1] // plan.dp), F32),
        )
        * extra,
        in_specs=[SMEM_SPEC] + [VMEM_SPEC] * len(parts),
        out_specs=(VMEM_SPEC,) * (2 + 2 * extra),
        compiler_params=PARAMS,
        name="unpack_split",
    )(where, *parts)


def unpack_join(plan, group, where, own, got):
    wide = plan.chunk // 2
    turned = [w == FOUT for w in group]

    def body(where_ref, own_ref, got_ref, *refs):
        core = where_ref[3]
        at = 0
        for n, w in enumerate(group):
            out_ref = refs[-1] if turned[n] else refs[n]
            high, count = plan.half[w], plan.chunks[w]
            own_rows = pl.ds(pl.multiple_of(core * high, 16), high)
            got_rows = pl.ds(pl.multiple_of((1 - core) * high, 16), high)
            for b in range(count):
                row, cut = at + b * high, slice(b * wide, (b + 1) * wide)
                out_ref[own_rows, cut] = own_ref[row : row + high, :]
                out_ref[got_rows, cut] = got_ref[row : row + high, :]
            at += count * high
            if turned[n]:
                refs[n][...] = out_ref[...].T

    shapes = [(2 * plan.half[w], plan.cols[w]) for w in group]
    done = pl.pallas_call(
        body,
        out_shape=tuple(
            jax.ShapeDtypeStruct(shape[::-1] if turn else shape, F32)
            for shape, turn in zip(shapes, turned)
        ),
        in_specs=[SMEM_SPEC, VMEM_SPEC, VMEM_SPEC],
        out_specs=(VMEM_SPEC,) * len(group),
        scratch_shapes=[pltpu.VMEM(shapes[-1], F32)],
        compiler_params=PARAMS,
        name="unpack_join",
    )(where, own, got)
    return [value.T if turn else value for value, turn in zip(done, turned)]


class GatheringSmall:
    def __init__(self, plan, where, vectors, bias):
        self.plan, self.where, self.shape = plan, where, vectors.shape
        flat = jnp.concatenate([vectors.reshape(-1), bias])
        self.size = flat.shape[0]
        self.held, self.bit = [jnp.pad(flat, (0, -self.size % 2048)).reshape(1, -1, 128)], 4

    def advance(self):
        every = jnp.concatenate(self.held)
        self.held = [every, send(every, self.plan.flip(lambda i: self.bit))]
        self.bit *= 2

    def result(self):
        plan, (count, part) = self.plan, self.shape
        while self.bit < plan.devices:
            self.advance()
        every = jnp.concatenate(self.held).reshape(plan.dp, -1)
        slot = jnp.arange(plan.dp, dtype=jnp.int32) ^ (self.where[0] * 2 + self.where[1])
        every = jnp.take(every, slot, axis=0)[:, : self.size].astype(F32)
        rows = every[:, : count * part].reshape(plan.dp, count, part)
        rows = rows.transpose(1, 0, 2).reshape(count, plan.dp * part)
        bias = every[:, count * part :].reshape(1, -1)
        return jnp.pad(rows, ((0, -count % 8), (0, 0))), bias


def fetch_plain(weights, vectors, bias):
    whole = [
        lax.all_gather(lax.all_gather(w, "dp", axis=0, tiled=True), "patch", axis=1, tiled=True)
        for w in weights
    ]
    rows = lax.all_gather(vectors, "dp", axis=1, tiled=True)
    return whole, rows.astype(F32), lax.all_gather(bias, "dp", axis=0, tiled=True).astype(F32)


def reduce_plain(grad):
    part = lax.psum_scatter(grad, "dp", scatter_dimension=0, tiled=True)
    return lax.psum_scatter(part, "patch", scatter_dimension=1, tiled=True).astype(F32)


def reduce_small_plain(rows, bias):
    rows = lax.psum_scatter(rows, "dp", scatter_dimension=1, tiled=True)
    bias = lax.psum_scatter(bias, "dp", scatter_dimension=0, tiled=True)
    return lax.psum(rows, "patch"), lax.psum(bias, "patch")


TAIL = (0.112528827, 0.117839666, 0.0706314405, 0.2046457425, -0.190499398, 0.3478185715, -0.201092832, 0.03812798145)


def dot(a, b):
    return lax.dot_general(a, b, (((1,), (0,)), ((), ())), preferred_element_type=F32)


def dot_t(a, b):
    return lax.dot_general(a, b, (((1,), (1,)), ((), ())), preferred_element_type=F32)


def dot_l(a, b):
    return lax.dot_general(a, b, (((0,), (0,)), ((), ())), preferred_element_type=F32)


def norm_parts(total):
    center = total - jnp.mean(total, -1, keepdims=True)
    spread = lax.rsqrt(jnp.mean(center * center, -1, keepdims=True) + EPS)
    return center * spread, spread


def norm_pull(grad, hat, spread, gain):
    scaled = grad * gain
    return spread * (
        scaled
        - jnp.mean(scaled, -1, keepdims=True)
        - hat * jnp.mean(scaled * hat, -1, keepdims=True)
    )


def gelu_parts(x):
    bell = jnp.exp(-0.5 * (x * x))
    t = 1.0 / (1.0 + (0.4 * 0.5**0.5) * jnp.abs(x))
    tail = jnp.full_like(t, TAIL[-1])
    for c in TAIL[-2::-1]:
        tail = tail * t + c
    tail = tail * (t * bell)
    return jnp.where(x < 0.0, tail, 1.0 - tail), bell


def col_sum(value):
    return jnp.sum(value.astype(F32), 0, keepdims=True)


def soft(scores):
    grown = jnp.exp(scores - jnp.max(scores, 0, keepdims=True))
    return grown * (1.0 / jnp.sum(grown, 0, keepdims=True))


def soft_pull(probs, grad):
    return probs * (grad - jnp.sum(probs * grad, 0, keepdims=True))


def spread_heads(value, low, high):
    return jnp.concatenate([value * low, value * high], 0)


def join_heads(value):
    count = value.shape[1] // 2
    value = jnp.concatenate([value[:HEAD, :count], value[HEAD:, count:]], 0)
    return value.astype(BF16).T


def lane_masks():
    lane = lax.broadcasted_iota(jnp.int32, (1, 2 * HEAD), 1)
    low = (lane < HEAD).astype(F32)
    return low.astype(BF16), (1.0 - low).astype(BF16)


def whole(shape):
    return pl.BlockSpec(
        shape, lambda i: (0,) * len(shape), pipeline_mode=pl.Buffered(1)
    )


def summed(shape):
    return pl.BlockSpec(shape, lambda i: (0,) * len(shape))


def tiled(shape):
    return pl.BlockSpec(shape, lambda i: (i,) + (0,) * (len(shape) - 1))


def spec_of(shape, dtype):
    return jax.ShapeDtypeStruct(shape, dtype)


def call(body, name, steps, ins, outs, flops, scratch=()):
    out_shape = tuple(shape for shape, _ in outs)
    moved = sum(a.size * a.dtype.itemsize for a, _ in ins)
    moved += sum(o.size * jnp.dtype(o.dtype).itemsize for o in out_shape)
    return pl.pallas_call(
        body,
        grid=(steps,),
        out_shape=out_shape,
        in_specs=[spec for _, spec in ins],
        out_specs=tuple(spec for _, spec in outs),
        scratch_shapes=list(scratch),
        compiler_params=PARAMS,
        cost_estimate=pl.CostEstimate(
            flops=int(flops), bytes_accessed=int(moved), transcendentals=0
        ),
        name=name,
    )(*[a for a, _ in ins])


class Source:
    def __init__(self, plan, group, where, given, kept=True):
        self.plan, self.group, self.pieces, self.given = plan, group, plan.fast, given
        self.outs, self.scratch = [], []
        if not self.pieces:
            self.ins = [(w, whole(w.shape)) for w in given]
            return
        self.ins = [(where, SMEM_SPEC)] + [(part, whole(part.shape)) for part in given]
        if kept:
            self.outs = [(spec_of(plan.full[w], BF16), summed(plan.full[w])) for w in group]
        else:
            self.scratch = [pltpu.VMEM(plan.full[w], BF16) for w in group]

    def open(self, in_refs, out_refs):
        if not self.pieces:
            return list(in_refs)
        where_ref, parts = in_refs[0], in_refs[1:]
        full = dict(zip(self.group, out_refs))
        plan = self.plan

        def visit(other, second, first, k, row, w, j, to_row, to_y, high):
            to_col = pl.multiple_of(to_y * (plan.full[w][1] // 2) + j * plan.chunk, 128)
            part = parts[other * 4 + second * 2 + first]
            full[w][pl.ds(to_row, high), pl.ds(to_col, plan.chunk)] = part[k, row : row + high, :]

        @pl.when(pl.program_id(0) == 0)
        def _():
            each_place(plan, self.group, where_ref, visit)

        return list(out_refs)

    def split(self, done):
        if not self.pieces:
            return done, self.given
        return done[: -len(self.group)], done[-len(self.group) :]


def self_forward(dims, source, text, rows, lengths):
    d, items, length, group = dims.d, dims.items, dims.length, dims.group
    pairs, tokens, block = d // (2 * HEAD), items * length, group * length
    scale = HEAD ** (-0.5)

    n_in = len(source.ins)

    def body(len_ref, x_ref, row_ref, *refs):
        qkv_ref, prob_ref, ctx_ref = refs[n_in : n_in + 3]
        (wqkv_ref,) = source.open(refs[:n_in], refs[n_in + 3 :])
        step = pl.program_id(0)
        low, high = lane_masks()
        x = x_ref[...]
        for part, bias in ((0, 0), (1, None), (2, 1)):
            cut = slice(part * d, (part + 1) * d)
            value = dot(x, wqkv_ref[:, cut])
            if bias is not None:
                value = value + row_ref[bias : bias + 1, :]
            qkv_ref[:, cut] = value.astype(BF16)
        place = lax.broadcasted_iota(jnp.int32, (length, 1), 0)
        for i in range(group):
            ok = place < len_ref[step * group + i]
            r = slice(i * length, (i + 1) * length)
            for p in range(pairs):
                q, k, v = (
                    qkv_ref[r, part * d + p * 128 : part * d + (p + 1) * 128] for part in range(3)
                )
                scores = dot_t(k, spread_heads(q, low, high)) * scale
                probs = soft(jnp.where(ok, scores, NEG)).astype(BF16)
                prob_ref[i, p] = probs
                ctx_ref[r, p * 128 : (p + 1) * 128] = join_heads(dot(v.T, probs))
    done = call(
        body,
        "self_forward",
        items // group,
        [(lengths, SMEM_SPEC), (text, tiled((block, d))), (rows, whole(rows.shape))] + source.ins,
        [
            (spec_of((tokens, 3 * d), BF16), tiled((block, 3 * d))),
            (spec_of((items, pairs, length, 2 * length), BF16), tiled((group, pairs, length, 2 * length))),
            (spec_of((tokens, d), BF16), tiled((block, d))),
        ]
        + source.outs,
        2 * tokens * d * 5 * d,
    )
    return source.split(done)


def cross_keys(dims, source, grids, cls, rows, count):
    d, items, group = dims.d, dims.items, dims.group
    part, vis, parts = grids[0].shape[0] // items, cls.shape[2], len(grids)
    n_in = len(source.ins)

    def body(*refs):
        grid_refs, cls_ref, row_ref = refs[:parts], refs[parts], refs[parts + 1]
        refs = refs[parts + 2 :]
        kv_ref, patch_ref = refs[n_in : n_in + 2]
        _, _, wckv_ref, _ = source.open(refs[:n_in], refs[n_in + 2 :])
        for i in range(group):
            for k in range(parts):
                patch_ref[i, k * part : (k + 1) * part, :] = grid_refs[k][i * part : (i + 1) * part, :]
            rest = jnp.zeros((count - parts * part - 1, vis), BF16)
            patch_ref[i, parts * part :, :] = jnp.concatenate([cls_ref[i], rest], 0)
        patch = patch_ref[...].reshape(group * count, vis)
        keys = dot(patch, wckv_ref[:, :d]).astype(BF16)
        kv_ref[:, :, :d] = keys.reshape(group, count, d)
        values = (dot(patch, wckv_ref[:, d:]) + row_ref[6:7, :]).astype(BF16)
        kv_ref[:, :, d:] = values.reshape(group, count, d)

    done = call(
        body,
        "cross_keys",
        items // group,
        [(grid, tiled((group * part, vis))) for grid in grids]
        + [(cls, tiled((group, 1, vis))), (rows, whole(rows.shape))]
        + source.ins,
        [
            (spec_of((items, count, 2 * d), BF16), tiled((group, count, 2 * d))),
            (spec_of((items, count, vis), BF16), tiled((group, count, vis))),
        ]
        + source.outs,
        2 * items * count * vis * 2 * d,
    )
    return source.split(done)


def cross_forward(dims, text, self_ctx, kv, mask, w_out, w_cq, w_cout, rows):
    d, items, length, group = dims.d, dims.items, dims.length, dims.group
    pairs, tokens, block = d // (2 * HEAD), items * length, group * length
    count = kv.shape[1]
    scale = HEAD ** (-0.5)

    def body(x_ref, self_ref, kv_ref, mask_ref, wout_ref, wcq_ref, wcout_ref, row_ref,
             one_ref, h_ref, cq_ref, prob_ref, ctx_ref, two_ref):
        low, high = lane_masks()
        total = x_ref[...].astype(F32) + dot(self_ref[...], wout_ref[...]) + row_ref[2:3, :]
        one_ref[...] = total
        hat, _ = norm_parts(total)
        hidden = hat * row_ref[3:4, :] + row_ref[4:5, :]
        h_ref[...] = hidden.astype(BF16)
        cq_ref[...] = (dot(h_ref[...], wcq_ref[...]) + row_ref[5:6, :]).astype(BF16)
        for i in range(group):
            ok = mask_ref[i].astype(F32) > 0.5
            ok = jnp.concatenate([ok, ok], 1)
            r = slice(i * length, (i + 1) * length)
            for p in range(pairs):
                c = slice(p * 128, (p + 1) * 128)
                q, k, v = cq_ref[r, c], kv_ref[i, :, c], kv_ref[i, :, d + p * 128 : d + (p + 1) * 128]
                scores = dot_t(k, spread_heads(q, low, high)) * scale
                probs = soft(jnp.where(ok, scores, NEG)).astype(BF16)
                prob_ref[i, p] = probs
                ctx_ref[r, c] = join_heads(dot(v.T, probs))
        two_ref[...] = hidden + dot(ctx_ref[...], wcout_ref[...]) + row_ref[7:8, :]

    return call(
        body,
        "cross_forward",
        items // group,
        [
            (text, tiled((block, d))),
            (self_ctx, tiled((block, d))),
            (kv, tiled((group, count, 2 * d))),
            (mask, tiled((group, count, length))),
            (w_out, whole((d, d))),
            (w_cq, whole((d, d))),
            (w_cout, whole((d, d))),
            (rows, whole(rows.shape)),
        ],
        [
            (spec_of((tokens, d), F32), tiled((block, d))),
            (spec_of((tokens, d), BF16), tiled((block, d))),
            (spec_of((tokens, d), BF16), tiled((block, d))),
            (spec_of((items, pairs, count, 2 * length), BF16), tiled((group, pairs, count, 2 * length))),
            (spec_of((tokens, d), BF16), tiled((block, d))),
            (spec_of((tokens, d), F32), tiled((block, d))),
        ],
        2 * tokens * d * 6 * d,
    )


def ffn_both(dims, source, total_two, cotangent, rows, bias):
    d, items, length, group = dims.d, dims.items, dims.length, dims.group
    tokens, block, ff = items * length, group * length, bias.shape[1]
    piece = d
    n_in = len(source.ins)

    def body(tot_ref, cot_ref, row_ref, bias_ref, *refs):
        (out_ref, h_ref, act_ref, glow_ref, pre_ref, two_ref, twolow_ref, sum_ref, bsum_ref) = refs[
            n_in : n_in + 9
        ]
        slope_ref = refs[n_in + 9]
        win_ref, wout_ref = source.open(refs[:n_in], refs[n_in + 10 :])

        @pl.when(pl.program_id(0) == 0)
        def _():
            sum_ref[...] = jnp.zeros_like(sum_ref)
            bsum_ref[...] = jnp.zeros_like(bsum_ref)

        hat_two, spread_two = norm_parts(tot_ref[...])
        hidden = hat_two * row_ref[8:9, :] + row_ref[9:10, :]
        h_ref[...] = hidden.astype(BF16)
        total = hidden + row_ref[10:11, :]
        cuts = [slice(at, at + piece) for at in range(0, ff, piece)]

        def into(cut):
            return dot(h_ref[...], win_ref[:, cut]) + bias_ref[:, cut]

        def middle(pre, cut):
            under, bell = gelu_parts(pre)
            act_ref[:, cut] = (pre * under).astype(BF16)
            slope_ref[:, cut] = under + (pre * 0.3989422804014327) * bell

        for cut in cuts:
            middle(into(cut), cut)
            total = total + dot(act_ref[:, cut], wout_ref[cut, :])
        hat, spread = norm_parts(total)
        gain = row_ref[11:12, :]
        out_ref[...] = hat * gain + row_ref[12:13, :]
        cot = cot_ref[...].astype(F32)
        grad = norm_pull(cot, hat, spread, gain)
        glow_ref[...] = grad.astype(BF16)
        sum_ref[0:1, :] += col_sum(cot * hat)
        sum_ref[1:2, :] += col_sum(cot)
        sum_ref[2:3, :] += col_sum(glow_ref[...])
        for cut in cuts:
            pre = (dot_t(glow_ref[...], wout_ref[cut, :]) * slope_ref[:, cut]).astype(BF16)
            pre_ref[:, cut] = pre
            bsum_ref[0:1, cut] += col_sum(pre)
            grad = grad + dot_t(pre, win_ref[:, cut])
        two = norm_pull(grad, hat_two, spread_two, row_ref[8:9, :])
        two_ref[...] = two
        low = two.astype(BF16)
        twolow_ref[...] = low
        sum_ref[3:4, :] += col_sum(grad * hat_two)
        sum_ref[4:5, :] += col_sum(grad)
        sum_ref[5:6, :] += col_sum(low)

    return call(
        body,
        "ffn_both",
        items // group,
        [
            (total_two, tiled((block, d))),
            (cotangent, tiled((block, d))),
            (rows, whole(rows.shape)),
            (bias, whole(bias.shape)),
        ]
        + source.ins,
        [
            (spec_of((tokens, d), F32), tiled((block, d))),
            (spec_of((tokens, d), BF16), tiled((block, d))),
            (spec_of((tokens, ff), BF16), tiled((block, ff))),
            (spec_of((tokens, d), BF16), tiled((block, d))),
            (spec_of((tokens, ff), BF16), tiled((block, ff))),
            (spec_of((tokens, d), F32), tiled((block, d))),
            (spec_of((tokens, d), BF16), tiled((block, d))),
            (spec_of((8, d), F32), summed((8, d))),
            (spec_of((8, ff), F32), summed((8, ff))),
        ],
        8 * tokens * d * ff,
        [pltpu.VMEM((block, ff), F32)] + source.scratch,
    )


def pair_pull(q, k, v, out, probs, low, high):
    outs = spread_heads(out, low, high)
    score = soft_pull(probs.astype(F32), dot_t(v, outs)).astype(BF16)
    grad_k = dot(score, spread_heads(q, low, high))
    return dot(k.T, score), grad_k, dot(probs, outs)


def cross_attend_back(dims, grad_low, query, kv, probs, w_cout):
    d, items, length, group = dims.d, dims.items, dims.length, dims.group
    pairs, tokens, block = d // (2 * HEAD), items * length, group * length
    count = kv.shape[1]
    scale = HEAD ** (-0.5)

    def body(glow_ref, q_ref, kv_ref, prob_ref, wcout_ref, gq_ref, gkv_ref, sum_ref, ctx_ref):
        @pl.when(pl.program_id(0) == 0)
        def _():
            sum_ref[...] = jnp.zeros_like(sum_ref)

        low, high = lane_masks()
        ctx_ref[...] = dot_t(glow_ref[...], wcout_ref[...]).astype(BF16)
        for i in range(group):
            r = slice(i * length, (i + 1) * length)
            for p in range(pairs):
                c = slice(p * 128, (p + 1) * 128)
                cv = slice(d + p * 128, d + (p + 1) * 128)
                grad_q, grad_k, grad_v = pair_pull(
                    q_ref[r, c], kv_ref[i, :, c], kv_ref[i, :, cv], ctx_ref[r, c], prob_ref[i, p], low, high
                )
                gq_ref[r, c] = join_heads(grad_q * scale)
                gkv_ref[i, :, c] = (grad_k * scale).astype(BF16)
                gkv_ref[i, :, cv] = grad_v.astype(BF16)
        sum_ref[0:1, :] += col_sum(gq_ref[...])
        sum_ref[1:2, :] += col_sum(gkv_ref[:, :, d:].reshape(group * count, d))

    return call(
        body,
        "cross_attend_back",
        items // group,
        [
            (grad_low, tiled((block, d))),
            (query, tiled((block, d))),
            (kv, tiled((group, count, 2 * d))),
            (probs, tiled((group, pairs, count, 2 * length))),
            (w_cout, whole((d, d))),
        ],
        [
            (spec_of((tokens, d), BF16), tiled((block, d))),
            (spec_of((items, count, 2 * d), BF16), tiled((group, count, 2 * d))),
            (spec_of((8, d), F32), summed((8, d))),
        ],
        2 * tokens * d * 4 * d,
        [pltpu.VMEM((block, d), BF16)],
    )


def cross_project_back(dims, grad_two, grad_query, grad_kv, total_one, w_cq, w_ckv, rows, parts, part):
    d, items, length, group = dims.d, dims.items, dims.length, dims.group
    tokens, block = items * length, group * length
    count, vis = grad_kv.shape[1], w_ckv.shape[0]

    def body(g_ref, gq_ref, gkv_ref, tot_ref, wcq_ref, wckv_ref, row_ref, *refs):
        grid_refs, (cls_ref, one_ref, onelow_ref, sum_ref) = refs[:parts], refs[parts:]

        @pl.when(pl.program_id(0) == 0)
        def _():
            sum_ref[...] = jnp.zeros_like(sum_ref)

        for i in range(group):
            value = dot_t(gkv_ref[i], wckv_ref[...])
            for k in range(parts):
                grid_refs[k][i * part : (i + 1) * part, :] = value[k * part : (k + 1) * part, :].astype(BF16)
            cls_ref[i] = value[parts * part : parts * part + 1, :]
        grad = g_ref[...] + dot_t(gq_ref[...], wcq_ref[...])
        hat, spread = norm_parts(tot_ref[...])
        one = norm_pull(grad, hat, spread, row_ref[3:4, :])
        one_ref[...] = one
        one_low = one.astype(BF16)
        onelow_ref[...] = one_low
        sum_ref[0:1, :] += col_sum(grad * hat)
        sum_ref[1:2, :] += col_sum(grad)
        sum_ref[2:3, :] += col_sum(one_low)

    return call(
        body,
        "cross_project_back",
        items // group,
        [
            (grad_two, tiled((block, d))),
            (grad_query, tiled((block, d))),
            (grad_kv, tiled((group, count, 2 * d))),
            (total_one, tiled((block, d))),
            (w_cq, whole((d, d))),
            (w_ckv, whole((vis, 2 * d))),
            (rows, whole(rows.shape)),
        ],
        [(spec_of((items * part, vis), BF16), tiled((group * part, vis)))] * parts
        + [
            (spec_of((items, 1, vis), F32), tiled((group, 1, vis))),
            (spec_of((tokens, d), F32), tiled((block, d))),
            (spec_of((tokens, d), BF16), tiled((block, d))),
            (spec_of((8, d), F32), summed((8, d))),
        ],
        2 * tokens * d * d + 2 * items * count * vis * 2 * d,
    )


def self_attend_back(dims, grad_low, qkv, probs, w_out):
    d, items, length, group = dims.d, dims.items, dims.length, dims.group
    pairs, tokens, block = d // (2 * HEAD), items * length, group * length
    scale = HEAD ** (-0.5)

    def body(glow_ref, qkv_ref, prob_ref, wout_ref, gqkv_ref, sum_ref, ctx_ref):
        @pl.when(pl.program_id(0) == 0)
        def _():
            sum_ref[...] = jnp.zeros_like(sum_ref)

        low, high = lane_masks()
        ctx_ref[...] = dot_t(glow_ref[...], wout_ref[...]).astype(BF16)
        for i in range(group):
            r = slice(i * length, (i + 1) * length)
            for p in range(pairs):
                cuts = [slice(part * d + p * 128, part * d + (p + 1) * 128) for part in range(3)]
                q, k, v = (qkv_ref[r, cut] for cut in cuts)
                grad_q, grad_k, grad_v = pair_pull(q, k, v, ctx_ref[r, cuts[0]], prob_ref[i, p], low, high)
                gqkv_ref[r, cuts[0]] = join_heads(grad_q * scale)
                gqkv_ref[r, cuts[1]] = (grad_k * scale).astype(BF16)
                gqkv_ref[r, cuts[2]] = grad_v.astype(BF16)
        sum_ref[0:1, :] += col_sum(gqkv_ref[:, :d])
        sum_ref[1:2, :] += col_sum(gqkv_ref[:, 2 * d :])

    return call(
        body,
        "self_attend_back",
        items // group,
        [
            (grad_low, tiled((block, d))),
            (qkv, tiled((block, 3 * d))),
            (probs, tiled((group, pairs, length, 2 * length))),
            (w_out, whole((d, d))),
        ],
        [
            (spec_of((tokens, 3 * d), BF16), tiled((block, 3 * d))),
            (spec_of((8, d), F32), summed((8, d))),
        ],
        2 * tokens * d * 4 * d,
        [pltpu.VMEM((block, d), BF16)],
    )


def self_project_back(dims, grad_one, grad_qkv, w_qkv):
    d, items, length, group = dims.d, dims.items, dims.length, dims.group
    tokens, block = items * length, group * length

    def body(g_ref, gqkv_ref, wqkv_ref, text_ref):
        text_ref[...] = g_ref[...] + dot_t(gqkv_ref[...], wqkv_ref[...])

    return call(
        body,
        "self_project_back",
        items // group,
        [
            (grad_one, tiled((block, d))),
            (grad_qkv, tiled((block, 3 * d))),
            (w_qkv, whole((d, 3 * d))),
        ],
        [(spec_of((tokens, d), F32), tiled((block, d)))],
        2 * tokens * d * 3 * d,
    )[0]


def cut_grids(turn, image_grid, parts):
    micro, items, part, vis = image_grid.shape
    each = items // parts

    def body(turn_ref, grid_ref, *out_refs):
        def fill(own):
            value = jnp.swapaxes(grid_ref[0], 0, 1)
            for s in range(parts):
                mine = value[s * each : (s + 1) * each]
                out_refs[s ^ own][...] = mine.reshape(each * part, vis)

        for own in range(parts):
            pl.when(turn_ref[0] == own)(functools.partial(fill, own))

    return call(
        body,
        "cut_grids",
        micro,
        [
            (turn, SMEM_SPEC),
            (image_grid.transpose(0, 2, 1, 3), tiled((1, part, items, vis))),
        ],
        [(spec_of((micro * each * part, vis), BF16), tiled((each * part, vis)))] * parts,
        0,
    )


def place_grids(turn, micro, items, pieces):
    part, vis = pieces[0].shape[0] // items, pieces[0].shape[1]
    each, parts = items // micro, len(pieces)

    def body(turn_ref, *refs):
        def fill(own):
            value = [
                refs[s ^ own][...].astype(F32).reshape(each, part, vis) for s in range(parts)
            ]
            refs[-1][0] = jnp.swapaxes(jnp.concatenate(value, 0), 0, 1)

        for own in range(parts):
            pl.when(turn_ref[0] == own)(functools.partial(fill, own))

    shape = (micro, part, each * parts, vis)
    done = call(
        body,
        "place_grids",
        micro,
        [(turn, SMEM_SPEC)] + [(p, tiled((each * part, vis))) for p in pieces],
        [(spec_of(shape, F32), tiled((1,) + shape[1:]))],
        0,
    )[0]
    return done.transpose(0, 2, 1, 3)


SUMS = ((0, 0, 2), (2, 2, 1), (2, 0, 2), (1, 0, 2), (3, 5, 1), (3, 3, 2), (3, 2, 1), (3, 0, 2))


def rows_of(sums):
    return jnp.concatenate([sums[n][row : row + count] for n, row, count in SUMS])


def weight_grads(plan, group, where, factors, extra=()):
    high_rows = max(plan.full[w][0] for w in group)
    wide = max(plan.full[w][1] for w in group)
    flat = [a for pair in factors for a in pair]
    count, base = len(flat), plan.rows(group)

    def body(where_ref, *refs):
        far, (own_ref, other_ref) = refs[:count], refs[count + len(extra) : count + len(extra) + 2]
        stack_refs = (own_ref, other_ref)
        scratch = refs[count + len(extra) + 2 :]
        near, made, sems = scratch[:count], scratch[count], scratch[count + 1]
        copies = [pltpu.make_async_copy(far[n], near[n], sems.at[n]) for n in range(count)]
        for copy in copies:
            copy.start()
        if extra:
            add_extra(where_ref, refs[count : count + len(extra)], stack_refs, *scratch[count + 2 :])
        for n, w in enumerate(group):
            left, right = near[2 * n], near[2 * n + 1]
            rows, cols = plan.full[w]
            copies[2 * n].wait()
            copies[2 * n + 1].wait()
            for at in range(0, rows, 256):
                value = dot_l(left[:, at : at + 256], right[...])
                made[at : at + 256, :cols] = value.astype(BF16)

            def visit(other, second, first, k, row, w_at, j, to_row, to_y, high):
                if w_at == w:
                    col = pl.multiple_of(to_y * (cols // 2) + j * plan.chunk, 128)
                    stack_refs[other][second * 2 + first, k, row : row + high, :] = made[
                        pl.ds(to_row, high), pl.ds(col, plan.chunk)
                    ]

            each_place(plan, group, where_ref, visit)

    def add_extra(where_ref, sum_refs, stack_refs, table, lines):
        width = lines.shape[1] // plan.dp
        step = plan.full[FIN][1] // plan.dp
        at = 0
        for n, row, many in SUMS:
            lines[at : at + many, :] = sum_refs[n][row : row + many, :]
            at += many
        table[...] = jnp.zeros_like(table)
        for n in range(plan.dp):
            table[n, :ROWS, :width] = lines[:ROWS, n * width : (n + 1) * width]
            table[n, ROWS : ROWS + 1, :step] = sum_refs[-1][0:1, n * step : (n + 1) * step]
        z, x, _, core = (where_ref[i] for i in range(4))
        for other in range(2):
            for second in range(2):
                for first in range(2):
                    x_at = x ^ jnp.where((core ^ other) == 0, first, second)
                    for k in range(plan.zs):
                        value = table[(z ^ k) * 2 + x_at].astype(BF16)
                        stack_refs[other][second * 2 + first, k, base : base + EXTRA, :] = value

    high = base + (EXTRA if extra else 0)
    shape = jax.ShapeDtypeStruct((4, plan.zs, high, plan.chunk), BF16)
    flops = sum(2 * a.shape[0] * a.shape[1] * b.shape[1] for a, b in factors)
    moved = sum(a.size * 2 for a in flat) + 2 * shape.size * 2
    table = []
    if extra:
        table.append(pltpu.VMEM((plan.dp, EXTRA, plan.chunk), F32))
        table.append(pltpu.VMEM((EXTRA, plan.full[OUT][1]), F32))
    return pl.pallas_call(
        body,
        out_shape=(shape,) * 2,
        in_specs=[SMEM_SPEC]
        + [pl.BlockSpec(memory_space=pl.ANY)] * count
        + [VMEM_SPEC] * len(extra),
        out_specs=(VMEM_SPEC,) * 2,
        scratch_shapes=[pltpu.VMEM(a.shape, BF16) for a in flat]
        + [pltpu.VMEM((high_rows, wide), BF16), pltpu.SemaphoreType.DMA((count,))]
        + table,
        compiler_params=PARAMS,
        cost_estimate=pl.CostEstimate(flops=flops, bytes_accessed=moved, transcendentals=0),
        name="weight_grads",
    )(where, *flat, *extra)


class Dims:
    def __init__(self, d, items, length):
        self.d, self.items, self.length = d, items, length
        self.group = 2 if items % 2 == 0 else 1


def cross_mask(lengths, counts, boxes, length, count):
    place = jnp.arange(length, dtype=jnp.int32)[None, :]
    boxed = (counts[:, None] > 0) & (place < lengths[:, None])
    phrase = jnp.where(boxed, place * counts[:, None] // lengths[:, None], 0)
    chosen = phrase[:, None, :] == jnp.arange(boxes.shape[1], dtype=jnp.int32)[None, :, None]
    inside = jnp.einsum(
        "ijp,ijt->ipt",
        (boxes > 0).astype(BF16),
        chosen.astype(BF16),
        preferred_element_type=F32,
    )
    grid_ok = jnp.where(boxed[:, None, :], inside, 1.0).astype(BF16)
    items, real = grid_ok.shape[:2]
    own = jnp.ones((items, 1, length), BF16)
    return jnp.concatenate([grid_ok, own, jnp.zeros((items, count - real - 1, length), BF16)], 1)


def trade(pieces):
    parts = lax.axis_size("patch")
    return [pieces[0]] + [
        lax.ppermute(pieces[k], "patch", [(i, i ^ k) for i in range(parts)])
        for k in range(1, len(pieces))
    ]


class Work:
    def __init__(self, args, parts):
        (self.text_in, self.image_grid, self.image_cls, lengths, counts, boxes, cot) = args
        self.parts = parts
        self.micro, d = self.text_in.shape[0], self.text_in.shape[2]
        self.items = lengths.size
        self.text, self.cot = self.text_in.reshape(-1, d), cot.reshape(-1, d)
        self.lengths, self.counts = lengths.reshape(-1), counts.reshape(-1)
        self.boxes = boxes.reshape((self.items,) + boxes.shape[2:])
        self.dims = Dims(d, self.items, self.text.shape[0] // self.items)
        self.turn = lax.axis_index("patch").astype(jnp.int32).reshape(1)
        self.part, self.vis = self.image_grid.shape[2:]
        self.each = self.items // self.micro
        self.count = -(-(parts * self.part + 1) // 16) * 16
        self.cls = self.image_cls.reshape(self.items, 1, self.vis)

    def mask(self):
        boxes = self.boxes.reshape(self.items, -1, self.parts, self.part)
        order = jnp.arange(self.parts, dtype=jnp.int32) ^ self.turn[0]
        boxes = jnp.take(boxes, order, axis=2).reshape(self.boxes.shape)
        return cross_mask(self.lengths, self.counts, boxes, self.dims.length, self.count)

    def finish(self, layer_out, text_grad, grid_grad, cls, grads, rows_grad, bias_grad):
        return (
            layer_out.reshape(self.text_in.shape),
            text_grad.reshape(self.text_in.shape),
            grid_grad,
            cls.reshape(self.image_cls.shape),
            *grads,
            rows_grad,
            bias_grad,
        )


def on_device(plan, *args):
    work, shards, vectors, ffn_bias = Work(args[:7], plan.patch), args[7:14], args[14], args[15]
    dims, where, parts = work.dims, coords(), plan.patch

    own, give = pack_split(plan, where, shards)
    units = pack_join(plan, where, own, send(give, plan.core()))
    grids = list(cut_grids(work.turn, work.image_grid, parts))
    vectors, bias, grids, units = lax.optimization_barrier((vectors, ffn_bias, grids, units))
    one, two, three = (Gathering(plan, unit) for unit in units)
    small = GatheringSmall(plan, where, vectors, bias)

    def source(g, gather, kept=True):
        return Source(plan, GATHER[g], where, gather.held, kept)

    one.along_z(*range(1, plan.zs))
    grids[2] = trade(grids[:3])[2]
    small.advance()
    grids = fence([one, two, small], grids)
    one.first()
    two.along_z(*range(1, plan.zs // 2 + 1))
    grids[3] = trade(grids)[3]
    small.advance()
    grids = fence([one, two, three, small], grids)
    one.second()
    two.along_z(*range(plan.zs // 2 + 1, plan.zs))
    rows, bias = small.result()
    rows, bias, grids = fence([one, two, three], [rows, bias, grids])
    one.core()
    two.first()
    three.along_z(*range(1, plan.zs // 2 + 1))
    (qkv, probs, ctx), (w_qkv,) = self_forward(dims, source(0, one), work.text, rows, work.lengths)
    (ctx,) = fence([two, three], [ctx])
    two.second()
    three.along_z(*range(plan.zs // 2 + 1, plan.zs))
    grids[1] = trade(grids[:2])[1]
    mask = work.mask()
    ctx, grids, mask = fence([two, three], [ctx, grids, mask])
    two.core()
    three.first()
    (kv, patches), (w_out, w_cq, w_ckv, w_cout) = cross_keys(
        dims, source(1, two), grids, work.cls, rows, work.count
    )
    kv, ctx = fence([three], [kv, ctx])
    three.second()
    total_one, hidden_one, query, cross_probs, cross_ctx, total_two = cross_forward(
        dims, work.text, ctx, kv, mask, w_out, w_cq, w_cout, rows
    )
    total_two = fence([three], total_two)
    three.core()
    layer_out, hidden_two, act, low_three, grad_pre, grad_two, low_two, sum_ffn, sum_pre = ffn_both(
        dims, source(2, three, kept=False), total_two, work.cot, rows, bias
    )

    reduces = {}

    def reduce(g, factors, twice=False, extra=()):
        stacks = weight_grads(plan, REDUCE[g], where, factors, extra)
        reduces[g] = Reducing(plan, REDUCE[g], where, stacks, twice, 1 if extra else 0)

    def hold(*values, on=None):
        chains = [reduces[g] for g in (reduces if on is None else on)]
        return fence(chains, list(values))

    def go(*groups):
        for g in groups:
            reduces[g].advance()

    reduce(2, [(hidden_two, grad_pre), (act, low_three)], twice=True)
    (low_two,) = hold(low_two)
    go(2)
    grad_query, grad_kv, sum_attend = cross_attend_back(dims, low_two, query, kv, cross_probs, w_cout)
    grad_query, grad_kv = hold(grad_query, grad_kv)
    go(2)
    reduces[2].held[0], grad_query, grad_kv = lax.optimization_barrier(
        (reduces[2].held[0], grad_query, grad_kv)
    )
    reduce(
        1,
        [
            (hidden_one, grad_query),
            (patches.reshape(-1, work.vis), grad_kv.reshape(-1, grad_kv.shape[2])),
            (cross_ctx, low_two),
        ],
    )
    grad_query, grad_kv = hold(grad_query, grad_kv)
    go(2, 1)
    *grids, cls, grad_one, low_one, sum_one = cross_project_back(
        dims, grad_two, grad_query, grad_kv, total_one, w_cq, w_ckv, rows, parts, work.part
    )
    low_one, *grids = hold(low_one, *grids)
    go(2)
    grids[1] = trade(grids[:2])[1]
    grad_qkv, sum_self = self_attend_back(dims, low_one, qkv, probs, w_out)
    grad_qkv, *grids = hold(grad_qkv, *grids)
    go(1, 2)
    sums = (sum_self, sum_attend, sum_one, sum_ffn, sum_pre)
    reduce(0, [(work.text, grad_qkv), (ctx, low_one)], extra=sums)
    (grad_qkv,) = hold(grad_qkv)
    go(0, 1, 2)
    grids[2] = trade(grids[:3])[2]
    text_grad = self_project_back(dims, grad_one, grad_qkv, w_qkv)
    text_grad, *grids = hold(text_grad, *grids)
    go(0, 1)
    hold()
    go(0, 1, 2)
    grids = hold(*grids)
    go(0, 0, 1, 2)
    grids[3] = trade(grids)[3]
    grids = hold(*grids)
    go(0, 1)
    grid_grad = place_grids(work.turn, work.micro, work.items, grids)
    go(0)
    *done, rows_grad, bias_grad = reduces[0].held
    grads = [None] * 7
    for g, group in enumerate(REDUCE):
        for w, value in zip(group, done if g == 0 else reduces[g].held):
            grads[w] = value
    return work.finish(
        layer_out, text_grad, grid_grad, cls, grads, rows_grad, bias_grad.reshape(-1)
    )


def on_device_plain(plan, *args):
    work, parts = Work(args[:7], plan.patch), plan.patch
    dims = work.dims
    weights, rows, bias = fetch_plain(args[7:14], args[14], args[15])
    rows = jnp.pad(rows, ((0, -rows.shape[0] % 8), (0, 0)))
    grids = trade(cut_grids(work.turn, work.image_grid, parts))

    def source(g):
        return Source(plan, GATHER[g], None, [weights[w] for w in GATHER[g]])

    (qkv, probs, ctx), _ = self_forward(dims, source(0), work.text, rows, work.lengths)
    (kv, patches), _ = cross_keys(dims, source(1), grids, work.cls, rows, work.count)
    total_one, hidden_one, query, cross_probs, cross_ctx, total_two = cross_forward(
        dims, work.text, ctx, kv, work.mask(), weights[OUT], weights[CQ], weights[COUT], rows
    )
    layer_out, hidden_two, act, low_three, grad_pre, grad_two, low_two, sum_ffn, sum_pre = ffn_both(
        dims, source(2), total_two, work.cot, rows, bias[None]
    )
    grad_query, grad_kv, sum_attend = cross_attend_back(
        dims, low_two, query, kv, cross_probs, weights[COUT]
    )
    *grids, cls, grad_one, low_one, sum_one = cross_project_back(
        dims, grad_two, grad_query, grad_kv, total_one, weights[CQ], weights[CKV], rows, parts, work.part
    )
    grad_qkv, sum_self = self_attend_back(dims, low_one, qkv, probs, weights[OUT])
    text_grad = self_project_back(dims, grad_one, grad_qkv, weights[QKV])
    flat_kv = grad_kv.reshape(-1, grad_kv.shape[2])
    factors = [
        (work.text, grad_qkv),
        (ctx, low_one),
        (hidden_one, grad_query),
        (patches.reshape(-1, work.vis), flat_kv),
        (cross_ctx, low_two),
        (hidden_two, grad_pre),
        (act, low_three),
    ]
    grads = [reduce_plain(dot_l(a, b).astype(BF16)) for a, b in factors]
    sums = rows_of([sum_self, sum_attend, sum_one, sum_ffn])
    small = reduce_small_plain(sums, sum_pre[0])
    grid_grad = place_grids(work.turn, work.micro, work.items, trade(grids))
    return work.finish(layer_out, text_grad, grid_grad, cls, grads, *small)


def solution(mesh):
    dp, patch = mesh.shape["dp"], mesh.shape["patch"]
    both = P(None, ("dp", "patch"), None)
    weight = P("dp", "patch")

    def run(*args):
        shards = [(w.shape[0] // dp, w.shape[1] // patch) for w in args[7:14]]
        plan = Plan(dp, patch, shards)
        return jax.shard_map(
            functools.partial(on_device if plan.fast else on_device_plain, plan),
            mesh=mesh,
            in_specs=(
                both,
                P(None, "dp", "patch", None),
                both,
                P(None, ("dp", "patch")),
                P(None, ("dp", "patch")),
                P(None, ("dp", "patch"), None, None),
                both,
            )
            + (weight,) * 7
            + (P(None, "dp"), P("dp")),
            out_specs=(both, both, P(None, "dp", "patch", None), both)
            + (weight,) * 7
            + (P(None, "dp"), P("dp")),
            check_vma=False,
        )(*args)

    return run
```

```python
import functools

import jax
import jax.numpy as jnp
from jax import lax
from jax.experimental import pallas as pl
from jax.experimental.pallas import tpu as pltpu
from jax.sharding import PartitionSpec as P

HEAD = 64
EPS = 1e-06
NEG = -1e30
BF16 = jnp.bfloat16
F32 = jnp.float32
AXES = ("dp", "patch")
VMEM_SPEC = pl.BlockSpec(memory_space=pltpu.VMEM)
SMEM_SPEC = pl.BlockSpec(memory_space=pltpu.SMEM)
PARAMS = pltpu.CompilerParams(vmem_limit_bytes=62 * 2**20)

QKV, OUT, CQ, CKV, COUT, FIN, FOUT = range(7)
ROWS = 13
EXTRA = 16
TOGETHER = 6
GATHER = ((QKV,), (OUT, CQ, CKV, COUT), (FIN, FOUT))
REDUCE = ((QKV, OUT), (CQ, CKV, COUT), (FIN, FOUT))


class Plan:
    def __init__(self, dp, patch, shards):
        self.dp, self.patch = dp, patch
        self.zs = dp // 2
        self.devices = dp * patch
        self.chunk = shards[OUT][1] * 2
        self.half = [s[0] // 2 for s in shards]
        self.cols = [s[1] for s in shards]
        self.chunks = [s[1] * 2 // self.chunk for s in shards]
        self.full = [(s[0] * dp, s[1] * patch) for s in shards]
        self.fast = (
            dp % 2 == 0
            and self.zs & (self.zs - 1) == 0
            and patch == 4
            and all(h % 16 == 0 for h in self.half)
            and all(s[1] * 2 % self.chunk == 0 for s in shards)
            and self.chunk % 128 == 0
            and shards[FIN][1] * patch // dp <= self.chunk
        )

    def rows(self, group):
        return sum(self.half[w] * self.chunks[w] for w in group)

    def flip(self, pick):
        return [(i, i ^ pick(i)) for i in range(self.devices)]

    def core(self):
        return self.flip(lambda i: 1)

    def first(self):
        return self.flip(lambda i: 4 if i % 2 == 0 else 2)

    def second(self):
        return self.flip(lambda i: 2 if i % 2 == 0 else 4)

    def along_z(self, k):
        return self.flip(lambda i: 8 * k)


def send(value, perm):
    return lax.ppermute(value, AXES, perm)


def coords():
    dp, patch = lax.axis_index("dp"), lax.axis_index("patch")
    return jnp.stack([dp // 2, dp % 2, patch // 2, patch % 2]).astype(jnp.int32)


def piece_rows(group, plan):
    at, found = 0, []
    for w in group:
        for j in range(plan.chunks[w]):
            found.append((w, j, at))
            at += plan.half[w]
    return found


def group_starts(plan):
    starts, at = [], 0
    for group in GATHER:
        starts.append(at)
        at += plan.rows(group)
    return starts, at


def pack_split(plan, where, shards):
    _, total = group_starts(plan)
    wide = plan.chunk // 2

    def body(where_ref, *refs):
        shard_refs, (own_ref, send_ref, turned) = list(refs[:7]), refs[7:]
        core = where_ref[3]
        turned[...] = shard_refs[FOUT][...].T
        shard_refs[FOUT] = turned
        at = 0
        for group in GATHER:
            for w in group:
                high = plan.half[w]
                for b in range(plan.chunks[w]):
                    cut = slice(b * wide, (b + 1) * wide)
                    own_ref[at : at + high, :] = shard_refs[w][pl.ds(core * high, high), cut]
                    send_ref[at : at + high, :] = shard_refs[w][
                        pl.ds((1 - core) * high, high), cut
                    ]
                    at += high

    shape = jax.ShapeDtypeStruct((total, wide), BF16)
    return pl.pallas_call(
        body,
        out_shape=(shape, shape),
        in_specs=[SMEM_SPEC] + [VMEM_SPEC] * 7,
        out_specs=(VMEM_SPEC, VMEM_SPEC),
        scratch_shapes=[pltpu.VMEM(shards[FOUT].shape, BF16)],
        compiler_params=PARAMS,
        name="pack_split",
    )(where, *shards[:FOUT], shards[FOUT].T)


def pack_join(plan, where, own, got):
    starts, total = group_starts(plan)
    wide = plan.chunk // 2

    def body(where_ref, own_ref, got_ref, *unit_refs):
        core = where_ref[3]

        def fill(low_ref, high_ref):
            for g, group in enumerate(GATHER):
                at = starts[g]
                for w in group:
                    high, count = plan.half[w], plan.chunks[w]
                    for j in range(count):
                        pair = []
                        for b in (2 * j, 2 * j + 1):
                            src = low_ref if b < count else high_ref
                            row = at + (b % count) * high
                            pair.append(src[row : row + high, :])
                        to = at - starts[g] + j * high
                        unit_refs[g][to : to + high, :] = jnp.concatenate(pair, axis=1)
                    at += count * high

        @pl.when(core == 0)
        def _():
            fill(own_ref, got_ref)

        @pl.when(core == 1)
        def _():
            fill(got_ref, own_ref)

    return pl.pallas_call(
        body,
        out_shape=tuple(jax.ShapeDtypeStruct((plan.rows(g), plan.chunk), BF16) for g in GATHER),
        in_specs=[SMEM_SPEC, VMEM_SPEC, VMEM_SPEC],
        out_specs=(VMEM_SPEC,) * len(GATHER),
        compiler_params=PARAMS,
        name="pack_join",
    )(where, own, got)


class Gathering:
    def __init__(self, plan, unit):
        self.plan, self.held = plan, [unit]

    def along_z(self, *steps):
        self.held += [send(self.held[0], self.plan.along_z(k)) for k in steps]

    def first(self):
        stack = jnp.stack(self.held)
        self.held = [stack, send(stack, self.plan.first())]

    def second(self):
        side = [send(part, self.plan.second()) for part in self.held]
        self.held += side + [send(part, self.plan.core()) for part in self.held]

    def core(self):
        self.held += [send(part, self.plan.core()) for part in self.held[2:4]]


def each_place(plan, group, where_ref, visit):
    z, x, y, core = (where_ref[i] for i in range(4))
    for other in range(2):
        half = core ^ other
        for second in range(2):
            for first in range(2):
                x_at = x ^ jnp.where(half == 0, first, second)
                y_at = y ^ jnp.where(half == 0, second, first)
                for k in range(plan.zs):
                    place = ((z ^ k) * 2 + x_at) * 2 + half
                    for w, j, row in piece_rows(group, plan):
                        high = plan.half[w]
                        to_row = pl.multiple_of(place * high, 16)
                        visit(other, second, first, k, row, w, j, to_row, y_at, high)


def add_low(one, two):
    return (one.astype(F32) + two.astype(F32)).astype(BF16)


class Reducing:
    def __init__(self, plan, group, where, stacks, twice=False, extra=0):
        self.plan, self.group, self.where = plan, group, where
        self.twice, self.extra = twice, extra
        self.held = list(stacks)
        self.steps = [self.core, self.second] + [self.again] * twice
        self.steps += [self.first, self.near_z, self.far_z, self.split, self.join]

    def advance(self):
        self.held = list(self.steps.pop(0)(*self.held))

    def core(self, keep, give):
        return keep, send(give, self.plan.core())

    def second(self, keep, got):
        ends = (2, 3, 4) if self.twice else (2, 4)
        gives = [add_low(keep[a:b], got[a:b]) for a, b in zip(ends, ends[1:])]
        gives[0] = send(gives[0], self.plan.second())
        return add_low(keep[:2], got[:2]), *gives

    def again(self, keep, got, give):
        return keep, got, send(give, self.plan.second())

    def first(self, keep, *got):
        near, far = (got[0], got[1][0]) if self.twice else (got[0][:1], got[0][1])
        give = add_low(keep[1], far)
        return add_low(keep[0], near[0]), send(give, self.plan.first())

    def near_z(self, keep, got):
        plan, slots = self.plan, [add_low(keep[k], got[k]) for k in range(self.plan.zs)]
        for k in range(1, plan.zs // 2 + 1):
            slots[k] = send(slots[k], plan.along_z(k))
        return slots

    def far_z(self, *slots):
        plan, slots = self.plan, list(slots)
        for k in range(plan.zs // 2 + 1, plan.zs):
            slots[k] = send(slots[k], plan.along_z(k))
        return slots

    def split(self, *parts):
        own, give, *rest = unpack_split(self.plan, self.group, self.where, parts, self.extra)
        return own, send(give, self.plan.core()), *rest

    def join(self, own, got, *rest):
        return *unpack_join(self.plan, self.group, self.where, own, got), *rest


def fence(chains, values):
    flat, tree = jax.tree.flatten([values, [chain.held for chain in chains]])
    values, held = jax.tree.unflatten(tree, lax.optimization_barrier(flat))
    for chain, arrays in zip(chains, held):
        chain.held = arrays
    return values


def unpack_split(plan, group, where, parts, extra):
    rows, wide = plan.rows(group), plan.chunk // 2
    count = len(parts)

    def body(where_ref, *refs):
        part_refs, (own_ref, give_ref) = refs[:count], refs[count : count + 2]
        core = where_ref[3]
        if extra:
            value = sum(p[rows : rows + EXTRA, :].astype(F32) for p in part_refs)
            refs[-2][...] = value[:ROWS, : refs[-2].shape[1]]
            refs[-1][...] = value[ROWS : ROWS + 1, : refs[-1].shape[1]]

        def fill(low_ref, high_ref):
            at = 0
            for w in group:
                high, count = plan.half[w], plan.chunks[w]
                for j in range(count):
                    row = at + j * high
                    value = sum(p[row : row + high, :].astype(F32) for p in part_refs)
                    for b in (2 * j, 2 * j + 1):
                        dst = low_ref if b < count else high_ref
                        to = at + (b % count) * high
                        cut = (b - 2 * j) * wide
                        dst[to : to + high, :] = value[:, cut : cut + wide]
                at += count * high

        @pl.when(core == 0)
        def _():
            fill(own_ref, give_ref)

        @pl.when(core == 1)
        def _():
            fill(give_ref, own_ref)

    shape = jax.ShapeDtypeStruct((rows, wide), F32)
    return pl.pallas_call(
        body,
        out_shape=(shape, shape)
        + (
            jax.ShapeDtypeStruct((ROWS, plan.full[OUT][1] // plan.dp), F32),
            jax.ShapeDtypeStruct((1, plan.full[FIN][1] // plan.dp), F32),
        )
        * extra,
        in_specs=[SMEM_SPEC] + [VMEM_SPEC] * len(parts),
        out_specs=(VMEM_SPEC,) * (2 + 2 * extra),
        compiler_params=PARAMS,
        name="unpack_split",
    )(where, *parts)


def unpack_join(plan, group, where, own, got):
    wide = plan.chunk // 2
    turned = [w == FOUT for w in group]

    def body(where_ref, own_ref, got_ref, *refs):
        core = where_ref[3]
        at = 0
        for n, w in enumerate(group):
            out_ref = refs[-1] if turned[n] else refs[n]
            high, count = plan.half[w], plan.chunks[w]
            own_rows = pl.ds(pl.multiple_of(core * high, 16), high)
            got_rows = pl.ds(pl.multiple_of((1 - core) * high, 16), high)
            for b in range(count):
                row, cut = at + b * high, slice(b * wide, (b + 1) * wide)
                out_ref[own_rows, cut] = own_ref[row : row + high, :]
                out_ref[got_rows, cut] = got_ref[row : row + high, :]
            at += count * high
            if turned[n]:
                refs[n][...] = out_ref[...].T

    shapes = [(2 * plan.half[w], plan.cols[w]) for w in group]
    done = pl.pallas_call(
        body,
        out_shape=tuple(
            jax.ShapeDtypeStruct(shape[::-1] if turn else shape, F32)
            for shape, turn in zip(shapes, turned)
        ),
        in_specs=[SMEM_SPEC, VMEM_SPEC, VMEM_SPEC],
        out_specs=(VMEM_SPEC,) * len(group),
        scratch_shapes=[pltpu.VMEM(shapes[-1], F32)],
        compiler_params=PARAMS,
        name="unpack_join",
    )(where, own, got)
    return [value.T if turn else value for value, turn in zip(done, turned)]


class GatheringSmall:
    def __init__(self, plan, where, vectors, bias):
        self.plan, self.where, self.shape = plan, where, vectors.shape
        flat = jnp.concatenate([vectors.reshape(-1), bias])
        self.size = flat.shape[0]
        self.held, self.bit = [jnp.pad(flat, (0, -self.size % 2048)).reshape(1, -1, 128)], 4

    def advance(self):
        every = jnp.concatenate(self.held)
        self.held = [every, send(every, self.plan.flip(lambda i: self.bit))]
        self.bit *= 2

    def result(self):
        plan, (count, part) = self.plan, self.shape
        while self.bit < plan.devices:
            self.advance()
        every = jnp.concatenate(self.held).reshape(plan.dp, -1)
        slot = jnp.arange(plan.dp, dtype=jnp.int32) ^ (self.where[0] * 2 + self.where[1])
        every = jnp.take(every, slot, axis=0)[:, : self.size].astype(F32)
        rows = every[:, : count * part].reshape(plan.dp, count, part)
        rows = rows.transpose(1, 0, 2).reshape(count, plan.dp * part)
        bias = every[:, count * part :].reshape(1, -1)
        return jnp.pad(rows, ((0, -count % 8), (0, 0))), bias


def fetch_plain(weights, vectors, bias):
    whole = [
        lax.all_gather(lax.all_gather(w, "dp", axis=0, tiled=True), "patch", axis=1, tiled=True)
        for w in weights
    ]
    rows = lax.all_gather(vectors, "dp", axis=1, tiled=True)
    return whole, rows.astype(F32), lax.all_gather(bias, "dp", axis=0, tiled=True).astype(F32)


def reduce_plain(grad):
    part = lax.psum_scatter(grad, "dp", scatter_dimension=0, tiled=True)
    return lax.psum_scatter(part, "patch", scatter_dimension=1, tiled=True).astype(F32)


def reduce_small_plain(rows, bias):
    rows = lax.psum_scatter(rows, "dp", scatter_dimension=1, tiled=True)
    bias = lax.psum_scatter(bias, "dp", scatter_dimension=0, tiled=True)
    return lax.psum(rows, "patch"), lax.psum(bias, "patch")


TAIL = (0.112528827, 0.117839666, 0.0706314405, 0.2046457425, -0.190499398, 0.3478185715, -0.201092832, 0.03812798145)


def dot(a, b):
    return lax.dot_general(a, b, (((1,), (0,)), ((), ())), preferred_element_type=F32)


def dot_t(a, b):
    return lax.dot_general(a, b, (((1,), (1,)), ((), ())), preferred_element_type=F32)


def dot_l(a, b):
    return lax.dot_general(a, b, (((0,), (0,)), ((), ())), preferred_element_type=F32)


def norm_parts(total):
    center = total - jnp.mean(total, -1, keepdims=True)
    spread = lax.rsqrt(jnp.mean(center * center, -1, keepdims=True) + EPS)
    return center * spread, spread


def norm_pull(grad, hat, spread, gain):
    scaled = grad * gain
    return spread * (
        scaled
        - jnp.mean(scaled, -1, keepdims=True)
        - hat * jnp.mean(scaled * hat, -1, keepdims=True)
    )


def gelu_parts(x):
    bell = jnp.exp(-0.5 * (x * x))
    t = 1.0 / (1.0 + (0.4 * 0.5**0.5) * jnp.abs(x))
    tail = jnp.full_like(t, TAIL[-1])
    for c in TAIL[-2::-1]:
        tail = tail * t + c
    tail = tail * (t * bell)
    return jnp.where(x < 0.0, tail, 1.0 - tail), bell


def col_sum(value):
    return jnp.sum(value.astype(F32), 0, keepdims=True)


def soft(scores):
    grown = jnp.exp(scores - jnp.max(scores, 0, keepdims=True))
    return grown * (1.0 / jnp.sum(grown, 0, keepdims=True))


def soft_pull(probs, grad):
    return probs * (grad - jnp.sum(probs * grad, 0, keepdims=True))


def spread_heads(value, low, high):
    return jnp.concatenate([value * low, value * high], 0)


def join_heads(value):
    count = value.shape[1] // 2
    value = jnp.concatenate([value[:HEAD, :count], value[HEAD:, count:]], 0)
    return value.astype(BF16).T


def lane_masks():
    lane = lax.broadcasted_iota(jnp.int32, (1, 2 * HEAD), 1)
    low = (lane < HEAD).astype(F32)
    return low.astype(BF16), (1.0 - low).astype(BF16)


def whole(shape):
    return pl.BlockSpec(
        shape, lambda i: (0,) * len(shape), pipeline_mode=pl.Buffered(1)
    )


def summed(shape):
    return pl.BlockSpec(shape, lambda i: (0,) * len(shape))


def tiled(shape):
    return pl.BlockSpec(shape, lambda i: (i,) + (0,) * (len(shape) - 1))


def spec_of(shape, dtype):
    return jax.ShapeDtypeStruct(shape, dtype)


def call(body, name, steps, ins, outs, flops, scratch=()):
    out_shape = tuple(shape for shape, _ in outs)
    moved = sum(a.size * a.dtype.itemsize for a, _ in ins)
    moved += sum(o.size * jnp.dtype(o.dtype).itemsize for o in out_shape)
    return pl.pallas_call(
        body,
        grid=(steps,),
        out_shape=out_shape,
        in_specs=[spec for _, spec in ins],
        out_specs=tuple(spec for _, spec in outs),
        scratch_shapes=list(scratch),
        compiler_params=PARAMS,
        cost_estimate=pl.CostEstimate(
            flops=int(flops), bytes_accessed=int(moved), transcendentals=0
        ),
        name=name,
    )(*[a for a, _ in ins])


class Source:
    def __init__(self, plan, group, where, given, kept=True):
        self.plan, self.group, self.pieces, self.given = plan, group, plan.fast, given
        self.outs, self.scratch = [], []
        if not self.pieces:
            self.ins = [(w, whole(w.shape)) for w in given]
            return
        self.ins = [(where, SMEM_SPEC)] + [(part, whole(part.shape)) for part in given]
        if kept:
            self.outs = [(spec_of(plan.full[w], BF16), summed(plan.full[w])) for w in group]
        else:
            self.scratch = [pltpu.VMEM(plan.full[w], BF16) for w in group]

    def open(self, in_refs, out_refs):
        if not self.pieces:
            return list(in_refs)
        where_ref, parts = in_refs[0], in_refs[1:]
        full = dict(zip(self.group, out_refs))
        plan = self.plan

        def visit(other, second, first, k, row, w, j, to_row, to_y, high):
            to_col = pl.multiple_of(to_y * (plan.full[w][1] // 2) + j * plan.chunk, 128)
            part = parts[other * 4 + second * 2 + first]
            full[w][pl.ds(to_row, high), pl.ds(to_col, plan.chunk)] = part[k, row : row + high, :]

        @pl.when(pl.program_id(0) == 0)
        def _():
            each_place(plan, self.group, where_ref, visit)

        return list(out_refs)

    def split(self, done):
        if not self.pieces:
            return done, self.given
        return done[: -len(self.group)], done[-len(self.group) :]


def self_forward(dims, source, text, rows, lengths):
    d, items, length, group = dims.d, dims.items, dims.length, dims.group
    pairs, tokens, block = d // (2 * HEAD), items * length, group * length
    scale = HEAD ** (-0.5)

    n_in = len(source.ins)

    def body(len_ref, x_ref, row_ref, *refs):
        qkv_ref, prob_ref, ctx_ref = refs[n_in : n_in + 3]
        (wqkv_ref,) = source.open(refs[:n_in], refs[n_in + 3 :])
        step = pl.program_id(0)
        low, high = lane_masks()
        x = x_ref[...]
        for part, bias in ((0, 0), (1, None), (2, 1)):
            cut = slice(part * d, (part + 1) * d)
            value = dot(x, wqkv_ref[:, cut])
            if bias is not None:
                value = value + row_ref[bias : bias + 1, :]
            qkv_ref[:, cut] = value.astype(BF16)
        place = lax.broadcasted_iota(jnp.int32, (length, 1), 0)
        for i in range(group):
            ok = place < len_ref[step * group + i]
            r = slice(i * length, (i + 1) * length)
            for start in range(0, pairs, TOGETHER):
                many = range(start, min(start + TOGETHER, pairs))
                qs, ks, vs = (
                    [qkv_ref[r, part * d + p * 128 : part * d + (p + 1) * 128] for p in many]
                    for part in range(3)
                )
                probs, contexts = pairs_attend(qs, ks, vs, ok, low, high, scale)
                for n, p in enumerate(many):
                    prob_ref[i, p] = probs[n]
                    ctx_ref[r, p * 128 : (p + 1) * 128] = contexts[n]
    done = call(
        body,
        "self_forward",
        items // group,
        [(lengths, SMEM_SPEC), (text, tiled((block, d))), (rows, whole(rows.shape))] + source.ins,
        [
            (spec_of((tokens, 3 * d), BF16), tiled((block, 3 * d))),
            (spec_of((items, pairs, length, 2 * length), BF16), tiled((group, pairs, length, 2 * length))),
            (spec_of((tokens, d), BF16), tiled((block, d))),
        ]
        + source.outs,
        2 * tokens * d * 5 * d,
    )
    return source.split(done)


def cross_keys(dims, source, grids, cls, rows, count):
    d, items, group = dims.d, dims.items, dims.group
    part, vis, parts = grids[0].shape[0] // items, cls.shape[2], len(grids)
    n_in = len(source.ins)

    def body(*refs):
        grid_refs, cls_ref, row_ref = refs[:parts], refs[parts], refs[parts + 1]
        refs = refs[parts + 2 :]
        kv_ref, patch_ref = refs[n_in : n_in + 2]
        _, _, wckv_ref, _ = source.open(refs[:n_in], refs[n_in + 2 :])
        for i in range(group):
            for k in range(parts):
                patch_ref[i, k * part : (k + 1) * part, :] = grid_refs[k][i * part : (i + 1) * part, :]
            rest = jnp.zeros((count - parts * part - 1, vis), BF16)
            patch_ref[i, parts * part :, :] = jnp.concatenate([cls_ref[i], rest], 0)
        patch = patch_ref[...].reshape(group * count, vis)
        keys = dot(patch, wckv_ref[:, :d]).astype(BF16)
        kv_ref[:, :, :d] = keys.reshape(group, count, d)
        values = (dot(patch, wckv_ref[:, d:]) + row_ref[6:7, :]).astype(BF16)
        kv_ref[:, :, d:] = values.reshape(group, count, d)

    done = call(
        body,
        "cross_keys",
        items // group,
        [(grid, tiled((group * part, vis))) for grid in grids]
        + [(cls, tiled((group, 1, vis))), (rows, whole(rows.shape))]
        + source.ins,
        [
            (spec_of((items, count, 2 * d), BF16), tiled((group, count, 2 * d))),
            (spec_of((items, count, vis), BF16), tiled((group, count, vis))),
        ]
        + source.outs,
        2 * items * count * vis * 2 * d,
    )
    return source.split(done)


def cross_forward(dims, text, self_ctx, kv, mask, w_out, w_cq, w_cout, rows):
    d, items, length, group = dims.d, dims.items, dims.length, dims.group
    pairs, tokens, block = d // (2 * HEAD), items * length, group * length
    count = kv.shape[1]
    scale = HEAD ** (-0.5)

    def body(x_ref, self_ref, kv_ref, mask_ref, wout_ref, wcq_ref, wcout_ref, row_ref,
             one_ref, h_ref, cq_ref, prob_ref, ctx_ref, two_ref):
        low, high = lane_masks()
        total = x_ref[...].astype(F32) + dot(self_ref[...], wout_ref[...]) + row_ref[2:3, :]
        one_ref[...] = total
        hat, _ = norm_parts(total)
        hidden = hat * row_ref[3:4, :] + row_ref[4:5, :]
        h_ref[...] = hidden.astype(BF16)
        cq_ref[...] = (dot(h_ref[...], wcq_ref[...]) + row_ref[5:6, :]).astype(BF16)
        for i in range(group):
            ok = mask_ref[i].astype(F32) > 0.5
            ok = jnp.concatenate([ok, ok], 1)
            r = slice(i * length, (i + 1) * length)
            for start in range(0, pairs, TOGETHER):
                many = range(start, min(start + TOGETHER, pairs))
                cs = [slice(p * 128, (p + 1) * 128) for p in many]
                probs, contexts = pairs_attend(
                    [cq_ref[r, c] for c in cs],
                    [kv_ref[i, :, c] for c in cs],
                    [kv_ref[i, :, d + p * 128 : d + (p + 1) * 128] for p in many],
                    ok,
                    low,
                    high,
                    scale,
                )
                for n, p in enumerate(many):
                    prob_ref[i, p] = probs[n]
                    ctx_ref[r, cs[n]] = contexts[n]
        two_ref[...] = hidden + dot(ctx_ref[...], wcout_ref[...]) + row_ref[7:8, :]

    return call(
        body,
        "cross_forward",
        items // group,
        [
            (text, tiled((block, d))),
            (self_ctx, tiled((block, d))),
            (kv, tiled((group, count, 2 * d))),
            (mask, tiled((group, count, length))),
            (w_out, whole((d, d))),
            (w_cq, whole((d, d))),
            (w_cout, whole((d, d))),
            (rows, whole(rows.shape)),
        ],
        [
            (spec_of((tokens, d), F32), tiled((block, d))),
            (spec_of((tokens, d), BF16), tiled((block, d))),
            (spec_of((tokens, d), BF16), tiled((block, d))),
            (spec_of((items, pairs, count, 2 * length), BF16), tiled((group, pairs, count, 2 * length))),
            (spec_of((tokens, d), BF16), tiled((block, d))),
            (spec_of((tokens, d), F32), tiled((block, d))),
        ],
        2 * tokens * d * 6 * d,
    )


def ffn_both(dims, source, total_two, cotangent, rows, bias):
    d, items, length, group = dims.d, dims.items, dims.length, dims.group
    tokens, block, ff = items * length, group * length, bias.shape[1]
    piece = d
    n_in = len(source.ins)

    def body(tot_ref, cot_ref, row_ref, bias_ref, *refs):
        (out_ref, h_ref, act_ref, glow_ref, pre_ref, two_ref, twolow_ref, sum_ref, bsum_ref) = refs[
            n_in : n_in + 9
        ]
        slope_ref = refs[n_in + 9]
        win_ref, wout_ref = source.open(refs[:n_in], refs[n_in + 10 :])

        @pl.when(pl.program_id(0) == 0)
        def _():
            sum_ref[...] = jnp.zeros_like(sum_ref)
            bsum_ref[...] = jnp.zeros_like(bsum_ref)

        hat_two, spread_two = norm_parts(tot_ref[...])
        hidden = hat_two * row_ref[8:9, :] + row_ref[9:10, :]
        h_ref[...] = hidden.astype(BF16)
        total = hidden + row_ref[10:11, :]
        cuts = [slice(at, at + piece) for at in range(0, ff, piece)]

        def into(cut):
            return dot(h_ref[...], win_ref[:, cut]) + bias_ref[:, cut]

        def middle(pre, cut):
            under, bell = gelu_parts(pre)
            act_ref[:, cut] = (pre * under).astype(BF16)
            slope_ref[:, cut] = under + (pre * 0.3989422804014327) * bell

        for cut in cuts:
            middle(into(cut), cut)
            total = total + dot(act_ref[:, cut], wout_ref[cut, :])
        hat, spread = norm_parts(total)
        gain = row_ref[11:12, :]
        out_ref[...] = hat * gain + row_ref[12:13, :]
        cot = cot_ref[...].astype(F32)
        grad = norm_pull(cot, hat, spread, gain)
        glow_ref[...] = grad.astype(BF16)
        sum_ref[0:1, :] += col_sum(cot * hat)
        sum_ref[1:2, :] += col_sum(cot)
        sum_ref[2:3, :] += col_sum(glow_ref[...])
        for cut in cuts:
            pre = (dot_t(glow_ref[...], wout_ref[cut, :]) * slope_ref[:, cut]).astype(BF16)
            pre_ref[:, cut] = pre
            bsum_ref[0:1, cut] += col_sum(pre)
            grad = grad + dot_t(pre, win_ref[:, cut])
        two = norm_pull(grad, hat_two, spread_two, row_ref[8:9, :])
        two_ref[...] = two
        low = two.astype(BF16)
        twolow_ref[...] = low
        sum_ref[3:4, :] += col_sum(grad * hat_two)
        sum_ref[4:5, :] += col_sum(grad)
        sum_ref[5:6, :] += col_sum(low)

    return call(
        body,
        "ffn_both",
        items // group,
        [
            (total_two, tiled((block, d))),
            (cotangent, tiled((block, d))),
            (rows, whole(rows.shape)),
            (bias, whole(bias.shape)),
        ]
        + source.ins,
        [
            (spec_of((tokens, d), F32), tiled((block, d))),
            (spec_of((tokens, d), BF16), tiled((block, d))),
            (spec_of((tokens, ff), BF16), tiled((block, ff))),
            (spec_of((tokens, d), BF16), tiled((block, d))),
            (spec_of((tokens, ff), BF16), tiled((block, ff))),
            (spec_of((tokens, d), F32), tiled((block, d))),
            (spec_of((tokens, d), BF16), tiled((block, d))),
            (spec_of((8, d), F32), summed((8, d))),
            (spec_of((8, ff), F32), summed((8, ff))),
        ],
        8 * tokens * d * ff,
        [pltpu.VMEM((block, ff), F32)] + source.scratch,
    )


def pairs_pull(qs, ks, vs, outs, probs, low, high, scale):
    outs = [spread_heads(out, low, high) for out in outs]
    grads = [dot_t(v, out) for v, out in zip(vs, outs)]
    scores = [soft_pull(p.astype(F32), grad).astype(BF16) for p, grad in zip(probs, grads)]
    grad_q = [dot(k.T, score) for k, score in zip(ks, scores)]
    grad_k = [dot(score, spread_heads(q, low, high)) for q, score in zip(qs, scores)]
    grad_v = [dot(p, out) for p, out in zip(probs, outs)]
    return (
        [join_heads(value * scale) for value in grad_q],
        [(value * scale).astype(BF16) for value in grad_k],
        [value.astype(BF16) for value in grad_v],
    )


def pairs_attend(qs, ks, vs, ok, low, high, scale):
    scores = [dot_t(k, spread_heads(q, low, high)) for q, k in zip(qs, ks)]
    probs = [soft(jnp.where(ok, score * scale, NEG)).astype(BF16) for score in scores]
    contexts = [dot(v.T, p) for v, p in zip(vs, probs)]
    return probs, [join_heads(context) for context in contexts]


def cross_attend_back(dims, grad_low, query, kv, probs, w_cout):
    d, items, length, group = dims.d, dims.items, dims.length, dims.group
    pairs, tokens, block = d // (2 * HEAD), items * length, group * length
    count = kv.shape[1]
    scale = HEAD ** (-0.5)

    def body(glow_ref, q_ref, kv_ref, prob_ref, wcout_ref, gq_ref, gkv_ref, sum_ref, ctx_ref):
        @pl.when(pl.program_id(0) == 0)
        def _():
            sum_ref[...] = jnp.zeros_like(sum_ref)

        low, high = lane_masks()
        ctx_ref[...] = dot_t(glow_ref[...], wcout_ref[...]).astype(BF16)
        for i in range(group):
            r = slice(i * length, (i + 1) * length)
            for start in range(0, pairs, TOGETHER):
                many = range(start, min(start + TOGETHER, pairs))
                cs = [slice(p * 128, (p + 1) * 128) for p in many]
                cvs = [slice(d + p * 128, d + (p + 1) * 128) for p in many]
                done = pairs_pull(
                    [q_ref[r, c] for c in cs],
                    [kv_ref[i, :, c] for c in cs],
                    [kv_ref[i, :, c] for c in cvs],
                    [ctx_ref[r, c] for c in cs],
                    [prob_ref[i, p] for p in many],
                    low,
                    high,
                    scale,
                )
                for c, cv, grad_q, grad_k, grad_v in zip(cs, cvs, *done):
                    gq_ref[r, c] = grad_q
                    gkv_ref[i, :, c] = grad_k
                    gkv_ref[i, :, cv] = grad_v
        sum_ref[0:1, :] += col_sum(gq_ref[...])
        sum_ref[1:2, :] += col_sum(gkv_ref[:, :, d:].reshape(group * count, d))

    return call(
        body,
        "cross_attend_back",
        items // group,
        [
            (grad_low, tiled((block, d))),
            (query, tiled((block, d))),
            (kv, tiled((group, count, 2 * d))),
            (probs, tiled((group, pairs, count, 2 * length))),
            (w_cout, whole((d, d))),
        ],
        [
            (spec_of((tokens, d), BF16), tiled((block, d))),
            (spec_of((items, count, 2 * d), BF16), tiled((group, count, 2 * d))),
            (spec_of((8, d), F32), summed((8, d))),
        ],
        2 * tokens * d * 4 * d,
        [pltpu.VMEM((block, d), BF16)],
    )


def cross_project_back(dims, grad_two, grad_query, grad_kv, total_one, w_cq, w_ckv, rows, parts, part):
    d, items, length, group = dims.d, dims.items, dims.length, dims.group
    tokens, block = items * length, group * length
    count, vis = grad_kv.shape[1], w_ckv.shape[0]

    def body(g_ref, gq_ref, gkv_ref, tot_ref, wcq_ref, wckv_ref, row_ref, *refs):
        grid_refs, (cls_ref, one_ref, onelow_ref, sum_ref) = refs[:parts], refs[parts:]

        @pl.when(pl.program_id(0) == 0)
        def _():
            sum_ref[...] = jnp.zeros_like(sum_ref)

        for i in range(group):
            value = dot_t(gkv_ref[i], wckv_ref[...])
            for k in range(parts):
                grid_refs[k][i * part : (i + 1) * part, :] = value[k * part : (k + 1) * part, :].astype(BF16)
            cls_ref[i] = value[parts * part : parts * part + 1, :]
        grad = g_ref[...] + dot_t(gq_ref[...], wcq_ref[...])
        hat, spread = norm_parts(tot_ref[...])
        one = norm_pull(grad, hat, spread, row_ref[3:4, :])
        one_ref[...] = one
        one_low = one.astype(BF16)
        onelow_ref[...] = one_low
        sum_ref[0:1, :] += col_sum(grad * hat)
        sum_ref[1:2, :] += col_sum(grad)
        sum_ref[2:3, :] += col_sum(one_low)

    return call(
        body,
        "cross_project_back",
        items // group,
        [
            (grad_two, tiled((block, d))),
            (grad_query, tiled((block, d))),
            (grad_kv, tiled((group, count, 2 * d))),
            (total_one, tiled((block, d))),
            (w_cq, whole((d, d))),
            (w_ckv, whole((vis, 2 * d))),
            (rows, whole(rows.shape)),
        ],
        [(spec_of((items * part, vis), BF16), tiled((group * part, vis)))] * parts
        + [
            (spec_of((items, 1, vis), F32), tiled((group, 1, vis))),
            (spec_of((tokens, d), F32), tiled((block, d))),
            (spec_of((tokens, d), BF16), tiled((block, d))),
            (spec_of((8, d), F32), summed((8, d))),
        ],
        2 * tokens * d * d + 2 * items * count * vis * 2 * d,
    )


def self_attend_back(dims, grad_low, qkv, probs, w_out):
    d, items, length, group = dims.d, dims.items, dims.length, dims.group
    pairs, tokens, block = d // (2 * HEAD), items * length, group * length
    scale = HEAD ** (-0.5)

    def body(glow_ref, qkv_ref, prob_ref, wout_ref, gqkv_ref, sum_ref, ctx_ref):
        @pl.when(pl.program_id(0) == 0)
        def _():
            sum_ref[...] = jnp.zeros_like(sum_ref)

        low, high = lane_masks()
        ctx_ref[...] = dot_t(glow_ref[...], wout_ref[...]).astype(BF16)
        for i in range(group):
            r = slice(i * length, (i + 1) * length)
            for start in range(0, pairs, TOGETHER):
                many = range(start, min(start + TOGETHER, pairs))
                cuts = [
                    [slice(part * d + p * 128, part * d + (p + 1) * 128) for p in many]
                    for part in range(3)
                ]
                done = pairs_pull(
                    *[[qkv_ref[r, c] for c in cuts[part]] for part in range(3)],
                    [ctx_ref[r, c] for c in cuts[0]],
                    [prob_ref[i, p] for p in many],
                    low,
                    high,
                    scale,
                )
                for part in range(3):
                    for c, value in zip(cuts[part], done[part]):
                        gqkv_ref[r, c] = value
        sum_ref[0:1, :] += col_sum(gqkv_ref[:, :d])
        sum_ref[1:2, :] += col_sum(gqkv_ref[:, 2 * d :])

    return call(
        body,
        "self_attend_back",
        items // group,
        [
            (grad_low, tiled((block, d))),
            (qkv, tiled((block, 3 * d))),
            (probs, tiled((group, pairs, length, 2 * length))),
            (w_out, whole((d, d))),
        ],
        [
            (spec_of((tokens, 3 * d), BF16), tiled((block, 3 * d))),
            (spec_of((8, d), F32), summed((8, d))),
        ],
        2 * tokens * d * 4 * d,
        [pltpu.VMEM((block, d), BF16)],
    )


def self_project_back(dims, grad_one, grad_qkv, w_qkv):
    d, items, length, group = dims.d, dims.items, dims.length, dims.group
    tokens, block = items * length, group * length

    def body(g_ref, gqkv_ref, wqkv_ref, text_ref):
        text_ref[...] = g_ref[...] + dot_t(gqkv_ref[...], wqkv_ref[...])

    return call(
        body,
        "self_project_back",
        items // group,
        [
            (grad_one, tiled((block, d))),
            (grad_qkv, tiled((block, 3 * d))),
            (w_qkv, whole((d, 3 * d))),
        ],
        [(spec_of((tokens, d), F32), tiled((block, d)))],
        2 * tokens * d * 3 * d,
    )[0]


def cut_grids(turn, image_grid, parts):
    micro, items, part, vis = image_grid.shape
    each = items // parts

    def body(turn_ref, grid_ref, *out_refs):
        def fill(own):
            value = jnp.swapaxes(grid_ref[0], 0, 1)
            for s in range(parts):
                mine = value[s * each : (s + 1) * each]
                out_refs[s ^ own][...] = mine.reshape(each * part, vis)

        for own in range(parts):
            pl.when(turn_ref[0] == own)(functools.partial(fill, own))

    return call(
        body,
        "cut_grids",
        micro,
        [
            (turn, SMEM_SPEC),
            (image_grid.transpose(0, 2, 1, 3), tiled((1, part, items, vis))),
        ],
        [(spec_of((micro * each * part, vis), BF16), tiled((each * part, vis)))] * parts,
        0,
    )


def place_grids(turn, micro, items, pieces):
    part, vis = pieces[0].shape[0] // items, pieces[0].shape[1]
    each, parts = items // micro, len(pieces)

    def body(turn_ref, *refs):
        def fill(own):
            value = [
                refs[s ^ own][...].astype(F32).reshape(each, part, vis) for s in range(parts)
            ]
            refs[-1][0] = jnp.swapaxes(jnp.concatenate(value, 0), 0, 1)

        for own in range(parts):
            pl.when(turn_ref[0] == own)(functools.partial(fill, own))

    shape = (micro, part, each * parts, vis)
    done = call(
        body,
        "place_grids",
        micro,
        [(turn, SMEM_SPEC)] + [(p, tiled((each * part, vis))) for p in pieces],
        [(spec_of(shape, F32), tiled((1,) + shape[1:]))],
        0,
    )[0]
    return done.transpose(0, 2, 1, 3)


SUMS = ((0, 0, 2), (2, 2, 1), (2, 0, 2), (1, 0, 2), (3, 5, 1), (3, 3, 2), (3, 2, 1), (3, 0, 2))


def rows_of(sums):
    return jnp.concatenate([sums[n][row : row + count] for n, row, count in SUMS])


def weight_grads(plan, group, where, factors, extra=()):
    high_rows = max(plan.full[w][0] for w in group)
    wide = max(plan.full[w][1] for w in group)
    flat = [a for pair in factors for a in pair]
    count, base = len(flat), plan.rows(group)

    def body(where_ref, *refs):
        far, (own_ref, other_ref) = refs[:count], refs[count + len(extra) : count + len(extra) + 2]
        stack_refs = (own_ref, other_ref)
        scratch = refs[count + len(extra) + 2 :]
        near, made, sems = scratch[:count], scratch[count], scratch[count + 1]
        copies = [pltpu.make_async_copy(far[n], near[n], sems.at[n]) for n in range(count)]
        for copy in copies:
            copy.start()
        if extra:
            add_extra(where_ref, refs[count : count + len(extra)], stack_refs, *scratch[count + 2 :])
        for n, w in enumerate(group):
            left, right = near[2 * n], near[2 * n + 1]
            rows, cols = plan.full[w]
            copies[2 * n].wait()
            copies[2 * n + 1].wait()
            for at in range(0, rows, 256):
                value = dot_l(left[:, at : at + 256], right[...])
                made[at : at + 256, :cols] = value.astype(BF16)

            def visit(other, second, first, k, row, w_at, j, to_row, to_y, high):
                if w_at == w:
                    col = pl.multiple_of(to_y * (cols // 2) + j * plan.chunk, 128)
                    stack_refs[other][second * 2 + first, k, row : row + high, :] = made[
                        pl.ds(to_row, high), pl.ds(col, plan.chunk)
                    ]

            each_place(plan, group, where_ref, visit)

    def add_extra(where_ref, sum_refs, stack_refs, table, lines):
        width = lines.shape[1] // plan.dp
        step = plan.full[FIN][1] // plan.dp
        at = 0
        for n, row, many in SUMS:
            lines[at : at + many, :] = sum_refs[n][row : row + many, :]
            at += many
        table[...] = jnp.zeros_like(table)
        for n in range(plan.dp):
            table[n, :ROWS, :width] = lines[:ROWS, n * width : (n + 1) * width]
            table[n, ROWS : ROWS + 1, :step] = sum_refs[-1][0:1, n * step : (n + 1) * step]
        z, x, _, core = (where_ref[i] for i in range(4))
        for other in range(2):
            for second in range(2):
                for first in range(2):
                    x_at = x ^ jnp.where((core ^ other) == 0, first, second)
                    for k in range(plan.zs):
                        value = table[(z ^ k) * 2 + x_at].astype(BF16)
                        stack_refs[other][second * 2 + first, k, base : base + EXTRA, :] = value

    high = base + (EXTRA if extra else 0)
    shape = jax.ShapeDtypeStruct((4, plan.zs, high, plan.chunk), BF16)
    flops = sum(2 * a.shape[0] * a.shape[1] * b.shape[1] for a, b in factors)
    moved = sum(a.size * 2 for a in flat) + 2 * shape.size * 2
    table = []
    if extra:
        table.append(pltpu.VMEM((plan.dp, EXTRA, plan.chunk), F32))
        table.append(pltpu.VMEM((EXTRA, plan.full[OUT][1]), F32))
    return pl.pallas_call(
        body,
        out_shape=(shape,) * 2,
        in_specs=[SMEM_SPEC]
        + [pl.BlockSpec(memory_space=pl.ANY)] * count
        + [VMEM_SPEC] * len(extra),
        out_specs=(VMEM_SPEC,) * 2,
        scratch_shapes=[pltpu.VMEM(a.shape, BF16) for a in flat]
        + [pltpu.VMEM((high_rows, wide), BF16), pltpu.SemaphoreType.DMA((count,))]
        + table,
        compiler_params=PARAMS,
        cost_estimate=pl.CostEstimate(flops=flops, bytes_accessed=moved, transcendentals=0),
        name="weight_grads",
    )(where, *flat, *extra)


class Dims:
    def __init__(self, d, items, length):
        self.d, self.items, self.length = d, items, length
        self.group = 2 if items % 2 == 0 else 1


def cross_mask(lengths, counts, boxes, length, count):
    place = jnp.arange(length, dtype=jnp.int32)[None, :]
    boxed = (counts[:, None] > 0) & (place < lengths[:, None])
    phrase = jnp.where(boxed, place * counts[:, None] // lengths[:, None], 0)
    chosen = phrase[:, None, :] == jnp.arange(boxes.shape[1], dtype=jnp.int32)[None, :, None]
    inside = jnp.einsum(
        "ijp,ijt->ipt",
        (boxes > 0).astype(BF16),
        chosen.astype(BF16),
        preferred_element_type=F32,
    )
    grid_ok = jnp.where(boxed[:, None, :], inside, 1.0).astype(BF16)
    items, real = grid_ok.shape[:2]
    own = jnp.ones((items, 1, length), BF16)
    return jnp.concatenate([grid_ok, own, jnp.zeros((items, count - real - 1, length), BF16)], 1)


def trade(pieces):
    parts = lax.axis_size("patch")
    return [pieces[0]] + [
        lax.ppermute(pieces[k], "patch", [(i, i ^ k) for i in range(parts)])
        for k in range(1, len(pieces))
    ]


class Work:
    def __init__(self, args, parts):
        (self.text_in, self.image_grid, self.image_cls, lengths, counts, boxes, cot) = args
        self.parts = parts
        self.micro, d = self.text_in.shape[0], self.text_in.shape[2]
        self.items = lengths.size
        self.text, self.cot = self.text_in.reshape(-1, d), cot.reshape(-1, d)
        self.lengths, self.counts = lengths.reshape(-1), counts.reshape(-1)
        self.boxes = boxes.reshape((self.items,) + boxes.shape[2:])
        self.dims = Dims(d, self.items, self.text.shape[0] // self.items)
        self.turn = lax.axis_index("patch").astype(jnp.int32).reshape(1)
        self.part, self.vis = self.image_grid.shape[2:]
        self.each = self.items // self.micro
        self.count = -(-(parts * self.part + 1) // 16) * 16
        self.cls = self.image_cls.reshape(self.items, 1, self.vis)

    def mask(self):
        boxes = self.boxes.reshape(self.items, -1, self.parts, self.part)
        order = jnp.arange(self.parts, dtype=jnp.int32) ^ self.turn[0]
        boxes = jnp.take(boxes, order, axis=2).reshape(self.boxes.shape)
        return cross_mask(self.lengths, self.counts, boxes, self.dims.length, self.count)

    def finish(self, layer_out, text_grad, grid_grad, cls, grads, rows_grad, bias_grad):
        return (
            layer_out.reshape(self.text_in.shape),
            text_grad.reshape(self.text_in.shape),
            grid_grad,
            cls.reshape(self.image_cls.shape),
            *grads,
            rows_grad,
            bias_grad,
        )


def on_device(plan, *args):
    work, shards, vectors, ffn_bias = Work(args[:7], plan.patch), args[7:14], args[14], args[15]
    dims, where, parts = work.dims, coords(), plan.patch

    own, give = pack_split(plan, where, shards)
    units = pack_join(plan, where, own, send(give, plan.core()))
    grids = list(cut_grids(work.turn, work.image_grid, parts))
    vectors, bias, grids, units = lax.optimization_barrier((vectors, ffn_bias, grids, units))
    one, two, three = (Gathering(plan, unit) for unit in units)
    small = GatheringSmall(plan, where, vectors, bias)

    def source(g, gather, kept=True):
        return Source(plan, GATHER[g], where, gather.held, kept)

    one.along_z(*range(1, plan.zs))
    grids[2] = trade(grids[:3])[2]
    small.advance()
    grids = fence([one, two, small], grids)
    one.first()
    two.along_z(*range(1, plan.zs // 2 + 1))
    grids[3] = trade(grids)[3]
    small.advance()
    grids = fence([one, two, three, small], grids)
    one.second()
    two.along_z(*range(plan.zs // 2 + 1, plan.zs))
    rows, bias = small.result()
    rows, bias, grids = fence([one, two, three], [rows, bias, grids])
    one.core()
    two.first()
    three.along_z(*range(1, plan.zs // 2 + 1))
    (qkv, probs, ctx), (w_qkv,) = self_forward(dims, source(0, one), work.text, rows, work.lengths)
    (ctx,) = fence([two, three], [ctx])
    two.second()
    three.along_z(*range(plan.zs // 2 + 1, plan.zs))
    grids[1] = trade(grids[:2])[1]
    mask = work.mask()
    ctx, grids, mask = fence([two, three], [ctx, grids, mask])
    two.core()
    three.first()
    (kv, patches), (w_out, w_cq, w_ckv, w_cout) = cross_keys(
        dims, source(1, two), grids, work.cls, rows, work.count
    )
    kv, ctx = fence([three], [kv, ctx])
    three.second()
    total_one, hidden_one, query, cross_probs, cross_ctx, total_two = cross_forward(
        dims, work.text, ctx, kv, mask, w_out, w_cq, w_cout, rows
    )
    total_two = fence([three], total_two)
    three.core()
    layer_out, hidden_two, act, low_three, grad_pre, grad_two, low_two, sum_ffn, sum_pre = ffn_both(
        dims, source(2, three, kept=False), total_two, work.cot, rows, bias
    )

    reduces = {}

    def reduce(g, factors, twice=False, extra=()):
        stacks = weight_grads(plan, REDUCE[g], where, factors, extra)
        reduces[g] = Reducing(plan, REDUCE[g], where, stacks, twice, 1 if extra else 0)

    def hold(*values, on=None):
        chains = [reduces[g] for g in (reduces if on is None else on)]
        return fence(chains, list(values))

    def go(*groups):
        for g in groups:
            reduces[g].advance()

    reduce(2, [(hidden_two, grad_pre), (act, low_three)], twice=True)
    (low_two,) = hold(low_two)
    go(2)
    grad_query, grad_kv, sum_attend = cross_attend_back(dims, low_two, query, kv, cross_probs, w_cout)
    grad_query, grad_kv = hold(grad_query, grad_kv)
    go(2)
    reduces[2].held[0], grad_query, grad_kv = lax.optimization_barrier(
        (reduces[2].held[0], grad_query, grad_kv)
    )
    reduce(
        1,
        [
            (hidden_one, grad_query),
            (patches.reshape(-1, work.vis), grad_kv.reshape(-1, grad_kv.shape[2])),
            (cross_ctx, low_two),
        ],
    )
    grad_query, grad_kv = hold(grad_query, grad_kv)
    go(2, 1)
    *grids, cls, grad_one, low_one, sum_one = cross_project_back(
        dims, grad_two, grad_query, grad_kv, total_one, w_cq, w_ckv, rows, parts, work.part
    )
    low_one, *grids = hold(low_one, *grids)
    go(2)
    grids[1] = trade(grids[:2])[1]
    grad_qkv, sum_self = self_attend_back(dims, low_one, qkv, probs, w_out)
    grad_qkv, *grids = hold(grad_qkv, *grids)
    go(1, 2)
    sums = (sum_self, sum_attend, sum_one, sum_ffn, sum_pre)
    reduce(0, [(work.text, grad_qkv), (ctx, low_one)], extra=sums)
    (grad_qkv,) = hold(grad_qkv)
    go(0, 1, 2)
    grids[2] = trade(grids[:3])[2]
    text_grad = self_project_back(dims, grad_one, grad_qkv, w_qkv)
    text_grad, *grids = hold(text_grad, *grids)
    go(0, 1, 1)
    hold()
    go(0, 2)
    grids = hold(*grids)
    go(0, 0, 1, 2)
    grids[3] = trade(grids)[3]
    go(1)
    grids = hold(*grids)
    go(0)
    grid_grad = place_grids(work.turn, work.micro, work.items, grids)
    go(0)
    *done, rows_grad, bias_grad = reduces[0].held
    grads = [None] * 7
    for g, group in enumerate(REDUCE):
        for w, value in zip(group, done if g == 0 else reduces[g].held):
            grads[w] = value
    return work.finish(
        layer_out, text_grad, grid_grad, cls, grads, rows_grad, bias_grad.reshape(-1)
    )


def on_device_plain(plan, *args):
    work, parts = Work(args[:7], plan.patch), plan.patch
    dims = work.dims
    weights, rows, bias = fetch_plain(args[7:14], args[14], args[15])
    rows = jnp.pad(rows, ((0, -rows.shape[0] % 8), (0, 0)))
    grids = trade(cut_grids(work.turn, work.image_grid, parts))

    def source(g):
        return Source(plan, GATHER[g], None, [weights[w] for w in GATHER[g]])

    (qkv, probs, ctx), _ = self_forward(dims, source(0), work.text, rows, work.lengths)
    (kv, patches), _ = cross_keys(dims, source(1), grids, work.cls, rows, work.count)
    total_one, hidden_one, query, cross_probs, cross_ctx, total_two = cross_forward(
        dims, work.text, ctx, kv, work.mask(), weights[OUT], weights[CQ], weights[COUT], rows
    )
    layer_out, hidden_two, act, low_three, grad_pre, grad_two, low_two, sum_ffn, sum_pre = ffn_both(
        dims, source(2), total_two, work.cot, rows, bias[None]
    )
    grad_query, grad_kv, sum_attend = cross_attend_back(
        dims, low_two, query, kv, cross_probs, weights[COUT]
    )
    *grids, cls, grad_one, low_one, sum_one = cross_project_back(
        dims, grad_two, grad_query, grad_kv, total_one, weights[CQ], weights[CKV], rows, parts, work.part
    )
    grad_qkv, sum_self = self_attend_back(dims, low_one, qkv, probs, weights[OUT])
    text_grad = self_project_back(dims, grad_one, grad_qkv, weights[QKV])
    flat_kv = grad_kv.reshape(-1, grad_kv.shape[2])
    factors = [
        (work.text, grad_qkv),
        (ctx, low_one),
        (hidden_one, grad_query),
        (patches.reshape(-1, work.vis), flat_kv),
        (cross_ctx, low_two),
        (hidden_two, grad_pre),
        (act, low_three),
    ]
    grads = [reduce_plain(dot_l(a, b).astype(BF16)) for a, b in factors]
    sums = rows_of([sum_self, sum_attend, sum_one, sum_ffn])
    small = reduce_small_plain(sums, sum_pre[0])
    grid_grad = place_grids(work.turn, work.micro, work.items, trade(grids))
    return work.finish(layer_out, text_grad, grid_grad, cls, grads, *small)


def solution(mesh):
    dp, patch = mesh.shape["dp"], mesh.shape["patch"]
    both = P(None, ("dp", "patch"), None)
    weight = P("dp", "patch")

    def run(*args):
        shards = [(w.shape[0] // dp, w.shape[1] // patch) for w in args[7:14]]
        plan = Plan(dp, patch, shards)
        return jax.shard_map(
            functools.partial(on_device if plan.fast else on_device_plain, plan),
            mesh=mesh,
            in_specs=(
                both,
                P(None, "dp", "patch", None),
                both,
                P(None, ("dp", "patch")),
                P(None, ("dp", "patch")),
                P(None, ("dp", "patch"), None, None),
                both,
            )
            + (weight,) * 7
            + (P(None, "dp"), P("dp")),
            out_specs=(both, both, P(None, "dp", "patch", None), both)
            + (weight,) * 7
            + (P(None, "dp"), P("dp")),
            check_vma=False,
        )(*args)

    return run
```

```python
import functools

import jax
import jax.numpy as jnp
from jax import lax
from jax.experimental import pallas as pl
from jax.experimental.pallas import tpu as pltpu
from jax.sharding import PartitionSpec as P

HEAD = 64
EPS = 1e-06
NEG = -1e30
BF16 = jnp.bfloat16
F32 = jnp.float32
AXES = ("dp", "patch")
VMEM_SPEC = pl.BlockSpec(memory_space=pltpu.VMEM)
SMEM_SPEC = pl.BlockSpec(memory_space=pltpu.SMEM)
PARAMS = pltpu.CompilerParams(vmem_limit_bytes=62 * 2**20)

QKV, OUT, CQ, CKV, COUT, FIN, FOUT = range(7)
ROWS = 13
EXTRA = 16
TOGETHER = 6
PART = 768
GATHER = ((QKV,), (OUT, CQ, CKV, COUT), (FIN, FOUT))
REDUCE = ((QKV, OUT), (CQ, CKV, COUT), (FIN, FOUT))


class Plan:
    def __init__(self, dp, patch, shards):
        self.dp, self.patch = dp, patch
        self.zs = dp // 2
        self.devices = dp * patch
        self.chunk = shards[OUT][1] * 2
        self.half = [s[0] // 2 for s in shards]
        self.cols = [s[1] for s in shards]
        self.chunks = [s[1] * 2 // self.chunk for s in shards]
        self.full = [(s[0] * dp, s[1] * patch) for s in shards]
        self.fast = (
            dp % 2 == 0
            and self.zs & (self.zs - 1) == 0
            and patch == 4
            and all(h % 16 == 0 for h in self.half)
            and all(s[1] * 2 % self.chunk == 0 for s in shards)
            and self.chunk % 128 == 0
            and shards[FIN][1] * patch // dp <= self.chunk
        )

    def rows(self, group):
        return sum(self.half[w] * self.chunks[w] for w in group)

    def flip(self, pick):
        return [(i, i ^ pick(i)) for i in range(self.devices)]

    def core(self):
        return self.flip(lambda i: 1)

    def first(self):
        return self.flip(lambda i: 4 if i % 2 == 0 else 2)

    def second(self):
        return self.flip(lambda i: 2 if i % 2 == 0 else 4)

    def along_z(self, k):
        return self.flip(lambda i: 8 * k)


def send(value, perm):
    return lax.ppermute(value, AXES, perm)


def coords():
    dp, patch = lax.axis_index("dp"), lax.axis_index("patch")
    return jnp.stack([dp // 2, dp % 2, patch // 2, patch % 2]).astype(jnp.int32)


def piece_rows(group, plan):
    at, found = 0, []
    for w in group:
        for j in range(plan.chunks[w]):
            found.append((w, j, at))
            at += plan.half[w]
    return found


def group_starts(plan):
    starts, at = [], 0
    for group in GATHER:
        starts.append(at)
        at += plan.rows(group)
    return starts, at


def pack_split(plan, where, shards):
    _, total = group_starts(plan)
    wide = plan.chunk // 2

    def body(where_ref, *refs):
        shard_refs, (own_ref, send_ref, turned) = list(refs[:7]), refs[7:]
        core = where_ref[3]
        turned[...] = shard_refs[FOUT][...].T
        shard_refs[FOUT] = turned
        at = 0
        for group in GATHER:
            for w in group:
                high = plan.half[w]
                for b in range(plan.chunks[w]):
                    cut = slice(b * wide, (b + 1) * wide)
                    own_ref[at : at + high, :] = shard_refs[w][pl.ds(core * high, high), cut]
                    send_ref[at : at + high, :] = shard_refs[w][
                        pl.ds((1 - core) * high, high), cut
                    ]
                    at += high

    shape = jax.ShapeDtypeStruct((total, wide), BF16)
    return pl.pallas_call(
        body,
        out_shape=(shape, shape),
        in_specs=[SMEM_SPEC] + [VMEM_SPEC] * 7,
        out_specs=(VMEM_SPEC, VMEM_SPEC),
        scratch_shapes=[pltpu.VMEM(shards[FOUT].shape, BF16)],
        compiler_params=PARAMS,
        name="pack_split",
    )(where, *shards[:FOUT], shards[FOUT].T)


def pack_join(plan, where, own, got):
    starts, total = group_starts(plan)
    wide = plan.chunk // 2

    def body(where_ref, own_ref, got_ref, *unit_refs):
        core = where_ref[3]

        def fill(low_ref, high_ref):
            for g, group in enumerate(GATHER):
                at = starts[g]
                for w in group:
                    high, count = plan.half[w], plan.chunks[w]
                    for j in range(count):
                        pair = []
                        for b in (2 * j, 2 * j + 1):
                            src = low_ref if b < count else high_ref
                            row = at + (b % count) * high
                            pair.append(src[row : row + high, :])
                        to = at - starts[g] + j * high
                        unit_refs[g][to : to + high, :] = jnp.concatenate(pair, axis=1)
                    at += count * high

        @pl.when(core == 0)
        def _():
            fill(own_ref, got_ref)

        @pl.when(core == 1)
        def _():
            fill(got_ref, own_ref)

    return pl.pallas_call(
        body,
        out_shape=tuple(jax.ShapeDtypeStruct((plan.rows(g), plan.chunk), BF16) for g in GATHER),
        in_specs=[SMEM_SPEC, VMEM_SPEC, VMEM_SPEC],
        out_specs=(VMEM_SPEC,) * len(GATHER),
        compiler_params=PARAMS,
        name="pack_join",
    )(where, own, got)


class Gathering:
    def __init__(self, plan, unit):
        self.plan, self.held = plan, [unit]

    def along_z(self, *steps):
        self.held += [send(self.held[0], self.plan.along_z(k)) for k in steps]

    def first(self):
        stack = jnp.stack(self.held)
        self.held = [stack, send(stack, self.plan.first())]

    def second(self):
        side = [send(part, self.plan.second()) for part in self.held]
        self.held += side + [send(part, self.plan.core()) for part in self.held]

    def core(self):
        self.held += [send(part, self.plan.core()) for part in self.held[2:4]]


def each_place(plan, group, where_ref, visit):
    z, x, y, core = (where_ref[i] for i in range(4))
    for other in range(2):
        half = core ^ other
        for second in range(2):
            for first in range(2):
                x_at = x ^ jnp.where(half == 0, first, second)
                y_at = y ^ jnp.where(half == 0, second, first)
                for k in range(plan.zs):
                    place = ((z ^ k) * 2 + x_at) * 2 + half
                    for w, j, row in piece_rows(group, plan):
                        high = plan.half[w]
                        to_row = pl.multiple_of(place * high, 16)
                        visit(other, second, first, k, row, w, j, to_row, y_at, high)


def add_low(one, two):
    return (one.astype(F32) + two.astype(F32)).astype(BF16)


class Reducing:
    def __init__(self, plan, group, where, stacks, twice=False, extra=0):
        self.plan, self.group, self.where = plan, group, where
        self.twice, self.extra = twice, extra
        self.held = list(stacks)
        self.steps = [self.core, self.second] + [self.again] * twice
        self.steps += [self.first, self.near_z, self.far_z, self.split, self.join]

    def advance(self):
        self.held = list(self.steps.pop(0)(*self.held))

    def core(self, keep, give):
        return keep, send(give, self.plan.core())

    def second(self, keep, got):
        ends = (2, 3, 4) if self.twice else (2, 4)
        gives = [add_low(keep[a:b], got[a:b]) for a, b in zip(ends, ends[1:])]
        gives[0] = send(gives[0], self.plan.second())
        return add_low(keep[:2], got[:2]), *gives

    def again(self, keep, got, give):
        return keep, got, send(give, self.plan.second())

    def first(self, keep, *got):
        near, far = (got[0], got[1][0]) if self.twice else (got[0][:1], got[0][1])
        give = add_low(keep[1], far)
        return add_low(keep[0], near[0]), send(give, self.plan.first())

    def near_z(self, keep, got):
        plan, slots = self.plan, [add_low(keep[k], got[k]) for k in range(self.plan.zs)]
        for k in range(1, plan.zs // 2 + 1):
            slots[k] = send(slots[k], plan.along_z(k))
        return slots

    def far_z(self, *slots):
        plan, slots = self.plan, list(slots)
        for k in range(plan.zs // 2 + 1, plan.zs):
            slots[k] = send(slots[k], plan.along_z(k))
        return slots

    def split(self, *parts):
        own, give, *rest = unpack_split(self.plan, self.group, self.where, parts, self.extra)
        return own, send(give, self.plan.core()), *rest

    def join(self, own, got, *rest):
        return *unpack_join(self.plan, self.group, self.where, own, got), *rest


def fence(chains, values):
    flat, tree = jax.tree.flatten([values, [chain.held for chain in chains]])
    values, held = jax.tree.unflatten(tree, lax.optimization_barrier(flat))
    for chain, arrays in zip(chains, held):
        chain.held = arrays
    return values


def unpack_split(plan, group, where, parts, extra):
    rows, wide = plan.rows(group), plan.chunk // 2
    count = len(parts)

    def body(where_ref, *refs):
        part_refs, (own_ref, give_ref) = refs[:count], refs[count : count + 2]
        core = where_ref[3]
        if extra:
            value = sum(p[rows : rows + EXTRA, :].astype(F32) for p in part_refs)
            refs[-2][...] = value[:ROWS, : refs[-2].shape[1]]
            refs[-1][...] = value[ROWS, : refs[-1].shape[0]]

        def fill(low_ref, high_ref):
            at = 0
            for w in group:
                high, count = plan.half[w], plan.chunks[w]
                for j in range(count):
                    row = at + j * high
                    value = sum(p[row : row + high, :].astype(F32) for p in part_refs)
                    for b in (2 * j, 2 * j + 1):
                        dst = low_ref if b < count else high_ref
                        to = at + (b % count) * high
                        cut = (b - 2 * j) * wide
                        dst[to : to + high, :] = value[:, cut : cut + wide]
                at += count * high

        @pl.when(core == 0)
        def _():
            fill(own_ref, give_ref)

        @pl.when(core == 1)
        def _():
            fill(give_ref, own_ref)

    shape = jax.ShapeDtypeStruct((rows, wide), F32)
    return pl.pallas_call(
        body,
        out_shape=(shape, shape)
        + (
            jax.ShapeDtypeStruct((ROWS, plan.full[OUT][1] // plan.dp), F32),
            jax.ShapeDtypeStruct((plan.full[FIN][1] // plan.dp,), F32),
        )
        * extra,
        in_specs=[SMEM_SPEC] + [VMEM_SPEC] * len(parts),
        out_specs=(VMEM_SPEC,) * (2 + 2 * extra),
        compiler_params=PARAMS,
        name="unpack_split",
    )(where, *parts)


def unpack_join(plan, group, where, own, got):
    wide = plan.chunk // 2
    turned = [w == FOUT for w in group]

    def body(where_ref, own_ref, got_ref, *refs):
        core = where_ref[3]
        at = 0
        for n, w in enumerate(group):
            out_ref = refs[-1] if turned[n] else refs[n]
            high, count = plan.half[w], plan.chunks[w]
            own_rows = pl.ds(pl.multiple_of(core * high, 16), high)
            got_rows = pl.ds(pl.multiple_of((1 - core) * high, 16), high)
            for b in range(count):
                row, cut = at + b * high, slice(b * wide, (b + 1) * wide)
                out_ref[own_rows, cut] = own_ref[row : row + high, :]
                out_ref[got_rows, cut] = got_ref[row : row + high, :]
            at += count * high
            if turned[n]:
                refs[n][...] = out_ref[...].T

    shapes = [(2 * plan.half[w], plan.cols[w]) for w in group]
    done = pl.pallas_call(
        body,
        out_shape=tuple(
            jax.ShapeDtypeStruct(shape[::-1] if turn else shape, F32)
            for shape, turn in zip(shapes, turned)
        ),
        in_specs=[SMEM_SPEC, VMEM_SPEC, VMEM_SPEC],
        out_specs=(VMEM_SPEC,) * len(group),
        scratch_shapes=[pltpu.VMEM(shapes[-1], F32)],
        compiler_params=PARAMS,
        name="unpack_join",
    )(where, own, got)
    return [value.T if turn else value for value, turn in zip(done, turned)]


class GatheringSmall:
    def __init__(self, plan, where, vectors, bias):
        self.plan, self.where, self.shape = plan, where, vectors.shape
        flat = jnp.concatenate([vectors.reshape(-1), bias])
        self.size = flat.shape[0]
        self.held, self.bit = [jnp.pad(flat, (0, -self.size % 2048)).reshape(1, -1, 128)], 4

    def advance(self):
        every = jnp.concatenate(self.held)
        self.held = [every, send(every, self.plan.flip(lambda i: self.bit))]
        self.bit *= 2

    def result(self):
        plan, (count, part) = self.plan, self.shape
        while self.bit < plan.devices:
            self.advance()
        every = jnp.concatenate(self.held).reshape(plan.dp, -1)
        slot = jnp.arange(plan.dp, dtype=jnp.int32) ^ (self.where[0] * 2 + self.where[1])
        every = jnp.take(every, slot, axis=0)[:, : self.size].astype(F32)
        rows = every[:, : count * part].reshape(plan.dp, count, part)
        rows = rows.transpose(1, 0, 2).reshape(count, plan.dp * part)
        bias = every[:, count * part :].reshape(1, -1)
        return jnp.pad(rows, ((0, -count % 8), (0, 0))), bias


def fetch_plain(weights, vectors, bias):
    whole = [
        lax.all_gather(lax.all_gather(w, "dp", axis=0, tiled=True), "patch", axis=1, tiled=True)
        for w in weights
    ]
    rows = lax.all_gather(vectors, "dp", axis=1, tiled=True)
    return whole, rows.astype(F32), lax.all_gather(bias, "dp", axis=0, tiled=True).astype(F32)


def reduce_plain(grad):
    part = lax.psum_scatter(grad, "dp", scatter_dimension=0, tiled=True)
    return lax.psum_scatter(part, "patch", scatter_dimension=1, tiled=True).astype(F32)


def reduce_small_plain(rows, bias):
    rows = lax.psum_scatter(rows, "dp", scatter_dimension=1, tiled=True)
    bias = lax.psum_scatter(bias, "dp", scatter_dimension=0, tiled=True)
    return lax.psum(rows, "patch"), lax.psum(bias, "patch")


TAIL = (0.112528827, 0.117839666, 0.0706314405, 0.2046457425, -0.190499398, 0.3478185715, -0.201092832, 0.03812798145)


def dot(a, b):
    return lax.dot_general(a, b, (((1,), (0,)), ((), ())), preferred_element_type=F32)


def dot_t(a, b):
    return lax.dot_general(a, b, (((1,), (1,)), ((), ())), preferred_element_type=F32)


def dot_l(a, b):
    return lax.dot_general(a, b, (((0,), (0,)), ((), ())), preferred_element_type=F32)


def norm_parts(total):
    center = total - jnp.mean(total, -1, keepdims=True)
    spread = lax.rsqrt(jnp.mean(center * center, -1, keepdims=True) + EPS)
    return center * spread, spread


def norm_pull(grad, hat, spread, gain):
    scaled = grad * gain
    return spread * (
        scaled
        - jnp.mean(scaled, -1, keepdims=True)
        - hat * jnp.mean(scaled * hat, -1, keepdims=True)
    )


def gelu_parts(x):
    bell = jnp.exp(-0.5 * (x * x))
    t = 1.0 / (1.0 + (0.4 * 0.5**0.5) * jnp.abs(x))
    tail = jnp.full_like(t, TAIL[-1])
    for c in TAIL[-2::-1]:
        tail = tail * t + c
    tail = tail * (t * bell)
    return jnp.where(x < 0.0, tail, 1.0 - tail), bell


def col_sum(value):
    return jnp.sum(value.astype(F32), 0, keepdims=True)


def soft(scores):
    grown = jnp.exp(scores - jnp.max(scores, 0, keepdims=True))
    return grown * (1.0 / jnp.sum(grown, 0, keepdims=True))


def soft_pull(probs, grad):
    return probs * (grad - jnp.sum(probs * grad, 0, keepdims=True))


def spread_heads(value, low, high):
    return jnp.concatenate([value * low, value * high], 0)


def join_heads(value):
    count = value.shape[1] // 2
    value = jnp.concatenate([value[:HEAD, :count], value[HEAD:, count:]], 0)
    return value.astype(BF16).T


def lane_masks():
    lane = lax.broadcasted_iota(jnp.int32, (1, 2 * HEAD), 1)
    low = (lane < HEAD).astype(F32)
    return low.astype(BF16), (1.0 - low).astype(BF16)


def whole(shape):
    return pl.BlockSpec(
        shape, lambda i: (0,) * len(shape), pipeline_mode=pl.Buffered(1)
    )


def summed(shape):
    return pl.BlockSpec(shape, lambda i: (0,) * len(shape))


def tiled(shape):
    return pl.BlockSpec(shape, lambda i: (i,) + (0,) * (len(shape) - 1))


def spec_of(shape, dtype):
    return jax.ShapeDtypeStruct(shape, dtype)


def call(body, name, steps, ins, outs, flops, scratch=()):
    out_shape = tuple(shape for shape, _ in outs)
    moved = sum(a.size * a.dtype.itemsize for a, _ in ins)
    moved += sum(o.size * jnp.dtype(o.dtype).itemsize for o in out_shape)
    return pl.pallas_call(
        body,
        grid=(steps,),
        out_shape=out_shape,
        in_specs=[spec for _, spec in ins],
        out_specs=tuple(spec for _, spec in outs),
        scratch_shapes=list(scratch),
        compiler_params=PARAMS,
        cost_estimate=pl.CostEstimate(
            flops=int(flops), bytes_accessed=int(moved), transcendentals=0
        ),
        name=name,
    )(*[a for a, _ in ins])


class Source:
    def __init__(self, plan, group, where, given, kept=True):
        self.plan, self.group, self.pieces, self.given = plan, group, plan.fast, given
        self.outs, self.scratch = [], []
        if not self.pieces:
            self.ins = [(w, whole(w.shape)) for w in given]
            return
        self.ins = [(where, SMEM_SPEC)] + [(part, whole(part.shape)) for part in given]
        if kept:
            self.outs = [(spec_of(plan.full[w], BF16), summed(plan.full[w])) for w in group]
        else:
            self.scratch = [pltpu.VMEM(plan.full[w], BF16) for w in group]

    def open(self, in_refs, out_refs):
        if not self.pieces:
            return list(in_refs)
        where_ref, parts = in_refs[0], in_refs[1:]
        full = dict(zip(self.group, out_refs))
        plan = self.plan

        def visit(other, second, first, k, row, w, j, to_row, to_y, high):
            to_col = pl.multiple_of(to_y * (plan.full[w][1] // 2) + j * plan.chunk, 128)
            part = parts[other * 4 + second * 2 + first]
            full[w][pl.ds(to_row, high), pl.ds(to_col, plan.chunk)] = part[k, row : row + high, :]

        @pl.when(pl.program_id(0) == 0)
        def _():
            each_place(plan, self.group, where_ref, visit)

        return list(out_refs)

    def split(self, done):
        if not self.pieces:
            return done, self.given
        return done[: -len(self.group)], done[-len(self.group) :]


def self_forward(dims, source, text, rows, lengths):
    d, items, length, group = dims.d, dims.items, dims.length, dims.group
    pairs, tokens, block = d // (2 * HEAD), items * length, group * length
    scale = HEAD ** (-0.5)

    n_in = len(source.ins)

    def body(len_ref, x_ref, row_ref, *refs):
        qkv_ref, prob_ref, ctx_ref = refs[n_in : n_in + 3]
        (wqkv_ref,) = source.open(refs[:n_in], refs[n_in + 3 :])
        step = pl.program_id(0)
        low, high = lane_masks()
        x = x_ref[...]
        for part, bias in ((0, 0), (1, None), (2, 1)):
            cut = slice(part * d, (part + 1) * d)
            value = dot(x, wqkv_ref[:, cut])
            if bias is not None:
                value = value + row_ref[bias : bias + 1, :]
            qkv_ref[:, cut] = value.astype(BF16)
        place = lax.broadcasted_iota(jnp.int32, (length, 1), 0)
        for i in range(group):
            ok = place < len_ref[step * group + i]
            r = slice(i * length, (i + 1) * length)
            for start in range(0, pairs, TOGETHER):
                many = range(start, min(start + TOGETHER, pairs))
                qs, ks, vs = (
                    [qkv_ref[r, part * d + p * 128 : part * d + (p + 1) * 128] for p in many]
                    for part in range(3)
                )
                probs, contexts = pairs_attend(qs, ks, vs, ok, low, high, scale)
                for n, p in enumerate(many):
                    prob_ref[i, p] = probs[n]
                    ctx_ref[r, p * 128 : (p + 1) * 128] = contexts[n]
    done = call(
        body,
        "self_forward",
        items // group,
        [(lengths, SMEM_SPEC), (text, tiled((block, d))), (rows, whole(rows.shape))] + source.ins,
        [
            (spec_of((tokens, 3 * d), BF16), tiled((block, 3 * d))),
            (spec_of((items, pairs, length, 2 * length), BF16), tiled((group, pairs, length, 2 * length))),
            (spec_of((tokens, d), BF16), tiled((block, d))),
        ]
        + source.outs,
        2 * tokens * d * 5 * d,
    )
    return source.split(done)


def cross_keys(dims, source, grids, cls, rows, count):
    d, items, group = dims.d, dims.items, dims.group
    part, vis, parts = grids[0].shape[0] // items, cls.shape[2], len(grids)
    n_in = len(source.ins)

    def body(*refs):
        grid_refs, cls_ref, row_ref = refs[:parts], refs[parts], refs[parts + 1]
        refs = refs[parts + 2 :]
        kv_ref, patch_ref = refs[n_in : n_in + 2]
        _, _, wckv_ref, _ = source.open(refs[:n_in], refs[n_in + 2 :])
        for i in range(group):
            for k in range(parts):
                patch_ref[i, k * part : (k + 1) * part, :] = grid_refs[k][i * part : (i + 1) * part, :]
            rest = jnp.zeros((count - parts * part - 1, vis), BF16)
            patch_ref[i, parts * part :, :] = jnp.concatenate([cls_ref[i], rest], 0)
        patch = patch_ref[...].reshape(group * count, vis)
        keys = dot(patch, wckv_ref[:, :d]).astype(BF16)
        kv_ref[:, :, :d] = keys.reshape(group, count, d)
        values = (dot(patch, wckv_ref[:, d:]) + row_ref[6:7, :]).astype(BF16)
        kv_ref[:, :, d:] = values.reshape(group, count, d)

    done = call(
        body,
        "cross_keys",
        items // group,
        [(grid, tiled((group * part, vis))) for grid in grids]
        + [(cls, tiled((group, 1, vis))), (rows, whole(rows.shape))]
        + source.ins,
        [
            (spec_of((items, count, 2 * d), BF16), tiled((group, count, 2 * d))),
            (spec_of((items, count, vis), BF16), tiled((group, count, vis))),
        ]
        + source.outs,
        2 * items * count * vis * 2 * d,
    )
    return source.split(done)


def cross_forward(dims, text, self_ctx, kv, mask, w_out, w_cq, w_cout, rows):
    d, items, length, group = dims.d, dims.items, dims.length, dims.group
    pairs, tokens, block = d // (2 * HEAD), items * length, group * length
    count = kv.shape[1]
    scale = HEAD ** (-0.5)

    def body(x_ref, self_ref, kv_ref, mask_ref, wout_ref, wcq_ref, wcout_ref, row_ref,
             one_ref, h_ref, cq_ref, prob_ref, ctx_ref, two_ref):
        low, high = lane_masks()
        total = x_ref[...].astype(F32) + dot(self_ref[...], wout_ref[...]) + row_ref[2:3, :]
        one_ref[...] = total
        hat, _ = norm_parts(total)
        hidden = hat * row_ref[3:4, :] + row_ref[4:5, :]
        h_ref[...] = hidden.astype(BF16)
        cq_ref[...] = (dot(h_ref[...], wcq_ref[...]) + row_ref[5:6, :]).astype(BF16)
        for i in range(group):
            ok = mask_ref[i].astype(F32) > 0.5
            ok = jnp.concatenate([ok, ok], 1)
            r = slice(i * length, (i + 1) * length)
            for start in range(0, pairs, TOGETHER):
                many = range(start, min(start + TOGETHER, pairs))
                cs = [slice(p * 128, (p + 1) * 128) for p in many]
                probs, contexts = pairs_attend(
                    [cq_ref[r, c] for c in cs],
                    [kv_ref[i, :, c] for c in cs],
                    [kv_ref[i, :, d + p * 128 : d + (p + 1) * 128] for p in many],
                    ok,
                    low,
                    high,
                    scale,
                )
                for n, p in enumerate(many):
                    prob_ref[i, p] = probs[n]
                    ctx_ref[r, cs[n]] = contexts[n]
        two_ref[...] = hidden + dot(ctx_ref[...], wcout_ref[...]) + row_ref[7:8, :]

    return call(
        body,
        "cross_forward",
        items // group,
        [
            (text, tiled((block, d))),
            (self_ctx, tiled((block, d))),
            (kv, tiled((group, count, 2 * d))),
            (mask, tiled((group, count, length))),
            (w_out, whole((d, d))),
            (w_cq, whole((d, d))),
            (w_cout, whole((d, d))),
            (rows, whole(rows.shape)),
        ],
        [
            (spec_of((tokens, d), F32), tiled((block, d))),
            (spec_of((tokens, d), BF16), tiled((block, d))),
            (spec_of((tokens, d), BF16), tiled((block, d))),
            (spec_of((items, pairs, count, 2 * length), BF16), tiled((group, pairs, count, 2 * length))),
            (spec_of((tokens, d), BF16), tiled((block, d))),
            (spec_of((tokens, d), F32), tiled((block, d))),
        ],
        2 * tokens * d * 6 * d,
    )


def ffn_both(dims, source, total_two, cotangent, rows, bias):
    d, items, length, group = dims.d, dims.items, dims.length, dims.group
    tokens, block, ff = items * length, group * length, bias.shape[1]
    piece = d
    n_in = len(source.ins)

    def body(tot_ref, cot_ref, row_ref, bias_ref, *refs):
        (out_ref, h_ref, act_ref, glow_ref, pre_ref, two_ref, twolow_ref, sum_ref, bsum_ref) = refs[
            n_in : n_in + 9
        ]
        slope_ref = refs[n_in + 9]
        win_ref, wout_ref = source.open(refs[:n_in], refs[n_in + 10 :])

        @pl.when(pl.program_id(0) == 0)
        def _():
            sum_ref[...] = jnp.zeros_like(sum_ref)
            bsum_ref[...] = jnp.zeros_like(bsum_ref)

        hat_two, spread_two = norm_parts(tot_ref[...])
        hidden = hat_two * row_ref[8:9, :] + row_ref[9:10, :]
        h_ref[...] = hidden.astype(BF16)
        total = hidden + row_ref[10:11, :]
        cuts = [slice(at, at + piece) for at in range(0, ff, piece)]

        def into(cut):
            return dot(h_ref[...], win_ref[:, cut]) + bias_ref[:, cut]

        def middle(pre, cut):
            under, bell = gelu_parts(pre)
            act_ref[:, cut] = (pre * under).astype(BF16)
            slope_ref[:, cut] = under + (pre * 0.3989422804014327) * bell

        for cut in cuts:
            middle(into(cut), cut)
            total = total + dot(act_ref[:, cut], wout_ref[cut, :])
        hat, spread = norm_parts(total)
        gain = row_ref[11:12, :]
        out_ref[...] = hat * gain + row_ref[12:13, :]
        cot = cot_ref[...].astype(F32)
        grad = norm_pull(cot, hat, spread, gain)
        glow_ref[...] = grad.astype(BF16)
        sum_ref[0:1, :] += col_sum(cot * hat)
        sum_ref[1:2, :] += col_sum(cot)
        sum_ref[2:3, :] += col_sum(glow_ref[...])
        for cut in cuts:
            pre = (dot_t(glow_ref[...], wout_ref[cut, :]) * slope_ref[:, cut]).astype(BF16)
            pre_ref[:, cut] = pre
            bsum_ref[0:1, cut] += col_sum(pre)
            grad = grad + dot_t(pre, win_ref[:, cut])
        two = norm_pull(grad, hat_two, spread_two, row_ref[8:9, :])
        two_ref[...] = two
        low = two.astype(BF16)
        twolow_ref[...] = low
        sum_ref[3:4, :] += col_sum(grad * hat_two)
        sum_ref[4:5, :] += col_sum(grad)
        sum_ref[5:6, :] += col_sum(low)

    return call(
        body,
        "ffn_both",
        items // group,
        [
            (total_two, tiled((block, d))),
            (cotangent, tiled((block, d))),
            (rows, whole(rows.shape)),
            (bias, whole(bias.shape)),
        ]
        + source.ins,
        [
            (spec_of((tokens, d), F32), tiled((block, d))),
            (spec_of((tokens, d), BF16), tiled((block, d))),
            (spec_of((tokens, ff), BF16), tiled((block, ff))),
            (spec_of((tokens, d), BF16), tiled((block, d))),
            (spec_of((tokens, ff), BF16), tiled((block, ff))),
            (spec_of((tokens, d), F32), tiled((block, d))),
            (spec_of((tokens, d), BF16), tiled((block, d))),
            (spec_of((8, d), F32), summed((8, d))),
            (spec_of((8, ff), F32), summed((8, ff))),
        ],
        8 * tokens * d * ff,
        [pltpu.VMEM((block, ff), F32)] + source.scratch,
    )


def pairs_pull(qs, ks, vs, outs, probs, low, high, scale):
    outs = [spread_heads(out, low, high) for out in outs]
    grads = [dot_t(v, out) for v, out in zip(vs, outs)]
    scores = [soft_pull(p.astype(F32), grad).astype(BF16) for p, grad in zip(probs, grads)]
    grad_q = [dot(k.T, score) for k, score in zip(ks, scores)]
    grad_k = [dot(score, spread_heads(q, low, high)) for q, score in zip(qs, scores)]
    grad_v = [dot(p, out) for p, out in zip(probs, outs)]
    return (
        [join_heads(value * scale) for value in grad_q],
        [(value * scale).astype(BF16) for value in grad_k],
        [value.astype(BF16) for value in grad_v],
    )


def pairs_attend(qs, ks, vs, ok, low, high, scale):
    scores = [dot_t(k, spread_heads(q, low, high)) for q, k in zip(qs, ks)]
    probs = [soft(jnp.where(ok, score * scale, NEG)).astype(BF16) for score in scores]
    contexts = [dot(v.T, p) for v, p in zip(vs, probs)]
    return probs, [join_heads(context) for context in contexts]


def cross_attend_back(dims, grad_low, query, kv, probs, w_cout):
    d, items, length, group = dims.d, dims.items, dims.length, dims.group
    pairs, tokens, block = d // (2 * HEAD), items * length, group * length
    count = kv.shape[1]
    scale = HEAD ** (-0.5)

    def body(glow_ref, q_ref, kv_ref, prob_ref, wcout_ref, gq_ref, gkv_ref, sum_ref, ctx_ref):
        @pl.when(pl.program_id(0) == 0)
        def _():
            sum_ref[...] = jnp.zeros_like(sum_ref)

        low, high = lane_masks()
        ctx_ref[...] = dot_t(glow_ref[...], wcout_ref[...]).astype(BF16)
        for i in range(group):
            r = slice(i * length, (i + 1) * length)
            for start in range(0, pairs, TOGETHER):
                many = range(start, min(start + TOGETHER, pairs))
                cs = [slice(p * 128, (p + 1) * 128) for p in many]
                cvs = [slice(d + p * 128, d + (p + 1) * 128) for p in many]
                done = pairs_pull(
                    [q_ref[r, c] for c in cs],
                    [kv_ref[i, :, c] for c in cs],
                    [kv_ref[i, :, c] for c in cvs],
                    [ctx_ref[r, c] for c in cs],
                    [prob_ref[i, p] for p in many],
                    low,
                    high,
                    scale,
                )
                for c, cv, grad_q, grad_k, grad_v in zip(cs, cvs, *done):
                    gq_ref[r, c] = grad_q
                    gkv_ref[i, :, c] = grad_k
                    gkv_ref[i, :, cv] = grad_v
        sum_ref[0:1, :] += col_sum(gq_ref[...])
        sum_ref[1:2, :] += col_sum(gkv_ref[:, :, d:].reshape(group * count, d))

    return call(
        body,
        "cross_attend_back",
        items // group,
        [
            (grad_low, tiled((block, d))),
            (query, tiled((block, d))),
            (kv, tiled((group, count, 2 * d))),
            (probs, tiled((group, pairs, count, 2 * length))),
            (w_cout, whole((d, d))),
        ],
        [
            (spec_of((tokens, d), BF16), tiled((block, d))),
            (spec_of((items, count, 2 * d), BF16), tiled((group, count, 2 * d))),
            (spec_of((8, d), F32), summed((8, d))),
        ],
        2 * tokens * d * 4 * d,
        [pltpu.VMEM((block, d), BF16)],
    )


def cross_project_back(dims, grad_two, grad_query, grad_kv, total_one, w_cq, w_ckv, rows, parts, part):
    d, items, length, group = dims.d, dims.items, dims.length, dims.group
    tokens, block = items * length, group * length
    count, vis = grad_kv.shape[1], w_ckv.shape[0]

    def body(g_ref, gq_ref, gkv_ref, tot_ref, wcq_ref, wckv_ref, row_ref, *refs):
        grid_refs, (cls_ref, one_ref, onelow_ref, sum_ref) = refs[:parts], refs[parts:]

        @pl.when(pl.program_id(0) == 0)
        def _():
            sum_ref[...] = jnp.zeros_like(sum_ref)

        for i in range(group):
            value = dot_t(gkv_ref[i], wckv_ref[...])
            for k in range(parts):
                grid_refs[k][i * part : (i + 1) * part, :] = value[k * part : (k + 1) * part, :].astype(BF16)
            cls_ref[i] = value[parts * part : parts * part + 1, :]
        grad = g_ref[...] + dot_t(gq_ref[...], wcq_ref[...])
        hat, spread = norm_parts(tot_ref[...])
        one = norm_pull(grad, hat, spread, row_ref[3:4, :])
        one_ref[...] = one
        one_low = one.astype(BF16)
        onelow_ref[...] = one_low
        sum_ref[0:1, :] += col_sum(grad * hat)
        sum_ref[1:2, :] += col_sum(grad)
        sum_ref[2:3, :] += col_sum(one_low)

    return call(
        body,
        "cross_project_back",
        items // group,
        [
            (grad_two, tiled((block, d))),
            (grad_query, tiled((block, d))),
            (grad_kv, tiled((group, count, 2 * d))),
            (total_one, tiled((block, d))),
            (w_cq, whole((d, d))),
            (w_ckv, whole((vis, 2 * d))),
            (rows, whole(rows.shape)),
        ],
        [(spec_of((items * part, vis), BF16), tiled((group * part, vis)))] * parts
        + [
            (spec_of((items, 1, vis), F32), tiled((group, 1, vis))),
            (spec_of((tokens, d), F32), tiled((block, d))),
            (spec_of((tokens, d), BF16), tiled((block, d))),
            (spec_of((8, d), F32), summed((8, d))),
        ],
        2 * tokens * d * d + 2 * items * count * vis * 2 * d,
    )


def self_attend_back(dims, grad_low, qkv, probs, w_out):
    d, items, length, group = dims.d, dims.items, dims.length, dims.group
    pairs, tokens, block = d // (2 * HEAD), items * length, group * length
    scale = HEAD ** (-0.5)

    def body(glow_ref, qkv_ref, prob_ref, wout_ref, gqkv_ref, sum_ref, ctx_ref):
        @pl.when(pl.program_id(0) == 0)
        def _():
            sum_ref[...] = jnp.zeros_like(sum_ref)

        low, high = lane_masks()
        ctx_ref[...] = dot_t(glow_ref[...], wout_ref[...]).astype(BF16)
        for i in range(group):
            r = slice(i * length, (i + 1) * length)
            for start in range(0, pairs, TOGETHER):
                many = range(start, min(start + TOGETHER, pairs))
                cuts = [
                    [slice(part * d + p * 128, part * d + (p + 1) * 128) for p in many]
                    for part in range(3)
                ]
                done = pairs_pull(
                    *[[qkv_ref[r, c] for c in cuts[part]] for part in range(3)],
                    [ctx_ref[r, c] for c in cuts[0]],
                    [prob_ref[i, p] for p in many],
                    low,
                    high,
                    scale,
                )
                for part in range(3):
                    for c, value in zip(cuts[part], done[part]):
                        gqkv_ref[r, c] = value
        sum_ref[0:1, :] += col_sum(gqkv_ref[:, :d])
        sum_ref[1:2, :] += col_sum(gqkv_ref[:, 2 * d :])

    return call(
        body,
        "self_attend_back",
        items // group,
        [
            (grad_low, tiled((block, d))),
            (qkv, tiled((block, 3 * d))),
            (probs, tiled((group, pairs, length, 2 * length))),
            (w_out, whole((d, d))),
        ],
        [
            (spec_of((tokens, 3 * d), BF16), tiled((block, 3 * d))),
            (spec_of((8, d), F32), summed((8, d))),
        ],
        2 * tokens * d * 4 * d,
        [pltpu.VMEM((block, d), BF16)],
    )


def self_project_back(dims, grad_one, grad_qkv, w_qkv):
    d, items, length, group = dims.d, dims.items, dims.length, dims.group
    tokens, block = items * length, group * length

    def body(g_ref, gqkv_ref, wqkv_ref, text_ref):
        text_ref[...] = g_ref[...] + dot_t(gqkv_ref[...], wqkv_ref[...])

    return call(
        body,
        "self_project_back",
        items // group,
        [
            (grad_one, tiled((block, d))),
            (grad_qkv, tiled((block, 3 * d))),
            (w_qkv, whole((d, 3 * d))),
        ],
        [(spec_of((tokens, d), F32), tiled((block, d)))],
        2 * tokens * d * 3 * d,
    )[0]


def cut_grids(turn, image_grid, parts):
    micro, items, part, vis = image_grid.shape
    each = items // parts

    def body(turn_ref, grid_ref, *out_refs):
        def fill(own):
            value = jnp.swapaxes(grid_ref[0], 0, 1)
            for s in range(parts):
                mine = value[s * each : (s + 1) * each]
                out_refs[s ^ own][...] = mine.reshape(each * part, vis)

        for own in range(parts):
            pl.when(turn_ref[0] == own)(functools.partial(fill, own))

    return call(
        body,
        "cut_grids",
        micro,
        [
            (turn, SMEM_SPEC),
            (image_grid.transpose(0, 2, 1, 3), tiled((1, part, items, vis))),
        ],
        [(spec_of((micro * each * part, vis), BF16), tiled((each * part, vis)))] * parts,
        0,
    )


def place_grids(turn, micro, items, pieces):
    part, vis = pieces[0].shape[0] // items, pieces[0].shape[1]
    each, parts = items // micro, len(pieces)

    def body(turn_ref, *refs):
        def fill(own):
            value = [
                refs[s ^ own][...].astype(F32).reshape(each, part, vis) for s in range(parts)
            ]
            refs[-1][0] = jnp.swapaxes(jnp.concatenate(value, 0), 0, 1)

        for own in range(parts):
            pl.when(turn_ref[0] == own)(functools.partial(fill, own))

    shape = (micro, part, each * parts, vis)
    done = call(
        body,
        "place_grids",
        micro,
        [(turn, SMEM_SPEC)] + [(p, tiled((each * part, vis))) for p in pieces],
        [(spec_of(shape, F32), tiled((1,) + shape[1:]))],
        0,
    )[0]
    return done.transpose(0, 2, 1, 3)


SUMS = ((0, 0, 2), (2, 2, 1), (2, 0, 2), (1, 0, 2), (3, 5, 1), (3, 3, 2), (3, 2, 1), (3, 0, 2))


def rows_of(sums):
    return jnp.concatenate([sums[n][row : row + count] for n, row, count in SUMS])


def weight_grads(plan, group, where, factors, extra=()):
    high_rows = max(plan.full[w][0] for w in group)
    wide = max(plan.full[w][1] for w in group)
    flat = [a for pair in factors for a in pair]
    count, base = len(flat), plan.rows(group)

    def first_bytes(n):
        left, right = factors[n]
        return left.shape[0] * min(left.shape[1], PART) + right.size

    order = sorted(range(len(group)), key=first_bytes)
    begins = {w: row for w, j, row in reversed(piece_rows(group, plan))}
    parts = [
        [slice(at, at + PART) for at in range(0, left.shape[1], PART)]
        if left.shape[1] > 2 * PART and left.shape[1] % PART == 0
        else [slice(0, left.shape[1])]
        for left, _ in factors
    ]

    def body(where_ref, *refs):
        far, outs = refs[:count], refs[count + len(extra) : count + len(extra) + 2]
        scratch = refs[count + len(extra) + 2 :]
        near, stack_refs = scratch[:count], scratch[count : count + 2]
        made, in_sems, out_sems = scratch[count + 2 : count + 5]
        lefts, rights, used = {}, {}, 0
        for n in order:
            rights[n] = pltpu.make_async_copy(far[2 * n + 1], near[2 * n + 1], in_sems.at[used])
            used += 1
            for m, cut in enumerate(parts[n]):
                lefts[n, m] = pltpu.make_async_copy(
                    far[2 * n].at[:, cut], near[2 * n].at[:, cut], in_sems.at[used]
                )
                used += 1
            rights[n].start()
            for m in range(len(parts[n])):
                lefts[n, m].start()
        flushes = []

        def flush(low, high):
            for stack_ref, out in zip(stack_refs, outs):
                copy = pltpu.make_async_copy(
                    stack_ref.at[:, :, low:high, :],
                    out.at[:, :, low:high, :],
                    out_sems.at[len(flushes)],
                )
                copy.start()
                flushes.append(copy)

        if extra:
            add_extra(
                where_ref, refs[count : count + len(extra)], stack_refs, *scratch[count + 5 :]
            )
            flush(base, base + EXTRA)
        for n in order:
            w, (left, right) = group[n], near[2 * n : 2 * n + 2]
            cols = plan.full[w][1]
            rights[n].wait()
            for m, cut in enumerate(parts[n]):
                lefts[n, m].wait()
                for at in range(cut.start, cut.stop, 256):
                    value = dot_l(left[:, at : at + 256], right[...])
                    made[at : at + 256, :cols] = value.astype(BF16)

            def visit(other, second, first, k, row, w_at, j, to_row, to_y, high):
                if w_at == w:
                    col = pl.multiple_of(to_y * (cols // 2) + j * plan.chunk, 128)
                    stack_refs[other][second * 2 + first, k, row : row + high, :] = made[
                        pl.ds(to_row, high), pl.ds(col, plan.chunk)
                    ]

            each_place(plan, group, where_ref, visit)
            flush(begins[w], begins[w] + plan.half[w] * plan.chunks[w])
        for copy in flushes:
            copy.wait()

    def add_extra(where_ref, sum_refs, stack_refs, table, lines):
        width = lines.shape[1] // plan.dp
        step = plan.full[FIN][1] // plan.dp
        at = 0
        for n, row, many in SUMS:
            lines[at : at + many, :] = sum_refs[n][row : row + many, :]
            at += many
        table[...] = jnp.zeros_like(table)
        for n in range(plan.dp):
            table[n, :ROWS, :width] = lines[:ROWS, n * width : (n + 1) * width]
            table[n, ROWS : ROWS + 1, :step] = sum_refs[-1][0:1, n * step : (n + 1) * step]
        z, x, _, core = (where_ref[i] for i in range(4))
        for other in range(2):
            for second in range(2):
                for first in range(2):
                    x_at = x ^ jnp.where((core ^ other) == 0, first, second)
                    for k in range(plan.zs):
                        value = table[(z ^ k) * 2 + x_at].astype(BF16)
                        stack_refs[other][second * 2 + first, k, base : base + EXTRA, :] = value

    high = base + (EXTRA if extra else 0)
    shape = jax.ShapeDtypeStruct((4, plan.zs, high, plan.chunk), BF16)
    flops = sum(2 * a.shape[0] * a.shape[1] * b.shape[1] for a, b in factors)
    moved = sum(a.size * 2 for a in flat) + 2 * shape.size * 2
    table = []
    if extra:
        table.append(pltpu.VMEM((plan.dp, EXTRA, plan.chunk), F32))
        table.append(pltpu.VMEM((EXTRA, plan.full[OUT][1]), F32))
    return pl.pallas_call(
        body,
        out_shape=(shape,) * 2,
        in_specs=[SMEM_SPEC]
        + [pl.BlockSpec(memory_space=pl.ANY)] * count
        + [VMEM_SPEC] * len(extra),
        out_specs=(pl.BlockSpec(memory_space=pl.ANY),) * 2,
        scratch_shapes=[pltpu.VMEM(a.shape, BF16) for a in flat]
        + [pltpu.VMEM(shape.shape, BF16)] * 2
        + [
            pltpu.VMEM((high_rows, wide), BF16),
            pltpu.SemaphoreType.DMA((len(group) + sum(len(cuts) for cuts in parts),)),
            pltpu.SemaphoreType.DMA((2 * len(group) + 2,)),
        ]
        + table,
        compiler_params=PARAMS,
        cost_estimate=pl.CostEstimate(flops=flops, bytes_accessed=moved, transcendentals=0),
        name="weight_grads",
    )(where, *flat, *extra)


class Dims:
    def __init__(self, d, items, length):
        self.d, self.items, self.length = d, items, length
        self.group = 2 if items % 2 == 0 else 1


def cross_mask(lengths, counts, boxes, length, count):
    place = jnp.arange(length, dtype=jnp.int32)[None, :]
    boxed = (counts[:, None] > 0) & (place < lengths[:, None])
    phrase = jnp.where(boxed, place * counts[:, None] // lengths[:, None], 0)
    chosen = phrase[:, None, :] == jnp.arange(boxes.shape[1], dtype=jnp.int32)[None, :, None]
    inside = jnp.einsum(
        "ijp,ijt->ipt",
        (boxes > 0).astype(BF16),
        chosen.astype(BF16),
        preferred_element_type=F32,
    )
    grid_ok = jnp.where(boxed[:, None, :], inside, 1.0).astype(BF16)
    items, real = grid_ok.shape[:2]
    own = jnp.ones((items, 1, length), BF16)
    return jnp.concatenate([grid_ok, own, jnp.zeros((items, count - real - 1, length), BF16)], 1)


def trade(pieces):
    parts = lax.axis_size("patch")
    return [pieces[0]] + [
        lax.ppermute(pieces[k], "patch", [(i, i ^ k) for i in range(parts)])
        for k in range(1, len(pieces))
    ]


class Work:
    def __init__(self, args, parts):
        (self.text_in, self.image_grid, self.image_cls, lengths, counts, boxes, cot) = args
        self.parts = parts
        self.micro, d = self.text_in.shape[0], self.text_in.shape[2]
        self.items = lengths.size
        self.text, self.cot = self.text_in.reshape(-1, d), cot.reshape(-1, d)
        self.lengths, self.counts = lengths.reshape(-1), counts.reshape(-1)
        self.boxes = boxes.reshape((self.items,) + boxes.shape[2:])
        self.dims = Dims(d, self.items, self.text.shape[0] // self.items)
        self.turn = lax.axis_index("patch").astype(jnp.int32).reshape(1)
        self.part, self.vis = self.image_grid.shape[2:]
        self.each = self.items // self.micro
        self.count = -(-(parts * self.part + 1) // 16) * 16
        self.cls = self.image_cls.reshape(self.items, 1, self.vis)

    def mask(self):
        boxes = self.boxes.reshape(self.items, -1, self.parts, self.part)
        order = jnp.arange(self.parts, dtype=jnp.int32) ^ self.turn[0]
        boxes = jnp.take(boxes, order, axis=2).reshape(self.boxes.shape)
        return cross_mask(self.lengths, self.counts, boxes, self.dims.length, self.count)

    def finish(self, layer_out, text_grad, grid_grad, cls, grads, rows_grad, bias_grad):
        return (
            layer_out.reshape(self.text_in.shape),
            text_grad.reshape(self.text_in.shape),
            grid_grad,
            cls.reshape(self.image_cls.shape),
            *grads,
            rows_grad,
            bias_grad,
        )


def on_device(plan, *args):
    work, shards, vectors, ffn_bias = Work(args[:7], plan.patch), args[7:14], args[14], args[15]
    dims, where, parts = work.dims, coords(), plan.patch

    own, give = pack_split(plan, where, shards)
    units = pack_join(plan, where, own, send(give, plan.core()))
    grids = list(cut_grids(work.turn, work.image_grid, parts))
    vectors, bias, grids, units = lax.optimization_barrier((vectors, ffn_bias, grids, units))
    one, two, three = (Gathering(plan, unit) for unit in units)
    small = GatheringSmall(plan, where, vectors, bias)

    def source(g, gather, kept=True):
        return Source(plan, GATHER[g], where, gather.held, kept)

    one.along_z(*range(1, plan.zs))
    grids[2] = trade(grids[:3])[2]
    small.advance()
    grids = fence([one, two, small], grids)
    one.first()
    two.along_z(*range(1, plan.zs // 2 + 1))
    grids[3] = trade(grids)[3]
    small.advance()
    grids = fence([one, two, three, small], grids)
    one.second()
    two.along_z(*range(plan.zs // 2 + 1, plan.zs))
    rows, bias = small.result()
    rows, bias, grids = fence([one, two, three], [rows, bias, grids])
    one.core()
    two.first()
    three.along_z(*range(1, plan.zs // 2 + 1))
    (qkv, probs, ctx), (w_qkv,) = self_forward(dims, source(0, one), work.text, rows, work.lengths)
    (ctx,) = fence([two, three], [ctx])
    two.second()
    three.along_z(*range(plan.zs // 2 + 1, plan.zs))
    grids[1] = trade(grids[:2])[1]
    mask = work.mask()
    ctx, grids, mask = fence([two, three], [ctx, grids, mask])
    two.core()
    three.first()
    (kv, patches), (w_out, w_cq, w_ckv, w_cout) = cross_keys(
        dims, source(1, two), grids, work.cls, rows, work.count
    )
    kv, ctx = fence([three], [kv, ctx])
    three.second()
    total_one, hidden_one, query, cross_probs, cross_ctx, total_two = cross_forward(
        dims, work.text, ctx, kv, mask, w_out, w_cq, w_cout, rows
    )
    total_two = fence([three], total_two)
    three.core()
    layer_out, hidden_two, act, low_three, grad_pre, grad_two, low_two, sum_ffn, sum_pre = ffn_both(
        dims, source(2, three, kept=False), total_two, work.cot, rows, bias
    )

    reduces = {}

    def reduce(g, factors, twice=False, extra=()):
        stacks = weight_grads(plan, REDUCE[g], where, factors, extra)
        reduces[g] = Reducing(plan, REDUCE[g], where, stacks, twice, 1 if extra else 0)

    def hold(*values, on=None):
        chains = [reduces[g] for g in (reduces if on is None else on)]
        return fence(chains, list(values))

    def go(*groups):
        for g in groups:
            reduces[g].advance()

    reduce(2, [(hidden_two, grad_pre), (act, low_three)], twice=True)
    (low_two,) = hold(low_two)
    go(2)
    grad_query, grad_kv, sum_attend = cross_attend_back(dims, low_two, query, kv, cross_probs, w_cout)
    grad_query, grad_kv = hold(grad_query, grad_kv)
    go(2)
    reduces[2].held[0], grad_query, grad_kv = lax.optimization_barrier(
        (reduces[2].held[0], grad_query, grad_kv)
    )
    reduce(
        1,
        [
            (hidden_one, grad_query),
            (patches.reshape(-1, work.vis), grad_kv.reshape(-1, grad_kv.shape[2])),
            (cross_ctx, low_two),
        ],
    )
    grad_query, grad_kv = hold(grad_query, grad_kv)
    go(2, 1)
    *grids, cls, grad_one, low_one, sum_one = cross_project_back(
        dims, grad_two, grad_query, grad_kv, total_one, w_cq, w_ckv, rows, parts, work.part
    )
    low_one, *grids = hold(low_one, *grids)
    go(2)
    grids[1] = trade(grids[:2])[1]
    grad_qkv, sum_self = self_attend_back(dims, low_one, qkv, probs, w_out)
    grad_qkv, *grids = hold(grad_qkv, *grids)
    go(1, 2)
    sums = (sum_self, sum_attend, sum_one, sum_ffn, sum_pre)
    reduce(0, [(work.text, grad_qkv), (ctx, low_one)], extra=sums)
    (grad_qkv,) = hold(grad_qkv)
    go(0, 1, 2)
    grids[2] = trade(grids[:3])[2]
    text_grad = self_project_back(dims, grad_one, grad_qkv, w_qkv)
    cls = cls.reshape(work.image_cls.shape)
    text_grad, cls, *grids = hold(text_grad, cls, *grids)
    go(0, 1, 1)
    hold()
    go(0, 2)
    grids = hold(*grids)
    go(0, 0, 1, 2)
    grids[3] = trade(grids)[3]
    go(1)
    grids = hold(*grids)
    go(0)
    grid_grad = place_grids(work.turn, work.micro, work.items, grids)
    go(0)
    *done, rows_grad, bias_grad = reduces[0].held
    grads = [None] * 7
    for g, group in enumerate(REDUCE):
        for w, value in zip(group, done if g == 0 else reduces[g].held):
            grads[w] = value
    return work.finish(
        layer_out, text_grad, grid_grad, cls, grads, rows_grad, bias_grad
    )


def on_device_plain(plan, *args):
    work, parts = Work(args[:7], plan.patch), plan.patch
    dims = work.dims
    weights, rows, bias = fetch_plain(args[7:14], args[14], args[15])
    rows = jnp.pad(rows, ((0, -rows.shape[0] % 8), (0, 0)))
    grids = trade(cut_grids(work.turn, work.image_grid, parts))

    def source(g):
        return Source(plan, GATHER[g], None, [weights[w] for w in GATHER[g]])

    (qkv, probs, ctx), _ = self_forward(dims, source(0), work.text, rows, work.lengths)
    (kv, patches), _ = cross_keys(dims, source(1), grids, work.cls, rows, work.count)
    total_one, hidden_one, query, cross_probs, cross_ctx, total_two = cross_forward(
        dims, work.text, ctx, kv, work.mask(), weights[OUT], weights[CQ], weights[COUT], rows
    )
    layer_out, hidden_two, act, low_three, grad_pre, grad_two, low_two, sum_ffn, sum_pre = ffn_both(
        dims, source(2), total_two, work.cot, rows, bias[None]
    )
    grad_query, grad_kv, sum_attend = cross_attend_back(
        dims, low_two, query, kv, cross_probs, weights[COUT]
    )
    *grids, cls, grad_one, low_one, sum_one = cross_project_back(
        dims, grad_two, grad_query, grad_kv, total_one, weights[CQ], weights[CKV], rows, parts, work.part
    )
    grad_qkv, sum_self = self_attend_back(dims, low_one, qkv, probs, weights[OUT])
    text_grad = self_project_back(dims, grad_one, grad_qkv, weights[QKV])
    flat_kv = grad_kv.reshape(-1, grad_kv.shape[2])
    factors = [
        (work.text, grad_qkv),
        (ctx, low_one),
        (hidden_one, grad_query),
        (patches.reshape(-1, work.vis), flat_kv),
        (cross_ctx, low_two),
        (hidden_two, grad_pre),
        (act, low_three),
    ]
    grads = [reduce_plain(dot_l(a, b).astype(BF16)) for a, b in factors]
    sums = rows_of([sum_self, sum_attend, sum_one, sum_ffn])
    small = reduce_small_plain(sums, sum_pre[0])
    grid_grad = place_grids(work.turn, work.micro, work.items, trade(grids))
    return work.finish(layer_out, text_grad, grid_grad, cls, grads, *small)


def solution(mesh):
    dp, patch = mesh.shape["dp"], mesh.shape["patch"]
    both = P(None, ("dp", "patch"), None)
    weight = P("dp", "patch")

    def run(*args):
        shards = [(w.shape[0] // dp, w.shape[1] // patch) for w in args[7:14]]
        plan = Plan(dp, patch, shards)
        return jax.shard_map(
            functools.partial(on_device if plan.fast else on_device_plain, plan),
            mesh=mesh,
            in_specs=(
                both,
                P(None, "dp", "patch", None),
                both,
                P(None, ("dp", "patch")),
                P(None, ("dp", "patch")),
                P(None, ("dp", "patch"), None, None),
                both,
            )
            + (weight,) * 7
            + (P(None, "dp"), P("dp")),
            out_specs=(both, both, P(None, "dp", "patch", None), both)
            + (weight,) * 7
            + (P(None, "dp"), P("dp")),
            check_vma=False,
        )(*args)

    return run
```

```python
import functools

import jax
import jax.numpy as jnp
from jax import lax
from jax.experimental import pallas as pl
from jax.experimental.pallas import tpu as pltpu
from jax.sharding import PartitionSpec as P

HEAD = 64
EPS = 1e-06
NEG = -1e30
BF16 = jnp.bfloat16
F32 = jnp.float32
AXES = ("dp", "patch")
VMEM_SPEC = pl.BlockSpec(memory_space=pltpu.VMEM)
SMEM_SPEC = pl.BlockSpec(memory_space=pltpu.SMEM)
PARAMS = pltpu.CompilerParams(vmem_limit_bytes=62 * 2**20)

QKV, OUT, CQ, CKV, COUT, FIN, FOUT = range(7)
ROWS = 13
EXTRA = 16
TOGETHER = 6
PART = 768
GATHER = ((QKV,), (OUT, CQ, CKV, COUT), (FIN, FOUT))
REDUCE = ((QKV, OUT), (CQ, CKV, COUT), (FIN, FOUT))


class Plan:
    def __init__(self, dp, patch, shards):
        self.dp, self.patch = dp, patch
        self.zs = dp // 2
        self.devices = dp * patch
        self.chunk = shards[OUT][1] * 2
        self.half = [s[0] // 2 for s in shards]
        self.cols = [s[1] for s in shards]
        self.chunks = [s[1] * 2 // self.chunk for s in shards]
        self.full = [(s[0] * dp, s[1] * patch) for s in shards]
        self.fast = (
            dp % 2 == 0
            and self.zs & (self.zs - 1) == 0
            and patch == 4
            and all(h % 16 == 0 for h in self.half)
            and all(s[1] * 2 % self.chunk == 0 for s in shards)
            and self.chunk % 128 == 0
            and shards[FIN][1] * patch // dp <= self.chunk
        )

    def rows(self, group):
        return sum(self.half[w] * self.chunks[w] for w in group)

    def flip(self, pick):
        return [(i, i ^ pick(i)) for i in range(self.devices)]

    def core(self):
        return self.flip(lambda i: 1)

    def first(self):
        return self.flip(lambda i: 4 if i % 2 == 0 else 2)

    def second(self):
        return self.flip(lambda i: 2 if i % 2 == 0 else 4)

    def along_z(self, k):
        return self.flip(lambda i: 8 * k)


def send(value, perm):
    return lax.ppermute(value, AXES, perm)


def coords():
    dp, patch = lax.axis_index("dp"), lax.axis_index("patch")
    return jnp.stack([dp // 2, dp % 2, patch // 2, patch % 2]).astype(jnp.int32)


def piece_rows(group, plan):
    at, found = 0, []
    for w in group:
        for j in range(plan.chunks[w]):
            found.append((w, j, at))
            at += plan.half[w]
    return found


def group_starts(plan):
    starts, at = [], 0
    for group in GATHER:
        starts.append(at)
        at += plan.rows(group)
    return starts, at


def pack_split(plan, where, shards):
    _, total = group_starts(plan)
    wide = plan.chunk // 2

    def body(where_ref, *refs):
        shard_refs, (own_ref, send_ref, turned) = list(refs[:7]), refs[7:]
        core = where_ref[3]
        turned[...] = shard_refs[FOUT][...].T
        shard_refs[FOUT] = turned
        at = 0
        for group in GATHER:
            for w in group:
                high = plan.half[w]
                for b in range(plan.chunks[w]):
                    cut = slice(b * wide, (b + 1) * wide)
                    own_ref[at : at + high, :] = shard_refs[w][pl.ds(core * high, high), cut]
                    send_ref[at : at + high, :] = shard_refs[w][
                        pl.ds((1 - core) * high, high), cut
                    ]
                    at += high

    shape = jax.ShapeDtypeStruct((total, wide), BF16)
    return pl.pallas_call(
        body,
        out_shape=(shape, shape),
        in_specs=[SMEM_SPEC] + [VMEM_SPEC] * 7,
        out_specs=(VMEM_SPEC, VMEM_SPEC),
        scratch_shapes=[pltpu.VMEM(shards[FOUT].shape, BF16)],
        compiler_params=PARAMS,
        name="pack_split",
    )(where, *shards[:FOUT], shards[FOUT].T)


def pack_join(plan, where, own, got):
    starts, total = group_starts(plan)
    wide = plan.chunk // 2

    def body(where_ref, own_ref, got_ref, *unit_refs):
        core = where_ref[3]

        def fill(low_ref, high_ref):
            for g, group in enumerate(GATHER):
                at = starts[g]
                for w in group:
                    high, count = plan.half[w], plan.chunks[w]
                    for j in range(count):
                        pair = []
                        for b in (2 * j, 2 * j + 1):
                            src = low_ref if b < count else high_ref
                            row = at + (b % count) * high
                            pair.append(src[row : row + high, :])
                        to = at - starts[g] + j * high
                        unit_refs[g][to : to + high, :] = jnp.concatenate(pair, axis=1)
                    at += count * high

        @pl.when(core == 0)
        def _():
            fill(own_ref, got_ref)

        @pl.when(core == 1)
        def _():
            fill(got_ref, own_ref)

    return pl.pallas_call(
        body,
        out_shape=tuple(jax.ShapeDtypeStruct((plan.rows(g), plan.chunk), BF16) for g in GATHER),
        in_specs=[SMEM_SPEC, VMEM_SPEC, VMEM_SPEC],
        out_specs=(VMEM_SPEC,) * len(GATHER),
        compiler_params=PARAMS,
        name="pack_join",
    )(where, own, got)


class Gathering:
    def __init__(self, plan, unit):
        self.plan, self.held = plan, [unit]

    def along_z(self, *steps):
        self.held += [send(self.held[0], self.plan.along_z(k)) for k in steps]

    def first(self):
        stack = jnp.stack(self.held)
        self.held = [stack, send(stack, self.plan.first())]

    def second(self):
        side = [send(part, self.plan.second()) for part in self.held]
        self.held += side + [send(part, self.plan.core()) for part in self.held]

    def core(self):
        self.held += [send(part, self.plan.core()) for part in self.held[2:4]]


def each_place(plan, group, where_ref, visit):
    z, x, y, core = (where_ref[i] for i in range(4))
    for other in range(2):
        half = core ^ other
        for second in range(2):
            for first in range(2):
                x_at = x ^ jnp.where(half == 0, first, second)
                y_at = y ^ jnp.where(half == 0, second, first)
                for k in range(plan.zs):
                    place = ((z ^ k) * 2 + x_at) * 2 + half
                    for w, j, row in piece_rows(group, plan):
                        high = plan.half[w]
                        to_row = pl.multiple_of(place * high, 16)
                        visit(other, second, first, k, row, w, j, to_row, y_at, high)


def add_low(one, two):
    return (one.astype(F32) + two.astype(F32)).astype(BF16)


class Reducing:
    def __init__(self, plan, group, where, stacks, twice=False, extra=0):
        self.plan, self.group, self.where = plan, group, where
        self.twice, self.extra = twice, extra
        self.held = list(stacks)
        self.steps = [self.core, self.second] + [self.again] * twice
        self.steps += [self.first, self.near_z, self.far_z, self.split, self.join]

    def advance(self):
        self.held = list(self.steps.pop(0)(*self.held))

    def core(self, keep, give):
        return keep, send(give, self.plan.core())

    def second(self, keep, got):
        ends = (2, 3, 4) if self.twice else (2, 4)
        gives = [add_low(keep[a:b], got[a:b]) for a, b in zip(ends, ends[1:])]
        gives[0] = send(gives[0], self.plan.second())
        return add_low(keep[:2], got[:2]), *gives

    def again(self, keep, got, give):
        return keep, got, send(give, self.plan.second())

    def first(self, keep, *got):
        near, far = (got[0], got[1][0]) if self.twice else (got[0][:1], got[0][1])
        give = add_low(keep[1], far)
        return add_low(keep[0], near[0]), send(give, self.plan.first())

    def near_z(self, keep, got):
        plan, slots = self.plan, [add_low(keep[k], got[k]) for k in range(self.plan.zs)]
        for k in range(1, plan.zs // 2 + 1):
            slots[k] = send(slots[k], plan.along_z(k))
        return slots

    def far_z(self, *slots):
        plan, slots = self.plan, list(slots)
        for k in range(plan.zs // 2 + 1, plan.zs):
            slots[k] = send(slots[k], plan.along_z(k))
        return slots

    def split(self, *parts):
        own, give, *rest = unpack_split(self.plan, self.group, self.where, parts, self.extra)
        return own, send(give, self.plan.core()), *rest

    def join(self, own, got, *rest):
        return *unpack_join(self.plan, self.group, self.where, own, got), *rest


def fence(chains, values):
    flat, tree = jax.tree.flatten([values, [chain.held for chain in chains]])
    values, held = jax.tree.unflatten(tree, lax.optimization_barrier(flat))
    for chain, arrays in zip(chains, held):
        chain.held = arrays
    return values


def unpack_split(plan, group, where, parts, extra):
    rows, wide = plan.rows(group), plan.chunk // 2
    count = len(parts)

    def body(where_ref, *refs):
        part_refs, (own_ref, give_ref) = refs[:count], refs[count : count + 2]
        core = where_ref[3]
        if extra:
            value = sum(p[rows : rows + EXTRA, :].astype(F32) for p in part_refs)
            refs[-2][...] = value[:ROWS, : refs[-2].shape[1]]
            refs[-1][...] = value[ROWS, : refs[-1].shape[0]]

        def fill(low_ref, high_ref):
            at = 0
            for w in group:
                high, count = plan.half[w], plan.chunks[w]
                for j in range(count):
                    row = at + j * high
                    value = sum(p[row : row + high, :].astype(F32) for p in part_refs)
                    for b in (2 * j, 2 * j + 1):
                        dst = low_ref if b < count else high_ref
                        to = at + (b % count) * high
                        cut = (b - 2 * j) * wide
                        dst[to : to + high, :] = value[:, cut : cut + wide]
                at += count * high

        @pl.when(core == 0)
        def _():
            fill(own_ref, give_ref)

        @pl.when(core == 1)
        def _():
            fill(give_ref, own_ref)

    shape = jax.ShapeDtypeStruct((rows, wide), F32)
    return pl.pallas_call(
        body,
        out_shape=(shape, shape)
        + (
            jax.ShapeDtypeStruct((ROWS, plan.full[OUT][1] // plan.dp), F32),
            jax.ShapeDtypeStruct((plan.full[FIN][1] // plan.dp,), F32),
        )
        * extra,
        in_specs=[SMEM_SPEC] + [VMEM_SPEC] * len(parts),
        out_specs=(VMEM_SPEC,) * (2 + 2 * extra),
        compiler_params=PARAMS,
        name="unpack_split",
    )(where, *parts)


def unpack_join(plan, group, where, own, got):
    wide = plan.chunk // 2
    turned = [w == FOUT for w in group]

    def body(where_ref, own_ref, got_ref, *refs):
        core = where_ref[3]
        at = 0
        for n, w in enumerate(group):
            out_ref = refs[-1] if turned[n] else refs[n]
            high, count = plan.half[w], plan.chunks[w]
            own_rows = pl.ds(pl.multiple_of(core * high, 16), high)
            got_rows = pl.ds(pl.multiple_of((1 - core) * high, 16), high)
            for b in range(count):
                row, cut = at + b * high, slice(b * wide, (b + 1) * wide)
                out_ref[own_rows, cut] = own_ref[row : row + high, :]
                out_ref[got_rows, cut] = got_ref[row : row + high, :]
            at += count * high
            if turned[n]:
                refs[n][...] = out_ref[...].T

    shapes = [(2 * plan.half[w], plan.cols[w]) for w in group]
    done = pl.pallas_call(
        body,
        out_shape=tuple(
            jax.ShapeDtypeStruct(shape[::-1] if turn else shape, F32)
            for shape, turn in zip(shapes, turned)
        ),
        in_specs=[SMEM_SPEC, VMEM_SPEC, VMEM_SPEC],
        out_specs=(VMEM_SPEC,) * len(group),
        scratch_shapes=[pltpu.VMEM(shapes[-1], F32)],
        compiler_params=PARAMS,
        name="unpack_join",
    )(where, own, got)
    return [value.T if turn else value for value, turn in zip(done, turned)]


class GatheringSmall:
    def __init__(self, plan, where, vectors, bias):
        self.plan, self.where, self.shape = plan, where, vectors.shape
        flat = jnp.concatenate([vectors.reshape(-1), bias])
        self.size = flat.shape[0]
        self.held, self.bit = [jnp.pad(flat, (0, -self.size % 2048)).reshape(1, -1, 128)], 4

    def advance(self):
        every = jnp.concatenate(self.held)
        self.held = [every, send(every, self.plan.flip(lambda i: self.bit))]
        self.bit *= 2

    def result(self):
        plan, (count, part) = self.plan, self.shape
        while self.bit < plan.devices:
            self.advance()
        every = jnp.concatenate(self.held).reshape(plan.dp, -1)
        slot = jnp.arange(plan.dp, dtype=jnp.int32) ^ (self.where[0] * 2 + self.where[1])
        every = jnp.take(every, slot, axis=0)[:, : self.size].astype(F32)
        rows = every[:, : count * part].reshape(plan.dp, count, part)
        rows = rows.transpose(1, 0, 2).reshape(count, plan.dp * part)
        bias = every[:, count * part :].reshape(1, -1)
        return jnp.pad(rows, ((0, -count % 8), (0, 0))), bias


def fetch_plain(weights, vectors, bias):
    whole = [
        lax.all_gather(lax.all_gather(w, "dp", axis=0, tiled=True), "patch", axis=1, tiled=True)
        for w in weights
    ]
    rows = lax.all_gather(vectors, "dp", axis=1, tiled=True)
    return whole, rows.astype(F32), lax.all_gather(bias, "dp", axis=0, tiled=True).astype(F32)


def reduce_plain(grad):
    part = lax.psum_scatter(grad, "dp", scatter_dimension=0, tiled=True)
    return lax.psum_scatter(part, "patch", scatter_dimension=1, tiled=True).astype(F32)


def reduce_small_plain(rows, bias):
    rows = lax.psum_scatter(rows, "dp", scatter_dimension=1, tiled=True)
    bias = lax.psum_scatter(bias, "dp", scatter_dimension=0, tiled=True)
    return lax.psum(rows, "patch"), lax.psum(bias, "patch")


TAIL = (0.112528827, 0.117839666, 0.0706314405, 0.2046457425, -0.190499398, 0.3478185715, -0.201092832, 0.03812798145)


def dot(a, b):
    return lax.dot_general(a, b, (((1,), (0,)), ((), ())), preferred_element_type=F32)


def dot_t(a, b):
    return lax.dot_general(a, b, (((1,), (1,)), ((), ())), preferred_element_type=F32)


def dot_l(a, b):
    return lax.dot_general(a, b, (((0,), (0,)), ((), ())), preferred_element_type=F32)


def norm_parts(total):
    center = total - jnp.mean(total, -1, keepdims=True)
    spread = lax.rsqrt(jnp.mean(center * center, -1, keepdims=True) + EPS)
    return center * spread, spread


def norm_pull(grad, hat, spread, gain):
    scaled = grad * gain
    return spread * (
        scaled
        - jnp.mean(scaled, -1, keepdims=True)
        - hat * jnp.mean(scaled * hat, -1, keepdims=True)
    )


def gelu_parts(x):
    bell = jnp.exp(-0.5 * (x * x))
    t = 1.0 / (1.0 + (0.4 * 0.5**0.5) * jnp.abs(x))
    tail = jnp.full_like(t, TAIL[-1])
    for c in TAIL[-2::-1]:
        tail = tail * t + c
    tail = tail * (t * bell)
    return jnp.where(x < 0.0, tail, 1.0 - tail), bell


def col_sum(value):
    return jnp.sum(value.astype(F32), 0, keepdims=True)


def soft(scores):
    grown = jnp.exp(scores - jnp.max(scores, 0, keepdims=True))
    return grown * (1.0 / jnp.sum(grown, 0, keepdims=True))


def soft_pull(probs, grad):
    return probs * (grad - jnp.sum(probs * grad, 0, keepdims=True))


def spread_heads(value, low, high):
    return jnp.concatenate([value * low, value * high], 0)


def join_heads(value):
    count = value.shape[1] // 2
    value = jnp.concatenate([value[:HEAD, :count], value[HEAD:, count:]], 0)
    return value.astype(BF16).T


def lane_masks():
    lane = lax.broadcasted_iota(jnp.int32, (1, 2 * HEAD), 1)
    low = (lane < HEAD).astype(F32)
    return low.astype(BF16), (1.0 - low).astype(BF16)


def whole(shape):
    return pl.BlockSpec(
        shape, lambda i: (0,) * len(shape), pipeline_mode=pl.Buffered(1)
    )


def summed(shape):
    return pl.BlockSpec(shape, lambda i: (0,) * len(shape))


def tiled(shape):
    return pl.BlockSpec(shape, lambda i: (i,) + (0,) * (len(shape) - 1))


def spec_of(shape, dtype):
    return jax.ShapeDtypeStruct(shape, dtype)


def call(body, name, steps, ins, outs, flops, scratch=()):
    out_shape = tuple(shape for shape, _ in outs)
    moved = sum(a.size * a.dtype.itemsize for a, _ in ins)
    moved += sum(o.size * jnp.dtype(o.dtype).itemsize for o in out_shape)
    return pl.pallas_call(
        body,
        grid=(steps,),
        out_shape=out_shape,
        in_specs=[spec for _, spec in ins],
        out_specs=tuple(spec for _, spec in outs),
        scratch_shapes=list(scratch),
        compiler_params=PARAMS,
        cost_estimate=pl.CostEstimate(
            flops=int(flops), bytes_accessed=int(moved), transcendentals=0
        ),
        name=name,
    )(*[a for a, _ in ins])


class Source:
    def __init__(self, plan, group, where, given, kept=True):
        self.plan, self.group, self.pieces, self.given = plan, group, plan.fast, given
        self.outs, self.scratch = [], []
        if not self.pieces:
            self.ins = [(w, whole(w.shape)) for w in given]
            return
        self.ins = [(where, SMEM_SPEC)] + [(part, whole(part.shape)) for part in given]
        if kept:
            self.outs = [(spec_of(plan.full[w], BF16), summed(plan.full[w])) for w in group]
        else:
            self.scratch = [pltpu.VMEM(plan.full[w], BF16) for w in group]

    def open(self, in_refs, out_refs):
        if not self.pieces:
            return list(in_refs)
        where_ref, parts = in_refs[0], in_refs[1:]
        full = dict(zip(self.group, out_refs))
        plan = self.plan

        def visit(other, second, first, k, row, w, j, to_row, to_y, high):
            to_col = pl.multiple_of(to_y * (plan.full[w][1] // 2) + j * plan.chunk, 128)
            part = parts[other * 4 + second * 2 + first]
            full[w][pl.ds(to_row, high), pl.ds(to_col, plan.chunk)] = part[k, row : row + high, :]

        @pl.when(pl.program_id(0) == 0)
        def _():
            each_place(plan, self.group, where_ref, visit)

        return list(out_refs)

    def split(self, done):
        if not self.pieces:
            return done, self.given
        return done[: -len(self.group)], done[-len(self.group) :]


def self_forward(dims, source, text, rows, lengths):
    d, items, length, group = dims.d, dims.items, dims.length, dims.group
    pairs, tokens, block = d // (2 * HEAD), items * length, group * length
    scale = HEAD ** (-0.5)

    n_in = len(source.ins)

    def body(len_ref, x_ref, row_ref, *refs):
        qkv_ref, prob_ref, ctx_ref = refs[n_in : n_in + 3]
        (wqkv_ref,) = source.open(refs[:n_in], refs[n_in + 3 :])
        step = pl.program_id(0)
        low, high = lane_masks()
        x = x_ref[...]
        for part, bias in ((0, 0), (1, None), (2, 1)):
            cut = slice(part * d, (part + 1) * d)
            value = dot(x, wqkv_ref[:, cut])
            if bias is not None:
                value = value + row_ref[bias : bias + 1, :]
            qkv_ref[:, cut] = value.astype(BF16)
        place = lax.broadcasted_iota(jnp.int32, (length, 1), 0)
        for i in range(group):
            ok = place < len_ref[step * group + i]
            r = slice(i * length, (i + 1) * length)
            for start in range(0, pairs, TOGETHER):
                many = range(start, min(start + TOGETHER, pairs))
                qs, ks, vs = (
                    [qkv_ref[r, part * d + p * 128 : part * d + (p + 1) * 128] for p in many]
                    for part in range(3)
                )
                probs, contexts = pairs_attend(qs, ks, vs, ok, low, high, scale)
                for n, p in enumerate(many):
                    prob_ref[i, p] = probs[n]
                    ctx_ref[r, p * 128 : (p + 1) * 128] = contexts[n]
    done = call(
        body,
        "self_forward",
        items // group,
        [(lengths, SMEM_SPEC), (text, tiled((block, d))), (rows, whole(rows.shape))] + source.ins,
        [
            (spec_of((tokens, 3 * d), BF16), tiled((block, 3 * d))),
            (spec_of((items, pairs, length, 2 * length), BF16), tiled((group, pairs, length, 2 * length))),
            (spec_of((tokens, d), BF16), tiled((block, d))),
        ]
        + source.outs,
        2 * tokens * d * 5 * d,
    )
    return source.split(done)


def cross_keys(dims, source, grids, cls, rows, count):
    d, items, group = dims.d, dims.items, dims.group
    part, vis, parts = grids[0].shape[0] // items, cls.shape[2], len(grids)
    n_in = len(source.ins)

    def body(*refs):
        grid_refs, cls_ref, row_ref = refs[:parts], refs[parts], refs[parts + 1]
        refs = refs[parts + 2 :]
        kv_ref, patch_ref = refs[n_in : n_in + 2]
        _, _, wckv_ref, _ = source.open(refs[:n_in], refs[n_in + 2 :])
        for i in range(group):
            for k in range(parts):
                patch_ref[i, k * part : (k + 1) * part, :] = grid_refs[k][i * part : (i + 1) * part, :]
            rest = jnp.zeros((count - parts * part - 1, vis), BF16)
            patch_ref[i, parts * part :, :] = jnp.concatenate([cls_ref[i], rest], 0)
        patch = patch_ref[...].reshape(group * count, vis)
        keys = dot(patch, wckv_ref[:, :d]).astype(BF16)
        kv_ref[:, :, :d] = keys.reshape(group, count, d)
        values = (dot(patch, wckv_ref[:, d:]) + row_ref[6:7, :]).astype(BF16)
        kv_ref[:, :, d:] = values.reshape(group, count, d)

    done = call(
        body,
        "cross_keys",
        items // group,
        [(grid, tiled((group * part, vis))) for grid in grids]
        + [(cls, tiled((group, 1, vis))), (rows, whole(rows.shape))]
        + source.ins,
        [
            (spec_of((items, count, 2 * d), BF16), tiled((group, count, 2 * d))),
            (spec_of((items, count, vis), BF16), tiled((group, count, vis))),
        ]
        + source.outs,
        2 * items * count * vis * 2 * d,
    )
    return source.split(done)


def cross_forward(dims, text, self_ctx, kv, mask, w_out, w_cq, w_cout, rows):
    d, items, length, group = dims.d, dims.items, dims.length, dims.group
    pairs, tokens, block = d // (2 * HEAD), items * length, group * length
    count = kv.shape[1]
    scale = HEAD ** (-0.5)

    def body(x_ref, self_ref, kv_ref, mask_ref, wout_ref, wcq_ref, wcout_ref, row_ref,
             one_ref, h_ref, cq_ref, prob_ref, ctx_ref, two_ref):
        low, high = lane_masks()
        total = x_ref[...].astype(F32) + dot(self_ref[...], wout_ref[...]) + row_ref[2:3, :]
        one_ref[...] = total
        hat, _ = norm_parts(total)
        hidden = hat * row_ref[3:4, :] + row_ref[4:5, :]
        h_ref[...] = hidden.astype(BF16)
        cq_ref[...] = (dot(h_ref[...], wcq_ref[...]) + row_ref[5:6, :]).astype(BF16)
        for i in range(group):
            ok = mask_ref[i].astype(F32) > 0.5
            ok = jnp.concatenate([ok, ok], 1)
            r = slice(i * length, (i + 1) * length)
            for start in range(0, pairs, TOGETHER):
                many = range(start, min(start + TOGETHER, pairs))
                cs = [slice(p * 128, (p + 1) * 128) for p in many]
                probs, contexts = pairs_attend(
                    [cq_ref[r, c] for c in cs],
                    [kv_ref[i, :, c] for c in cs],
                    [kv_ref[i, :, d + p * 128 : d + (p + 1) * 128] for p in many],
                    ok,
                    low,
                    high,
                    scale,
                )
                for n, p in enumerate(many):
                    prob_ref[i, p] = probs[n]
                    ctx_ref[r, cs[n]] = contexts[n]
        two_ref[...] = hidden + dot(ctx_ref[...], wcout_ref[...]) + row_ref[7:8, :]

    return call(
        body,
        "cross_forward",
        items // group,
        [
            (text, tiled((block, d))),
            (self_ctx, tiled((block, d))),
            (kv, tiled((group, count, 2 * d))),
            (mask, tiled((group, count, length))),
            (w_out, whole((d, d))),
            (w_cq, whole((d, d))),
            (w_cout, whole((d, d))),
            (rows, whole(rows.shape)),
        ],
        [
            (spec_of((tokens, d), F32), tiled((block, d))),
            (spec_of((tokens, d), BF16), tiled((block, d))),
            (spec_of((tokens, d), BF16), tiled((block, d))),
            (spec_of((items, pairs, count, 2 * length), BF16), tiled((group, pairs, count, 2 * length))),
            (spec_of((tokens, d), BF16), tiled((block, d))),
            (spec_of((tokens, d), F32), tiled((block, d))),
        ],
        2 * tokens * d * 6 * d,
    )


def ffn_both(dims, source, total_two, cotangent, rows, bias):
    d, items, length, group = dims.d, dims.items, dims.length, dims.group
    tokens, block, ff = items * length, group * length, bias.shape[1]
    piece = d
    n_in = len(source.ins)

    def body(tot_ref, cot_ref, row_ref, bias_ref, *refs):
        (out_ref, h_ref, act_ref, glow_ref, pre_ref, two_ref, twolow_ref, sum_ref, bsum_ref) = refs[
            n_in : n_in + 9
        ]
        slope_ref = refs[n_in + 9]
        win_ref, wout_ref = source.open(refs[:n_in], refs[n_in + 10 :])

        @pl.when(pl.program_id(0) == 0)
        def _():
            sum_ref[...] = jnp.zeros_like(sum_ref)
            bsum_ref[...] = jnp.zeros_like(bsum_ref)

        hat_two, spread_two = norm_parts(tot_ref[...])
        hidden = hat_two * row_ref[8:9, :] + row_ref[9:10, :]
        h_ref[...] = hidden.astype(BF16)
        total = hidden + row_ref[10:11, :]
        cuts = [slice(at, at + piece) for at in range(0, ff, piece)]

        def into(cut):
            return dot(h_ref[...], win_ref[:, cut]) + bias_ref[:, cut]

        def middle(pre, cut):
            under, bell = gelu_parts(pre)
            act_ref[:, cut] = (pre * under).astype(BF16)
            slope_ref[:, cut] = under + (pre * 0.3989422804014327) * bell

        for cut in cuts:
            middle(into(cut), cut)
            total = total + dot(act_ref[:, cut], wout_ref[cut, :])
        hat, spread = norm_parts(total)
        gain = row_ref[11:12, :]
        out_ref[...] = hat * gain + row_ref[12:13, :]
        cot = cot_ref[...].astype(F32)
        grad = norm_pull(cot, hat, spread, gain)
        glow_ref[...] = grad.astype(BF16)
        sum_ref[0:1, :] += col_sum(cot * hat)
        sum_ref[1:2, :] += col_sum(cot)
        sum_ref[2:3, :] += col_sum(glow_ref[...])
        for cut in cuts:
            pre = (dot_t(glow_ref[...], wout_ref[cut, :]) * slope_ref[:, cut]).astype(BF16)
            pre_ref[:, cut] = pre
            bsum_ref[0:1, cut] += col_sum(pre)
            grad = grad + dot_t(pre, win_ref[:, cut])
        two = norm_pull(grad, hat_two, spread_two, row_ref[8:9, :])
        two_ref[...] = two
        low = two.astype(BF16)
        twolow_ref[...] = low
        sum_ref[3:4, :] += col_sum(grad * hat_two)
        sum_ref[4:5, :] += col_sum(grad)
        sum_ref[5:6, :] += col_sum(low)

    return call(
        body,
        "ffn_both",
        items // group,
        [
            (total_two, tiled((block, d))),
            (cotangent, tiled((block, d))),
            (rows, whole(rows.shape)),
            (bias, whole(bias.shape)),
        ]
        + source.ins,
        [
            (spec_of((tokens, d), F32), tiled((block, d))),
            (spec_of((tokens, d), BF16), tiled((block, d))),
            (spec_of((tokens, ff), BF16), tiled((block, ff))),
            (spec_of((tokens, d), BF16), tiled((block, d))),
            (spec_of((tokens, ff), BF16), tiled((block, ff))),
            (spec_of((tokens, d), F32), tiled((block, d))),
            (spec_of((tokens, d), BF16), tiled((block, d))),
            (spec_of((8, d), F32), summed((8, d))),
            (spec_of((8, ff), F32), summed((8, ff))),
        ],
        8 * tokens * d * ff,
        [pltpu.VMEM((block, ff), F32)] + source.scratch,
    )


def pairs_pull(qs, ks, vs, outs, probs, low, high, scale):
    outs = [spread_heads(out, low, high) for out in outs]
    grads = [dot_t(v, out) for v, out in zip(vs, outs)]
    scores = [soft_pull(p.astype(F32), grad).astype(BF16) for p, grad in zip(probs, grads)]
    grad_q = [dot(k.T, score) for k, score in zip(ks, scores)]
    grad_k = [dot(score, spread_heads(q, low, high)) for q, score in zip(qs, scores)]
    grad_v = [dot(p, out) for p, out in zip(probs, outs)]
    return (
        [join_heads(value * scale) for value in grad_q],
        [(value * scale).astype(BF16) for value in grad_k],
        [value.astype(BF16) for value in grad_v],
    )


def pairs_attend(qs, ks, vs, ok, low, high, scale):
    scores = [dot_t(k, spread_heads(q, low, high)) for q, k in zip(qs, ks)]
    probs = [soft(jnp.where(ok, score * scale, NEG)).astype(BF16) for score in scores]
    contexts = [dot(v.T, p) for v, p in zip(vs, probs)]
    return probs, [join_heads(context) for context in contexts]


def cross_attend_back(dims, grad_low, query, kv, probs, w_cout):
    d, items, length, group = dims.d, dims.items, dims.length, dims.group
    pairs, tokens, block = d // (2 * HEAD), items * length, group * length
    count = kv.shape[1]
    scale = HEAD ** (-0.5)

    def body(glow_ref, q_ref, kv_ref, prob_ref, wcout_ref, gq_ref, gkv_ref, sum_ref, ctx_ref):
        @pl.when(pl.program_id(0) == 0)
        def _():
            sum_ref[...] = jnp.zeros_like(sum_ref)

        low, high = lane_masks()
        ctx_ref[...] = dot_t(glow_ref[...], wcout_ref[...]).astype(BF16)
        for i in range(group):
            r = slice(i * length, (i + 1) * length)
            for start in range(0, pairs, TOGETHER):
                many = range(start, min(start + TOGETHER, pairs))
                cs = [slice(p * 128, (p + 1) * 128) for p in many]
                cvs = [slice(d + p * 128, d + (p + 1) * 128) for p in many]
                done = pairs_pull(
                    [q_ref[r, c] for c in cs],
                    [kv_ref[i, :, c] for c in cs],
                    [kv_ref[i, :, c] for c in cvs],
                    [ctx_ref[r, c] for c in cs],
                    [prob_ref[i, p] for p in many],
                    low,
                    high,
                    scale,
                )
                for c, cv, grad_q, grad_k, grad_v in zip(cs, cvs, *done):
                    gq_ref[r, c] = grad_q
                    gkv_ref[i, :, c] = grad_k
                    gkv_ref[i, :, cv] = grad_v
        sum_ref[0:1, :] += col_sum(gq_ref[...])
        sum_ref[1:2, :] += col_sum(gkv_ref[:, :, d:].reshape(group * count, d))

    return call(
        body,
        "cross_attend_back",
        items // group,
        [
            (grad_low, tiled((block, d))),
            (query, tiled((block, d))),
            (kv, tiled((group, count, 2 * d))),
            (probs, tiled((group, pairs, count, 2 * length))),
            (w_cout, whole((d, d))),
        ],
        [
            (spec_of((tokens, d), BF16), tiled((block, d))),
            (spec_of((items, count, 2 * d), BF16), tiled((group, count, 2 * d))),
            (spec_of((8, d), F32), summed((8, d))),
        ],
        2 * tokens * d * 4 * d,
        [pltpu.VMEM((block, d), BF16)],
    )


def cross_project_back(dims, grad_two, grad_query, grad_kv, total_one, w_cq, w_ckv, rows, parts, part):
    d, items, length, group = dims.d, dims.items, dims.length, dims.group
    tokens, block = items * length, group * length
    count, vis = grad_kv.shape[1], w_ckv.shape[0]

    def body(g_ref, gq_ref, gkv_ref, tot_ref, wcq_ref, wckv_ref, row_ref, *refs):
        grid_refs, (cls_ref, one_ref, onelow_ref, sum_ref) = refs[:parts], refs[parts:]

        @pl.when(pl.program_id(0) == 0)
        def _():
            sum_ref[...] = jnp.zeros_like(sum_ref)

        grad = g_ref[...] + dot_t(gq_ref[...], wcq_ref[...])
        values = [dot_t(gkv_ref[i], wckv_ref[...]) for i in range(group)]
        for i, value in enumerate(values):
            for k in range(parts):
                grid_refs[k][i * part : (i + 1) * part, :] = value[k * part : (k + 1) * part, :].astype(BF16)
            cls_ref[i] = value[parts * part : parts * part + 1, :]
        hat, spread = norm_parts(tot_ref[...])
        one = norm_pull(grad, hat, spread, row_ref[3:4, :])
        one_ref[...] = one
        one_low = one.astype(BF16)
        onelow_ref[...] = one_low
        sum_ref[0:1, :] += col_sum(grad * hat)
        sum_ref[1:2, :] += col_sum(grad)
        sum_ref[2:3, :] += col_sum(one_low)

    return call(
        body,
        "cross_project_back",
        items // group,
        [
            (grad_two, tiled((block, d))),
            (grad_query, tiled((block, d))),
            (grad_kv, tiled((group, count, 2 * d))),
            (total_one, tiled((block, d))),
            (w_cq, whole((d, d))),
            (w_ckv, whole((vis, 2 * d))),
            (rows, whole(rows.shape)),
        ],
        [(spec_of((items * part, vis), BF16), tiled((group * part, vis)))] * parts
        + [
            (spec_of((items, 1, vis), F32), tiled((group, 1, vis))),
            (spec_of((tokens, d), F32), tiled((block, d))),
            (spec_of((tokens, d), BF16), tiled((block, d))),
            (spec_of((8, d), F32), summed((8, d))),
        ],
        2 * tokens * d * d + 2 * items * count * vis * 2 * d,
    )


def self_attend_back(dims, grad_low, qkv, probs, w_out):
    d, items, length, group = dims.d, dims.items, dims.length, dims.group
    pairs, tokens, block = d // (2 * HEAD), items * length, group * length
    scale = HEAD ** (-0.5)

    def body(glow_ref, qkv_ref, prob_ref, wout_ref, gqkv_ref, sum_ref, ctx_ref):
        @pl.when(pl.program_id(0) == 0)
        def _():
            sum_ref[...] = jnp.zeros_like(sum_ref)

        low, high = lane_masks()
        ctx_ref[...] = dot_t(glow_ref[...], wout_ref[...]).astype(BF16)
        for i in range(group):
            r = slice(i * length, (i + 1) * length)
            for start in range(0, pairs, TOGETHER):
                many = range(start, min(start + TOGETHER, pairs))
                cuts = [
                    [slice(part * d + p * 128, part * d + (p + 1) * 128) for p in many]
                    for part in range(3)
                ]
                done = pairs_pull(
                    *[[qkv_ref[r, c] for c in cuts[part]] for part in range(3)],
                    [ctx_ref[r, c] for c in cuts[0]],
                    [prob_ref[i, p] for p in many],
                    low,
                    high,
                    scale,
                )
                for part in range(3):
                    for c, value in zip(cuts[part], done[part]):
                        gqkv_ref[r, c] = value
        sum_ref[0:1, :] += col_sum(gqkv_ref[:, :d])
        sum_ref[1:2, :] += col_sum(gqkv_ref[:, 2 * d :])

    return call(
        body,
        "self_attend_back",
        items // group,
        [
            (grad_low, tiled((block, d))),
            (qkv, tiled((block, 3 * d))),
            (probs, tiled((group, pairs, length, 2 * length))),
            (w_out, whole((d, d))),
        ],
        [
            (spec_of((tokens, 3 * d), BF16), tiled((block, 3 * d))),
            (spec_of((8, d), F32), summed((8, d))),
        ],
        2 * tokens * d * 4 * d,
        [pltpu.VMEM((block, d), BF16)],
    )


def self_project_back(dims, grad_one, grad_qkv, w_qkv):
    d, items, length, group = dims.d, dims.items, dims.length, dims.group
    tokens, block = items * length, group * length

    def body(g_ref, gqkv_ref, wqkv_ref, text_ref):
        text_ref[...] = g_ref[...] + dot_t(gqkv_ref[...], wqkv_ref[...])

    return call(
        body,
        "self_project_back",
        items // group,
        [
            (grad_one, tiled((block, d))),
            (grad_qkv, tiled((block, 3 * d))),
            (w_qkv, whole((d, 3 * d))),
        ],
        [(spec_of((tokens, d), F32), tiled((block, d)))],
        2 * tokens * d * 3 * d,
    )[0]


def cut_grids(turn, image_grid, parts):
    micro, items, part, vis = image_grid.shape
    each = items // parts

    def body(turn_ref, grid_ref, *out_refs):
        def fill(own):
            value = jnp.swapaxes(grid_ref[0], 0, 1)
            for s in range(parts):
                mine = value[s * each : (s + 1) * each]
                out_refs[s ^ own][...] = mine.reshape(each * part, vis)

        for own in range(parts):
            pl.when(turn_ref[0] == own)(functools.partial(fill, own))

    return call(
        body,
        "cut_grids",
        micro,
        [
            (turn, SMEM_SPEC),
            (image_grid.transpose(0, 2, 1, 3), tiled((1, part, items, vis))),
        ],
        [(spec_of((micro * each * part, vis), BF16), tiled((each * part, vis)))] * parts,
        0,
    )


def place_grids(turn, micro, items, pieces):
    part, vis = pieces[0].shape[0] // items, pieces[0].shape[1]
    each, parts = items // micro, len(pieces)

    def body(turn_ref, *refs):
        def fill(own):
            value = [
                refs[s ^ own][...].astype(F32).reshape(each, part, vis) for s in range(parts)
            ]
            refs[-1][0] = jnp.swapaxes(jnp.concatenate(value, 0), 0, 1)

        for own in range(parts):
            pl.when(turn_ref[0] == own)(functools.partial(fill, own))

    shape = (micro, part, each * parts, vis)
    done = call(
        body,
        "place_grids",
        micro,
        [(turn, SMEM_SPEC)] + [(p, tiled((each * part, vis))) for p in pieces],
        [(spec_of(shape, F32), tiled((1,) + shape[1:]))],
        0,
    )[0]
    return done.transpose(0, 2, 1, 3)


SUMS = ((0, 0, 2), (2, 2, 1), (2, 0, 2), (1, 0, 2), (3, 5, 1), (3, 3, 2), (3, 2, 1), (3, 0, 2))


def rows_of(sums):
    return jnp.concatenate([sums[n][row : row + count] for n, row, count in SUMS])


def weight_grads(plan, group, where, factors, extra=()):
    high_rows = max(plan.full[w][0] for w in group)
    wide = max(plan.full[w][1] for w in group)
    flat = [a for pair in factors for a in pair]
    count, base = len(flat), plan.rows(group)

    def first_bytes(n):
        left, right = factors[n]
        return left.shape[0] * min(left.shape[1], PART) + right.size

    order = sorted(range(len(group)), key=first_bytes)
    begins = {w: row for w, j, row in reversed(piece_rows(group, plan))}
    parts = [
        [slice(at, at + PART) for at in range(0, left.shape[1], PART)]
        if left.shape[1] > 2 * PART and left.shape[1] % PART == 0
        else [slice(0, left.shape[1])]
        for left, _ in factors
    ]

    def body(where_ref, *refs):
        far, outs = refs[:count], refs[count + len(extra) : count + len(extra) + 2]
        scratch = refs[count + len(extra) + 2 :]
        near, stack_refs = scratch[:count], scratch[count : count + 2]
        made, in_sems, out_sems = scratch[count + 2 : count + 5]
        lefts, rights, used = {}, {}, 0
        for n in order:
            rights[n] = pltpu.make_async_copy(far[2 * n + 1], near[2 * n + 1], in_sems.at[used])
            used += 1
            for m, cut in enumerate(parts[n]):
                lefts[n, m] = pltpu.make_async_copy(
                    far[2 * n].at[:, cut], near[2 * n].at[:, cut], in_sems.at[used]
                )
                used += 1
            rights[n].start()
            for m in range(len(parts[n])):
                lefts[n, m].start()
        flushes = []

        def flush(low, high):
            for stack_ref, out in zip(stack_refs, outs):
                copy = pltpu.make_async_copy(
                    stack_ref.at[:, :, low:high, :],
                    out.at[:, :, low:high, :],
                    out_sems.at[len(flushes)],
                )
                copy.start()
                flushes.append(copy)

        if extra:
            add_extra(
                where_ref, refs[count : count + len(extra)], stack_refs, *scratch[count + 5 :]
            )
            flush(base, base + EXTRA)
        for n in order:
            w, (left, right) = group[n], near[2 * n : 2 * n + 2]
            cols = plan.full[w][1]
            rights[n].wait()
            for m, cut in enumerate(parts[n]):
                lefts[n, m].wait()
                for at in range(cut.start, cut.stop, 256):
                    value = dot_l(left[:, at : at + 256], right[...])
                    made[at : at + 256, :cols] = value.astype(BF16)

            def visit(other, second, first, k, row, w_at, j, to_row, to_y, high):
                if w_at == w:
                    col = pl.multiple_of(to_y * (cols // 2) + j * plan.chunk, 128)
                    stack_refs[other][second * 2 + first, k, row : row + high, :] = made[
                        pl.ds(to_row, high), pl.ds(col, plan.chunk)
                    ]

            each_place(plan, group, where_ref, visit)
            flush(begins[w], begins[w] + plan.half[w] * plan.chunks[w])
        for copy in flushes:
            copy.wait()

    def add_extra(where_ref, sum_refs, stack_refs, table, lines):
        width = lines.shape[1] // plan.dp
        step = plan.full[FIN][1] // plan.dp
        at = 0
        for n, row, many in SUMS:
            lines[at : at + many, :] = sum_refs[n][row : row + many, :]
            at += many
        table[...] = jnp.zeros_like(table)
        for n in range(plan.dp):
            table[n, :ROWS, :width] = lines[:ROWS, n * width : (n + 1) * width]
            table[n, ROWS : ROWS + 1, :step] = sum_refs[-1][0:1, n * step : (n + 1) * step]
        z, x, _, core = (where_ref[i] for i in range(4))
        for other in range(2):
            for second in range(2):
                for first in range(2):
                    x_at = x ^ jnp.where((core ^ other) == 0, first, second)
                    for k in range(plan.zs):
                        value = table[(z ^ k) * 2 + x_at].astype(BF16)
                        stack_refs[other][second * 2 + first, k, base : base + EXTRA, :] = value

    high = base + (EXTRA if extra else 0)
    shape = jax.ShapeDtypeStruct((4, plan.zs, high, plan.chunk), BF16)
    flops = sum(2 * a.shape[0] * a.shape[1] * b.shape[1] for a, b in factors)
    moved = sum(a.size * 2 for a in flat) + 2 * shape.size * 2
    table = []
    if extra:
        table.append(pltpu.VMEM((plan.dp, EXTRA, plan.chunk), F32))
        table.append(pltpu.VMEM((EXTRA, plan.full[OUT][1]), F32))
    return pl.pallas_call(
        body,
        out_shape=(shape,) * 2,
        in_specs=[SMEM_SPEC]
        + [pl.BlockSpec(memory_space=pl.ANY)] * count
        + [VMEM_SPEC] * len(extra),
        out_specs=(pl.BlockSpec(memory_space=pl.ANY),) * 2,
        scratch_shapes=[pltpu.VMEM(a.shape, BF16) for a in flat]
        + [pltpu.VMEM(shape.shape, BF16)] * 2
        + [
            pltpu.VMEM((high_rows, wide), BF16),
            pltpu.SemaphoreType.DMA((len(group) + sum(len(cuts) for cuts in parts),)),
            pltpu.SemaphoreType.DMA((2 * len(group) + 2,)),
        ]
        + table,
        compiler_params=PARAMS,
        cost_estimate=pl.CostEstimate(flops=flops, bytes_accessed=moved, transcendentals=0),
        name="weight_grads",
    )(where, *flat, *extra)


class Dims:
    def __init__(self, d, items, length):
        self.d, self.items, self.length = d, items, length
        self.group = 2 if items % 2 == 0 else 1


def cross_mask(lengths, counts, boxes, length, count):
    place = jnp.arange(length, dtype=jnp.int32)[None, :]
    boxed = (counts[:, None] > 0) & (place < lengths[:, None])
    phrase = jnp.where(boxed, place * counts[:, None] // lengths[:, None], 0)
    chosen = phrase[:, None, :] == jnp.arange(boxes.shape[1], dtype=jnp.int32)[None, :, None]
    inside = jnp.einsum(
        "ijp,ijt->ipt",
        (boxes > 0).astype(BF16),
        chosen.astype(BF16),
        preferred_element_type=F32,
    )
    grid_ok = jnp.where(boxed[:, None, :], inside, 1.0).astype(BF16)
    items, real = grid_ok.shape[:2]
    own = jnp.ones((items, 1, length), BF16)
    return jnp.concatenate([grid_ok, own, jnp.zeros((items, count - real - 1, length), BF16)], 1)


def trade(pieces):
    parts = lax.axis_size("patch")
    return [pieces[0]] + [
        lax.ppermute(pieces[k], "patch", [(i, i ^ k) for i in range(parts)])
        for k in range(1, len(pieces))
    ]


class Work:
    def __init__(self, args, parts):
        (self.text_in, self.image_grid, self.image_cls, lengths, counts, boxes, cot) = args
        self.parts = parts
        self.micro, d = self.text_in.shape[0], self.text_in.shape[2]
        self.items = lengths.size
        self.text, self.cot = self.text_in.reshape(-1, d), cot.reshape(-1, d)
        self.lengths, self.counts = lengths.reshape(-1), counts.reshape(-1)
        self.boxes = boxes.reshape((self.items,) + boxes.shape[2:])
        self.dims = Dims(d, self.items, self.text.shape[0] // self.items)
        self.turn = lax.axis_index("patch").astype(jnp.int32).reshape(1)
        self.part, self.vis = self.image_grid.shape[2:]
        self.each = self.items // self.micro
        self.count = -(-(parts * self.part + 1) // 16) * 16
        self.cls = self.image_cls.reshape(self.items, 1, self.vis)

    def mask(self):
        boxes = self.boxes.reshape(self.items, -1, self.parts, self.part)
        order = jnp.arange(self.parts, dtype=jnp.int32) ^ self.turn[0]
        boxes = jnp.take(boxes, order, axis=2).reshape(self.boxes.shape)
        return cross_mask(self.lengths, self.counts, boxes, self.dims.length, self.count)

    def finish(self, layer_out, text_grad, grid_grad, cls, grads, rows_grad, bias_grad):
        return (
            layer_out.reshape(self.text_in.shape),
            text_grad.reshape(self.text_in.shape),
            grid_grad,
            cls.reshape(self.image_cls.shape),
            *grads,
            rows_grad,
            bias_grad,
        )


def on_device(plan, *args):
    work, shards, vectors, ffn_bias = Work(args[:7], plan.patch), args[7:14], args[14], args[15]
    dims, where, parts = work.dims, coords(), plan.patch

    own, give = pack_split(plan, where, shards)
    units = pack_join(plan, where, own, send(give, plan.core()))
    grids = list(cut_grids(work.turn, work.image_grid, parts))
    vectors, bias, grids, units = lax.optimization_barrier((vectors, ffn_bias, grids, units))
    one, two, three = (Gathering(plan, unit) for unit in units)
    small = GatheringSmall(plan, where, vectors, bias)

    def source(g, gather, kept=True):
        return Source(plan, GATHER[g], where, gather.held, kept)

    one.along_z(*range(1, plan.zs))
    grids[2] = trade(grids[:3])[2]
    small.advance()
    grids = fence([one, two, small], grids)
    one.first()
    two.along_z(*range(1, plan.zs // 2 + 1))
    grids[3] = trade(grids)[3]
    small.advance()
    grids = fence([one, two, three, small], grids)
    one.second()
    two.along_z(*range(plan.zs // 2 + 1, plan.zs))
    rows, bias = small.result()
    rows, bias, grids = fence([one, two, three], [rows, bias, grids])
    one.core()
    two.first()
    three.along_z(*range(1, plan.zs // 2 + 1))
    (qkv, probs, ctx), (w_qkv,) = self_forward(dims, source(0, one), work.text, rows, work.lengths)
    (ctx,) = fence([two, three], [ctx])
    two.second()
    three.along_z(*range(plan.zs // 2 + 1, plan.zs))
    grids[1] = trade(grids[:2])[1]
    mask = work.mask()
    ctx, grids, mask = fence([two, three], [ctx, grids, mask])
    two.core()
    three.first()
    (kv, patches), (w_out, w_cq, w_ckv, w_cout) = cross_keys(
        dims, source(1, two), grids, work.cls, rows, work.count
    )
    kv, ctx = fence([three], [kv, ctx])
    three.second()
    total_one, hidden_one, query, cross_probs, cross_ctx, total_two = cross_forward(
        dims, work.text, ctx, kv, mask, w_out, w_cq, w_cout, rows
    )
    total_two = fence([three], total_two)
    three.core()
    layer_out, hidden_two, act, low_three, grad_pre, grad_two, low_two, sum_ffn, sum_pre = ffn_both(
        dims, source(2, three, kept=False), total_two, work.cot, rows, bias
    )

    reduces = {}

    def reduce(g, factors, twice=False, extra=()):
        stacks = weight_grads(plan, REDUCE[g], where, factors, extra)
        reduces[g] = Reducing(plan, REDUCE[g], where, stacks, twice, 1 if extra else 0)

    def hold(*values, on=None):
        chains = [reduces[g] for g in (reduces if on is None else on)]
        return fence(chains, list(values))

    def go(*groups):
        for g in groups:
            reduces[g].advance()

    reduce(2, [(hidden_two, grad_pre), (act, low_three)], twice=True)
    (low_two,) = hold(low_two)
    go(2)
    grad_query, grad_kv, sum_attend = cross_attend_back(dims, low_two, query, kv, cross_probs, w_cout)
    grad_query, grad_kv = hold(grad_query, grad_kv)
    go(2)
    reduces[2].held[0], grad_query, grad_kv = lax.optimization_barrier(
        (reduces[2].held[0], grad_query, grad_kv)
    )
    reduce(
        1,
        [
            (hidden_one, grad_query),
            (patches.reshape(-1, work.vis), grad_kv.reshape(-1, grad_kv.shape[2])),
            (cross_ctx, low_two),
        ],
    )
    grad_query, grad_kv = hold(grad_query, grad_kv)
    go(2, 1)
    *grids, cls, grad_one, low_one, sum_one = cross_project_back(
        dims, grad_two, grad_query, grad_kv, total_one, w_cq, w_ckv, rows, parts, work.part
    )
    low_one, *grids = hold(low_one, *grids)
    go(2)
    grids[1] = trade(grids[:2])[1]
    grad_qkv, sum_self = self_attend_back(dims, low_one, qkv, probs, w_out)
    grad_qkv, *grids = hold(grad_qkv, *grids)
    go(1, 2)
    sums = (sum_self, sum_attend, sum_one, sum_ffn, sum_pre)
    reduce(0, [(work.text, grad_qkv), (ctx, low_one)], extra=sums)
    (grad_qkv,) = hold(grad_qkv)
    go(0, 1, 2)
    grids[2] = trade(grids[:3])[2]
    text_grad = self_project_back(dims, grad_one, grad_qkv, w_qkv)
    cls = cls.reshape(work.image_cls.shape)
    text_grad, cls, *grids = hold(text_grad, cls, *grids)
    go(0, 1, 1)
    hold()
    go(0, 2)
    grids = hold(*grids)
    go(0, 0, 1, 2)
    grids[3] = trade(grids)[3]
    go(1)
    grids = hold(*grids)
    go(0)
    grid_grad = place_grids(work.turn, work.micro, work.items, grids)
    go(0)
    *done, rows_grad, bias_grad = reduces[0].held
    grads = [None] * 7
    for g, group in enumerate(REDUCE):
        for w, value in zip(group, done if g == 0 else reduces[g].held):
            grads[w] = value
    return work.finish(
        layer_out, text_grad, grid_grad, cls, grads, rows_grad, bias_grad
    )


def on_device_plain(plan, *args):
    work, parts = Work(args[:7], plan.patch), plan.patch
    dims = work.dims
    weights, rows, bias = fetch_plain(args[7:14], args[14], args[15])
    rows = jnp.pad(rows, ((0, -rows.shape[0] % 8), (0, 0)))
    grids = trade(cut_grids(work.turn, work.image_grid, parts))

    def source(g):
        return Source(plan, GATHER[g], None, [weights[w] for w in GATHER[g]])

    (qkv, probs, ctx), _ = self_forward(dims, source(0), work.text, rows, work.lengths)
    (kv, patches), _ = cross_keys(dims, source(1), grids, work.cls, rows, work.count)
    total_one, hidden_one, query, cross_probs, cross_ctx, total_two = cross_forward(
        dims, work.text, ctx, kv, work.mask(), weights[OUT], weights[CQ], weights[COUT], rows
    )
    layer_out, hidden_two, act, low_three, grad_pre, grad_two, low_two, sum_ffn, sum_pre = ffn_both(
        dims, source(2), total_two, work.cot, rows, bias[None]
    )
    grad_query, grad_kv, sum_attend = cross_attend_back(
        dims, low_two, query, kv, cross_probs, weights[COUT]
    )
    *grids, cls, grad_one, low_one, sum_one = cross_project_back(
        dims, grad_two, grad_query, grad_kv, total_one, weights[CQ], weights[CKV], rows, parts, work.part
    )
    grad_qkv, sum_self = self_attend_back(dims, low_one, qkv, probs, weights[OUT])
    text_grad = self_project_back(dims, grad_one, grad_qkv, weights[QKV])
    flat_kv = grad_kv.reshape(-1, grad_kv.shape[2])
    factors = [
        (work.text, grad_qkv),
        (ctx, low_one),
        (hidden_one, grad_query),
        (patches.reshape(-1, work.vis), flat_kv),
        (cross_ctx, low_two),
        (hidden_two, grad_pre),
        (act, low_three),
    ]
    grads = [reduce_plain(dot_l(a, b).astype(BF16)) for a, b in factors]
    sums = rows_of([sum_self, sum_attend, sum_one, sum_ffn])
    small = reduce_small_plain(sums, sum_pre[0])
    grid_grad = place_grids(work.turn, work.micro, work.items, trade(grids))
    return work.finish(layer_out, text_grad, grid_grad, cls, grads, *small)


def solution(mesh):
    dp, patch = mesh.shape["dp"], mesh.shape["patch"]
    both = P(None, ("dp", "patch"), None)
    weight = P("dp", "patch")

    def run(*args):
        shards = [(w.shape[0] // dp, w.shape[1] // patch) for w in args[7:14]]
        plan = Plan(dp, patch, shards)
        return jax.shard_map(
            functools.partial(on_device if plan.fast else on_device_plain, plan),
            mesh=mesh,
            in_specs=(
                both,
                P(None, "dp", "patch", None),
                both,
                P(None, ("dp", "patch")),
                P(None, ("dp", "patch")),
                P(None, ("dp", "patch"), None, None),
                both,
            )
            + (weight,) * 7
            + (P(None, "dp"), P("dp")),
            out_specs=(both, both, P(None, "dp", "patch", None), both)
            + (weight,) * 7
            + (P(None, "dp"), P("dp")),
            check_vma=False,
        )(*args)

    return run
```
